32 devices in a mesh: dp: 16 (over z, x, core), tensor: 2 (over y).
Axes of the slice: x: 2, y: 2, z: 4, core: 2. Of those that a mesh axis runs over, the one named last changes fastest.
Arguments:
- tokens: bfloat16 [32768, 768], P(('dp', 'tensor')), may hold values from -6 to 6
- segments: int32 [32, 1024], P('dp'), may hold values from 0 to 2, never falling along the last dimension, each value on 1 to 512 neighbouring positions
- projections: bfloat16 [4, 768, 768], P(None, 'dp', 'tensor'), may hold values from -0.21875 to 0.21875
- combiner: bfloat16 [768, 768], P('tensor', 'dp'), may hold values from -1.75 to 1.75
- offsets: float32 [3, 768], P(None, 'tensor'), may hold values from -3 to 3
- sameness: float32 [2, 768], P(None, 'tensor'), may hold values from -5 to 5
- postbias: float32 [768], replicated, may hold values from -3 to 3
- scaling: float32 [768], replicated, may hold values from 0.5 to 1.5
- centring: float32 [768], replicated, may hold values from -3 to 3
- widener: bfloat16 [768, 3072], P('dp', 'tensor'), may hold values from -0.21875 to 0.21875
- widebias: float32 [3072], P('tensor'), may hold values from -3 to 3
- narrower: bfloat16 [3072, 768], P('tensor', 'dp'), may hold values from -0.109375 to 0.109375
- narrowbias: float32 [768], replicated, may hold values from -3 to 3
- rescale: float32 [768], replicated, may hold values from 0.5 to 1.5
- recentre: float32 [768], replicated, may hold values from -3 to 3
- cotangent: bfloat16 [16384, 768], P(('dp', 'tensor')), may hold values from -6 to 6
Outputs:
- result: bfloat16 [16384, 768], P(('dp', 'tensor'))
- tokens_grad: float32 [32768, 768], P(('dp', 'tensor'))
- projections_grad: float32 [4, 768, 768], P(None, 'dp', 'tensor')
- combiner_grad: float32 [768, 768], P('tensor', 'dp')
- offsets_grad: float32 [3, 768], P(None, 'tensor')
- sameness_grad: float32 [2, 768], P(None, 'tensor')
- postbias_grad: float32 [768], replicated
- scaling_grad: float32 [768], replicated
- centring_grad: float32 [768], replicated
- widener_grad: float32 [768, 3072], P('dp', 'tensor')
- widebias_grad: float32 [3072], P('tensor')
- narrower_grad: float32 [3072, 768], P('tensor', 'dp')
- narrowbias_grad: float32 [768], replicated
- rescale_grad: float32 [768], replicated
- recentre_grad: float32 [768], replicated
The draws below stay inside these ranges and needn't reach their ends.
Inputs may be any that keep to these rules, and one draw needn't show every extreme that they name: `segments`: segment numbers never fall along a sequence; each segment holds 1 to 512 tokens.
All inputs are finite; a program needn't handle non-finite values.
Results may differ from the reference program's by a relative error of at most 0.015.
The reference program's roundings to bfloat16 on the way count: a program that leaves them out, or rounds other values in their place, can miss the bound.
Values may be sent and summed in bfloat16 or wider, within the bound.
No kernel may reach another device: no remote copies, remote signals or barrier semaphores. Data moves between devices by JAX's collectives and lax.ppermute only.
A program may use at most 256 MiB of HBM per device.

```python
import math
import jax
import jax.numpy as jnp
import numpy as np
from jax import lax

D = 768
H = 12
DH = 64
FF = 3072
LEN = 1024
SEGS = 3
HD = 768
SEQS = 32
TOKENS = 32768
POOLED = 16384


def block_levels(key, extent, pieces, least, high):
    gain, own = 1.0, jax.random.fold_in(key, 6)
    for dim, blocks in pieces:
        steps = jnp.exp(jax.random.uniform(jax.random.fold_in(own, dim), (blocks,), jnp.float32, least / len(pieces), high / len(pieces)))
        gain = gain * jnp.repeat(steps, extent[dim] // blocks).reshape([-1 if axis == dim else 1 for axis in range(len(extent))])
    return gain


def split_up(count, total, most, skew):
    portions = [(1 << 20) // math.isqrt(rank ** skew) + 1 for rank in range(2, count + 1)]
    rest, counts = total - most - (count - 1), [1] * (count - 1)
    while rest > 0:
        movable = [i for i in range(count - 1) if counts[i] < most]
        pool, remaining = sum([portions[i] for i in movable]), rest
        for i in movable:
            extra = min(most - counts[i], max(1, remaining * portions[i] // pool), rest)
            counts[i] = counts[i] + extra
            rest = rest - extra
    return np.array([most] + counts)


def uneven_parts(rng, count, total, limit, lean):
    if count == 2:
        one = jax.random.randint(rng, (), max(1, total - limit), min(limit, total - 1) + 1)
        return jnp.stack([one, total - one])
    lengths = jnp.asarray(split_up(count, total, limit, lean), jnp.int32)
    twos = (count - 1) // 2
    giver, taker = lengths[1:1 + 2 * twos:2], lengths[2:2 + 2 * twos:2]
    slack = jnp.minimum(giver - 1, limit - taker)
    moved = jax.random.randint(jax.random.fold_in(rng, 1), (twos,), 0, 1 << 20) % (slack + 1)
    lengths = lengths.at[1:1 + 2 * twos:2].set(giver - moved).at[2:2 + 2 * twos:2].set(taker + moved)
    return lengths[jax.random.permutation(jax.random.fold_in(rng, 2), count)]


def gaussian(rng, dims, spread, most, pieces=(), kind=jnp.bfloat16):
    gain = block_levels(rng, dims, pieces, -0.22, 0.18) if pieces else 1.0
    entries = jax.random.normal(rng, dims, jnp.float32) * spread * gain
    return jnp.minimum(jnp.maximum(entries, -most), most).astype(kind)


def setup_inputs(seed: int = 0) -> dict:
    key_of = jax.random.split(jax.random.key(seed), 17)
    tokens = gaussian(key_of[0], (TOKENS, D), 1.0, 6.0, ((0, 32),))
    segments = jax.vmap(lambda own: jnp.searchsorted(jnp.cumsum(uneven_parts(own, SEGS, LEN, LEN // 2, 0)), jnp.arange(LEN), side="right"))(jax.random.split(key_of[1], SEQS)).reshape((SEQS, LEN)).astype(jnp.int32)
    projections = gaussian(key_of[2], (4, D, HD), D ** -0.5, 0.21875, ((1, 16), (2, 2)))
    combiner = gaussian(key_of[3], (HD, D), (max(HD // 64, 1)) ** -0.5, 1.75, ((0, 2), (1, 16)))
    offsets = gaussian(key_of[4], (3, HD), 0.5, 3.0, ((1, 2),), jnp.float32)
    sameness = gaussian(key_of[5], (2, HD), 1.0, 5.0, ((1, 2),), jnp.float32)
    postbias = gaussian(key_of[6], (D,), 0.5, 3.0, (), jnp.float32)
    scaling = jnp.clip(1.0 + 0.1 * jax.random.normal(key_of[7], (D,), jnp.float32), 0.5, 1.5)
    centring = gaussian(key_of[8], (D,), 0.5, 3.0, (), jnp.float32)
    widener = gaussian(key_of[9], (D, FF), D ** -0.5, 0.21875, ((0, 16), (1, 2)))
    widebias = gaussian(key_of[10], (FF,), 0.5, 3.0, ((0, 2),), jnp.float32)
    narrower = gaussian(key_of[11], (FF, D), FF ** -0.5, 0.109375, ((0, 2), (1, 16)))
    narrowbias = gaussian(key_of[12], (D,), 0.5, 3.0, (), jnp.float32)
    rescale = jnp.clip(1.0 + 0.1 * jax.random.normal(key_of[13], (D,), jnp.float32), 0.5, 1.5)
    recentre = gaussian(key_of[14], (D,), 0.5, 3.0, (), jnp.float32)
    cotangent = gaussian(key_of[15], (POOLED, D), 1.0, 6.0, ((0, 32),))
    return dict(tokens=tokens, segments=segments, projections=projections, combiner=combiner, offsets=offsets, sameness=sameness, postbias=postbias, scaling=scaling, centring=centring, widener=widener, widebias=widebias, narrower=narrower, narrowbias=narrowbias, rescale=rescale, recentre=recentre, cotangent=cotangent)


highest = lax.Precision.HIGHEST
epsilon = 1e-05

@jax.custom_vjp
def low(v):
    return lax.optimization_barrier(v.astype(jnp.bfloat16)).astype(jnp.float32)

@jax.custom_vjp
def low_back(v):
    return v

def low_keep(v):
    return (low(v), None)

def low_pass(kept, grad):
    return (grad,)

def back_keep(v):
    return (v, None)

def back_low(kept, grad):
    return (low(grad),)
low.defvjp(low_keep, low_pass)
low_back.defvjp(back_keep, back_low)

def position_table(length, model_width):
    row_index = jnp.arange(2 * length, dtype=jnp.float32)
    offset = length - row_index
    half_width = model_width // 2
    frequency = jnp.exp(jnp.arange(half_width, dtype=jnp.float32) * (-math.log(10000.0) / half_width))
    angles = offset[:, None] * frequency[None, :]
    return jnp.concatenate([jnp.sin(angles), jnp.cos(angles)], axis=1)

def rel_shift(dense_score, length):
    head_count, row_count, _ = dense_score.shape
    flat_rows = dense_score.reshape(head_count, row_count * 2 * length)[:, length:]
    return flat_rows.reshape(head_count, row_count, 2 * length - 2)[:, :, :length]

def normalize(values_in, gain_row, shift_row):
    row_mean = lax.optimization_barrier(jnp.mean(values_in, axis=-1, keepdims=True))
    centred = values_in - row_mean
    variance = lax.optimization_barrier(jnp.mean(centred * centred, axis=-1, keepdims=True))
    return centred * lax.rsqrt(variance + epsilon) * gain_row + shift_row

def forward(params, tokens, segments):
    projections, combiner, offsets, sameness, postbias, scaling, centring, widener, widebias, narrower, narrowbias, rescale, recentre = params
    token_count, model_width = tokens.shape
    seq_count = segments.shape[0]
    half_len = LEN // 2
    width_all = H * DH
    paired = tokens.reshape(token_count // 2, 2, model_width)
    pooled = lax.optimization_barrier(jnp.mean(paired, axis=1))
    query_rows = low_back(low(jnp.dot(low(pooled), projections[0], precision=highest)))
    key_rows = low_back(low(jnp.dot(tokens, projections[1], precision=highest)))
    value_rows = low_back(low(jnp.dot(tokens, projections[2], precision=highest)))
    phase_rows = low(position_table(LEN, model_width))
    relative = low(jnp.dot(phase_rows, projections[3], precision=highest))
    rel_heads = relative.reshape(2 * LEN, H, DH)
    score_scale = DH ** (-0.5)

    def attend(block_items):
        query_seq, key_seq, value_seq, seg_ids = block_items
        query_three = query_seq.reshape(half_len, H, DH)
        content = low(query_three + offsets[0].reshape(H, DH))
        position = low(query_three + offsets[1].reshape(H, DH))
        typed_query = query_three + offsets[2].reshape(H, DH)
        content_score = jnp.einsum('qhd,khd->hqk', content, key_seq.reshape(LEN, H, DH), precision=highest)
        dense_score = jnp.einsum('qhd,vhd->hqv', position, rel_heads, precision=highest)
        type_table = jnp.einsum('qhd,chd->hqc', typed_query, sameness.reshape(2, H, DH), precision=highest)
        same_mask = seg_ids[0::2][:, None] == seg_ids[None, :]
        type_score = jnp.where(same_mask[None], type_table[:, :, 1:2], type_table[:, :, 0:1])
        scores = low_back((content_score + rel_shift(dense_score, LEN) + type_score) * score_scale)
        probability = low(jax.nn.softmax(scores, axis=-1))
        mixed_seq = jnp.einsum('hqk,khd->qhd', probability, value_seq.reshape(LEN, H, DH), precision=highest)
        return mixed_seq.reshape(half_len, width_all)
    mixed_rows = lax.map(jax.checkpoint(attend), (query_rows.reshape(seq_count, half_len, width_all), key_rows.reshape(seq_count, LEN, width_all), value_rows.reshape(seq_count, LEN, width_all), segments))
    mixed_rows = low_back(low(mixed_rows.reshape(token_count // 2, width_all)))
    branch = low_back(jnp.dot(mixed_rows, combiner, precision=highest) + postbias)
    first = normalize(pooled + branch, scaling, centring)
    hidden_pre = low_back(jnp.dot(low(first), widener, precision=highest) + widebias)
    hidden_act = low(jax.nn.gelu(hidden_pre, approximate=True))
    second = low_back(jnp.dot(hidden_act, narrower, precision=highest) + narrowbias)
    return normalize(first + second, rescale, recentre)

def reference(tokens, segments, projections, combiner, offsets, sameness, postbias, scaling, centring, widener, widebias, narrower, narrowbias, rescale, recentre, cotangent):
    params = (projections.astype(jnp.float32), combiner.astype(jnp.float32), offsets.astype(jnp.float32), sameness.astype(jnp.float32), postbias.astype(jnp.float32), scaling.astype(jnp.float32), centring.astype(jnp.float32), widener.astype(jnp.float32), widebias.astype(jnp.float32), narrower.astype(jnp.float32), narrowbias.astype(jnp.float32), rescale.astype(jnp.float32), recentre.astype(jnp.float32))

    def run_layer(params_in, tokens_in):
        return forward(params_in, tokens_in, segments)
    output_rows, pull_back = jax.vjp(run_layer, params, tokens.astype(jnp.float32))
    param_grads, tokens_grad = pull_back(cotangent.astype(jnp.float32))
    return (output_rows.astype(jnp.bfloat16), tokens_grad, param_grads[0], param_grads[1], param_grads[2], param_grads[3], param_grads[4], param_grads[5], param_grads[6], param_grads[7], param_grads[8], param_grads[9], param_grads[10], param_grads[11], param_grads[12])
```

```python
from functools import partial
import math

import jax
import jax.numpy as jnp
from jax import lax
from jax.experimental import pallas as pl
from jax.experimental.pallas import tpu as pltpu
from jax.sharding import PartitionSpec as P

epsilon = 1e-05
bf16=jnp.bfloat16; f32=jnp.float32
DH=64
AUG=16
TN=(((0,),(0,)),((),()))
NT=(((1,),(1,)),((),()))
NN=(((1,),(0,)),((),()))

def split3(u):
    row=lax.broadcasted_iota(jnp.int32,u.shape,0)
    hi=u.astype(bf16).astype(f32)
    r1=u-hi
    mid=r1.astype(bf16).astype(f32)
    lo=r1-mid
    return jnp.where(row<3,hi,jnp.where(row<6,mid,jnp.where(row<9,lo,0.0))).astype(bf16)

def fwd_kernel(q_ref,k_ref,v_ref,r_ref,s_ref,segq_ref,segk_ref,p_ref,m_ref,c_sc,k_sc,*,tq):
    nq=q_ref.shape[1]; nk=k_ref.shape[1]
    q=q_ref[...].astype(f32)
    sm=s_ref[...]
    c_sc[:DH]=(q+sm[:,0:1]).astype(bf16)*jnp.asarray(0.125,bf16)
    pos=(q+sm[:,1:2]).astype(bf16)*jnp.asarray(0.125,bf16)
    typed=q+sm[:,2:3]
    t0=jnp.sum(typed*sm[:,3:4],axis=0,keepdims=True)*0.125
    t1=jnp.sum(typed*sm[:,4:5],axis=0,keepdims=True)*0.125
    kind=lax.rem(lax.broadcasted_iota(jnp.int32,(AUG,nq),0),3)
    c_sc[DH:]=split3(jnp.where(segq_ref[...]==kind,t1,t0))
    k_sc[:DH]=k_ref[...]
    rowk=lax.broadcasted_iota(jnp.int32,(AUG,nk),0)
    k_sc[DH:]=jnp.where((segk_ref[...]==lax.rem(rowk,3)) & (rowk<9),1.0,0.0).astype(bf16)
    w=nk+2*tq
    for b in range(nq//tq):
        i0=b*tq
        w0=nk-2*i0-2*tq
        c=lax.dot_general(c_sc[:,i0:i0+tq],k_sc[...],TN,preferred_element_type=f32)
        d=lax.dot_general(pos[:,i0:i0+tq],r_ref[:,w0:w0+w],TN,preferred_element_type=f32)
        d=pltpu.roll(d,w-2*tq,1,stride=2,stride_axis=0)
        s=c+d[:,:nk]
        mx=jnp.max(s,axis=1,keepdims=True)
        e=jnp.exp(s-mx)
        l=jnp.sum(e,axis=1,keepdims=True)
        p=(e*(1.0/l)).astype(bf16)
        p_ref[i0:i0+tq,:]=p
        m_ref[:,i0:i0+tq]=lax.dot_general(v_ref[...],p,NT,preferred_element_type=f32)

def attn_fwd(qT,kT,vT,relT,small,segq,segk,tq=128):
    hd,nq=qT.shape; nk=kT.shape[1]; heads=hd//DH
    return pl.pallas_call(partial(fwd_kernel,tq=tq),grid=(heads,),
        in_specs=[pl.BlockSpec((DH,nq),lambda h:(h,0)),pl.BlockSpec((DH,nk),lambda h:(h,0)),pl.BlockSpec((DH,nk),lambda h:(h,0)),
          pl.BlockSpec((DH,2*nk),lambda h:(h,0)),pl.BlockSpec((DH,small.shape[1]),lambda h:(h,0)),
          pl.BlockSpec((1,nq),lambda h:(0,0)),pl.BlockSpec((1,nk),lambda h:(0,0))],
        out_specs=[pl.BlockSpec((None,nq,nk),lambda h:(h,0,0)),pl.BlockSpec((DH,nq),lambda h:(h,0))],
        out_shape=[jax.ShapeDtypeStruct((heads,nq,nk),bf16),jax.ShapeDtypeStruct((hd,nq),f32)],
        scratch_shapes=[pltpu.VMEM((DH+AUG,nq),bf16),pltpu.VMEM((DH+AUG,nk),bf16)],
        compiler_params=pltpu.CompilerParams(vmem_limit_bytes=56<<20),name="attend")(qT,kT,vT,relT,small,segq,segk)

def bwd_kernel(q_ref,k_ref,v_ref,r_ref,s_ref,segq_ref,segk_ref,p_ref,m_ref,dm_ref,
               dq_ref,dk_ref,dv_ref,dr_ref,sg_ref,k_sc,v_sc,dm_sc,ds_sc,dg_sc,*,tq,first):
    nq=q_ref.shape[1]; nk=k_ref.shape[1]
    q=q_ref[...].astype(f32)
    sm=s_ref[...]
    content=(q+sm[:,0:1]).astype(bf16)*jnp.asarray(0.125,bf16)
    pos=(q+sm[:,1:2]).astype(bf16)*jnp.asarray(0.125,bf16)
    typed=q+sm[:,2:3]
    k_sc[:DH]=k_ref[...]
    rowk=lax.broadcasted_iota(jnp.int32,(AUG,nk),0)
    k_sc[DH:]=((segk_ref[...]==rowk)).astype(f32).astype(bf16)
    v_sc[:DH]=v_ref[...]
    v_sc[DH:]=jnp.where(rowk<3,1.0,0.0).astype(bf16)
    dm=dm_ref[...]
    dm_sc[:DH]=dm
    delta=-jnp.sum(dm.astype(f32)*m_ref[...],axis=0,keepdims=True)
    rowq=lax.broadcasted_iota(jnp.int32,(AUG,nq),0)
    hi=delta.astype(bf16).astype(f32); r1=delta-hi; mid=r1.astype(bf16).astype(f32); lo=r1-mid
    dm_sc[DH:]=jnp.where(rowq==0,hi,jnp.where(rowq==1,mid,jnp.where(rowq==2,lo,0.0))).astype(bf16)
    w=nk+2*tq
    flip=(lax.broadcasted_iota(jnp.int32,(tq,tq),0)+lax.broadcasted_iota(jnp.int32,(tq,tq),1)==tq-1).astype(f32).astype(bf16)
    def turn16(x):
        parts=[lax.dot_general(x[:,i:i+tq],flip,NN,preferred_element_type=f32) for i in range(0,nq,tq)]
        return jnp.concatenate(parts,axis=1).astype(bf16)
    def turn(x):
        hi=x.astype(bf16); r1=x-hi.astype(f32); mid=r1.astype(bf16); lo=(r1-mid.astype(f32)).astype(bf16)
        cat=jnp.concatenate([hi,mid,lo],axis=0)
        parts=[lax.dot_general(cat[:,i:i+tq],flip,NN,preferred_element_type=f32) for i in range(0,nq,tq)]
        y=jnp.concatenate(parts,axis=1)
        return y[:DH]+y[DH:2*DH]+y[2*DH:]
    dg_sc[...]=jnp.zeros_like(dg_sc)
    for b in range(nq//tq):
        i0=b*tq
        w0=nk-2*i0-2*tq
        dp=lax.dot_general(dm_sc[:,i0:i0+tq],v_sc[...],TN,preferred_element_type=f32)
        ds=p_ref[i0:i0+tq,:].astype(f32)*dp
        ds16=ds.astype(bf16)
        ds_sc[i0:i0+tq,:]=ds16
        back=lax.dot_general(flip,ds16,NN,preferred_element_type=f32)
        g=jnp.concatenate([back,jnp.zeros((tq,2*tq),f32)],axis=1)
        g=pltpu.roll(g,2,1,stride=2,stride_axis=0)
        dg_sc[i0:i0+tq,w0:w0+w]=g.astype(bf16)
    dv_ref[...]=lax.dot_general(dm,p_ref[...],NN,preferred_element_type=f32).astype(bf16)
    dk_ref[...]=lax.dot_general(content,ds_sc[...],NN,preferred_element_type=f32).astype(bf16)
    dc=lax.dot_general(k_sc[...],ds_sc[...],NT,preferred_element_type=f32)
    dpos=turn(lax.dot_general(r_ref[...],dg_sc[...],NT,preferred_element_type=f32))*0.125
    dr=lax.dot_general(turn16(pos),dg_sc[...],NN,preferred_element_type=f32)
    if first is None:
        dr_ref[...]=dr
    else:
        dr_ref[...]=first[0][...]+dr
    dcontent=dc[:DH]*0.125
    seg=dc[DH:]*0.125
    rows=lax.broadcasted_iota(jnp.int32,(AUG,nq),0)
    g1=jnp.sum(jnp.where(segq_ref[...]==rows,seg,0.0),axis=0,keepdims=True)
    g0=jnp.sum(seg,axis=0,keepdims=True)-g1
    dtyped=sm[:,3:4]*g0+sm[:,4:5]*g1
    dq_ref[...]=(dcontent+dpos+dtyped).astype(bf16)
    lane=lax.broadcasted_iota(jnp.int32,(DH,128),1)
    total=jnp.zeros((DH,128),f32)
    for n,val in enumerate((dcontent,dpos,dtyped,typed*g0,typed*g1)):
        total=jnp.where(lane==n,jnp.sum(val,axis=1,keepdims=True),total)
    if first is None:
        sg_ref[...]=total
    else:
        sg_ref[...]=first[1][...]+total

def bwd_kernel_first(*refs,tq):
    bwd_kernel(*refs,tq=tq,first=None)
def bwd_kernel_next(*refs,tq):
    bwd_kernel(*refs[:10],*refs[12:],tq=tq,first=refs[10:12])

def attn_bwd(qT,kT,vT,relT,small,segq,segk,probs,mixedT,dmixedT,carry=None,tq=128):
    hd,nq=qT.shape; nk=kT.shape[1]; heads=hd//DH
    row=lambda n: pl.BlockSpec((DH,n),lambda h:(h,0))
    ins=[row(nq),row(nk),row(nk),row(2*nk),row(small.shape[1]),pl.BlockSpec((1,nq),lambda h:(0,0)),pl.BlockSpec((1,nk),lambda h:(0,0)),
         pl.BlockSpec((None,nq,nk),lambda h:(h,0,0)),row(nq),row(nq)]
    args=[qT,kT,vT,relT,small,segq,segk,probs,mixedT,dmixedT]
    kern=bwd_kernel_first
    if carry is not None:
        ins+= [row(2*nk),row(128)]; args+=list(carry); kern=bwd_kernel_next
    return pl.pallas_call(partial(kern,tq=tq),grid=(heads,),in_specs=ins,
        out_specs=[row(nq),row(nk),row(nk),row(2*nk),row(128)],
        out_shape=[jax.ShapeDtypeStruct((hd,nq),bf16),jax.ShapeDtypeStruct((hd,nk),bf16),jax.ShapeDtypeStruct((hd,nk),bf16),
           jax.ShapeDtypeStruct((hd,2*nk),f32),jax.ShapeDtypeStruct((hd,128),f32)],
        scratch_shapes=[pltpu.VMEM((DH+AUG,nk),bf16),pltpu.VMEM((DH+AUG,nk),bf16),pltpu.VMEM((DH+AUG,nq),bf16),pltpu.VMEM((nq,nk),bf16),pltpu.VMEM((nq,2*nk),bf16)],
        compiler_params=pltpu.CompilerParams(vmem_limit_bytes=56<<20),name="attend_back")(*args)


def position_table(length, model_width):
    row_index = jnp.arange(2 * length, dtype=jnp.float32)
    offset = length - row_index
    half_width = model_width // 2
    frequency = jnp.exp(
        jnp.arange(half_width, dtype=jnp.float32) * (-math.log(10000.0) / half_width)
    )
    angles = offset[:, None] * frequency[None, :]
    return jnp.concatenate([jnp.sin(angles), jnp.cos(angles)], axis=1)


def normalize(values_in, gain_row, shift_row):
    row_mean = jnp.mean(values_in, axis=-1, keepdims=True)
    centred = values_in - row_mean
    variance = jnp.mean(centred * centred, axis=-1, keepdims=True)
    return centred * lax.rsqrt(variance + epsilon) * gain_row + shift_row


def pair_matrix(count):
    rows = lax.broadcasted_iota(jnp.int32, (count, 2 * count), 0)
    columns = lax.broadcasted_iota(jnp.int32, (count, 2 * count), 1)
    return jnp.where(columns // 2 == rows, 0.5, 0.0).astype(bf16)


def spread_pairs(grad_rows):
    halved = grad_rows[:, None, :] * 0.5
    return jnp.broadcast_to(halved, (grad_rows.shape[0], 2, grad_rows.shape[1])).reshape(
        2 * grad_rows.shape[0], grad_rows.shape[1]
    )


def swap(piece):
    return lax.ppermute(piece, "tensor", [(0, 1), (1, 0)])


def dot(left, right, dims):
    return lax.dot_general(left, right, (dims, ((), ())), preferred_element_type=f32)


def shards(
    tokens,
    segments,
    projections,
    combiner,
    offsets,
    sameness,
    postbias,
    scaling,
    centring,
    widener,
    widebias,
    narrower,
    narrowbias,
    rescale,
    recentre,
    cotangent,
):
    tensor_part = lax.axis_index("tensor")
    tensor_count = lax.axis_size("tensor")
    peer_tokens = swap(tokens)
    inwards = lax.all_gather(projections, "dp", axis=1, tiled=True)
    outwards = lax.all_gather(combiner, "dp", axis=1, tiled=True)
    widen_full = lax.all_gather(widener, "dp", axis=0, tiled=True)
    narrow_full = lax.all_gather(narrower, "dp", axis=1, tiled=True)
    peer_outwards = swap(outwards)
    length, model_width = tokens.shape
    half_len = length // 2
    local_width = offsets.shape[1]
    pairs = pair_matrix(half_len)
    pooled = dot(pairs, tokens, ((1,), (0,)))
    pooled_low = pooled.astype(bf16)
    peer_pooled_low = dot(pairs, peer_tokens, ((1,), (0,))).astype(bf16)
    phase_low = position_table(length, model_width).astype(bf16)

    def project(weight, rows):
        return dot(weight, rows, ((0,), (1,))).astype(bf16)

    relative = project(inwards[3], phase_low)
    small = jnp.concatenate([offsets, sameness], axis=0).T
    seg_pair = lax.dynamic_slice_in_dim(segments, tensor_part, 1, 0)
    seg_peer = lax.dynamic_slice_in_dim(segments, 1 - tensor_part, 1, 0)

    def sequence(rows, low, seg):
        return (
            project(inwards[0], low),
            project(inwards[1], rows),
            project(inwards[2], rows),
            relative,
            small,
            seg[:, ::2],
            seg,
        )

    peer_args = sequence(peer_tokens, peer_pooled_low, seg_peer)
    own_args = sequence(tokens, pooled_low, seg_pair)
    peer_probs, peer_mixed = attn_fwd(*peer_args)
    sent_mixed = swap(peer_mixed.astype(bf16))
    own_probs, own_mixed = attn_fwd(*own_args)
    own_mixed_low = own_mixed.astype(bf16)
    branch = (
        dot(own_mixed_low, outwards, ((0,), (0,)))
        + dot(sent_mixed, peer_outwards, ((0,), (0,)))
        + postbias
    )
    first, first_pull = jax.vjp(normalize, pooled + branch, scaling, centring)
    first_low = first.astype(bf16)
    peer_first = swap(first_low)
    gelu_tanh = partial(jax.nn.gelu, approximate=True)

    def widen(rows):
        hidden_pre = dot(rows, widen_full, ((1,), (0,))) + widebias
        hidden_val, gelu_pull = jax.vjp(gelu_tanh, hidden_pre)
        return hidden_val.astype(bf16), gelu_pull

    own_act, own_gelu_pull = widen(first_low)
    peer_act, peer_gelu_pull = widen(peer_first)
    sent_second = swap(dot(peer_act, narrow_full, ((1,), (0,))).astype(bf16))
    second = dot(own_act, narrow_full, ((1,), (0,))) + sent_second.astype(f32) + narrowbias
    final_rows, final_pull = jax.vjp(normalize, first + second, rescale, recentre)
    result = final_rows.astype(bf16)
    dfinal, rescale_grad, recentre_grad = final_pull(cotangent.astype(f32))
    dsecond = dfinal.astype(bf16)
    narrowbias_grad = jnp.sum(dsecond.astype(f32), axis=0)
    peer_dsecond = swap(dsecond)
    own_dhidden = own_gelu_pull(dot(dsecond, narrow_full, ((1,), (1,))))[0].astype(bf16)
    peer_dhidden = peer_gelu_pull(dot(peer_dsecond, narrow_full, ((1,), (1,))))[0].astype(bf16)
    sent_dfirst = swap(dot(peer_dhidden, widen_full, ((1,), (1,))).astype(bf16))
    dfirst = dfinal + dot(own_dhidden, widen_full, ((1,), (1,))) + sent_dfirst.astype(f32)
    narrower_local = dot(own_act, dsecond, ((0,), (0,))) + dot(peer_act, peer_dsecond, ((0,), (0,)))
    widener_local = dot(first_low, own_dhidden, ((0,), (0,))) + dot(
        peer_first, peer_dhidden, ((0,), (0,))
    )
    widebias_local = jnp.sum(own_dhidden.astype(f32), axis=0) + jnp.sum(
        peer_dhidden.astype(f32), axis=0
    )
    widener_grad = lax.psum_scatter(
        widener_local.astype(bf16), "dp", scatter_dimension=0, tiled=True
    ).astype(f32)
    narrower_grad = lax.psum_scatter(
        narrower_local.astype(bf16), "dp", scatter_dimension=1, tiled=True
    ).astype(f32)
    dfirst_in, scaling_grad, centring_grad = first_pull(dfirst)
    dbranch = dfirst_in.astype(bf16)
    postbias_grad = jnp.sum(dbranch.astype(f32), axis=0)
    peer_dmixed = swap(dot(peer_outwards, dbranch, ((1,), (1,))).astype(bf16))
    own_dmixed = dot(outwards, dbranch, ((1,), (1,))).astype(bf16)
    combiner_local = dot(own_mixed_low, dbranch, ((1,), (0,)))
    sent_combiner = swap(dot(sent_mixed, dbranch, ((1,), (0,))).astype(bf16))
    combiner_local = combiner_local + sent_combiner.astype(f32)
    dq, dk, dv, drel, sums = attn_bwd(*own_args, own_probs, own_mixed, own_dmixed)
    peer_dq, peer_dk, peer_dv, drel, sums = attn_bwd(
        *peer_args, peer_probs, peer_mixed, peer_dmixed, (drel, sums)
    )
    offsets_local = sums[:, :3].T
    sameness_local = sums[:, 3:5].T
    upper = drel.astype(bf16)
    lower = (drel - upper.astype(f32)).astype(bf16)

    def weigh(rows, grad):
        return dot(rows, grad, ((0,), (1,)))

    projections_local = jnp.stack(
        [
            weigh(pooled_low, dq) + weigh(peer_pooled_low, peer_dq),
            weigh(tokens, dk) + weigh(peer_tokens, peer_dk),
            weigh(tokens, dv) + weigh(peer_tokens, peer_dv),
            weigh(phase_low, upper) + weigh(phase_low, lower),
        ]
    ).astype(bf16)
    projections_grad = lax.psum_scatter(
        projections_local, "dp", scatter_dimension=1, tiled=True
    ).astype(f32)
    combiner_grad = lax.psum_scatter(
        combiner_local.astype(bf16), "dp", scatter_dimension=1, tiled=True
    ).astype(f32)

    def token_part(dq_rows, dk_rows, dv_rows):
        from_query = dot(dq_rows, inwards[0], ((0,), (1,)))
        return (
            dot(dk_rows, inwards[1], ((0,), (1,))) + dot(dv_rows, inwards[2], ((0,), (1,))),
            from_query,
        )

    peer_keys, peer_query = token_part(peer_dq, peer_dk, peer_dv)
    sent_tokens = swap((peer_keys + spread_pairs(peer_query)).astype(bf16))
    own_keys, own_query = token_part(dq, dk, dv)
    tokens_grad = own_keys + spread_pairs(own_query + dfirst_in) + sent_tokens.astype(f32)

    def place_half(piece_part):
        piece_width = piece_part.shape[-1]
        zeros_full = jnp.zeros(piece_part.shape[:-1] + (piece_width * tensor_count,), f32)
        return lax.dynamic_update_slice_in_dim(
            zeros_full, piece_part, tensor_part * piece_width, piece_part.ndim - 1
        )

    def take_half(summed, piece_width):
        return lax.dynamic_slice_in_dim(
            summed, tensor_part * piece_width, piece_width, summed.ndim - 1
        )

    summed_small = lax.psum(
        (
            place_half(offsets_local),
            place_half(sameness_local),
            place_half(widebias_local),
            postbias_grad,
            scaling_grad,
            centring_grad,
            narrowbias_grad,
            rescale_grad,
            recentre_grad,
        ),
        ("dp", "tensor"),
    )
    return (
        result,
        tokens_grad,
        projections_grad,
        combiner_grad,
        take_half(summed_small[0], local_width),
        take_half(summed_small[1], local_width),
        summed_small[3],
        summed_small[4],
        summed_small[5],
        widener_grad,
        take_half(summed_small[2], widebias.shape[0]),
        narrower_grad,
        summed_small[6],
        summed_small[7],
        summed_small[8],
    )


def solution(mesh):
    placed = (
        P(("dp", "tensor"), None),
        P("dp", None),
        P(None, "dp", "tensor"),
        P("tensor", "dp"),
        P(None, "tensor"),
        P(None, "tensor"),
        P(),
        P(),
        P(),
        P("dp", "tensor"),
        P("tensor"),
        P("tensor", "dp"),
        P(),
        P(),
        P(),
        P(("dp", "tensor"), None),
    )
    return jax.shard_map(
        shards,
        mesh=mesh,
        in_specs=placed,
        out_specs=(
            P(("dp", "tensor"), None),
            P(("dp", "tensor"), None),
            P(None, "dp", "tensor"),
            P("tensor", "dp"),
            P(None, "tensor"),
            P(None, "tensor"),
            P(),
            P(),
            P(),
            P("dp", "tensor"),
            P("tensor"),
            P("tensor", "dp"),
            P(),
            P(),
            P(),
        ),
        check_vma=False,
    )
```

```python
from functools import partial
import math

import jax
import jax.numpy as jnp
from jax import lax
from jax.experimental import pallas as pl
from jax.experimental.pallas import tpu as pltpu
from jax.sharding import PartitionSpec as P

epsilon = 1e-05
bf16=jnp.bfloat16; f32=jnp.float32
DH=64
AUG=16
TN=(((0,),(0,)),((),()))
NT=(((1,),(1,)),((),()))
NN=(((1,),(0,)),((),()))

def split3(u):
    row=lax.broadcasted_iota(jnp.int32,u.shape,0)
    hi=u.astype(bf16).astype(f32)
    r1=u-hi
    mid=r1.astype(bf16).astype(f32)
    lo=r1-mid
    return jnp.where(row<3,hi,jnp.where(row<6,mid,jnp.where(row<9,lo,0.0))).astype(bf16)

def fwd_kernel(q_ref,k_ref,v_ref,r_ref,s_ref,segq_ref,segk_ref,p_ref,m_ref,ml_ref,c_sc,k_sc,*,tq):
    nq=q_ref.shape[1]; nk=k_ref.shape[1]
    q=q_ref[...].astype(f32)
    sm=s_ref[...]
    c_sc[:DH]=(q+sm[:,0:1]).astype(bf16)*jnp.asarray(0.125,bf16)
    pos=(q+sm[:,1:2]).astype(bf16)*jnp.asarray(0.125,bf16)
    typed=q+sm[:,2:3]
    t0=jnp.sum(typed*sm[:,3:4],axis=0,keepdims=True)*0.125
    t1=jnp.sum(typed*sm[:,4:5],axis=0,keepdims=True)*0.125
    kind=lax.rem(lax.broadcasted_iota(jnp.int32,(AUG,nq),0),3)
    c_sc[DH:]=split3(jnp.where(segq_ref[...]==kind,t1,t0))
    k_sc[:DH]=k_ref[...]
    rowk=lax.broadcasted_iota(jnp.int32,(AUG,nk),0)
    k_sc[DH:]=jnp.where((segk_ref[...]==lax.rem(rowk,3)) & (rowk<9),1.0,0.0).astype(bf16)
    w=nk+2*tq
    for b in range(nq//tq):
        i0=b*tq
        w0=nk-2*i0-2*tq
        c=lax.dot_general(c_sc[:,i0:i0+tq],k_sc[...],TN,preferred_element_type=f32)
        d=lax.dot_general(pos[:,i0:i0+tq],r_ref[:,w0:w0+w],TN,preferred_element_type=f32)
        d=pltpu.roll(d,w-2*tq,1,stride=2,stride_axis=0)
        s=c+d[:,:nk]
        mx=jnp.max(s,axis=1,keepdims=True)
        e=jnp.exp(s-mx)
        l=jnp.sum(e,axis=1,keepdims=True)
        p=(e*(1.0/l)).astype(bf16)
        p_ref[i0:i0+tq,:]=p
        mixed=lax.dot_general(v_ref[...],p,NT,preferred_element_type=f32)
        m_ref[:,i0:i0+tq]=mixed
        ml_ref[:,i0:i0+tq]=mixed.astype(bf16)

def attn_fwd(qT,kT,vT,relT,small,segq,segk,tq=128):
    hd,nq=qT.shape; nk=kT.shape[1]; heads=hd//DH
    return pl.pallas_call(partial(fwd_kernel,tq=tq),grid=(heads,),
        in_specs=[pl.BlockSpec((DH,nq),lambda h:(h,0)),pl.BlockSpec((DH,nk),lambda h:(h,0)),pl.BlockSpec((DH,nk),lambda h:(h,0)),
          pl.BlockSpec((DH,2*nk),lambda h:(h,0)),pl.BlockSpec((DH,small.shape[1]),lambda h:(h,0)),
          pl.BlockSpec((1,nq),lambda h:(0,0)),pl.BlockSpec((1,nk),lambda h:(0,0))],
        out_specs=[pl.BlockSpec((None,nq,nk),lambda h:(h,0,0)),pl.BlockSpec((DH,nq),lambda h:(h,0)),pl.BlockSpec((DH,nq),lambda h:(h,0))],
        out_shape=[jax.ShapeDtypeStruct((heads,nq,nk),bf16),jax.ShapeDtypeStruct((hd,nq),f32),jax.ShapeDtypeStruct((hd,nq),bf16)],
        scratch_shapes=[pltpu.VMEM((DH+AUG,nq),bf16),pltpu.VMEM((DH+AUG,nk),bf16)],
        compiler_params=pltpu.CompilerParams(vmem_limit_bytes=56<<20),name="attend")(qT,kT,vT,relT,small,segq,segk)

def bwd_kernel(q_ref,k_ref,v_ref,r_ref,s_ref,segq_ref,segk_ref,p_ref,m_ref,dm_ref,
               dq_ref,dk_ref,dv_ref,dr_ref,sg_ref,k_sc,v_sc,dm_sc,ds_sc,dg_sc,*,tq,first):
    nq=q_ref.shape[1]; nk=k_ref.shape[1]
    q=q_ref[...].astype(f32)
    sm=s_ref[...]
    content=(q+sm[:,0:1]).astype(bf16)*jnp.asarray(0.125,bf16)
    pos=(q+sm[:,1:2]).astype(bf16)*jnp.asarray(0.125,bf16)
    typed=q+sm[:,2:3]
    k_sc[:DH]=k_ref[...]
    rowk=lax.broadcasted_iota(jnp.int32,(AUG,nk),0)
    k_sc[DH:]=((segk_ref[...]==rowk)).astype(f32).astype(bf16)
    v_sc[:DH]=v_ref[...]
    v_sc[DH:]=jnp.where(rowk<3,1.0,0.0).astype(bf16)
    dm=dm_ref[...]
    dm_sc[:DH]=dm
    delta=-jnp.sum(dm.astype(f32)*m_ref[...],axis=0,keepdims=True)
    rowq=lax.broadcasted_iota(jnp.int32,(AUG,nq),0)
    hi=delta.astype(bf16).astype(f32); r1=delta-hi; mid=r1.astype(bf16).astype(f32); lo=r1-mid
    dm_sc[DH:]=jnp.where(rowq==0,hi,jnp.where(rowq==1,mid,jnp.where(rowq==2,lo,0.0))).astype(bf16)
    w=nk+2*tq
    flip=(lax.broadcasted_iota(jnp.int32,(tq,tq),0)+lax.broadcasted_iota(jnp.int32,(tq,tq),1)==tq-1).astype(f32).astype(bf16)
    def turn16(x):
        parts=[lax.dot_general(x[:,i:i+tq],flip,NN,preferred_element_type=f32) for i in range(0,nq,tq)]
        return jnp.concatenate(parts,axis=1).astype(bf16)
    def turn(x):
        hi=x.astype(bf16); r1=x-hi.astype(f32); mid=r1.astype(bf16); lo=(r1-mid.astype(f32)).astype(bf16)
        cat=jnp.concatenate([hi,mid,lo],axis=0)
        parts=[lax.dot_general(cat[:,i:i+tq],flip,NN,preferred_element_type=f32) for i in range(0,nq,tq)]
        y=jnp.concatenate(parts,axis=1)
        return y[:DH]+y[DH:2*DH]+y[2*DH:]
    dg_sc[...]=jnp.zeros_like(dg_sc)
    for b in range(nq//tq):
        i0=b*tq
        w0=nk-2*i0-2*tq
        dp=lax.dot_general(dm_sc[:,i0:i0+tq],v_sc[...],TN,preferred_element_type=f32)
        ds=p_ref[i0:i0+tq,:].astype(f32)*dp
        ds16=ds.astype(bf16)
        ds_sc[i0:i0+tq,:]=ds16
        back=lax.dot_general(flip,ds16,NN,preferred_element_type=f32)
        g=jnp.concatenate([back,jnp.zeros((tq,2*tq),f32)],axis=1)
        g=pltpu.roll(g,2,1,stride=2,stride_axis=0)
        dg_sc[i0:i0+tq,w0:w0+w]=g.astype(bf16)
    dv_ref[...]=lax.dot_general(dm,p_ref[...],NN,preferred_element_type=f32).astype(bf16)
    dk_ref[...]=lax.dot_general(content,ds_sc[...],NN,preferred_element_type=f32).astype(bf16)
    dc=lax.dot_general(k_sc[...],ds_sc[...],NT,preferred_element_type=f32)
    dpos=turn(lax.dot_general(r_ref[...],dg_sc[...],NT,preferred_element_type=f32))*0.125
    dr=lax.dot_general(turn16(pos),dg_sc[...],NN,preferred_element_type=f32)
    if first is None:
        dr_ref[...]=dr
    else:
        dr_ref[...]=first[0][...]+dr
    dcontent=dc[:DH]*0.125
    seg=dc[DH:]*0.125
    rows=lax.broadcasted_iota(jnp.int32,(AUG,nq),0)
    g1=jnp.sum(jnp.where(segq_ref[...]==rows,seg,0.0),axis=0,keepdims=True)
    g0=jnp.sum(seg,axis=0,keepdims=True)-g1
    dtyped=sm[:,3:4]*g0+sm[:,4:5]*g1
    dq_ref[...]=(dcontent+dpos+dtyped).astype(bf16)
    lane=lax.broadcasted_iota(jnp.int32,(DH,128),1)
    total=jnp.zeros((DH,128),f32)
    for n,val in enumerate((dcontent,dpos,dtyped,typed*g0,typed*g1)):
        total=jnp.where(lane==n,jnp.sum(val,axis=1,keepdims=True),total)
    if first is None:
        sg_ref[...]=total
    else:
        sg_ref[...]=first[1][...]+total

def bwd_kernel_first(*refs,tq):
    bwd_kernel(*refs,tq=tq,first=None)
def bwd_kernel_next(*refs,tq):
    bwd_kernel(*refs[:10],*refs[12:],tq=tq,first=refs[10:12])

def attn_bwd(qT,kT,vT,relT,small,segq,segk,probs,mixedT,dmixedT,carry=None,tq=128):
    hd,nq=qT.shape; nk=kT.shape[1]; heads=hd//DH
    row=lambda n: pl.BlockSpec((DH,n),lambda h:(h,0))
    ins=[row(nq),row(nk),row(nk),row(2*nk),row(small.shape[1]),pl.BlockSpec((1,nq),lambda h:(0,0)),pl.BlockSpec((1,nk),lambda h:(0,0)),
         pl.BlockSpec((None,nq,nk),lambda h:(h,0,0)),row(nq),row(nq)]
    args=[qT,kT,vT,relT,small,segq,segk,probs,mixedT,dmixedT]
    kern=bwd_kernel_first
    if carry is not None:
        ins+= [row(2*nk),row(128)]; args+=list(carry); kern=bwd_kernel_next
    return pl.pallas_call(partial(kern,tq=tq),grid=(heads,),in_specs=ins,
        out_specs=[row(nq),row(nk),row(nk),row(2*nk),row(128)],
        out_shape=[jax.ShapeDtypeStruct((hd,nq),bf16),jax.ShapeDtypeStruct((hd,nk),bf16),jax.ShapeDtypeStruct((hd,nk),bf16),
           jax.ShapeDtypeStruct((hd,2*nk),f32),jax.ShapeDtypeStruct((hd,128),f32)],
        scratch_shapes=[pltpu.VMEM((DH+AUG,nk),bf16),pltpu.VMEM((DH+AUG,nk),bf16),pltpu.VMEM((DH+AUG,nq),bf16),pltpu.VMEM((nq,nk),bf16),pltpu.VMEM((nq,2*nk),bf16)],
        compiler_params=pltpu.CompilerParams(vmem_limit_bytes=56<<20),name="attend_back")(*args)


PARTS = 5


def pair_matrix(count, axis):
    shape = (count, 2 * count) if axis == 1 else (2 * count, count)
    longer = lax.broadcasted_iota(jnp.int32, shape, axis)
    shorter = lax.broadcasted_iota(jnp.int32, shape, 1 - axis)
    return jnp.where(jnp.right_shift(longer, 1) == shorter, 0.5, 0.0).astype(bf16)


def project_kernel(
    place_ref, near_ref, far_ref, own_ref, peer_ref, phase_ref,
    own_q, own_k, own_v, peer_q, peer_k, peer_v, rel_ref, pooled_ref, own_low, peer_low, weights_ref, combiner_ref,
    turned_sc,
):
    step = pl.program_id(0)
    chip, core = place_ref[0], place_ref[1]
    depth = near_ref.shape[2]

    @pl.when(step == 0)
    def _():
        for i in range(PARTS):
            for d in range(near_ref.shape[0]):
                spot = jnp.bitwise_xor(chip, d)
                for ref, which in ((near_ref, core), (far_ref, 1 - core)):
                    if i < PARTS - 1:
                        weights_ref[i, 2 * spot + which] = ref[d, i]
                    else:
                        combiner_ref[2 * spot + which] = ref[d, i]
            if i < PARTS - 1:
                turned_sc[i] = weights_ref[i].reshape(-1, near_ref.shape[3]).T

    def sequence(rows_ref, q_ref, k_ref, v_ref, low_ref, keep_ref):
        rows = rows_ref[...]
        pooled = jnp.dot(pair_matrix(rows.shape[0] // 2, 1), rows, preferred_element_type=f32)
        low = pooled.astype(bf16)
        low_ref[...] = low
        if keep_ref is not None:
            keep_ref[...] = pooled
        for i, (source, target) in enumerate(((low, q_ref), (rows, k_ref), (rows, v_ref))):
            target[...] = lax.dot_general(turned_sc[i], source, NT, preferred_element_type=f32).astype(bf16)

    @pl.when(step == 0)
    def _():
        sequence(own_ref, own_q, own_k, own_v, own_low, pooled_ref)

    @pl.when(step == 1)
    def _():
        sequence(peer_ref, peer_q, peer_k, peer_v, peer_low, None)

    @pl.when(step == 2)
    def _():
        rel_ref[...] = lax.dot_general(turned_sc[3], phase_ref[...], NT, preferred_element_type=f32).astype(bf16)


def whole(array):
    return pl.BlockSpec(array.shape, lambda *step: (0,) * array.ndim, pipeline_mode=pl.Buffered(1))


def out(shape, dtype):
    return jax.ShapeDtypeStruct(shape, dtype)


def project(place, near, far, tokens, peer_tokens, phase):
    length, model = tokens.shape
    half = length // 2
    count, _, depth, width = near.shape
    ins = [near, far, tokens, peer_tokens, phase]
    outs = [
        out((width, half), bf16), out((width, length), bf16), out((width, length), bf16),
        out((width, half), bf16), out((width, length), bf16), out((width, length), bf16),
        out((width, 2 * length), bf16), out((half, model), f32), out((half, model), bf16), out((half, model), bf16),
        out((PARTS - 1, 2 * count, depth, width), bf16), out((2 * count, depth, width), bf16),
    ]
    return pl.pallas_call(
        project_kernel,
        grid=(3,),
        in_specs=[pl.BlockSpec(memory_space=pltpu.SMEM)] + [whole(a) for a in ins],
        out_specs=[whole(a) for a in outs],
        out_shape=outs,
        scratch_shapes=[pltpu.VMEM((PARTS - 1, width, model), bf16)],
        compiler_params=pltpu.CompilerParams(vmem_limit_bytes=56 << 20),
        name="project",
    )(place, *ins)


def weigh_kernel(
    place_ref, own_rows, peer_rows, own_low, peer_low, phase_ref, own_dq, own_dk, own_dv, peer_dq, peer_dk, peer_dv,
    drel_ref, own_dc, sent_dc, small_ref, pieces_ref, total_sc,
):
    step = pl.program_id(0)

    @pl.when(step == 0)
    def _():
        total_sc[...] = jnp.zeros_like(total_sc)

    for i, pairs in enumerate((
        ((own_dq, own_low), (peer_dq, peer_low)),
        ((own_dk, own_rows), (peer_dk, peer_rows)),
        ((own_dv, own_rows), (peer_dv, peer_rows)),
        ((drel_ref, phase_ref),),
    )):
        for grad, rows in pairs:
            total_sc[i] += jnp.dot(grad[...].astype(bf16), rows[...], preferred_element_type=f32)

    @pl.when(step == pl.num_programs(0) - 1)
    def _():
        chip, core = place_ref[0], place_ref[1]
        _, count, _, width = pieces_ref.shape
        depth = own_dc.shape[1]
        for i in range(PARTS):
            if i < PARTS - 1:
                value = total_sc[i].astype(bf16).T.reshape(count, 2, depth, width)
            else:
                value = (own_dc[...].astype(f32) + sent_dc[...].astype(f32)).astype(bf16).reshape(count, 2, depth, width)
            for d in range(count):
                for c in range(2):
                    pieces_ref[jnp.bitwise_xor(core, c), jnp.bitwise_xor(chip, d), i * depth:(i + 1) * depth] = value[d, c]
        small = small_ref[...].astype(bf16)
        for d in range(count):
            for c in range(2):
                pieces_ref[c, d, PARTS * depth:] = small


def weigh(place, own_rows, peer_rows, own_low, peer_low, phase, own_grads, peer_grads, drel, own_dc, sent_dc, small, steps=4):
    blocks, depth, width = own_dc.shape
    model = own_rows.shape[1]

    def rows(array):
        return pl.BlockSpec((array.shape[0] // steps, model), lambda s: (s, 0))

    def columns(array):
        return pl.BlockSpec((width, array.shape[1] // steps), lambda s: (0, s))

    ins = [own_rows, peer_rows, own_low, peer_low, phase]
    grads = [*own_grads, *peer_grads, drel]
    rest = [own_dc, sent_dc, small]
    pieces = out((2, blocks // 2, PARTS * depth + small.shape[0], width), bf16)
    return pl.pallas_call(
        weigh_kernel,
        grid=(steps,),
        in_specs=[pl.BlockSpec(memory_space=pltpu.SMEM)] + [rows(a) for a in ins] + [columns(a) for a in grads] + [whole(a) for a in rest],
        out_specs=whole(pieces),
        out_shape=pieces,
        scratch_shapes=[pltpu.VMEM((PARTS - 1, width, model), f32)],
        compiler_params=pltpu.CompilerParams(vmem_limit_bytes=56 << 20),
        name="weigh",
    )(place, *ins, *grads, *rest)


def token_kernel(dq_ref, dk_ref, dv_ref, w_ref, *refs):
    model = refs[-1].shape[1]
    width = dk_ref.shape[0]
    half = dq_ref.shape[1]
    doubled = jnp.dot(dq_ref[...], pair_matrix(half, 1), preferred_element_type=f32).astype(bf16)
    total = None
    for i, grad in enumerate((doubled, dk_ref[...], dv_ref[...])):
        term = lax.dot_general(grad.T, w_ref[i].reshape(model, width), NT, preferred_element_type=f32)
        total = term if total is None else total + term
    if len(refs) > 1:
        high = refs[0][...].astype(bf16)
        low = (refs[0][...] - high.astype(f32)).astype(bf16)
        pairs = pair_matrix(half, 0)
        total = total + jnp.dot(pairs, high, preferred_element_type=f32) + jnp.dot(pairs, low, preferred_element_type=f32)
    refs[-1][...] = total.astype(refs[-1].dtype)


def token_grad(grads, weights, extra, dtype):
    length = grads[1].shape[1]
    model = weights.shape[1] * weights.shape[2]
    ins = [*grads, weights[:3]] + ([extra] if extra is not None else [])
    specs = [whole(a) for a in ins]
    result = out((length, model), dtype)
    return pl.pallas_call(
        token_kernel,
        grid=(1,),
        in_specs=specs,
        out_specs=whole(result),
        out_shape=result,
        compiler_params=pltpu.CompilerParams(vmem_limit_bytes=56 << 20),
        name="token_grad",
    )(*ins)


def layer_norm(values_in):
    row_mean = jnp.mean(values_in, axis=1, keepdims=True)
    centred = values_in - row_mean
    variance = jnp.mean(centred * centred, axis=1, keepdims=True)
    scale = lax.rsqrt(variance + epsilon)
    return centred * scale, scale


def layer_norm_back(grad, normed, scale, gain):
    inner = grad * gain
    return scale * (
        inner
        - jnp.mean(inner, axis=1, keepdims=True)
        - normed * jnp.mean(inner * normed, axis=1, keepdims=True)
    )


def row_sum(values_in):
    return jnp.sum(values_in, axis=0, keepdims=True)


def middle_kernel(
    pooled_ref, mixed_ref, sent_ref, own_c_ref, peer_c_ref, vec_ref, cot_ref, wide_ref, narrow_ref, bias_ref,
    result_ref, dfirst_ref, own_dm_ref, peer_dm_ref, own_dc_ref, peer_dc_ref, sums_ref, bias_sum_ref, grads_ref,
    slope_sc, act_sc, dhid_sc, first_sc, norm_sc, scale_sc, total_sc, low_sc, low_t_sc, dsec_sc, dsec_t_sc,
    *, chunks,
):
    step = pl.program_id(0)
    model = pooled_ref.shape[1]
    rows = pooled_ref.shape[0]
    part = wide_ref.shape[-1]
    vec = vec_ref[...]
    postbias, scaling, centring = vec[0:1], vec[1:2], vec[2:3]
    narrowbias, rescale, recentre = vec[3:4], vec[4:5], vec[5:6]

    @pl.when(step == 0)
    def _():
        own_c = own_c_ref[...].reshape(model, -1)
        peer_c = peer_c_ref[...].reshape(model, -1)
        mixed = mixed_ref[...].astype(bf16).T
        sent = sent_ref[...].T
        branch = (
            lax.dot_general(mixed, own_c, NT, preferred_element_type=f32)
            + lax.dot_general(sent, peer_c, NT, preferred_element_type=f32)
            + postbias
        )
        normed, scale = layer_norm(pooled_ref[...] + branch)
        norm_sc[...] = normed
        scale_sc[...] = scale
        first = normed * scaling + centring
        first_sc[...] = first
        low = first.astype(bf16)
        low_sc[...] = low
        low_t_sc[...] = low.T
        total_sc[...] = jnp.zeros_like(total_sc)

    @pl.when(step < chunks)
    def _():
        wide = wide_ref[...].reshape(model, part)
        hidden = jnp.dot(low_sc[...], wide, preferred_element_type=f32) + bias_ref[0]
        square = hidden * hidden
        root = math.sqrt(2.0 / math.pi)
        turn = jnp.tanh(hidden * (root + (root * 0.044715) * square))
        half = 0.5 * turn + 0.5
        act = (hidden * half).astype(bf16)
        slope_sc[step] = half + hidden * (half * (1.0 - turn)) * (root + (3.0 * root * 0.044715) * square)
        act_sc[step] = act
        narrow = narrow_ref[...].reshape(model, part)
        total_sc[...] += lax.dot_general(act, narrow, NT, preferred_element_type=f32)

    @pl.when(step == chunks - 1)
    def _():
        normed, scale = layer_norm(first_sc[...] + (total_sc[...] + narrowbias))
        result_ref[...] = (normed * rescale + recentre).astype(bf16)
        cot = cot_ref[...].astype(f32)
        dfinal = layer_norm_back(cot, normed, scale, rescale)
        dsec = dfinal.astype(bf16)
        dsec_sc[...] = dsec
        dsec_t_sc[...] = dsec.T
        sums_ref[3:4] = row_sum(dsec.astype(f32))
        sums_ref[4:5] = row_sum(cot * normed)
        sums_ref[5:6] = row_sum(cot)
        total_sc[...] = dfinal

    back = step - chunks

    @pl.when((back >= 0) & (lax.rem(back, 2) == 0))
    def _():
        chunk = back // 2
        narrow = narrow_ref[...].reshape(model, part)
        dact = jnp.dot(dsec_sc[...], narrow, preferred_element_type=f32)
        dhid = (dact * slope_sc[chunk]).astype(bf16)
        dhid_sc[...] = dhid
        bias_sum_ref[0] = row_sum(dhid.astype(f32))
        grad = jnp.dot(dsec_t_sc[...], act_sc[chunk], preferred_element_type=f32)
        grads_ref[...] = grad.astype(bf16).reshape(grads_ref.shape)

    @pl.when((back >= 0) & (lax.rem(back, 2) == 1))
    def _():
        wide = wide_ref[...].reshape(model, part)
        total_sc[...] += lax.dot_general(dhid_sc[...], wide, NT, preferred_element_type=f32)
        grad = jnp.dot(low_t_sc[...], dhid_sc[...], preferred_element_type=f32)
        grads_ref[...] = grad.astype(bf16).reshape(grads_ref.shape)

    @pl.when(back == 2 * chunks - 1)
    def _():
        dfirst = total_sc[...]
        normed = norm_sc[...]
        dfirst_in = layer_norm_back(dfirst, normed, scale_sc[...], scaling)
        dfirst_ref[...] = dfirst_in
        dbranch = dfirst_in.astype(bf16)
        sums_ref[0:1] = row_sum(dbranch.astype(f32))
        sums_ref[1:2] = row_sum(dfirst * normed)
        sums_ref[2:3] = row_sum(dfirst)
        dbranch_t = dbranch.T
        for c_ref, m_ref, dm_ref, dc_ref in (
            (own_c_ref, mixed_ref, own_dm_ref, own_dc_ref),
            (peer_c_ref, sent_ref, peer_dm_ref, peer_dc_ref),
        ):
            c = c_ref[...].reshape(model, -1)
            dm_ref[...] = lax.dot_general(c, dbranch_t, TN, preferred_element_type=f32).astype(bf16)
            dc = lax.dot_general(dbranch_t, m_ref[...].astype(bf16), NT, preferred_element_type=f32)
            dc_ref[...] = dc.astype(bf16).reshape(dc_ref.shape)


def middle(pooled, mixed, sent, own_c, peer_c, vec, cot, weights, bias):
    rows, model = pooled.shape
    blocks, halves, depth, width = weights.shape
    part = width // 4
    each = (width // 2) // part
    chunks = halves * each

    def chunk_of(step):
        return jnp.where(step < chunks, step, (step - chunks) // 2)

    def weight_spec(offset):
        def index(step):
            c = chunk_of(step)
            return (0, c // each, 0, offset * each + lax.rem(c, each))

        return pl.BlockSpec((blocks, None, depth, part), index)

    def grad_index(step):
        back = jnp.maximum(step - chunks, 0)
        c = back // 2
        return (0, c // each, 0, jnp.where(lax.rem(back, 2) == 0, each, 0) + lax.rem(c, each))

    outs = [
        out((rows, model), bf16), out((rows, model), f32), out(mixed.shape, bf16), out(mixed.shape, bf16),
        out(own_c.shape, bf16), out(own_c.shape, bf16), out((8, model), f32),
    ]
    whole_ins = [pooled, mixed, sent, own_c, peer_c, vec, cot]
    return pl.pallas_call(
        partial(middle_kernel, chunks=chunks),
        grid=(3 * chunks,),
        in_specs=[whole(a) for a in whole_ins]
        + [weight_spec(0), weight_spec(1), pl.BlockSpec((1, 1, part), lambda s: (chunk_of(s), 0, 0))],
        out_specs=[whole(a) for a in outs]
        + [
            pl.BlockSpec((1, 1, part), lambda s: (jnp.maximum(s - chunks, 0) // 2, 0, 0)),
            pl.BlockSpec((blocks, None, depth, part), grad_index),
        ],
        out_shape=outs + [out((chunks, 1, part), f32), out(weights.shape, bf16)],
        scratch_shapes=[
            pltpu.VMEM((chunks, rows, part), f32),
            pltpu.VMEM((chunks, rows, part), bf16),
            pltpu.VMEM((rows, part), bf16),
            pltpu.VMEM((rows, model), f32),
            pltpu.VMEM((rows, model), f32),
            pltpu.VMEM((rows, 1), f32),
            pltpu.VMEM((rows, model), f32),
            pltpu.VMEM((rows, model), bf16),
            pltpu.VMEM((model, rows), bf16),
            pltpu.VMEM((rows, model), bf16),
            pltpu.VMEM((model, rows), bf16),
        ],
        compiler_params=pltpu.CompilerParams(vmem_limit_bytes=56 << 20),
        name="middle",
    )(*whole_ins, weights, weights, bias.reshape(chunks, 1, part))


def position_table(length, model_width):
    row_index = jnp.arange(2 * length, dtype=jnp.float32)
    offset = length - row_index
    half_width = model_width // 2
    frequency = jnp.exp(
        jnp.arange(half_width, dtype=jnp.float32) * (-math.log(10000.0) / half_width)
    )
    angles = offset[:, None] * frequency[None, :]
    return jnp.concatenate([jnp.sin(angles), jnp.cos(angles)], axis=1)


CHIPS = 8


def swap(piece):
    return lax.ppermute(piece, "tensor", [(0, 1), (1, 0)])


def exchange(piece, mask):
    count = lax.axis_size("dp")
    return lax.ppermute(piece, "dp", [(i, i ^ mask) for i in range(count)])


def shards(
    tokens,
    segments,
    projections,
    combiner,
    offsets,
    sameness,
    postbias,
    scaling,
    centring,
    widener,
    widebias,
    narrower,
    narrowbias,
    rescale,
    recentre,
    cotangent,
):
    tensor_part = lax.axis_index("tensor")
    dp_part = lax.axis_index("dp")
    dp_count = lax.axis_size("dp")
    length, model = tokens.shape
    width = offsets.shape[1]
    hidden = widener.shape[1]
    blocks = 2 * CHIPS
    depth = model // blocks
    direct = dp_count == blocks
    if direct:
        place = jnp.stack([dp_part // 2, dp_part % 2]).astype(jnp.int32)
    else:
        place = jnp.zeros((2,), jnp.int32)

    own_piece = jnp.concatenate([projections, combiner.T[None]], axis=0)
    if direct:
        near = jnp.stack([own_piece] + [exchange(own_piece, 2 * d) for d in range(1, CHIPS)])
        far = exchange(near, 1)
    else:
        every = lax.all_gather(own_piece, "dp", axis=1, tiled=True)
        every = every.reshape(PARTS, CHIPS, 2, depth, width).transpose(2, 1, 0, 3, 4)
        near, far = every[0], every[1]
    peer_tokens = swap(tokens)
    mine = jnp.concatenate([widener, narrower.T], axis=1)
    weights = lax.all_gather(mine, ("dp", "tensor"), axis=0, tiled=False)
    if not direct:
        weights = weights.reshape(dp_count, 2, model // dp_count, 2 * hidden).transpose(1, 0, 2, 3)
        weights = weights.reshape(2, blocks, depth, 2 * hidden).transpose(1, 0, 2, 3)
    weights = weights.reshape(blocks, 2, depth, 2 * hidden)
    peer_bias = swap(widebias)
    bias = jnp.where(
        tensor_part == 0,
        jnp.concatenate([widebias, peer_bias]),
        jnp.concatenate([peer_bias, widebias]),
    )
    phase = position_table(length, model).astype(bf16)
    own_q, own_k, own_v, peer_q, peer_k, peer_v, relative, pooled, own_low, peer_low, inwards, own_c = project(
        place, near, far, tokens, peer_tokens, phase
    )
    peer_c = swap(own_c)
    small = jnp.concatenate([offsets, sameness], axis=0).T
    own_seg = lax.dynamic_slice_in_dim(segments, tensor_part, 1, 0)
    peer_seg = lax.dynamic_slice_in_dim(segments, 1 - tensor_part, 1, 0)
    own_args = (own_q, own_k, own_v, relative, small, own_seg[:, ::2], own_seg)
    peer_args = (peer_q, peer_k, peer_v, relative, small, peer_seg[:, ::2], peer_seg)
    peer_probs, peer_mixed, peer_mixed_low = attn_fwd(*peer_args)
    sent_mixed = swap(peer_mixed_low)
    own_probs, own_mixed, own_mixed_low = attn_fwd(*own_args)
    vec = jnp.stack([postbias, scaling, centring, narrowbias, rescale, recentre, postbias, postbias])
    result, dfirst_in, own_dmixed, peer_dmixed, own_dc, peer_dc, sums, bias_sums, grads = middle(
        pooled, own_mixed_low, sent_mixed, own_c, peer_c, vec, cotangent, weights, bias
    )
    sent_dmixed = swap(peer_dmixed)
    if not direct:
        grads = grads.transpose(1, 0, 2, 3).reshape(2, dp_count, model // dp_count, 2 * hidden).transpose(1, 0, 2, 3)
    grads = lax.psum_scatter(
        grads.reshape(2 * dp_count, model // dp_count, 2 * hidden),
        ("dp", "tensor"),
        scatter_dimension=0,
        tiled=True,
    )[0].astype(f32)
    sent_dc = swap(peer_dc)
    early = jnp.concatenate([sums[:6], bias_sums.reshape(-1, model)], axis=0)
    early = early + swap(early)
    own_dq, own_dk, own_dv, drel, late = attn_bwd(*own_args, own_probs, own_mixed, own_dmixed)
    peer_dq, peer_dk, peer_dv, drel, late = attn_bwd(
        *peer_args, peer_probs, peer_mixed, sent_dmixed, (drel, late)
    )
    own_grads = (own_dq, own_dk, own_dv)
    peer_grads = (peer_dq, peer_dk, peer_dv)
    early_rows = early.reshape(-1, width)
    used = 5 + early_rows.shape[0]
    padding = jnp.zeros((-used % 16, width), f32)
    extras = jnp.concatenate([late[:, :5].T, early_rows, padding], axis=0)
    pieces = weigh(
        place, tokens, peer_tokens, own_low, peer_low, phase, own_grads, peer_grads, drel, own_dc, sent_dc, extras
    )
    if direct:
        held = (pieces[0].astype(f32) + exchange(pieces[1], 1).astype(f32)).astype(bf16)
        total = held[0].astype(f32)
        for d in range(1, CHIPS):
            total = total + exchange(held[d], 2 * d).astype(f32)
        big = total[: PARTS * depth].reshape(PARTS, depth, width)
        extras = total[PARTS * depth :]
    else:
        big = pieces[:, :, : PARTS * depth].reshape(2, CHIPS, PARTS, depth, width).transpose(2, 1, 0, 3, 4)
        big = lax.psum_scatter(
            big.reshape(PARTS, model, width), "dp", scatter_dimension=1, tiled=True
        ).astype(f32)
        extras = lax.psum(extras, "dp")
    projections_grad = big[:4]
    combiner_grad = big[4].T
    early = extras[5:used].reshape(-1, model)
    bias_grad = lax.dynamic_slice_in_dim(early[6:].reshape(-1), tensor_part * hidden, hidden, 0)
    sent_tokens = swap(token_grad(peer_grads, inwards, None, bf16))
    tokens_grad = token_grad(own_grads, inwards, dfirst_in, f32) + sent_tokens.astype(f32)
    return (
        result,
        tokens_grad,
        projections_grad,
        combiner_grad,
        extras[:3],
        extras[3:5],
        early[0],
        early[1],
        early[2],
        grads[:, :hidden],
        bias_grad,
        grads[:, hidden:].T,
        early[3],
        early[4],
        early[5],
    )


def solution(mesh):
    placed = (
        P(("dp", "tensor"), None),
        P("dp", None),
        P(None, "dp", "tensor"),
        P("tensor", "dp"),
        P(None, "tensor"),
        P(None, "tensor"),
        P(),
        P(),
        P(),
        P("dp", "tensor"),
        P("tensor"),
        P("tensor", "dp"),
        P(),
        P(),
        P(),
        P(("dp", "tensor"), None),
    )
    return jax.shard_map(
        shards,
        mesh=mesh,
        in_specs=placed,
        out_specs=(
            P(("dp", "tensor"), None),
            P(("dp", "tensor"), None),
            P(None, "dp", "tensor"),
            P("tensor", "dp"),
            P(None, "tensor"),
            P(None, "tensor"),
            P(),
            P(),
            P(),
            P("dp", "tensor"),
            P("tensor"),
            P("tensor", "dp"),
            P(),
            P(),
            P(),
        ),
        check_vma=False,
    )
```

```python
from functools import partial
import math

import jax
import jax.numpy as jnp
from jax import lax
from jax.experimental import pallas as pl
from jax.experimental.pallas import tpu as pltpu
from jax.sharding import PartitionSpec as P

epsilon = 1e-05
bf16=jnp.bfloat16; f32=jnp.float32
DH=64
AUG=16
TN=(((0,),(0,)),((),()))
NT=(((1,),(1,)),((),()))
NN=(((1,),(0,)),((),()))

def split3(u):
    row=lax.broadcasted_iota(jnp.int32,u.shape,0)
    hi=u.astype(bf16).astype(f32)
    r1=u-hi
    mid=r1.astype(bf16).astype(f32)
    lo=r1-mid
    return jnp.where(row<3,hi,jnp.where(row<6,mid,jnp.where(row<9,lo,0.0))).astype(bf16)

def fwd_kernel(q_ref,k_ref,v_ref,r_ref,s_ref,segq_ref,segk_ref,p_ref,m_ref,ml_ref,c_sc,k_sc,*,tq):
    nq=q_ref.shape[1]; nk=k_ref.shape[1]
    q=q_ref[...].astype(f32)
    sm=s_ref[...]
    c_sc[:DH]=(q+sm[:,0:1]).astype(bf16)*jnp.asarray(0.125,bf16)
    pos=(q+sm[:,1:2]).astype(bf16)*jnp.asarray(0.125,bf16)
    typed=q+sm[:,2:3]
    t0=jnp.sum(typed*sm[:,3:4],axis=0,keepdims=True)*0.125
    t1=jnp.sum(typed*sm[:,4:5],axis=0,keepdims=True)*0.125
    kind=lax.rem(lax.broadcasted_iota(jnp.int32,(AUG,nq),0),3)
    c_sc[DH:]=split3(jnp.where(segq_ref[...]==kind,t1,t0))
    k_sc[:DH]=k_ref[...]
    rowk=lax.broadcasted_iota(jnp.int32,(AUG,nk),0)
    k_sc[DH:]=jnp.where((segk_ref[...]==lax.rem(rowk,3)) & (rowk<9),1.0,0.0).astype(bf16)
    w=nk+2*tq
    for b in range(nq//tq):
        i0=b*tq
        w0=nk-2*i0-2*tq
        c=lax.dot_general(c_sc[:,i0:i0+tq],k_sc[...],TN,preferred_element_type=f32)
        d=lax.dot_general(pos[:,i0:i0+tq],r_ref[:,w0:w0+w],TN,preferred_element_type=f32)
        d=pltpu.roll(d,w-2*tq,1,stride=2,stride_axis=0)
        s=c+d[:,:nk]
        mx=jnp.max(s,axis=1,keepdims=True)
        e=jnp.exp(s-mx)
        l=jnp.sum(e,axis=1,keepdims=True)
        p=(e*(1.0/l)).astype(bf16)
        p_ref[i0:i0+tq,:]=p
        mixed=lax.dot_general(v_ref[...],p,NT,preferred_element_type=f32)
        m_ref[:,i0:i0+tq]=mixed
        ml_ref[:,i0:i0+tq]=mixed.astype(bf16)

def attn_fwd(qT,kT,vT,relT,small,segq,segk,tq=128):
    hd,nq=qT.shape; nk=kT.shape[1]; heads=hd//DH
    return pl.pallas_call(partial(fwd_kernel,tq=tq),grid=(heads,),
        in_specs=[pl.BlockSpec((DH,nq),lambda h:(h,0)),pl.BlockSpec((DH,nk),lambda h:(h,0)),pl.BlockSpec((DH,nk),lambda h:(h,0)),
          pl.BlockSpec((DH,2*nk),lambda h:(h,0)),pl.BlockSpec((DH,small.shape[1]),lambda h:(h,0)),
          pl.BlockSpec((1,nq),lambda h:(0,0)),pl.BlockSpec((1,nk),lambda h:(0,0))],
        out_specs=[pl.BlockSpec((None,nq,nk),lambda h:(h,0,0)),pl.BlockSpec((DH,nq),lambda h:(h,0)),pl.BlockSpec((DH,nq),lambda h:(h,0))],
        out_shape=[jax.ShapeDtypeStruct((heads,nq,nk),bf16),jax.ShapeDtypeStruct((hd,nq),f32),jax.ShapeDtypeStruct((hd,nq),bf16)],
        scratch_shapes=[pltpu.VMEM((DH+AUG,nq),bf16),pltpu.VMEM((DH+AUG,nk),bf16)],
        name="attend",**limits(15<<20))(qT,kT,vT,relT,small,segq,segk)

def bwd_kernel(q_ref,k_ref,v_ref,r_ref,s_ref,segq_ref,segk_ref,p_ref,m_ref,dm_ref,
               dq_ref,dk_ref,dv_ref,dr_ref,sg_ref,k_sc,v_sc,dm_sc,ds_sc,dg_sc,*,tq,first):
    nq=q_ref.shape[1]; nk=k_ref.shape[1]
    q=q_ref[...].astype(f32)
    sm=s_ref[...]
    content=(q+sm[:,0:1]).astype(bf16)*jnp.asarray(0.125,bf16)
    pos=(q+sm[:,1:2]).astype(bf16)*jnp.asarray(0.125,bf16)
    typed=q+sm[:,2:3]
    k_sc[:DH]=k_ref[...]
    rowk=lax.broadcasted_iota(jnp.int32,(AUG,nk),0)
    k_sc[DH:]=((segk_ref[...]==rowk)).astype(f32).astype(bf16)
    v_sc[:DH]=v_ref[...]
    v_sc[DH:]=jnp.where(rowk<3,1.0,0.0).astype(bf16)
    dm=dm_ref[...]
    dm_sc[:DH]=dm
    delta=-jnp.sum(dm.astype(f32)*m_ref[...],axis=0,keepdims=True)
    rowq=lax.broadcasted_iota(jnp.int32,(AUG,nq),0)
    hi=delta.astype(bf16).astype(f32); r1=delta-hi; mid=r1.astype(bf16).astype(f32); lo=r1-mid
    dm_sc[DH:]=jnp.where(rowq==0,hi,jnp.where(rowq==1,mid,jnp.where(rowq==2,lo,0.0))).astype(bf16)
    w=nk+2*tq
    flip=(lax.broadcasted_iota(jnp.int32,(tq,tq),0)+lax.broadcasted_iota(jnp.int32,(tq,tq),1)==tq-1).astype(f32).astype(bf16)
    def turn16(x):
        parts=[lax.dot_general(x[:,i:i+tq],flip,NN,preferred_element_type=f32) for i in range(0,nq,tq)]
        return jnp.concatenate(parts,axis=1).astype(bf16)
    def turn(x):
        hi=x.astype(bf16); r1=x-hi.astype(f32); mid=r1.astype(bf16); lo=(r1-mid.astype(f32)).astype(bf16)
        cat=jnp.concatenate([hi,mid,lo],axis=0)
        parts=[lax.dot_general(cat[:,i:i+tq],flip,NN,preferred_element_type=f32) for i in range(0,nq,tq)]
        y=jnp.concatenate(parts,axis=1)
        return y[:DH]+y[DH:2*DH]+y[2*DH:]
    dg_sc[...]=jnp.zeros_like(dg_sc)
    for b in range(nq//tq):
        i0=b*tq
        w0=nk-2*i0-2*tq
        dp=lax.dot_general(dm_sc[:,i0:i0+tq],v_sc[...],TN,preferred_element_type=f32)
        ds=p_ref[i0:i0+tq,:].astype(f32)*dp
        ds16=ds.astype(bf16)
        ds_sc[i0:i0+tq,:]=ds16
        back=lax.dot_general(flip,ds16,NN,preferred_element_type=f32)
        g=jnp.concatenate([back,jnp.zeros((tq,2*tq),f32)],axis=1)
        g=pltpu.roll(g,2,1,stride=2,stride_axis=0)
        dg_sc[i0:i0+tq,w0:w0+w]=g.astype(bf16)
    dv_ref[...]=lax.dot_general(dm,p_ref[...],NN,preferred_element_type=f32).astype(bf16)
    dk_ref[...]=lax.dot_general(content,ds_sc[...],NN,preferred_element_type=f32).astype(bf16)
    dc=lax.dot_general(k_sc[...],ds_sc[...],NT,preferred_element_type=f32)
    dpos=turn(lax.dot_general(r_ref[...],dg_sc[...],NT,preferred_element_type=f32))*0.125
    dr=lax.dot_general(turn16(pos),dg_sc[...],NN,preferred_element_type=f32)
    if first is None:
        dr_ref[...]=dr
    else:
        dr_ref[...]=first[0][...]+dr
    dcontent=dc[:DH]*0.125
    seg=dc[DH:]*0.125
    rows=lax.broadcasted_iota(jnp.int32,(AUG,nq),0)
    g1=jnp.sum(jnp.where(segq_ref[...]==rows,seg,0.0),axis=0,keepdims=True)
    g0=jnp.sum(seg,axis=0,keepdims=True)-g1
    dtyped=sm[:,3:4]*g0+sm[:,4:5]*g1
    dq_ref[...]=(dcontent+dpos+dtyped).astype(bf16)
    lane=lax.broadcasted_iota(jnp.int32,(DH,128),1)
    total=jnp.zeros((DH,128),f32)
    for n,val in enumerate((dcontent,dpos,dtyped,typed*g0,typed*g1)):
        total=jnp.where(lane==n,jnp.sum(val,axis=1,keepdims=True),total)
    if first is None:
        sg_ref[...]=total
    else:
        sg_ref[...]=first[1][...]+total

def bwd_kernel_first(*refs,tq):
    bwd_kernel(*refs,tq=tq,first=None)
def bwd_kernel_next(*refs,tq):
    bwd_kernel(*refs[:10],*refs[12:],tq=tq,first=refs[10:12])

def attn_bwd(qT,kT,vT,relT,small,segq,segk,probs,mixedT,dmixedT,carry=None,tq=128):
    hd,nq=qT.shape; nk=kT.shape[1]; heads=hd//DH
    row=lambda n: pl.BlockSpec((DH,n),lambda h:(h,0))
    ins=[row(nq),row(nk),row(nk),row(2*nk),row(small.shape[1]),pl.BlockSpec((1,nq),lambda h:(0,0)),pl.BlockSpec((1,nk),lambda h:(0,0)),
         pl.BlockSpec((None,nq,nk),lambda h:(h,0,0)),row(nq),row(nq)]
    args=[qT,kT,vT,relT,small,segq,segk,probs,mixedT,dmixedT]
    kern=bwd_kernel_first
    if carry is not None:
        ins+= [row(2*nk),row(128)]; args+=list(carry); kern=bwd_kernel_next
    return pl.pallas_call(partial(kern,tq=tq),grid=(heads,),in_specs=ins,
        out_specs=[row(nq),row(nk),row(nk),row(2*nk),row(128)],
        out_shape=[jax.ShapeDtypeStruct((hd,nq),bf16),jax.ShapeDtypeStruct((hd,nk),bf16),jax.ShapeDtypeStruct((hd,nk),bf16),
           jax.ShapeDtypeStruct((hd,2*nk),f32),jax.ShapeDtypeStruct((hd,128),f32)],
        scratch_shapes=[pltpu.VMEM((DH+AUG,nk),bf16),pltpu.VMEM((DH+AUG,nk),bf16),pltpu.VMEM((DH+AUG,nq),bf16),pltpu.VMEM((nq,nk),bf16),pltpu.VMEM((nq,2*nk),bf16)],
        name="attend_back",**limits(15<<20))(*args)


PARTS = 4


def pair_matrix(count, axis):
    shape = (count, 2 * count) if axis == 1 else (2 * count, count)
    longer = lax.broadcasted_iota(jnp.int32, shape, axis)
    shorter = lax.broadcasted_iota(jnp.int32, shape, 1 - axis)
    return jnp.where(jnp.right_shift(longer, 1) == shorter, 0.5, 0.0).astype(bf16)


def spot(place_ref, core, column, line):
    return (
        4 * jnp.bitwise_xor(place_ref[0], line)
        + 2 * jnp.bitwise_xor(place_ref[1], column)
        + jnp.bitwise_xor(place_ref[2], core)
    )


def project_kernel(
    place_ref, near0_ref, near1_ref, far0_ref, far1_ref, own_ref, peer_ref, phase_ref,
    own_q, own_k, own_v, peer_q, peer_k, peer_v, rel_ref, pooled_ref, own_low, peer_low, weights_ref,
    turned_sc,
):
    step = pl.program_id(0)

    @pl.when(step == 0)
    def _():
        for i in range(PARTS):
            for n, ref in enumerate((near0_ref, near1_ref, far0_ref, far1_ref)):
                for d in range(ref.shape[0]):
                    weights_ref[i, spot(place_ref, n // 2, n % 2, d)] = ref[d, i]
            turned_sc[i] = weights_ref[i].reshape(-1, near0_ref.shape[3]).T

    def sequence(rows_ref, q_ref, k_ref, v_ref, low_ref, keep_ref):
        rows = rows_ref[...]
        pooled = jnp.dot(pair_matrix(rows.shape[0] // 2, 1), rows, preferred_element_type=f32)
        low = pooled.astype(bf16)
        low_ref[...] = low
        if keep_ref is not None:
            keep_ref[...] = pooled
        for i, (source, target) in enumerate(((low, q_ref), (rows, k_ref), (rows, v_ref))):
            target[...] = lax.dot_general(turned_sc[i], source, NT, preferred_element_type=f32).astype(bf16)

    @pl.when(step == 0)
    def _():
        sequence(own_ref, own_q, own_k, own_v, own_low, pooled_ref)

    @pl.when(step == 1)
    def _():
        sequence(peer_ref, peer_q, peer_k, peer_v, peer_low, None)

    @pl.when(step == 2)
    def _():
        rel_ref[...] = lax.dot_general(turned_sc[3], phase_ref[...], NT, preferred_element_type=f32).astype(bf16)


def whole(array):
    return pl.BlockSpec(array.shape, lambda *step: (0,) * array.ndim, pipeline_mode=pl.Buffered(1))


def out(shape, dtype):
    return jax.ShapeDtypeStruct(shape, dtype)


def limits(moved):
    return dict(
        compiler_params=pltpu.CompilerParams(vmem_limit_bytes=56 << 20),
        cost_estimate=pl.CostEstimate(flops=moved, bytes_accessed=moved, transcendentals=0),
    )


def project(place, stacks, tokens, peer_tokens, phase):
    length, model = tokens.shape
    half = length // 2
    count, _, depth, width = stacks[0].shape
    ins = [*stacks, tokens, peer_tokens, phase]
    outs = [
        out((width, half), bf16), out((width, length), bf16), out((width, length), bf16),
        out((width, half), bf16), out((width, length), bf16), out((width, length), bf16),
        out((width, 2 * length), bf16), out((half, model), f32), out((half, model), bf16), out((half, model), bf16),
        out((PARTS, 4 * count, depth, width), bf16),
    ]
    return pl.pallas_call(
        project_kernel,
        grid=(3,),
        in_specs=[pl.BlockSpec(memory_space=pltpu.SMEM)] + [whole(a) for a in ins],
        out_specs=[whole(a) for a in outs],
        out_shape=outs,
        scratch_shapes=[pltpu.VMEM((PARTS, width, model), bf16)],
        name="project",
        **limits(10 << 20),
    )(place, *ins)


def weigh_kernel(
    place_ref, own_rows, peer_rows, own_low, peer_low, phase_ref, own_dq, own_dk, own_dv, peer_dq, peer_dk, peer_dv,
    drel_ref, small_ref, keep_ref, send_ref, total_sc, value_sc,
):
    step = pl.program_id(0)

    @pl.when(step == 0)
    def _():
        total_sc[...] = jnp.zeros_like(total_sc)

    for i, pairs in enumerate((
        ((own_dq, own_low), (peer_dq, peer_low)),
        ((own_dk, own_rows), (peer_dk, peer_rows)),
        ((own_dv, own_rows), (peer_dv, peer_rows)),
        ((drel_ref, phase_ref),),
    )):
        for grad, rows in pairs:
            total_sc[i] += jnp.dot(grad[...].astype(bf16), rows[...], preferred_element_type=f32)

    @pl.when(step == pl.num_programs(0) - 1)
    def _():
        columns, lines, _, width = keep_ref.shape
        depth = value_sc.shape[1]
        for i in range(PARTS):
            value_sc[...] = total_sc[i].astype(bf16).T.reshape(value_sc.shape)
            for core, ref in enumerate((keep_ref, send_ref)):
                for column in range(columns):
                    for line in range(lines):
                        ref[column, line, i * depth:(i + 1) * depth] = value_sc[spot(place_ref, core, column, line)]
        small = small_ref[...].astype(bf16)
        for column in range(columns):
            for line in range(lines):
                for ref in (keep_ref, send_ref):
                    ref[column, line, PARTS * depth:] = small


def weigh(place, own_rows, peer_rows, own_low, peer_low, phase, own_grads, peer_grads, drel, small, blocks, steps=4):
    model = own_rows.shape[1]
    depth = model // blocks
    width = small.shape[1]

    def rows(array):
        return pl.BlockSpec((array.shape[0] // steps, model), lambda s: (s, 0))

    def columns(array):
        return pl.BlockSpec((width, array.shape[1] // steps), lambda s: (0, s))

    ins = [own_rows, peer_rows, own_low, peer_low, phase]
    grads = [*own_grads, *peer_grads, drel]
    pieces = out((2, blocks // 4, PARTS * depth + small.shape[0], width), bf16)
    return pl.pallas_call(
        weigh_kernel,
        grid=(steps,),
        in_specs=[pl.BlockSpec(memory_space=pltpu.SMEM)] + [rows(a) for a in ins] + [columns(a) for a in grads] + [whole(small)],
        out_specs=[whole(pieces)] * 2,
        out_shape=[pieces] * 2,
        scratch_shapes=[pltpu.VMEM((PARTS, width, model), f32), pltpu.VMEM((blocks, depth, width), bf16)],
        name="weigh",
        **limits(8 << 20),
    )(place, *ins, *grads, small)


def token_kernel(dq_ref, dk_ref, dv_ref, w_ref, *refs):
    model = refs[-1].shape[1]
    width = dk_ref.shape[0]
    half = dq_ref.shape[1]
    doubled = jnp.dot(dq_ref[...], pair_matrix(half, 1), preferred_element_type=f32).astype(bf16)
    total = None
    for i, grad in enumerate((doubled, dk_ref[...], dv_ref[...])):
        term = lax.dot_general(grad.T, w_ref[i].reshape(model, width), NT, preferred_element_type=f32)
        total = term if total is None else total + term
    if len(refs) > 1:
        high = refs[0][...].astype(bf16)
        low = (refs[0][...] - high.astype(f32)).astype(bf16)
        pairs = pair_matrix(half, 0)
        total = total + jnp.dot(pairs, high, preferred_element_type=f32) + jnp.dot(pairs, low, preferred_element_type=f32)
    refs[-1][...] = total.astype(refs[-1].dtype)


def token_grad(grads, weights, extra, dtype):
    length = grads[1].shape[1]
    model = weights.shape[1] * weights.shape[2]
    ins = [*grads, weights] + ([extra] if extra is not None else [])
    specs = [whole(a) for a in ins]
    result = out((length, model), dtype)
    return pl.pallas_call(
        token_kernel,
        grid=(1,),
        in_specs=specs,
        out_specs=whole(result),
        out_shape=result,
        name="token_grad",
        **limits(5 << 20),
    )(*ins)


def layer_norm(values_in):
    row_mean = jnp.mean(values_in, axis=1, keepdims=True)
    centred = values_in - row_mean
    variance = jnp.mean(centred * centred, axis=1, keepdims=True)
    scale = lax.rsqrt(variance + epsilon)
    return centred * scale, scale


def layer_norm_back(grad, normed, scale, gain):
    inner = grad * gain
    return scale * (
        inner
        - jnp.mean(inner, axis=1, keepdims=True)
        - normed * jnp.mean(inner * normed, axis=1, keepdims=True)
    )


def row_sum(values_in):
    return jnp.sum(values_in, axis=0, keepdims=True)


def middle_kernel(
    place_ref, pooled_ref, mixed_ref, sent_ref, vec_ref, cot_ref, own_c_ref, peer_c_ref, wide_ref, narrow_ref, own_bias_ref, peer_bias_ref,
    result_ref, dfirst_ref, own_dm_ref, peer_dm_ref, keep_c_ref, send_c_ref, sums_ref, bias_sum_ref,
    keep_w_ref, send_w_ref, keep_n_ref, send_n_ref,
    value_sc, slope_sc, act_sc, dhid_sc, first_sc, norm_sc, scale_sc, total_sc, low_sc, low_t_sc, dsec_sc, dsec_t_sc,
    *, chunks,
):
    step = pl.program_id(0)
    model = pooled_ref.shape[1]
    rows = pooled_ref.shape[0]
    part = wide_ref.shape[-1]
    vec = vec_ref[...]

    def scatter(value, keep_ref, send_ref, half=0):
        value = value.astype(bf16)
        wide = value.shape[1]
        value_sc[:, :, :wide] = value.reshape(value_sc.shape[0], -1, wide)
        columns, lines = keep_ref.shape[1:3]
        for core, ref in enumerate((keep_ref, send_ref)):
            for column in range(columns):
                for line in range(lines):
                    ref[half, column, line] = value_sc[spot(place_ref, core, column, line), :, :wide]

    postbias, scaling, centring = vec[0:1], vec[1:2], vec[2:3]
    narrowbias, rescale, recentre = vec[3:4], vec[4:5], vec[5:6]

    @pl.when(step == 0)
    def _():
        own_c = own_c_ref[...].reshape(model, -1)
        peer_c = peer_c_ref[...].reshape(model, -1)
        mixed = mixed_ref[...].astype(bf16).T
        sent = sent_ref[...].T
        branch = (
            lax.dot_general(mixed, own_c, NT, preferred_element_type=f32)
            + lax.dot_general(sent, peer_c, NT, preferred_element_type=f32)
            + postbias
        )
        normed, scale = layer_norm(pooled_ref[...] + branch)
        norm_sc[...] = normed
        scale_sc[...] = scale
        first = normed * scaling + centring
        first_sc[...] = first
        low = first.astype(bf16)
        low_sc[...] = low
        low_t_sc[...] = low.T
        total_sc[...] = jnp.zeros_like(total_sc)

    @pl.when(step < chunks)
    def _():
        wide = wide_ref[...].reshape(model, part)
        each = own_bias_ref.shape[0]
        spot_bias = lax.rem(step, each)
        bias = jnp.where(step // each == place_ref[3], own_bias_ref[spot_bias], peer_bias_ref[spot_bias])
        hidden = jnp.dot(low_sc[...], wide, preferred_element_type=f32) + bias
        square = hidden * hidden
        root = math.sqrt(2.0 / math.pi)
        turn = jnp.tanh(hidden * (root + (root * 0.044715) * square))
        half = 0.5 * turn + 0.5
        act = (hidden * half).astype(bf16)
        slope_sc[step] = half + hidden * (half * (1.0 - turn)) * (root + (3.0 * root * 0.044715) * square)
        act_sc[step] = act
        narrow = narrow_ref[...].reshape(model, part)
        total_sc[...] += lax.dot_general(act, narrow, NT, preferred_element_type=f32)

    @pl.when(step == chunks - 1)
    def _():
        normed, scale = layer_norm(first_sc[...] + (total_sc[...] + narrowbias))
        result_ref[...] = (normed * rescale + recentre).astype(bf16)
        cot = cot_ref[...].astype(f32)
        dfinal = layer_norm_back(cot, normed, scale, rescale)
        dsec = dfinal.astype(bf16)
        dsec_sc[...] = dsec
        dsec_t_sc[...] = dsec.T
        sums_ref[3:4] = row_sum(dsec.astype(f32))
        sums_ref[4:5] = row_sum(cot * normed)
        sums_ref[5:6] = row_sum(cot)
        total_sc[...] = dfinal

    back = step - chunks

    @pl.when((back >= 0) & (lax.rem(back, 2) == 0))
    def _():
        chunk = back // 2
        narrow = narrow_ref[...].reshape(model, part)
        dact = jnp.dot(dsec_sc[...], narrow, preferred_element_type=f32)
        dhid = (dact * slope_sc[chunk]).astype(bf16)
        dhid_sc[...] = dhid
        bias_sum_ref[0] = row_sum(dhid.astype(f32))
        grad = jnp.dot(dsec_t_sc[...], act_sc[chunk], preferred_element_type=f32)
        scatter(grad, keep_n_ref, send_n_ref)

    @pl.when((back >= 0) & (lax.rem(back, 2) == 1))
    def _():
        wide = wide_ref[...].reshape(model, part)
        total_sc[...] += lax.dot_general(dhid_sc[...], wide, NT, preferred_element_type=f32)
        grad = jnp.dot(low_t_sc[...], dhid_sc[...], preferred_element_type=f32)
        scatter(grad, keep_w_ref, send_w_ref)

    @pl.when(back == 2 * chunks - 1)
    def _():
        dfirst = total_sc[...]
        normed = norm_sc[...]
        dfirst_in = layer_norm_back(dfirst, normed, scale_sc[...], scaling)
        dfirst_ref[...] = dfirst_in
        dbranch = dfirst_in.astype(bf16)
        sums_ref[0:1] = row_sum(dbranch.astype(f32))
        sums_ref[1:2] = row_sum(dfirst * normed)
        sums_ref[2:3] = row_sum(dfirst)
        dbranch_t = dbranch.T
        for half, c_ref, m_ref, dm_ref in (
            (0, own_c_ref, mixed_ref, own_dm_ref),
            (1, peer_c_ref, sent_ref, peer_dm_ref),
        ):
            c = c_ref[...].reshape(model, -1)
            dm_ref[...] = lax.dot_general(c, dbranch_t, TN, preferred_element_type=f32).astype(bf16)
            dc = lax.dot_general(dbranch_t, m_ref[...].astype(bf16), NT, preferred_element_type=f32)
            scatter(dc, keep_c_ref, send_c_ref, half)


def middle(place, pooled, mixed, sent, vec, cot, weights, own_bias, peer_bias):
    rows, model = pooled.shape
    blocks, halves, depth, columns = weights.shape
    width = mixed.shape[0]
    hidden = (columns - width) // 2
    part = hidden // 2
    each = hidden // part
    chunks = halves * each

    def chunk_of(step):
        return jnp.where(step < chunks, step, (step - chunks) // 2)

    def weight_spec(offset):
        def index(step, place_ref):
            c = chunk_of(step)
            return (0, c // each, 0, offset * each + lax.rem(c, each))

        return pl.BlockSpec((blocks, None, depth, part), index)

    def combiner_spec(flip):
        def index(step, place_ref):
            return (0, jnp.bitwise_xor(place_ref[3], flip), 0, 2 * hidden // width)

        return pl.BlockSpec((blocks, None, depth, width), index, pipeline_mode=pl.Buffered(1))

    def grad_index(delay):
        def index(step, place_ref):
            c = jnp.maximum(step - chunks - delay, 0) // 2
            return (jnp.bitwise_xor(c // each, place_ref[3]), 0, 0, 0, lax.rem(c, each))

        return index

    lines = blocks // 4
    outs = [
        out((rows, model), bf16), out((rows, model), f32), out(mixed.shape, bf16), out(mixed.shape, bf16),
        out((halves, 2, lines, depth, width), bf16), out((halves, 2, lines, depth, width), bf16), out((8, model), f32),
    ]
    grads = out((halves, 2, lines, depth, hidden), bf16)
    whole_ins = [pooled, mixed, sent, vec, cot]
    grad_spec = [pl.BlockSpec((1, 2, lines, depth, part), grad_index(delay)) for delay in (1, 1, 0, 0)]
    return pl.pallas_call(
        partial(middle_kernel, chunks=chunks),
        grid_spec=pltpu.PrefetchScalarGridSpec(
            num_scalar_prefetch=1,
            grid=(3 * chunks,),
            in_specs=[whole(a) for a in whole_ins]
            + [combiner_spec(0), combiner_spec(1), weight_spec(0), weight_spec(1)]
            + [pl.BlockSpec((each, 1, part), lambda s, p: (0, 0, 0))] * 2,
            out_specs=[whole(a) for a in outs]
            + [pl.BlockSpec((1, 1, part), lambda s, p: (jnp.maximum(s - chunks, 0) // 2, 0, 0))]
            + grad_spec,
            scratch_shapes=[
                pltpu.VMEM((blocks, depth, part), bf16),
                pltpu.VMEM((chunks, rows, part), f32),
                pltpu.VMEM((chunks, rows, part), bf16),
                pltpu.VMEM((rows, part), bf16),
                pltpu.VMEM((rows, model), f32),
                pltpu.VMEM((rows, model), f32),
                pltpu.VMEM((rows, 1), f32),
                pltpu.VMEM((rows, model), f32),
                pltpu.VMEM((rows, model), bf16),
                pltpu.VMEM((model, rows), bf16),
                pltpu.VMEM((rows, model), bf16),
                pltpu.VMEM((model, rows), bf16),
            ],
        ),
        out_shape=outs + [out((chunks, 1, part), f32)] + [grads] * 4,
        name="middle",
        **limits(24 << 20),
    )(place, *whole_ins, weights, weights, weights, weights, own_bias.reshape(each, 1, part), peer_bias.reshape(each, 1, part))


def position_table(length, model_width):
    row_index = jnp.arange(2 * length, dtype=jnp.float32)
    offset = length - row_index
    half_width = model_width // 2
    frequency = jnp.exp(
        jnp.arange(half_width, dtype=jnp.float32) * (-math.log(10000.0) / half_width)
    )
    angles = offset[:, None] * frequency[None, :]
    return jnp.concatenate([jnp.sin(angles), jnp.cos(angles)], axis=1)


BLOCKS = 16


def swap(piece):
    return lax.ppermute(piece, "tensor", [(0, 1), (1, 0)])


def exchange(piece, mask):
    count = lax.axis_size("dp")
    return lax.ppermute(piece, "dp", [(i, i ^ mask) for i in range(count)])


def shards(
    tokens,
    segments,
    projections,
    combiner,
    offsets,
    sameness,
    postbias,
    scaling,
    centring,
    widener,
    widebias,
    narrower,
    narrowbias,
    rescale,
    recentre,
    cotangent,
):
    tensor_part = lax.axis_index("tensor")
    dp_part = lax.axis_index("dp")
    dp_count = lax.axis_size("dp")
    length, model = tokens.shape
    width = offsets.shape[1]
    hidden = widener.shape[1]
    blocks = BLOCKS
    depth = model // blocks
    direct = dp_count == blocks
    if direct:
        place = jnp.stack([dp_part // 4, (dp_part // 2) % 2, dp_part % 2, tensor_part]).astype(jnp.int32)
    else:
        place = jnp.stack([tensor_part * 0] * 3 + [tensor_part]).astype(jnp.int32)

    if direct:
        near0 = jnp.stack([projections] + [exchange(projections, 4 * d) for d in range(1, 4)])
        near1 = exchange(near0, 2)
        stacks = (near0, near1, exchange(near0, 1), exchange(near1, 1))
    else:
        every = lax.all_gather(projections, "dp", axis=1, tiled=True)
        every = every.reshape(PARTS, blocks // 4, 2, 2, depth, width).transpose(3, 2, 1, 0, 4, 5)
        stacks = (every[0, 0], every[0, 1], every[1, 0], every[1, 1])
    peer_tokens = swap(tokens)
    mine = jnp.concatenate([widener, narrower.T, combiner.T], axis=1)
    columns = mine.shape[1]
    weights = lax.all_gather(mine, ("dp", "tensor"), axis=0, tiled=False)
    if not direct:
        weights = weights.reshape(dp_count, 2, model // dp_count, columns).transpose(1, 0, 2, 3)
        weights = weights.reshape(2, blocks, depth, columns).transpose(1, 0, 2, 3)
    weights = weights.reshape(blocks, 2, depth, columns)
    peer_tokens, peer_bias = lax.optimization_barrier((peer_tokens, swap(widebias)))
    phase = position_table(length, model).astype(bf16)
    own_q, own_k, own_v, peer_q, peer_k, peer_v, relative, pooled, own_low, peer_low, inwards = project(
        place, stacks, tokens, peer_tokens, phase
    )
    small = jnp.concatenate([offsets, sameness], axis=0).T
    own_seg = lax.dynamic_slice_in_dim(segments, tensor_part, 1, 0)
    peer_seg = lax.dynamic_slice_in_dim(segments, 1 - tensor_part, 1, 0)
    own_args = (own_q, own_k, own_v, relative, small, own_seg[:, ::2], own_seg)
    peer_args = (peer_q, peer_k, peer_v, relative, small, peer_seg[:, ::2], peer_seg)
    peer_probs, peer_mixed, peer_mixed_low = attn_fwd(*peer_args)
    sent_mixed = swap(peer_mixed_low)
    own_probs, own_mixed, own_mixed_low = attn_fwd(*own_args)
    vec = jnp.stack([postbias, scaling, centring, narrowbias, rescale, recentre, postbias, postbias])
    result, dfirst_in, own_dmixed, peer_dmixed, keep_c, send_c, sums, bias_sums, keep_w, send_w, keep_n, send_n = middle(
        place, pooled, own_mixed_low, sent_mixed, vec, cotangent, weights, widebias, peer_bias
    )
    sent_dmixed = swap(peer_dmixed)
    own_dq, own_dk, own_dv, drel, late = attn_bwd(*own_args, own_probs, own_mixed, own_dmixed)
    early = jnp.concatenate([sums[:6], bias_sums.reshape(-1, model)], axis=0)
    early = early + swap(early)
    if direct:

        def add(kept, sent):
            return (kept.astype(f32) + sent.astype(f32)).astype(bf16)

        wide = (keep_w, exchange(send_w, 1))
        narrow = (keep_n, exchange(send_n, 1))
        comb = (keep_c, exchange(send_c, 1))

        def joined(pick):
            return jnp.concatenate([add(*map(pick, narrow)), add(*map(pick, comb))], axis=-1)

        first_stage = (
            add(wide[0][0], wide[1][0]),
            add(wide[0][1], wide[1][1]),
            joined(lambda a: a[:, 0]),
            joined(lambda a: a[:, 1]),
        )
        drel, late, sent_dmixed, early, first_stage = lax.optimization_barrier(
            (drel, late, sent_dmixed, early, first_stage)
        )

    peer_dq, peer_dk, peer_dv, drel, late = attn_bwd(
        *peer_args, peer_probs, peer_mixed, sent_dmixed, (drel, late)
    )
    own_grads = (own_dq, own_dk, own_dv)
    peer_grads = (peer_dq, peer_dk, peer_dv)
    early_rows = early.reshape(-1, width)
    used = 5 + early_rows.shape[0]
    padding = jnp.zeros((-used % 16, width), f32)
    extras = jnp.concatenate([late[:, :5].T, early_rows, padding], axis=0)
    if direct:
        wide = (first_stage[0], swap(first_stage[1]))
        drel, wide = lax.optimization_barrier((drel, wide))
    keep, send = weigh(
        place, tokens, peer_tokens, own_low, peer_low, phase, own_grads, peer_grads, drel, extras, blocks
    )
    if direct:
        narrow = (first_stage[2], exchange(first_stage[3], 2))
        wide = (add(wide[0][0], wide[1][0]), add(wide[0][1], wide[1][1]))
        narrow = (add(narrow[0][0], narrow[1][0]), add(narrow[0][1], narrow[1][1]))
        peer_grads, wide, narrow = lax.optimization_barrier((peer_grads, wide, narrow))
        wide = (wide[0], exchange(wide[1], 2))
        narrow = (narrow[0], swap(narrow[1]))
        held = [jnp.concatenate([add(wide[0][d], wide[1][d]), add(narrow[0][d], narrow[1][d])], axis=-1) for d in range(4)]
        grads = held[0].astype(f32)
        for d in range(1, 4):
            grads = grads + exchange(held[d], 4 * d).astype(f32)
    else:

        def ordered(kept, sent, flip=False):
            value = jnp.stack([kept, sent]).transpose(3, 2, 0, 1, 4, 5)
            if flip:
                value = jnp.where(tensor_part == 0, value, value[:, :, :, ::-1])
            return value.transpose(3, 0, 1, 2, 4, 5).reshape(2, dp_count, model // dp_count, -1)

        grads = jnp.concatenate([ordered(keep_w, send_w, True), ordered(keep_n, send_n, True), ordered(keep_c, send_c, True)], axis=-1)
        grads = lax.psum_scatter(
            grads.transpose(1, 0, 2, 3).reshape(2 * dp_count, model // dp_count, columns),
            ("dp", "tensor"),
            scatter_dimension=0,
            tiled=True,
        )[0].astype(f32)
    if direct:
        sent = exchange(send, 1)
        held = (add(keep[0], sent[0]), add(keep[1], sent[1]))
        peer_grads, held = lax.optimization_barrier((peer_grads, held))
        held = (held[0], exchange(held[1], 2))
        held = [add(held[0][d], held[1][d]) for d in range(4)]
        total = held[0].astype(f32)
        for d in range(1, 4):
            total = total + exchange(held[d], 4 * d).astype(f32)
        projections_grad = total[: PARTS * depth].reshape(PARTS, depth, width)
        extras = total[PARTS * depth :]
    else:
        big = jnp.stack([keep, send])[:, :, :, : PARTS * depth]
        big = big.reshape(2, 2, blocks // 4, PARTS, depth, width).transpose(3, 2, 1, 0, 4, 5)
        projections_grad = lax.psum_scatter(
            big.reshape(PARTS, model, width), "dp", scatter_dimension=1, tiled=True
        ).astype(f32)
        extras = lax.psum(extras, "dp")
    combiner_grad = grads[:, 2 * hidden :].T
    early = extras[5:used].reshape(-1, model)
    bias_grad = lax.dynamic_slice_in_dim(early[6:].reshape(-1), tensor_part * hidden, hidden, 0)
    peer_part, own_grads = lax.optimization_barrier((token_grad(peer_grads, inwards, None, bf16), own_grads))
    sent_tokens = swap(peer_part)
    tokens_grad = token_grad(own_grads, inwards, dfirst_in, f32) + sent_tokens.astype(f32)
    return (
        result,
        tokens_grad,
        projections_grad,
        combiner_grad,
        extras[:3],
        extras[3:5],
        early[0],
        early[1],
        early[2],
        grads[:, :hidden],
        bias_grad,
        grads[:, hidden : 2 * hidden].T,
        early[3],
        early[4],
        early[5],
    )


def solution(mesh):
    placed = (
        P(("dp", "tensor"), None),
        P("dp", None),
        P(None, "dp", "tensor"),
        P("tensor", "dp"),
        P(None, "tensor"),
        P(None, "tensor"),
        P(),
        P(),
        P(),
        P("dp", "tensor"),
        P("tensor"),
        P("tensor", "dp"),
        P(),
        P(),
        P(),
        P(("dp", "tensor"), None),
    )
    return jax.shard_map(
        shards,
        mesh=mesh,
        in_specs=placed,
        out_specs=(
            P(("dp", "tensor"), None),
            P(("dp", "tensor"), None),
            P(None, "dp", "tensor"),
            P("tensor", "dp"),
            P(None, "tensor"),
            P(None, "tensor"),
            P(),
            P(),
            P(),
            P("dp", "tensor"),
            P("tensor"),
            P("tensor", "dp"),
            P(),
            P(),
            P(),
        ),
        check_vma=False,
    )
```

```python
from functools import partial
import math

import jax
import jax.numpy as jnp
from jax import lax
from jax.experimental import pallas as pl
from jax.experimental.pallas import tpu as pltpu
from jax.sharding import PartitionSpec as P

epsilon = 1e-05
bf16=jnp.bfloat16; f32=jnp.float32
DH=64
AUG=16
TN=(((0,),(0,)),((),()))
NT=(((1,),(1,)),((),()))
NN=(((1,),(0,)),((),()))

def split3(u):
    row=lax.broadcasted_iota(jnp.int32,u.shape,0)
    hi=u.astype(bf16).astype(f32)
    r1=u-hi
    mid=r1.astype(bf16).astype(f32)
    lo=r1-mid
    return jnp.where(row<3,hi,jnp.where(row<6,mid,jnp.where(row<9,lo,0.0))).astype(bf16)

def fwd_kernel(q_ref,k_ref,v_ref,r_ref,s_ref,segq_ref,segk_ref,p_ref,m_ref,ml_ref,c_sc,k_sc,*,tq):
    nq=q_ref.shape[1]; nk=k_ref.shape[1]
    q=q_ref[...].astype(f32)
    sm=s_ref[...]
    c_sc[:DH]=(q+sm[:,0:1]).astype(bf16)*jnp.asarray(0.125,bf16)
    pos=(q+sm[:,1:2]).astype(bf16)*jnp.asarray(0.125,bf16)
    typed=q+sm[:,2:3]
    t0=jnp.sum(typed*sm[:,3:4],axis=0,keepdims=True)*0.125
    t1=jnp.sum(typed*sm[:,4:5],axis=0,keepdims=True)*0.125
    kind=lax.rem(lax.broadcasted_iota(jnp.int32,(AUG,nq),0),3)
    c_sc[DH:]=split3(jnp.where(segq_ref[...]==kind,t1,t0))
    k_sc[:DH]=k_ref[...]
    rowk=lax.broadcasted_iota(jnp.int32,(AUG,nk),0)
    k_sc[DH:]=jnp.where((segk_ref[...]==lax.rem(rowk,3)) & (rowk<9),1.0,0.0).astype(bf16)

    tr=min(tq,128)
    def dense(b):
        i0=b*tq; w0=nk-2*i0-2*tq
        return lax.dot_general(pos[:,i0:i0+tq],r_ref[:,w0:w0+nk+2*tq],TN,preferred_element_type=f32)
    def cont(b):
        i0=b*tq
        return lax.dot_general(c_sc[:,i0:i0+tq],k_sc[...],TN,preferred_element_type=f32)
    def finish(b,c,d):
        i0=b*tq
        for t in range(tq//tr):
            lo=2*(tq-(t+1)*tr)
            g=pltpu.roll(d[t*tr:(t+1)*tr,lo:lo+nk+2*tr],nk,1,stride=2,stride_axis=0)
            s=c[t*tr:(t+1)*tr]+g[:,:nk]
            mx=jnp.max(s,axis=1,keepdims=True)
            e=jnp.exp(s-mx)
            l=jnp.sum(e,axis=1,keepdims=True)
            p_ref[i0+t*tr:i0+(t+1)*tr,:]=(e*(1.0/l)).astype(bf16)
    n=nq//tq
    prev=(cont(0),dense(0))
    for b in range(n):
        nxt=(cont(b+1),dense(b+1)) if b+1<n else None
        finish(b,*prev); prev=nxt
    mixed=lax.dot_general(v_ref[...],p_ref[...],NT,preferred_element_type=f32)
    m_ref[...]=mixed
    ml_ref[...]=mixed.astype(bf16)

def attn_fwd(qT,kT,vT,relT,small,segq,segk,tq=128):
    hd,nq=qT.shape; nk=kT.shape[1]; heads=hd//DH
    return pl.pallas_call(partial(fwd_kernel,tq=tq),grid=(heads,),
        in_specs=[pl.BlockSpec((DH,nq),lambda h:(h,0)),pl.BlockSpec((DH,nk),lambda h:(h,0)),pl.BlockSpec((DH,nk),lambda h:(h,0)),
          pl.BlockSpec((DH,2*nk),lambda h:(h,0)),pl.BlockSpec((DH,small.shape[1]),lambda h:(h,0)),
          pl.BlockSpec((1,nq),lambda h:(0,0)),pl.BlockSpec((1,nk),lambda h:(0,0))],
        out_specs=[pl.BlockSpec((None,nq,nk),lambda h:(h,0,0)),pl.BlockSpec((DH,nq),lambda h:(h,0)),pl.BlockSpec((DH,nq),lambda h:(h,0))],
        out_shape=[jax.ShapeDtypeStruct((heads,nq,nk),bf16),jax.ShapeDtypeStruct((hd,nq),f32),jax.ShapeDtypeStruct((hd,nq),bf16)],
        scratch_shapes=[pltpu.VMEM((DH+AUG,nq),bf16),pltpu.VMEM((DH+AUG,nk),bf16)],
        name="attend",**limits(15<<20))(qT,kT,vT,relT,small,segq,segk)

def bwd_kernel(q_ref,k_ref,v_ref,r_ref,s_ref,segq_ref,segk_ref,p_ref,m_ref,dm_ref,
               dq_ref,dk_ref,dv_ref,dr_ref,sg_ref,k_sc,v_sc,dm_sc,ds_sc,dg_sc,*,tq,first):
    nq=q_ref.shape[1]; nk=k_ref.shape[1]
    q=q_ref[...].astype(f32)
    sm=s_ref[...]
    content=(q+sm[:,0:1]).astype(bf16)*jnp.asarray(0.125,bf16)
    pos=(q+sm[:,1:2]).astype(bf16)*jnp.asarray(0.125,bf16)
    typed=q+sm[:,2:3]
    k_sc[:DH]=k_ref[...]
    rowk=lax.broadcasted_iota(jnp.int32,(AUG,nk),0)
    k_sc[DH:]=((segk_ref[...]==rowk)).astype(f32).astype(bf16)
    v_sc[:DH]=v_ref[...]
    v_sc[DH:]=jnp.where(rowk<3,1.0,0.0).astype(bf16)
    dm=dm_ref[...]
    dm_sc[:DH]=dm
    delta=-jnp.sum(dm.astype(f32)*m_ref[...],axis=0,keepdims=True)
    rowq=lax.broadcasted_iota(jnp.int32,(AUG,nq),0)
    hi=delta.astype(bf16).astype(f32); r1=delta-hi; mid=r1.astype(bf16).astype(f32); lo=r1-mid
    dm_sc[DH:]=jnp.where(rowq==0,hi,jnp.where(rowq==1,mid,jnp.where(rowq==2,lo,0.0))).astype(bf16)
    w=nk+2*tq
    flip=(lax.broadcasted_iota(jnp.int32,(tq,tq),0)+lax.broadcasted_iota(jnp.int32,(tq,tq),1)==tq-1).astype(f32).astype(bf16)
    def turn16(x):
        parts=[lax.dot_general(x[:,i:i+tq],flip,NN,preferred_element_type=f32) for i in range(0,nq,tq)]
        return jnp.concatenate(parts,axis=1).astype(bf16)
    def turn(x):
        hi=x.astype(bf16); r1=x-hi.astype(f32); mid=r1.astype(bf16); lo=(r1-mid.astype(f32)).astype(bf16)
        cat=jnp.concatenate([hi,mid,lo],axis=0)
        parts=[lax.dot_general(cat[:,i:i+tq],flip,NN,preferred_element_type=f32) for i in range(0,nq,tq)]
        y=jnp.concatenate(parts,axis=1)
        return y[:DH]+y[DH:2*DH]+y[2*DH:]

    @pl.when(pl.program_id(0)==0)
    def _():
        dg_sc[...]=jnp.zeros_like(dg_sc)
    def grad(b):
        i0=b*tq
        return lax.dot_general(dm_sc[:,i0:i0+tq],v_sc[...],TN,preferred_element_type=f32)
    def shift(b,dp):
        i0=b*tq
        w0=nk-2*i0-2*tq
        ds16=(p_ref[i0:i0+tq,:].astype(f32)*dp).astype(bf16)
        ds_sc[i0:i0+tq,:]=ds16
        back=lax.dot_general(flip,ds16,NN,preferred_element_type=f32)
        g=jnp.concatenate([back,jnp.zeros((tq,2*tq),f32)],axis=1)
        g=pltpu.roll(g,2,1,stride=2,stride_axis=0)
        dg_sc[i0:i0+tq,w0:w0+w]=g.astype(bf16)
    n=nq//tq
    for b in range(n): shift(b,grad(b))
    dv_ref[...]=lax.dot_general(dm,p_ref[...],NN,preferred_element_type=f32).astype(bf16)
    dk_ref[...]=lax.dot_general(content,ds_sc[...],NN,preferred_element_type=f32).astype(bf16)
    dc=lax.dot_general(k_sc[...],ds_sc[...],NT,preferred_element_type=f32)
    half=256
    tpos=turn16(pos)
    parts=[];drs=[]
    for c0 in range(0,nq,half):
        v0=nk-2*c0-2*half
        g=dg_sc[c0:c0+half,v0:v0+nk+2*half]
        parts.append(lax.dot_general(r_ref[:,v0:v0+nk+2*half],g,NT,preferred_element_type=f32))
        drs.append(lax.dot_general(tpos[:,c0:c0+half],g,NN,preferred_element_type=f32))
    dpos=turn(jnp.concatenate(parts,axis=1))*0.125
    z=jnp.zeros((DH,2*half),f32)
    dr=jnp.concatenate([z,drs[0]],axis=1)+jnp.concatenate([drs[1],z],axis=1)
    if first is None:
        dr_ref[...]=dr
    else:
        dr_ref[...]=first[0][...]+dr
    dcontent=dc[:DH]*0.125
    seg=dc[DH:]*0.125
    rows=lax.broadcasted_iota(jnp.int32,(AUG,nq),0)
    g1=jnp.sum(jnp.where(segq_ref[...]==rows,seg,0.0),axis=0,keepdims=True)
    g0=jnp.sum(seg,axis=0,keepdims=True)-g1
    dtyped=sm[:,3:4]*g0+sm[:,4:5]*g1
    dq_ref[...]=(dcontent+dpos+dtyped).astype(bf16)
    lane=lax.broadcasted_iota(jnp.int32,(DH,128),1)
    total=jnp.zeros((DH,128),f32)
    for n,val in enumerate((dcontent,dpos,dtyped,typed*g0,typed*g1)):
        total=jnp.where(lane==n,jnp.sum(val,axis=1,keepdims=True),total)
    if first is None:
        sg_ref[...]=total
    else:
        sg_ref[...]=first[1][...]+total

def bwd_kernel_first(*refs,tq,skip):
    bwd_kernel(*refs[:10],*refs[10+skip:],tq=tq,first=None)
def bwd_kernel_next(*refs,tq,skip):
    bwd_kernel(*refs[:10],*refs[12+skip:],tq=tq,first=refs[10:12])

def attn_bwd(qT,kT,vT,relT,small,segq,segk,probs,mixedT,dmixedT,carry=None,tq=256,heads=None,base=None):
    hd,nq=qT.shape; nk=kT.shape[1]
    start,count=heads or (0,hd//DH)
    row=lambda n: pl.BlockSpec((DH,n),lambda h:(h+start if start else h,0))
    ins=[row(nq),row(nk),row(nk),row(2*nk),row(small.shape[1]),pl.BlockSpec((1,nq),lambda h:(0,0)),pl.BlockSpec((1,nk),lambda h:(0,0)),
         pl.BlockSpec((None,nq,nk),lambda h:(h+start if start else h,0,0)),row(nq),row(nq)]
    args=[qT,kT,vT,relT,small,segq,segk,probs,mixedT,dmixedT]
    kern=bwd_kernel_first
    if carry is not None:
        ins+= [row(2*nk),row(128)]; args+=list(carry); kern=bwd_kernel_next
    aliases={}
    if base is not None:
        aliases={len(args)+n:n for n in range(5)}
        ins+=[pl.BlockSpec(memory_space=pl.ANY)]*5; args+=list(base)
    return pl.pallas_call(partial(kern,tq=tq,skip=len(aliases)),grid=(count,),in_specs=ins,
        out_specs=[row(nq),row(nk),row(nk),row(2*nk),row(128)],
        out_shape=[jax.ShapeDtypeStruct((hd,nq),bf16),jax.ShapeDtypeStruct((hd,nk),bf16),jax.ShapeDtypeStruct((hd,nk),bf16),
           jax.ShapeDtypeStruct((hd,2*nk),f32),jax.ShapeDtypeStruct((hd,128),f32)],
        input_output_aliases=aliases,
        scratch_shapes=[pltpu.VMEM((DH+AUG,nk),bf16),pltpu.VMEM((DH+AUG,nk),bf16),pltpu.VMEM((DH+AUG,nq),bf16),pltpu.VMEM((nq,nk),bf16),pltpu.VMEM((nq,2*nk),bf16)],
        name="attend_back",**limits((15*count//6)<<20))(*args)


PARTS = 4
LATE = 5


def pair_matrix(count, axis):
    shape = (count, 2 * count) if axis == 1 else (2 * count, count)
    longer = lax.broadcasted_iota(jnp.int32, shape, axis)
    shorter = lax.broadcasted_iota(jnp.int32, shape, 1 - axis)
    return jnp.where(jnp.right_shift(longer, 1) == shorter, 0.5, 0.0).astype(bf16)


def spot(place_ref, core, column, line):
    return (
        4 * jnp.bitwise_xor(place_ref[0], line)
        + 2 * jnp.bitwise_xor(place_ref[1], column)
        + jnp.bitwise_xor(place_ref[2], core)
    )


def project_kernel(
    place_ref, near0_ref, near1_ref, far0_ref, far1_ref, own_ref, peer_ref, phase_ref,
    own_q, own_k, own_v, peer_q, peer_k, peer_v, rel_ref, pooled_ref, own_low, peer_low, weights_ref,
    turned_sc,
):
    @pl.when(pl.program_id(0) == 0)
    def _():
        for i in range(PARTS):
            for n, ref in enumerate((near0_ref, near1_ref, far0_ref, far1_ref)):
                for d in range(ref.shape[0]):
                    weights_ref[i, spot(place_ref, n // 2, n % 2, d)] = ref[d, i]
            turned_sc[i] = weights_ref[i].reshape(-1, near0_ref.shape[3]).T

    pairs = pair_matrix(own_ref.shape[0] // 2, 1)

    def sequence(rows_ref, q_ref, k_ref, v_ref, low_ref, keep_ref):
        rows = rows_ref[...]
        pooled = jnp.dot(pairs, rows, preferred_element_type=f32)
        low = pooled.astype(bf16)
        low_ref[...] = low
        if keep_ref is not None:
            keep_ref[...] = pooled
        for i, (source, target) in enumerate(((low, q_ref), (rows, k_ref), (rows, v_ref))):
            target[...] = lax.dot_general(turned_sc[i], source, NT, preferred_element_type=f32).astype(bf16)

    sequence(own_ref, own_q, own_k, own_v, own_low, pooled_ref)
    sequence(peer_ref, peer_q, peer_k, peer_v, peer_low, None)
    rel_ref[...] = lax.dot_general(turned_sc[3], phase_ref[...], NT, preferred_element_type=f32).astype(bf16)


def whole(array):
    return pl.BlockSpec(array.shape, lambda *step: (0,) * array.ndim, pipeline_mode=pl.Buffered(1))


def out(shape, dtype):
    return jax.ShapeDtypeStruct(shape, dtype)


def limits(moved):
    return dict(
        compiler_params=pltpu.CompilerParams(vmem_limit_bytes=56 << 20),
        cost_estimate=pl.CostEstimate(flops=moved, bytes_accessed=moved, transcendentals=0),
    )


def project(place, stacks, tokens, peer_tokens, phase, steps=4):
    length, model = tokens.shape
    half = length // 2
    count, _, depth, width = stacks[0].shape
    ins = [*stacks, tokens, peer_tokens, phase]
    outs = [
        out((width, half), bf16), out((width, length), bf16), out((width, length), bf16),
        out((width, half), bf16), out((width, length), bf16), out((width, length), bf16),
        out((width, 2 * length), bf16), out((half, model), f32), out((half, model), bf16), out((half, model), bf16),
        out((PARTS, 4 * count, depth, width), bf16),
    ]
    def rows(array):
        return pl.BlockSpec((array.shape[0] // steps, array.shape[1]), lambda s: (s, 0))

    def columns(array):
        return pl.BlockSpec((array.shape[0], array.shape[1] // steps), lambda s: (0, s))

    return pl.pallas_call(
        project_kernel,
        grid=(steps,),
        in_specs=[pl.BlockSpec(memory_space=pltpu.SMEM)] + [whole(a) for a in stacks] + [rows(a) for a in ins[4:]],
        out_specs=[columns(a) for a in outs[:7]] + [rows(a) for a in outs[7:10]] + [whole(outs[10])],
        out_shape=outs,
        scratch_shapes=[pltpu.VMEM((PARTS, width, model), bf16)],
        name="project",
        **limits(10 << 20),
    )(place, *ins)


def weigh_kernel(
    place_ref, own_rows, peer_rows, own_low, peer_low, phase_ref, own_dq, own_dk, own_dv, peer_dq, peer_dk, peer_dv,
    drel_ref, late_ref, early_ref, keep_ref, send_ref, total_sc, value_sc, small_sc,
):
    step = pl.program_id(0)

    @pl.when(step == 0)
    def _():
        total_sc[...] = jnp.zeros_like(total_sc)

    for i, pairs in enumerate((
        ((own_dq, own_low), (peer_dq, peer_low)),
        ((own_dk, own_rows), (peer_dk, peer_rows)),
        ((own_dv, own_rows), (peer_dv, peer_rows)),
        ((drel_ref, phase_ref),),
    )):
        for grad, rows in pairs:
            total_sc[i] += jnp.dot(grad[...].astype(bf16), rows[...], preferred_element_type=f32)

    @pl.when(step == pl.num_programs(0) - 1)
    def _():
        columns, lines, _, width = keep_ref.shape
        depth = value_sc.shape[1]
        for i in range(PARTS):
            value_sc[...] = total_sc[i].astype(bf16).T.reshape(value_sc.shape)
            for core, ref in enumerate((keep_ref, send_ref)):
                for column in range(columns):
                    for line in range(lines):
                        ref[column, line, i * depth:(i + 1) * depth] = value_sc[spot(place_ref, core, column, line)]
        first, last = LATE, LATE + early_ref.shape[0]
        small_sc[...] = jnp.zeros_like(small_sc)
        small_sc[:first] = late_ref[...].T[:first]
        small_sc[first:last] = early_ref[:, :width]
        small_sc[last : 2 * last - first] = early_ref[:, width:]
        small = small_sc[...].astype(bf16)
        for column in range(columns):
            for line in range(lines):
                for ref in (keep_ref, send_ref):
                    ref[column, line, PARTS * depth:] = small


def weigh(place, own_rows, peer_rows, own_low, peer_low, phase, own_grads, peer_grads, drel, late, early, blocks, steps=4):
    model = own_rows.shape[1]
    depth = model // blocks
    width = drel.shape[0]
    extra = LATE + 2 * early.shape[0]
    extra += -extra % 16

    def rows(array):
        return pl.BlockSpec((array.shape[0] // steps, model), lambda s: (s, 0))

    def columns(array):
        return pl.BlockSpec((width, array.shape[1] // steps), lambda s: (0, s))

    ins = [own_rows, peer_rows, own_low, peer_low, phase]
    grads = [*own_grads, *peer_grads, drel]
    pieces = out((2, blocks // 4, PARTS * depth + extra, width), bf16)
    return pl.pallas_call(
        weigh_kernel,
        grid=(steps,),
        in_specs=[pl.BlockSpec(memory_space=pltpu.SMEM)] + [rows(a) for a in ins] + [columns(a) for a in grads] + [whole(late), whole(early)],
        out_specs=[whole(pieces)] * 2,
        out_shape=[pieces] * 2,
        scratch_shapes=[pltpu.VMEM((PARTS, width, model), f32), pltpu.VMEM((blocks, depth, width), bf16), pltpu.VMEM((extra, width), f32)],
        name="weigh",
        **limits(8 << 20),
    )(place, *ins, *grads, late, early)


def token_kernel(dq_ref, dk_ref, dv_ref, w_ref, *refs):
    model = refs[-1].shape[1]
    width = dk_ref.shape[0]
    half = dq_ref.shape[1]
    doubled = jnp.dot(dq_ref[...], pair_matrix(half, 1), preferred_element_type=f32).astype(bf16)
    total = None
    for i, grad in enumerate((doubled, dk_ref[...], dv_ref[...])):
        term = lax.dot_general(grad.T, w_ref[i].reshape(model, width), NT, preferred_element_type=f32)
        total = term if total is None else total + term
    if len(refs) > 1:
        high = refs[0][...].astype(bf16)
        low = (refs[0][...] - high.astype(f32)).astype(bf16)
        pairs = pair_matrix(half, 0)
        total = total + jnp.dot(pairs, high, preferred_element_type=f32) + jnp.dot(pairs, low, preferred_element_type=f32)
    refs[-1][...] = total.astype(refs[-1].dtype)


def token_grad(grads, weights, extra, dtype):
    length = grads[1].shape[1]
    model = weights.shape[1] * weights.shape[2]
    ins = [*grads, weights] + ([extra] if extra is not None else [])
    specs = [whole(a) for a in ins]
    result = out((length, model), dtype)
    return pl.pallas_call(
        token_kernel,
        grid=(1,),
        in_specs=specs,
        out_specs=whole(result),
        out_shape=result,
        name="token_grad",
        **limits(5 << 20),
    )(*ins)


def finish_kernel(place_ref, *refs, sources):
    total = refs[0][...].astype(f32)
    for ref in refs[1:sources]:
        total = total + ref[...].astype(f32)
    grads_ref, offsets_ref, sameness_ref, bias_ref, *vectors, total_sc = refs[sources:]
    parts, depth, width = grads_ref.shape
    for i in range(parts):
        grads_ref[i] = total[i * depth : (i + 1) * depth]
    total_sc[...] = total[parts * depth :]
    offsets_ref[...] = total_sc[:3]
    sameness_ref[...] = total_sc[3:LATE]
    count = len(vectors) + 4

    def row(n):
        return jnp.concatenate(
            [total_sc[LATE + n : LATE + n + 1], total_sc[LATE + count + n : LATE + count + n + 1]], axis=1
        )

    for n, ref in enumerate(vectors):
        ref[...] = row(n).reshape(ref.shape)
    n = len(vectors)
    first = place_ref[3] == 0
    bias = jnp.concatenate(
        [jnp.where(first, row(n), row(n + 2)), jnp.where(first, row(n + 1), row(n + 3))], axis=1
    )
    bias_ref[...] = bias.reshape(bias_ref.shape)


def finish(place, pieces, depth, model, hidden):
    extra = pieces[0].shape[0] - PARTS * depth
    width = pieces[0].shape[1]
    outs = [
        out((PARTS, depth, width), f32), out((3, width), f32), out((2, width), f32), out((hidden,), f32),
    ] + [out((model,), f32)] * 6
    return pl.pallas_call(
        partial(finish_kernel, sources=len(pieces)),
        grid=(1,),
        in_specs=[pl.BlockSpec(memory_space=pltpu.SMEM)] + [whole(a) for a in pieces],
        out_specs=[whole(a) for a in outs],
        out_shape=outs,
        scratch_shapes=[pltpu.VMEM((extra, width), f32)],
        name="finish",
        **limits(1 << 20),
    )(place, *pieces)


def layer_norm(values_in):
    row_mean = jnp.mean(values_in, axis=1, keepdims=True)
    centred = values_in - row_mean
    variance = jnp.mean(centred * centred, axis=1, keepdims=True)
    scale = lax.rsqrt(variance + epsilon)
    return centred * scale, scale


def layer_norm_back(grad, normed, scale, gain):
    inner = grad * gain
    return scale * (
        inner
        - jnp.mean(inner, axis=1, keepdims=True)
        - normed * jnp.mean(inner * normed, axis=1, keepdims=True)
    )


def row_sum(values_in):
    return jnp.sum(values_in, axis=0, keepdims=True)


def middle_kernel(
    place_ref, pooled_ref, mixed_ref, sent_ref, vec_ref, cot_ref, own_c_ref, peer_c_ref, wide_ref, narrow_ref, own_bias_ref, peer_bias_ref,
    result_ref, dfirst_ref, own_dm_ref, peer_dm_ref, keep_c_ref, send_c_ref, sums_ref,
    keep_w_ref, send_w_ref, keep_n_ref, send_n_ref,
    value_sc, slope_sc, act_sc, dhid_sc, first_sc, norm_sc, scale_sc, total_sc, low_sc, low_t_sc, dsec_sc, dsec_t_sc,
    *, chunks,
):
    step = pl.program_id(0)
    model = pooled_ref.shape[1]
    rows = pooled_ref.shape[0]
    part = wide_ref.shape[-1]
    vec = vec_ref[...]

    def scatter(value, keep_ref, send_ref, half=0, turned=False):
        value = value.astype(bf16)
        wide = value.shape[1]
        value_sc[:, :, :wide] = value.reshape(value_sc.shape[0], -1, wide)
        lines = keep_ref.shape[2]
        for core, ref in enumerate((keep_ref, send_ref)):
            for column in range(2):
                for line in range(lines):
                    ref[(column, half, line) if turned else (half, column, line)] = value_sc[spot(place_ref, core, column, line), :, :wide]

    postbias, scaling, centring = vec[0:1], vec[1:2], vec[2:3]
    narrowbias, rescale, recentre = vec[3:4], vec[4:5], vec[5:6]

    @pl.when(step == 0)
    def _():
        own_c = own_c_ref[...].reshape(model, -1)
        peer_c = peer_c_ref[...].reshape(model, -1)
        mixed = mixed_ref[...].astype(bf16).T
        sent = sent_ref[...].T
        branch = (
            lax.dot_general(mixed, own_c, NT, preferred_element_type=f32)
            + lax.dot_general(sent, peer_c, NT, preferred_element_type=f32)
            + postbias
        )
        normed, scale = layer_norm(pooled_ref[...] + branch)
        norm_sc[...] = normed
        scale_sc[...] = scale
        first = normed * scaling + centring
        first_sc[...] = first
        low = first.astype(bf16)
        low_sc[...] = low
        low_t_sc[...] = low.T
        total_sc[...] = jnp.zeros_like(total_sc)

    @pl.when(step < chunks)
    def _():
        wide = wide_ref[...].reshape(model, part)
        each = own_bias_ref.shape[0]
        spot_bias = lax.rem(step, each)
        bias = jnp.where(step // each == place_ref[3], own_bias_ref[spot_bias], peer_bias_ref[spot_bias])
        hidden = jnp.dot(low_sc[...], wide, preferred_element_type=f32) + bias
        square = hidden * hidden
        root = math.sqrt(2.0 / math.pi)
        turn = jnp.tanh(hidden * (root + (root * 0.044715) * square))
        half = 0.5 * turn + 0.5
        act = (hidden * half).astype(bf16)
        slope_sc[step] = half + hidden * (half * (1.0 - turn)) * (root + (3.0 * root * 0.044715) * square)
        act_sc[step] = act
        narrow = narrow_ref[...].reshape(model, part)
        total_sc[...] += lax.dot_general(act, narrow, NT, preferred_element_type=f32)

    @pl.when(step == chunks - 1)
    def _():
        normed, scale = layer_norm(first_sc[...] + (total_sc[...] + narrowbias))
        result_ref[...] = (normed * rescale + recentre).astype(bf16)
        cot = cot_ref[...].astype(f32)
        dfinal = layer_norm_back(cot, normed, scale, rescale)
        dsec = dfinal.astype(bf16)
        dsec_sc[...] = dsec
        dsec_t_sc[...] = dsec.T
        sums_ref[3:4] = row_sum(dsec.astype(f32))
        sums_ref[4:5] = row_sum(cot * normed)
        sums_ref[5:6] = row_sum(cot)
        total_sc[...] = dfinal

    back = step - chunks

    @pl.when((back >= 0) & (lax.rem(back, 2) == 0))
    def _():
        chunk = back // 2
        narrow = narrow_ref[...].reshape(model, part)
        dact = jnp.dot(dsec_sc[...], narrow, preferred_element_type=f32)
        dhid = (dact * slope_sc[chunk]).astype(bf16)
        dhid_sc[...] = dhid
        sums_ref[pl.ds(6 + chunk, 1)] = row_sum(dhid.astype(f32))
        grad = jnp.dot(dsec_t_sc[...], act_sc[chunk], preferred_element_type=f32)
        scatter(grad, keep_n_ref, send_n_ref, 0, True)

    @pl.when((back >= 0) & (lax.rem(back, 2) == 1))
    def _():
        wide = wide_ref[...].reshape(model, part)
        total_sc[...] += lax.dot_general(dhid_sc[...], wide, NT, preferred_element_type=f32)
        grad = jnp.dot(low_t_sc[...], dhid_sc[...], preferred_element_type=f32)
        scatter(grad, keep_w_ref, send_w_ref)

    @pl.when(back == 2 * chunks - 1)
    def _():
        dfirst = total_sc[...]
        normed = norm_sc[...]
        dfirst_in = layer_norm_back(dfirst, normed, scale_sc[...], scaling)
        dfirst_ref[...] = dfirst_in
        dbranch = dfirst_in.astype(bf16)
        sums_ref[0:1] = row_sum(dbranch.astype(f32))
        sums_ref[1:2] = row_sum(dfirst * normed)
        sums_ref[2:3] = row_sum(dfirst)
        dbranch_t = dbranch.T
        for half, c_ref, m_ref, dm_ref in (
            (0, own_c_ref, mixed_ref, own_dm_ref),
            (1, peer_c_ref, sent_ref, peer_dm_ref),
        ):
            c = c_ref[...].reshape(model, -1)
            dm_ref[...] = lax.dot_general(c, dbranch_t, TN, preferred_element_type=f32).astype(bf16)
            dc = lax.dot_general(dbranch_t, m_ref[...].astype(bf16), NT, preferred_element_type=f32)
            scatter(dc, keep_c_ref, send_c_ref, half, True)


def middle(place, pooled, mixed, sent, vec, cot, weights, own_bias, peer_bias):
    rows, model = pooled.shape
    blocks, halves, depth, columns = weights.shape
    width = mixed.shape[0]
    hidden = (columns - width) // 2
    part = hidden // 2
    each = hidden // part
    chunks = halves * each

    def chunk_of(step):
        return jnp.where(step < chunks, step, (step - chunks) // 2)

    def weight_spec(offset):
        def index(step, place_ref):
            c = chunk_of(step)
            return (0, c // each, 0, offset * each + lax.rem(c, each))

        return pl.BlockSpec((blocks, None, depth, part), index)

    def combiner_spec(flip):
        def index(step, place_ref):
            return (0, jnp.bitwise_xor(place_ref[3], flip), 0, 2 * hidden // width)

        return pl.BlockSpec((blocks, None, depth, width), index, pipeline_mode=pl.Buffered(1))

    def wide_index(step, place_ref):
        c = jnp.maximum(step - chunks - 1, 0) // 2
        return (jnp.bitwise_xor(c // each, place_ref[3]), 0, 0, 0, lax.rem(c, each))

    def narrow_index(step, place_ref):
        c = jnp.maximum(step - chunks, 0) // 2
        return (0, jnp.bitwise_xor(c // each, place_ref[3]), 0, 0, lax.rem(c, each))

    lines = blocks // 4
    outs = [
        out((rows, model), bf16), out((rows, model), f32), out(mixed.shape, bf16), out(mixed.shape, bf16),
        out((2, halves, lines, depth, width), bf16), out((2, halves, lines, depth, width), bf16), out((6 + chunks, model), f32),
    ]
    wide_grads = out((halves, 2, lines, depth, hidden), bf16)
    narrow_grads = out((2, halves, lines, depth, hidden), bf16)
    whole_ins = [pooled, mixed, sent, vec, cot]
    grad_spec = [pl.BlockSpec((1, 2, lines, depth, part), wide_index)] * 2
    grad_spec += [pl.BlockSpec((2, 1, lines, depth, part), narrow_index)] * 2
    return pl.pallas_call(
        partial(middle_kernel, chunks=chunks),
        grid_spec=pltpu.PrefetchScalarGridSpec(
            num_scalar_prefetch=1,
            grid=(3 * chunks,),
            in_specs=[whole(a) for a in whole_ins]
            + [combiner_spec(0), combiner_spec(1), weight_spec(0), weight_spec(1)]
            + [pl.BlockSpec((each, 1, part), lambda s, p: (0, 0, 0))] * 2,
            out_specs=[whole(a) for a in outs]
            + grad_spec,
            scratch_shapes=[
                pltpu.VMEM((blocks, depth, part), bf16),
                pltpu.VMEM((chunks, rows, part), f32),
                pltpu.VMEM((chunks, rows, part), bf16),
                pltpu.VMEM((rows, part), bf16),
                pltpu.VMEM((rows, model), f32),
                pltpu.VMEM((rows, model), f32),
                pltpu.VMEM((rows, 1), f32),
                pltpu.VMEM((rows, model), f32),
                pltpu.VMEM((rows, model), bf16),
                pltpu.VMEM((model, rows), bf16),
                pltpu.VMEM((rows, model), bf16),
                pltpu.VMEM((model, rows), bf16),
            ],
        ),
        out_shape=outs + [wide_grads] * 2 + [narrow_grads] * 2,
        name="middle",
        **limits(24 << 20),
    )(place, *whole_ins, weights, weights, weights, weights, own_bias.reshape(each, 1, part), peer_bias.reshape(each, 1, part))


def position_table(length, model_width):
    row_index = jnp.arange(2 * length, dtype=jnp.float32)
    offset = length - row_index
    half_width = model_width // 2
    frequency = jnp.exp(
        jnp.arange(half_width, dtype=jnp.float32) * (-math.log(10000.0) / half_width)
    )
    angles = offset[:, None] * frequency[None, :]
    return jnp.concatenate([jnp.sin(angles), jnp.cos(angles)], axis=1)


BLOCKS = 16


def swap(piece):
    return lax.ppermute(piece, "tensor", [(0, 1), (1, 0)])


def exchange(piece, mask):
    count = lax.axis_size("dp")
    return lax.ppermute(piece, "dp", [(i, i ^ mask) for i in range(count)])


def shards(
    tokens,
    segments,
    projections,
    combiner,
    offsets,
    sameness,
    postbias,
    scaling,
    centring,
    widener,
    widebias,
    narrower,
    narrowbias,
    rescale,
    recentre,
    cotangent,
):
    tensor_part = lax.axis_index("tensor")
    dp_part = lax.axis_index("dp")
    dp_count = lax.axis_size("dp")
    length, model = tokens.shape
    width = offsets.shape[1]
    hidden = widener.shape[1]
    blocks = BLOCKS
    depth = model // blocks
    direct = dp_count == blocks
    if direct:
        place = jnp.stack([dp_part // 4, (dp_part // 2) % 2, dp_part % 2, tensor_part]).astype(jnp.int32)
    else:
        place = jnp.stack([tensor_part * 0] * 3 + [tensor_part]).astype(jnp.int32)

    if direct:
        near0 = jnp.stack([projections] + [exchange(projections, 4 * d) for d in range(1, 4)])
        near1 = exchange(near0, 2)
        stacks = (near0, near1, exchange(near0, 1), exchange(near1, 1))
    else:
        every = lax.all_gather(projections, "dp", axis=1, tiled=True)
        every = every.reshape(PARTS, blocks // 4, 2, 2, depth, width).transpose(3, 2, 1, 0, 4, 5)
        stacks = (every[0, 0], every[0, 1], every[1, 0], every[1, 1])
    peer_tokens = swap(tokens)
    mine = jnp.concatenate([widener, narrower.T, combiner.T], axis=1)
    columns = mine.shape[1]
    weights = lax.all_gather(mine, ("dp", "tensor"), axis=0, tiled=False)
    if not direct:
        weights = weights.reshape(dp_count, 2, model // dp_count, columns).transpose(1, 0, 2, 3)
        weights = weights.reshape(2, blocks, depth, columns).transpose(1, 0, 2, 3)
    weights = weights.reshape(blocks, 2, depth, columns)
    peer_tokens, peer_bias = lax.optimization_barrier((peer_tokens, swap(widebias)))
    phase = position_table(length, model).astype(bf16)
    own_q, own_k, own_v, peer_q, peer_k, peer_v, relative, pooled, own_low, peer_low, inwards = project(
        place, stacks, tokens, peer_tokens, phase
    )
    small = jnp.concatenate([offsets, sameness], axis=0).T
    own_seg = lax.dynamic_slice_in_dim(segments, tensor_part, 1, 0)
    peer_seg = lax.dynamic_slice_in_dim(segments, 1 - tensor_part, 1, 0)
    own_args = (own_q, own_k, own_v, relative, small, own_seg[:, ::2], own_seg)
    peer_args = (peer_q, peer_k, peer_v, relative, small, peer_seg[:, ::2], peer_seg)
    peer_probs, peer_mixed, peer_mixed_low = attn_fwd(*peer_args)
    sent_mixed = swap(peer_mixed_low)
    own_probs, own_mixed, own_mixed_low = attn_fwd(*own_args)
    vec = jnp.stack([postbias, scaling, centring, narrowbias, rescale, recentre, postbias, postbias])
    result, dfirst_in, own_dmixed, peer_dmixed, keep_c, send_c, early, keep_w, send_w, keep_n, send_n = middle(
        place, pooled, own_mixed_low, sent_mixed, vec, cotangent, weights, widebias, peer_bias
    )
    sent_dmixed = swap(peer_dmixed)
    half = width // DH // 2
    part = attn_bwd(*own_args, own_probs, own_mixed, own_dmixed, heads=(0, half))
    early = early + swap(early)
    if direct:

        def add(kept, sent):
            return (kept.astype(f32) + sent.astype(f32)).astype(bf16)

        wide = (keep_w, exchange(send_w, 1))
        narrow = (keep_n, exchange(send_n, 1))
        comb = (keep_c, exchange(send_c, 1))

        def joined(pick):
            return jnp.concatenate([add(*map(pick, narrow)), add(*map(pick, comb))], axis=-1)

        first_stage = (
            add(wide[0][0], wide[1][0]),
            add(wide[0][1], wide[1][1]),
            joined(lambda a: a[0]),
            joined(lambda a: a[1]),
        )
        part, early, first_stage = lax.optimization_barrier((part, early, first_stage))

    own_dq, own_dk, own_dv, drel, late = attn_bwd(
        *own_args, own_probs, own_mixed, own_dmixed, heads=(half, width // DH - half), base=part
    )
    drel, late, sent_dmixed = lax.optimization_barrier((drel, late, sent_dmixed))
    peer_dq, peer_dk, peer_dv, drel, late = attn_bwd(
        *peer_args, peer_probs, peer_mixed, sent_dmixed, (drel, late)
    )
    own_grads = (own_dq, own_dk, own_dv)
    peer_grads = (peer_dq, peer_dk, peer_dv)
    if direct:
        wide = (first_stage[0], swap(first_stage[1]))
        narrow = (first_stage[2], exchange(first_stage[3], 2))
        wide = (add(wide[0][0], wide[1][0]), add(wide[0][1], wide[1][1]))
        narrow = (add(narrow[0][0], narrow[1][0]), add(narrow[0][1], narrow[1][1]))
        drel, wide, narrow = lax.optimization_barrier((drel, wide, narrow))
        wide = (wide[0], exchange(wide[1], 2))
        narrow = (narrow[0], swap(narrow[1]))
    keep, send = weigh(
        place, tokens, peer_tokens, own_low, peer_low, phase, own_grads, peer_grads, drel, late, early, blocks
    )
    if direct:
        keep, send, wide, narrow = lax.optimization_barrier((keep, send, wide, narrow))
        sent = exchange(send, 1)
        held = (add(keep[0], sent[0]), add(keep[1], sent[1]))
        last = [
            jnp.concatenate([add(wide[0][d], wide[1][d]), add(narrow[0][d], narrow[1][d])], axis=-1)
            for d in range(4)
        ]
        peer_grads, held, last = lax.optimization_barrier((peer_grads, held, last))
        held = (held[0], exchange(held[1], 2))
    peer_part = token_grad(peer_grads, inwards, None, bf16)
    sent_tokens = swap(peer_part)
    if direct:
        grads = last[0].astype(f32)
        for d in range(1, 4):
            grads = grads + exchange(last[d], 4 * d).astype(f32)
        held = [add(held[0][d], held[1][d]) for d in range(4)]
        own_grads, held, _ = lax.optimization_barrier((own_grads, held, peer_part))
        pieces = [held[0]] + [exchange(held[d], 4 * d) for d in range(1, 4)]
        sent_tokens, pieces = lax.optimization_barrier((sent_tokens, pieces))
    else:

        def ordered(kept, sent, turned):
            value = jnp.stack([kept, sent])
            value = value.transpose((3, 1, 0, 2, 4, 5) if turned else (3, 2, 0, 1, 4, 5))
            value = jnp.where(tensor_part == 0, value, value[:, :, :, ::-1])
            return value.transpose(3, 0, 1, 2, 4, 5).reshape(2, dp_count, model // dp_count, -1)

        grads = jnp.concatenate([ordered(keep_w, send_w, False), ordered(keep_n, send_n, True), ordered(keep_c, send_c, True)], axis=-1)
        grads = lax.psum_scatter(
            grads.transpose(1, 0, 2, 3).reshape(2 * dp_count, model // dp_count, columns),
            ("dp", "tensor"),
            scatter_dimension=0,
            tiled=True,
        )[0].astype(f32)
        big = jnp.stack([keep, send])[:, :, :, : PARTS * depth]
        big = big.reshape(2, 2, blocks // 4, PARTS, depth, width).transpose(3, 2, 1, 0, 4, 5)
        big = lax.psum_scatter(big.reshape(PARTS, model, width), "dp", scatter_dimension=1, tiled=True)
        extras = lax.psum(keep[0, 0, PARTS * depth :].astype(f32), "dp").astype(bf16)
        pieces = [jnp.concatenate([big.reshape(-1, width), extras], axis=0)]
    projections_grad, offsets_grad, sameness_grad, bias_grad, *vectors = finish(
        place, pieces, depth if direct else model // dp_count, model, hidden
    )
    combiner_grad = grads[:, 2 * hidden :].T
    tokens_grad = token_grad(own_grads, inwards, dfirst_in, f32) + sent_tokens.astype(f32)
    return (
        result,
        tokens_grad,
        projections_grad,
        combiner_grad,
        offsets_grad,
        sameness_grad,
        vectors[0],
        vectors[1],
        vectors[2],
        grads[:, :hidden],
        bias_grad,
        grads[:, hidden : 2 * hidden].T,
        vectors[3],
        vectors[4],
        vectors[5],
    )


def solution(mesh):
    placed = (
        P(("dp", "tensor"), None),
        P("dp", None),
        P(None, "dp", "tensor"),
        P("tensor", "dp"),
        P(None, "tensor"),
        P(None, "tensor"),
        P(),
        P(),
        P(),
        P("dp", "tensor"),
        P("tensor"),
        P("tensor", "dp"),
        P(),
        P(),
        P(),
        P(("dp", "tensor"), None),
    )
    return jax.shard_map(
        shards,
        mesh=mesh,
        in_specs=placed,
        out_specs=(
            P(("dp", "tensor"), None),
            P(("dp", "tensor"), None),
            P(None, "dp", "tensor"),
            P("tensor", "dp"),
            P(None, "tensor"),
            P(None, "tensor"),
            P(),
            P(),
            P(),
            P("dp", "tensor"),
            P("tensor"),
            P("tensor", "dp"),
            P(),
            P(),
            P(),
        ),
        check_vma=False,
    )
```

```python
from functools import partial
import math

import jax
import jax.numpy as jnp
from jax import lax
from jax.experimental import pallas as pl
from jax.experimental.pallas import tpu as pltpu
from jax.sharding import PartitionSpec as P

epsilon = 1e-05
bf16=jnp.bfloat16; f32=jnp.float32
DH=64
AUG=16
TN=(((0,),(0,)),((),()))
NT=(((1,),(1,)),((),()))
NN=(((1,),(0,)),((),()))

def split3(u):
    row=lax.broadcasted_iota(jnp.int32,u.shape,0)
    hi=u.astype(bf16).astype(f32)
    r1=u-hi
    mid=r1.astype(bf16).astype(f32)
    lo=r1-mid
    return jnp.where(row<3,hi,jnp.where(row<6,mid,jnp.where(row<9,lo,0.0))).astype(bf16)

def fwd_kernel(q_ref,k_ref,v_ref,r_ref,s_ref,segq_ref,segk_ref,p_ref,m_ref,ml_ref,c_sc,k_sc,*,tq):
    nq=q_ref.shape[1]; nk=k_ref.shape[1]
    q=q_ref[...].astype(f32)
    sm=s_ref[...]
    c_sc[:DH]=(q+sm[:,0:1]).astype(bf16)*jnp.asarray(0.125,bf16)
    pos=(q+sm[:,1:2]).astype(bf16)*jnp.asarray(0.125,bf16)
    typed=q+sm[:,2:3]
    t0=jnp.sum(typed*sm[:,3:4],axis=0,keepdims=True)*0.125
    t1=jnp.sum(typed*sm[:,4:5],axis=0,keepdims=True)*0.125
    kind=lax.rem(lax.broadcasted_iota(jnp.int32,(AUG,nq),0),3)
    c_sc[DH:]=split3(jnp.where(segq_ref[...]==kind,t1,t0))
    k_sc[:DH]=k_ref[...]
    rowk=lax.broadcasted_iota(jnp.int32,(AUG,nk),0)
    k_sc[DH:]=jnp.where((segk_ref[...]==lax.rem(rowk,3)) & (rowk<9),1.0,0.0).astype(bf16)

    tr=min(tq,128)
    def dense(b):
        i0=b*tq; w0=nk-2*i0-2*tq
        return lax.dot_general(pos[:,i0:i0+tq],r_ref[:,w0:w0+nk+2*tq],TN,preferred_element_type=f32)
    def cont(b):
        i0=b*tq
        return lax.dot_general(c_sc[:,i0:i0+tq],k_sc[...],TN,preferred_element_type=f32)
    def finish(b,c,d):
        i0=b*tq
        for t in range(tq//tr):
            lo=2*(tq-(t+1)*tr)
            g=pltpu.roll(d[t*tr:(t+1)*tr,lo:lo+nk+2*tr],nk,1,stride=2,stride_axis=0)
            s=c[t*tr:(t+1)*tr]+g[:,:nk]
            mx=jnp.max(s,axis=1,keepdims=True)
            e=jnp.exp(s-mx)
            l=jnp.sum(e,axis=1,keepdims=True)
            p_ref[i0+t*tr:i0+(t+1)*tr,:]=(e*(1.0/l)).astype(bf16)
    n=nq//tq
    prev=(cont(0),dense(0))
    for b in range(n):
        nxt=(cont(b+1),dense(b+1)) if b+1<n else None
        finish(b,*prev); prev=nxt
    mixed=lax.dot_general(v_ref[...],p_ref[...],NT,preferred_element_type=f32)
    m_ref[...]=mixed
    ml_ref[...]=mixed.astype(bf16)

def attn_fwd(qT,kT,vT,relT,small,segq,segk,row=0,tq=128):
    hd,nq=qT.shape; nk=kT.shape[1]; heads=hd//DH
    return pl.pallas_call(partial(fwd_kernel,tq=tq),grid=(heads,),
        in_specs=[pl.BlockSpec((DH,nq),lambda h:(h,0)),pl.BlockSpec((DH,nk),lambda h:(h,0)),pl.BlockSpec((DH,nk),lambda h:(h,0)),
          pl.BlockSpec((DH,2*nk),lambda h:(h,0)),pl.BlockSpec((DH,small.shape[1]),lambda h:(h,0)),
          pl.BlockSpec((None,1,nq),lambda h:(row,0,0)),pl.BlockSpec((None,1,nk),lambda h:(row,0,0))],
        out_specs=[pl.BlockSpec((None,nq,nk),lambda h:(h,0,0)),pl.BlockSpec((DH,nq),lambda h:(h,0)),pl.BlockSpec((DH,nq),lambda h:(h,0))],
        out_shape=[jax.ShapeDtypeStruct((heads,nq,nk),bf16),jax.ShapeDtypeStruct((hd,nq),f32),jax.ShapeDtypeStruct((hd,nq),bf16)],
        scratch_shapes=[pltpu.VMEM((DH+AUG,nq),bf16),pltpu.VMEM((DH+AUG,nk),bf16)],
        name="attend",**limits(15<<20))(qT,kT,vT,relT,small,segq,segk)

def bwd_kernel(q_ref,k_ref,v_ref,r_ref,s_ref,segq_ref,segk_ref,p_ref,m_ref,dm_ref,
               dq_ref,dk_ref,dv_ref,dr_ref,sg_ref,k_sc,v_sc,dm_sc,ds_sc,dg_sc,*,tq,first):
    nq=q_ref.shape[1]; nk=k_ref.shape[1]
    q=q_ref[...].astype(f32)
    sm=s_ref[...]
    content=(q+sm[:,0:1]).astype(bf16)*jnp.asarray(0.125,bf16)
    pos=(q+sm[:,1:2]).astype(bf16)*jnp.asarray(0.125,bf16)
    typed=q+sm[:,2:3]
    k_sc[:DH]=k_ref[...]
    rowk=lax.broadcasted_iota(jnp.int32,(AUG,nk),0)
    k_sc[DH:]=((segk_ref[...]==rowk)).astype(f32).astype(bf16)
    v_sc[:DH]=v_ref[...]
    v_sc[DH:]=jnp.where(rowk<3,1.0,0.0).astype(bf16)
    dm=dm_ref[...]
    dm_sc[:DH]=dm
    delta=-jnp.sum(dm.astype(f32)*m_ref[...],axis=0,keepdims=True)
    rowq=lax.broadcasted_iota(jnp.int32,(AUG,nq),0)
    hi=delta.astype(bf16).astype(f32); r1=delta-hi; mid=r1.astype(bf16).astype(f32); lo=r1-mid
    dm_sc[DH:]=jnp.where(rowq==0,hi,jnp.where(rowq==1,mid,jnp.where(rowq==2,lo,0.0))).astype(bf16)
    w=nk+2*tq
    flip=(lax.broadcasted_iota(jnp.int32,(tq,tq),0)+lax.broadcasted_iota(jnp.int32,(tq,tq),1)==tq-1).astype(f32).astype(bf16)
    def turn16(x):
        parts=[lax.dot_general(x[:,i:i+tq],flip,NN,preferred_element_type=f32) for i in range(0,nq,tq)]
        return jnp.concatenate(parts,axis=1).astype(bf16)
    def turn(x):
        hi=x.astype(bf16); r1=x-hi.astype(f32); mid=r1.astype(bf16); lo=(r1-mid.astype(f32)).astype(bf16)
        cat=jnp.concatenate([hi,mid,lo],axis=0)
        parts=[lax.dot_general(cat[:,i:i+tq],flip,NN,preferred_element_type=f32) for i in range(0,nq,tq)]
        y=jnp.concatenate(parts,axis=1)
        return y[:DH]+y[DH:2*DH]+y[2*DH:]

    @pl.when(pl.program_id(0)==0)
    def _():
        dg_sc[...]=jnp.zeros_like(dg_sc)
    def grad(b):
        i0=b*tq
        return lax.dot_general(dm_sc[:,i0:i0+tq],v_sc[...],TN,preferred_element_type=f32)
    def shift(b,dp):
        i0=b*tq
        w0=nk-2*i0-2*tq
        ds16=(p_ref[i0:i0+tq,:].astype(f32)*dp).astype(bf16)
        ds_sc[i0:i0+tq,:]=ds16
        back=lax.dot_general(flip,ds16,NN,preferred_element_type=f32)
        g=jnp.concatenate([back,jnp.zeros((tq,2*tq),f32)],axis=1)
        g=pltpu.roll(g,2,1,stride=2,stride_axis=0)
        dg_sc[i0:i0+tq,w0:w0+w]=g.astype(bf16)
    n=nq//tq
    for b in range(n): shift(b,grad(b))
    dv_ref[...]=lax.dot_general(dm,p_ref[...],NN,preferred_element_type=f32).astype(bf16)
    dk_ref[...]=lax.dot_general(content,ds_sc[...],NN,preferred_element_type=f32).astype(bf16)
    dc=lax.dot_general(k_sc[...],ds_sc[...],NT,preferred_element_type=f32)
    half=256
    tpos=turn16(pos)
    parts=[];drs=[]
    for c0 in range(0,nq,half):
        v0=nk-2*c0-2*half
        g=dg_sc[c0:c0+half,v0:v0+nk+2*half]
        parts.append(lax.dot_general(r_ref[:,v0:v0+nk+2*half],g,NT,preferred_element_type=f32))
        drs.append(lax.dot_general(tpos[:,c0:c0+half],g,NN,preferred_element_type=f32))
    dpos=turn(jnp.concatenate(parts,axis=1))*0.125
    z=jnp.zeros((DH,2*half),f32)
    dr=jnp.concatenate([z,drs[0]],axis=1)+jnp.concatenate([drs[1],z],axis=1)
    if first is None:
        dr_ref[...]=dr
    else:
        dr_ref[...]=first[0][...]+dr
    dcontent=dc[:DH]*0.125
    seg=dc[DH:]*0.125
    rows=lax.broadcasted_iota(jnp.int32,(AUG,nq),0)
    g1=jnp.sum(jnp.where(segq_ref[...]==rows,seg,0.0),axis=0,keepdims=True)
    g0=jnp.sum(seg,axis=0,keepdims=True)-g1
    dtyped=sm[:,3:4]*g0+sm[:,4:5]*g1
    dq_ref[...]=(dcontent+dpos+dtyped).astype(bf16)
    lane=lax.broadcasted_iota(jnp.int32,(DH,128),1)
    total=jnp.zeros((DH,128),f32)
    for n,val in enumerate((dcontent,dpos,dtyped,typed*g0,typed*g1)):
        total=jnp.where(lane==n,jnp.sum(val,axis=1,keepdims=True),total)
    if first is None:
        sg_ref[...]=total
    else:
        sg_ref[...]=first[1][...]+total

def bwd_kernel_first(*refs,tq,skip):
    bwd_kernel(*refs[:10],*refs[10+skip:],tq=tq,first=None)
def bwd_kernel_next(*refs,tq,skip):
    bwd_kernel(*refs[:10],*refs[12+skip:],tq=tq,first=refs[10:12])

def attn_bwd(which,qT,kT,vT,relT,small,segq,segk,probs,mixedT,dmixedT,carry=None,tq=256,heads=None,base=None):
    hd,nq=qT.shape; nk=kT.shape[1]
    start,count=heads or (0,hd//DH)
    row=lambda n: pl.BlockSpec((DH,n),lambda h:(h+start if start else h,0))
    ins=[row(nq),row(nk),row(nk),row(2*nk),row(small.shape[1]),pl.BlockSpec((None,1,nq),lambda h:(which,0,0)),pl.BlockSpec((None,1,nk),lambda h:(which,0,0)),
         pl.BlockSpec((None,nq,nk),lambda h:(h+start if start else h,0,0)),row(nq),row(nq)]
    args=[qT,kT,vT,relT,small,segq,segk,probs,mixedT,dmixedT]
    kern=bwd_kernel_first
    if carry is not None:
        ins+= [row(2*nk),row(128)]; args+=list(carry); kern=bwd_kernel_next
    aliases={}
    if base is not None:
        aliases={len(args)+n:n for n in range(5)}
        ins+=[pl.BlockSpec(memory_space=pl.ANY)]*5; args+=list(base)
    return pl.pallas_call(partial(kern,tq=tq,skip=len(aliases)),grid=(count,),in_specs=ins,
        out_specs=[row(nq),row(nk),row(nk),row(2*nk),row(128)],
        out_shape=[jax.ShapeDtypeStruct((hd,nq),bf16),jax.ShapeDtypeStruct((hd,nk),bf16),jax.ShapeDtypeStruct((hd,nk),bf16),
           jax.ShapeDtypeStruct((hd,2*nk),f32),jax.ShapeDtypeStruct((hd,128),f32)],
        input_output_aliases=aliases,
        scratch_shapes=[pltpu.VMEM((DH+AUG,nk),bf16),pltpu.VMEM((DH+AUG,nk),bf16),pltpu.VMEM((DH+AUG,nq),bf16),pltpu.VMEM((nq,nk),bf16),pltpu.VMEM((nq,2*nk),bf16)],
        name="attend_back",**limits((15*count//6)<<20))(*args)


PARTS = 4
LATE = 5


def pair_matrix(count, axis):
    shape = (count, 2 * count) if axis == 1 else (2 * count, count)
    longer = lax.broadcasted_iota(jnp.int32, shape, axis)
    shorter = lax.broadcasted_iota(jnp.int32, shape, 1 - axis)
    return jnp.where(jnp.right_shift(longer, 1) == shorter, 0.5, 0.0).astype(bf16)


def spot(place_ref, core, column, line):
    return (
        4 * jnp.bitwise_xor(place_ref[0], line)
        + 2 * jnp.bitwise_xor(place_ref[1], column)
        + jnp.bitwise_xor(place_ref[2], core)
    )


def project_kernel(
    place_ref, near0_ref, near1_ref, far0_ref, far1_ref, own_ref, peer_ref, phase_ref,
    own_q, own_k, own_v, peer_q, peer_k, peer_v, rel_ref, pooled_ref, own_low, peer_low, weights_ref,
    turned_sc,
):
    @pl.when(pl.program_id(0) == 0)
    def _():
        for i in range(PARTS):
            for n, ref in enumerate((near0_ref, near1_ref, far0_ref, far1_ref)):
                for d in range(ref.shape[0]):
                    weights_ref[i, spot(place_ref, n // 2, n % 2, d)] = ref[d, i]
            turned_sc[i] = weights_ref[i].reshape(-1, near0_ref.shape[3]).T

    pairs = pair_matrix(own_ref.shape[0] // 2, 1)

    def sequence(rows_ref, q_ref, k_ref, v_ref, low_ref, keep_ref):
        rows = rows_ref[...]
        pooled = jnp.dot(pairs, rows, preferred_element_type=f32)
        low = pooled.astype(bf16)
        low_ref[...] = low
        if keep_ref is not None:
            keep_ref[...] = pooled
        for i, (source, target) in enumerate(((low, q_ref), (rows, k_ref), (rows, v_ref))):
            target[...] = lax.dot_general(turned_sc[i], source, NT, preferred_element_type=f32).astype(bf16)

    sequence(own_ref, own_q, own_k, own_v, own_low, pooled_ref)
    sequence(peer_ref, peer_q, peer_k, peer_v, peer_low, None)
    rel_ref[...] = lax.dot_general(turned_sc[3], phase_ref[...], NT, preferred_element_type=f32).astype(bf16)


def whole(array):
    return pl.BlockSpec(array.shape, lambda *step: (0,) * array.ndim, pipeline_mode=pl.Buffered(1))


def out(shape, dtype):
    return jax.ShapeDtypeStruct(shape, dtype)


def limits(moved):
    return dict(
        compiler_params=pltpu.CompilerParams(vmem_limit_bytes=56 << 20),
        cost_estimate=pl.CostEstimate(flops=moved, bytes_accessed=moved, transcendentals=0),
    )


def project(place, stacks, tokens, peer_tokens, phase, steps=4):
    length, model = tokens.shape
    half = length // 2
    count, _, depth, width = stacks[0].shape
    ins = [*stacks, tokens, peer_tokens, phase]
    outs = [
        out((width, half), bf16), out((width, length), bf16), out((width, length), bf16),
        out((width, half), bf16), out((width, length), bf16), out((width, length), bf16),
        out((width, 2 * length), bf16), out((half, model), f32), out((half, model), bf16), out((half, model), bf16),
        out((PARTS, 4 * count, depth, width), bf16),
    ]
    def rows(array):
        return pl.BlockSpec((array.shape[0] // steps, array.shape[1]), lambda s: (s, 0))

    def columns(array):
        return pl.BlockSpec((array.shape[0], array.shape[1] // steps), lambda s: (0, s))

    return pl.pallas_call(
        project_kernel,
        grid=(steps,),
        in_specs=[pl.BlockSpec(memory_space=pltpu.SMEM)] + [whole(a) for a in stacks] + [rows(a) for a in ins[4:]],
        out_specs=[columns(a) for a in outs[:7]] + [rows(a) for a in outs[7:10]] + [whole(outs[10])],
        out_shape=outs,
        scratch_shapes=[pltpu.VMEM((PARTS, width, model), bf16)],
        name="project",
        **limits(10 << 20),
    )(place, *ins)


def weigh_kernel(
    place_ref, own_rows, peer_rows, own_low, peer_low, phase_ref, own_dq, own_dk, own_dv, peer_dq, peer_dk, peer_dv,
    drel_ref, late_ref, early_ref, keep_ref, send_ref, total_sc, value_sc, small_sc,
):
    step = pl.program_id(0)

    @pl.when(step == 0)
    def _():
        total_sc[...] = jnp.zeros_like(total_sc)

    for i, pairs in enumerate((
        ((own_dq, own_low), (peer_dq, peer_low)),
        ((own_dk, own_rows), (peer_dk, peer_rows)),
        ((own_dv, own_rows), (peer_dv, peer_rows)),
        ((drel_ref, phase_ref),),
    )):
        for grad, rows in pairs:
            total_sc[i] += jnp.dot(grad[...].astype(bf16), rows[...], preferred_element_type=f32)

    @pl.when(step == pl.num_programs(0) - 1)
    def _():
        columns, lines, _, width = keep_ref.shape
        depth = value_sc.shape[1]
        for i in range(PARTS):
            value_sc[...] = total_sc[i].astype(bf16).T.reshape(value_sc.shape)
            for core, ref in enumerate((keep_ref, send_ref)):
                for column in range(columns):
                    for line in range(lines):
                        ref[column, line, i * depth:(i + 1) * depth] = value_sc[spot(place_ref, core, column, line)]
        first, last = LATE, LATE + early_ref.shape[0]
        small_sc[...] = jnp.zeros_like(small_sc)
        small_sc[:first] = late_ref[...].T[:first]
        small_sc[first:last] = early_ref[:, :width]
        small_sc[last : 2 * last - first] = early_ref[:, width:]
        small = small_sc[...].astype(bf16)
        for column in range(columns):
            for line in range(lines):
                for ref in (keep_ref, send_ref):
                    ref[column, line, PARTS * depth:] = small


def weigh(place, own_rows, peer_rows, own_low, peer_low, phase, own_grads, peer_grads, drel, late, early, blocks, steps=4):
    model = own_rows.shape[1]
    depth = model // blocks
    width = drel.shape[0]
    extra = LATE + 2 * early.shape[0]
    extra += -extra % 16

    def rows(array):
        return pl.BlockSpec((array.shape[0] // steps, model), lambda s: (s, 0))

    def columns(array):
        return pl.BlockSpec((width, array.shape[1] // steps), lambda s: (0, s))

    ins = [own_rows, peer_rows, own_low, peer_low, phase]
    grads = [*own_grads, *peer_grads, drel]
    pieces = out((2, blocks // 4, PARTS * depth + extra, width), bf16)
    return pl.pallas_call(
        weigh_kernel,
        grid=(steps,),
        in_specs=[pl.BlockSpec(memory_space=pltpu.SMEM)] + [rows(a) for a in ins] + [columns(a) for a in grads] + [whole(late), whole(early)],
        out_specs=[whole(pieces)] * 2,
        out_shape=[pieces] * 2,
        scratch_shapes=[pltpu.VMEM((PARTS, width, model), f32), pltpu.VMEM((blocks, depth, width), bf16), pltpu.VMEM((extra, width), f32)],
        name="weigh",
        **limits(8 << 20),
    )(place, *ins, *grads, late, early)


def token_kernel(dq_ref, dk_ref, dv_ref, w_ref, *refs):
    model = refs[-1].shape[1]
    width = dk_ref.shape[0]
    half = dq_ref.shape[1]
    doubled = jnp.dot(dq_ref[...], pair_matrix(half, 1), preferred_element_type=f32).astype(bf16)
    total = None
    for i, grad in enumerate((doubled, dk_ref[...], dv_ref[...])):
        term = lax.dot_general(grad.T, w_ref[i].reshape(model, width), NT, preferred_element_type=f32)
        total = term if total is None else total + term
    if len(refs) > 1:
        high = refs[0][...].astype(bf16)
        low = (refs[0][...] - high.astype(f32)).astype(bf16)
        pairs = pair_matrix(half, 0)
        total = total + jnp.dot(pairs, high, preferred_element_type=f32) + jnp.dot(pairs, low, preferred_element_type=f32)
    refs[-1][...] = total.astype(refs[-1].dtype)


def token_grad(grads, weights, extra, dtype):
    length = grads[1].shape[1]
    model = weights.shape[1] * weights.shape[2]
    ins = [*grads, weights] + ([extra] if extra is not None else [])
    specs = [whole(a) for a in ins]
    result = out((length, model), dtype)
    return pl.pallas_call(
        token_kernel,
        grid=(1,),
        in_specs=specs,
        out_specs=whole(result),
        out_shape=result,
        name="token_grad",
        **limits(5 << 20),
    )(*ins)


def finish_kernel(place_ref, *refs, sources):
    total = refs[0][...].astype(f32)
    for ref in refs[1:sources]:
        total = total + ref[...].astype(f32)
    grads_ref, offsets_ref, sameness_ref, bias_ref, *vectors, total_sc = refs[sources:]
    parts, depth, width = grads_ref.shape
    for i in range(parts):
        grads_ref[i] = total[i * depth : (i + 1) * depth]
    total_sc[...] = total[parts * depth :]
    offsets_ref[...] = total_sc[:3]
    sameness_ref[...] = total_sc[3:LATE]
    count = len(vectors) + 4

    def row(n):
        return jnp.concatenate(
            [total_sc[LATE + n : LATE + n + 1], total_sc[LATE + count + n : LATE + count + n + 1]], axis=1
        )

    for n, ref in enumerate(vectors):
        ref[...] = row(n).reshape(ref.shape)
    n = len(vectors)
    first = place_ref[3] == 0
    bias = jnp.concatenate(
        [jnp.where(first, row(n), row(n + 2)), jnp.where(first, row(n + 1), row(n + 3))], axis=1
    )
    bias_ref[...] = bias.reshape(bias_ref.shape)


def finish(place, pieces, depth, model, hidden):
    extra = pieces[0].shape[0] - PARTS * depth
    width = pieces[0].shape[1]
    outs = [
        out((PARTS, depth, width), f32), out((3, width), f32), out((2, width), f32), out((hidden,), f32),
    ] + [out((model,), f32)] * 6
    return pl.pallas_call(
        partial(finish_kernel, sources=len(pieces)),
        grid=(1,),
        in_specs=[pl.BlockSpec(memory_space=pltpu.SMEM)] + [whole(a) for a in pieces],
        out_specs=[whole(a) for a in outs],
        out_shape=outs,
        scratch_shapes=[pltpu.VMEM((extra, width), f32)],
        name="finish",
        **limits(1 << 20),
    )(place, *pieces)


SPLIT = 1


def layer_norm(values_in):
    row_mean = jnp.mean(values_in, axis=1, keepdims=True)
    centred = values_in - row_mean
    variance = jnp.mean(centred * centred, axis=1, keepdims=True)
    scale = lax.rsqrt(variance + epsilon)
    return centred * scale, scale


def layer_norm_back(grad, normed, scale, gain):
    inner = grad * gain
    return scale * (
        inner
        - jnp.mean(inner, axis=1, keepdims=True)
        - normed * jnp.mean(inner * normed, axis=1, keepdims=True)
    )


def row_sum(values_in):
    return jnp.sum(values_in, axis=0, keepdims=True)


def middle_kernel(
    place_ref, pooled_ref, mixed_ref, sent_ref, vec_ref, cot_ref, own_c_ref, peer_c_ref, weights_ref, own_bias_ref, peer_bias_ref,
    result_ref, dfirst_ref, own_dm_ref, peer_dm_ref, keep_c_ref, send_c_ref, sums_ref,
    keep_w_ref, send_w_ref, keep_n_ref, send_n_ref,
    held_sc, held_sem, slope_sc, act_sc, dhid_sc, first_sc, norm_sc, scale_sc, total_sc, low_sc, low_t_sc, dsec_sc, dsec_t_sc,
    *, chunks,
):
    step = pl.program_id(0)
    model = pooled_ref.shape[1]
    rows = pooled_ref.shape[0]
    part = own_bias_ref.shape[-1]
    each = own_bias_ref.shape[0]

    def fetch(chunk, kind):
        return pltpu.make_async_copy(
            weights_ref.at[:, chunk // each, :, pl.ds((kind * each + chunk % each) * part, part)],
            held_sc.at[chunk, kind],
            held_sem.at[chunk, kind],
        )
    vec = vec_ref[...]

    def store(value, keep_ref, send_ref, *half):
        value = value.astype(bf16)
        for n, ref in enumerate((keep_ref, send_ref)):
            piece = value[n * (model // 2) : (n + 1) * (model // 2)]
            if half:
                shape = ref.shape[:1] + ref.shape[2:]
                ref[:, half[0]] = piece.reshape(shape)
            else:
                ref[...] = piece.reshape(ref.shape)

    def turn_rows(value, ref):
        value = value.T.reshape(ref.shape)
        count = ref.shape[0]
        for n in range(count):
            line, column, core = n // 4, n // 2 % 2, n % 2
            ref[
                (count // 2) * jnp.bitwise_xor(place_ref[2], core)
                + (count // 4) * jnp.bitwise_xor(place_ref[1], column)
                + jnp.bitwise_xor(place_ref[0], line)
            ] = value[n]

    postbias, scaling, centring = vec[0:1], vec[1:2], vec[2:3]
    narrowbias, rescale, recentre = vec[3:4], vec[4:5], vec[5:6]

    @pl.when(step == 0)
    def _():
        for chunk in range(chunks):
            for kind in range(2):
                fetch(chunk, kind).start()
        own_c = own_c_ref[...].reshape(model, -1)
        peer_c = peer_c_ref[...].reshape(model, -1)
        mixed = mixed_ref[...].astype(bf16).T
        sent = sent_ref[...].T
        branch = (
            lax.dot_general(mixed, own_c, NT, preferred_element_type=f32)
            + lax.dot_general(sent, peer_c, NT, preferred_element_type=f32)
            + postbias
        )
        normed, scale = layer_norm(pooled_ref[...] + branch)
        norm_sc[...] = normed
        scale_sc[...] = scale
        first = normed * scaling + centring
        first_sc[...] = first
        low = first.astype(bf16)
        low_sc[...] = low
        turn_rows(low, low_t_sc)
        total_sc[...] = jnp.zeros_like(total_sc)

    for chunk in range(chunks):

        @pl.when(step == chunk)
        def _():
            for kind in range(2):
                fetch(chunk, kind).wait()

    @pl.when(step < chunks)
    def _():
        wide = held_sc[step, 0].reshape(model, part)
        spot_bias = lax.rem(step, each)
        bias = jnp.where(step // each == place_ref[3], own_bias_ref[spot_bias], peer_bias_ref[spot_bias])
        hidden = jnp.dot(low_sc[...], wide, preferred_element_type=f32) + bias
        square = hidden * hidden
        root = math.sqrt(2.0 / math.pi)
        turn = jnp.tanh(hidden * (root + (root * 0.044715) * square))
        half = 0.5 * turn + 0.5
        act = (hidden * half).astype(bf16)
        slope_sc[step] = half + hidden * (half * (1.0 - turn)) * (root + (3.0 * root * 0.044715) * square)
        act_sc[step] = act
        narrow = held_sc[step, 1].reshape(model, part)
        total_sc[...] += lax.dot_general(act, narrow, NT, preferred_element_type=f32)

    @pl.when(step == chunks - 1)
    def _():
        normed, scale = layer_norm(first_sc[...] + (total_sc[...] + narrowbias))
        result_ref[...] = (normed * rescale + recentre).astype(bf16)
        cot = cot_ref[...].astype(f32)
        dfinal = layer_norm_back(cot, normed, scale, rescale)
        dsec = dfinal.astype(bf16)
        dsec_sc[...] = dsec
        turn_rows(dsec, dsec_t_sc)
        sums_ref[3:4] = row_sum(dsec.astype(f32))
        sums_ref[4:5] = row_sum(cot * normed)
        sums_ref[5:6] = row_sum(cot)
        total_sc[...] = dfinal

    back = step - chunks

    @pl.when((back >= 0) & (lax.rem(back, 2) == 0))
    def _():
        chunk = back // 2
        narrow = held_sc[chunk, 1].reshape(model, part)
        dact = jnp.dot(dsec_sc[...], narrow, preferred_element_type=f32)
        dhid = (dact * slope_sc[chunk]).astype(bf16)
        dhid_sc[...] = dhid
        bias_sum = row_sum(dhid.astype(f32))
        for n in range(part // model):
            sums_ref[pl.ds(6 + chunk * (part // model) + n, 1)] = bias_sum[:, n * model : (n + 1) * model]
        grad = jnp.dot(dsec_t_sc[...].reshape(model, rows), act_sc[chunk], preferred_element_type=f32)
        store(grad, keep_n_ref, send_n_ref)

    @pl.when((back >= 0) & (lax.rem(back, 2) == 1))
    def _():
        wide = held_sc[back // 2, 0].reshape(model, part)
        total_sc[...] += lax.dot_general(dhid_sc[...], wide, NT, preferred_element_type=f32)
        grad = jnp.dot(low_t_sc[...].reshape(model, rows), dhid_sc[...], preferred_element_type=f32)
        store(grad, keep_w_ref, send_w_ref)

    @pl.when(back == 2 * chunks - 1)
    def _():
        dfirst = total_sc[...]
        normed = norm_sc[...]
        dfirst_in = layer_norm_back(dfirst, normed, scale_sc[...], scaling)
        dfirst_ref[...] = dfirst_in
        dbranch = dfirst_in.astype(bf16)
        sums_ref[0:1] = row_sum(dbranch.astype(f32))
        sums_ref[1:2] = row_sum(dfirst * normed)
        sums_ref[2:3] = row_sum(dfirst)
        dbranch_t = dbranch.T
        turn_rows(dbranch, low_t_sc)
        turned = low_t_sc[...].reshape(model, rows)
        for half, c_ref, m_ref, dm_ref in (
            (0, own_c_ref, mixed_ref, own_dm_ref),
            (1, peer_c_ref, sent_ref, peer_dm_ref),
        ):
            c = c_ref[...].reshape(model, -1)
            dm_ref[...] = lax.dot_general(c, dbranch_t, TN, preferred_element_type=f32).astype(bf16)
            dc = lax.dot_general(turned, m_ref[...].astype(bf16), NT, preferred_element_type=f32)
            store(dc, keep_c_ref, send_c_ref, half)


def middle(place, pooled, mixed, sent, vec, cot, weights, own_bias, peer_bias):
    rows, model = pooled.shape
    blocks, halves, depth, columns = weights.shape
    width = mixed.shape[0]
    hidden = (columns - width) // 2
    part = hidden // SPLIT
    each = hidden // part
    chunks = halves * each

    def combiner_spec(flip):
        def index(step, place_ref):
            return (0, jnp.bitwise_xor(place_ref[3], flip), 0, 2 * hidden // width)

        return pl.BlockSpec((blocks, None, depth, width), index, pipeline_mode=pl.Buffered(1))

    def wide_index(step, place_ref):
        c = jnp.maximum(step - chunks - 1, 0) // 2
        return (jnp.bitwise_xor(c // each, place_ref[3]), 0, 0, 0, lax.rem(c, each))

    def narrow_index(step, place_ref):
        c = jnp.maximum(step - chunks, 0) // 2
        return (0, jnp.bitwise_xor(c // each, place_ref[3]), 0, 0, lax.rem(c, each))

    lines = blocks // 4
    outs = [
        out((rows, model), bf16), out((rows, model), f32), out(mixed.shape, bf16), out(mixed.shape, bf16),
        out((2, halves, lines, depth, width), bf16), out((2, halves, lines, depth, width), bf16), out((6 + halves * hidden // model, model), f32),
    ]
    wide_grads = out((halves, 2, lines, depth, hidden), bf16)
    narrow_grads = out((2, halves, lines, depth, hidden), bf16)
    whole_ins = [pooled, mixed, sent, vec, cot]
    grad_spec = [pl.BlockSpec((1, 2, lines, depth, part), wide_index)] * 2
    grad_spec += [pl.BlockSpec((2, 1, lines, depth, part), narrow_index)] * 2
    return pl.pallas_call(
        partial(middle_kernel, chunks=chunks),
        grid_spec=pltpu.PrefetchScalarGridSpec(
            num_scalar_prefetch=1,
            grid=(3 * chunks,),
            in_specs=[whole(a) for a in whole_ins]
            + [combiner_spec(0), combiner_spec(1), pl.BlockSpec(memory_space=pl.ANY)]
            + [pl.BlockSpec((each, 1, part), lambda s, p: (0, 0, 0))] * 2,
            out_specs=[whole(a) for a in outs]
            + grad_spec,
            scratch_shapes=[
                pltpu.VMEM((chunks, 2, blocks, depth, part), bf16),
                pltpu.SemaphoreType.DMA((chunks, 2)),
                pltpu.VMEM((chunks, rows, part), f32),
                pltpu.VMEM((chunks, rows, part), bf16),
                pltpu.VMEM((rows, part), bf16),
                pltpu.VMEM((rows, model), f32),
                pltpu.VMEM((rows, model), f32),
                pltpu.VMEM((rows, 1), f32),
                pltpu.VMEM((rows, model), f32),
                pltpu.VMEM((rows, model), bf16),
                pltpu.VMEM((blocks, depth, rows), bf16),
                pltpu.VMEM((rows, model), bf16),
                pltpu.VMEM((blocks, depth, rows), bf16),
            ],
        ),
        out_shape=outs + [wide_grads] * 2 + [narrow_grads] * 2,
        name="middle",
        **limits(24 << 20),
    )(place, *whole_ins, weights, weights, weights, own_bias.reshape(each, 1, part), peer_bias.reshape(each, 1, part))


def position_table(length, model_width):
    row_index = jnp.arange(2 * length, dtype=jnp.float32)
    offset = length - row_index
    half_width = model_width // 2
    frequency = jnp.exp(
        jnp.arange(half_width, dtype=jnp.float32) * (-math.log(10000.0) / half_width)
    )
    angles = offset[:, None] * frequency[None, :]
    return jnp.concatenate([jnp.sin(angles), jnp.cos(angles)], axis=1)


BLOCKS = 16


def swap(piece):
    return lax.ppermute(piece, "tensor", [(0, 1), (1, 0)])


def exchange(piece, mask):
    count = lax.axis_size("dp")
    return lax.ppermute(piece, "dp", [(i, i ^ mask) for i in range(count)])


def shards(
    tokens,
    segments,
    projections,
    combiner,
    offsets,
    sameness,
    postbias,
    scaling,
    centring,
    widener,
    widebias,
    narrower,
    narrowbias,
    rescale,
    recentre,
    cotangent,
):
    tensor_part = lax.axis_index("tensor")
    dp_part = lax.axis_index("dp")
    dp_count = lax.axis_size("dp")
    length, model = tokens.shape
    width = offsets.shape[1]
    hidden = widener.shape[1]
    blocks = BLOCKS
    depth = model // blocks
    direct = dp_count == blocks
    if direct:
        place = jnp.stack([dp_part // 4, (dp_part // 2) % 2, dp_part % 2, tensor_part]).astype(jnp.int32)
    else:
        place = jnp.stack([tensor_part * 0] * 3 + [tensor_part]).astype(jnp.int32)

    if direct:
        near0 = jnp.stack([projections] + [exchange(projections, 4 * d) for d in range(1, 4)])
        near1 = exchange(near0, 2)
        stacks = (near0, near1, exchange(near0, 1), exchange(near1, 1))
    else:
        every = lax.all_gather(projections, "dp", axis=1, tiled=True)
        every = every.reshape(PARTS, blocks // 4, 2, 2, depth, width).transpose(3, 2, 1, 0, 4, 5)
        stacks = (every[0, 0], every[0, 1], every[1, 0], every[1, 1])
    peer_tokens = swap(tokens)
    mine = jnp.concatenate([widener, narrower.T, combiner.T], axis=1)
    columns = mine.shape[1]
    weights = lax.all_gather(mine, ("dp", "tensor"), axis=0, tiled=False)
    if not direct:
        weights = weights.reshape(dp_count, 2, model // dp_count, columns).transpose(1, 0, 2, 3)
        weights = weights.reshape(2, blocks, depth, columns).transpose(1, 0, 2, 3)
    weights = weights.reshape(blocks, 2, depth, columns)
    small = jnp.concatenate([offsets, sameness], axis=0).T
    seg = jnp.where(tensor_part == 0, segments, segments[::-1])[:, None]
    vec = jnp.stack([postbias, scaling, centring, narrowbias, rescale, recentre, postbias, postbias])
    peer_tokens, peer_bias, small, seg, seg_q, vec = lax.optimization_barrier(
        (peer_tokens, swap(widebias), small, seg, seg[:, :, ::2], vec)
    )
    phase = position_table(length, model).astype(bf16)
    own_q, own_k, own_v, peer_q, peer_k, peer_v, relative, pooled, own_low, peer_low, inwards = project(
        place, stacks, tokens, peer_tokens, phase
    )
    own_args = (own_q, own_k, own_v, relative, small, seg_q, seg)
    peer_args = (peer_q, peer_k, peer_v, relative, small, seg_q, seg)
    peer_probs, peer_mixed, peer_mixed_low = attn_fwd(*peer_args, 1)
    sent_mixed = swap(peer_mixed_low)
    own_probs, own_mixed, own_mixed_low = attn_fwd(*own_args, 0)
    result, dfirst_in, own_dmixed, peer_dmixed, keep_c, send_c, early, keep_w, send_w, keep_n, send_n = middle(
        place, pooled, own_mixed_low, sent_mixed, vec, cotangent, weights, widebias, peer_bias
    )
    sent_dmixed = swap(peer_dmixed)
    half = width // DH // 2
    part = attn_bwd(0, *own_args, own_probs, own_mixed, own_dmixed, heads=(0, half))
    early = early + swap(early)
    if direct:

        def add(kept, sent):
            return (kept.astype(f32) + sent.astype(f32)).astype(bf16)

        wide = (keep_w, exchange(send_w, 1))
        narrow = (keep_n, exchange(send_n, 1))
        comb = (keep_c, exchange(send_c, 1))

        def joined(pick):
            return jnp.concatenate([add(*map(pick, narrow)), add(*map(pick, comb))], axis=-1)

        first_stage = (
            add(wide[0][0], wide[1][0]),
            add(wide[0][1], wide[1][1]),
            joined(lambda a: a[0]),
            joined(lambda a: a[1]),
        )
        part, early, first_stage, sent_dmixed = lax.optimization_barrier((part, early, first_stage, sent_dmixed))

    own_dq, own_dk, own_dv, drel, late = attn_bwd(
        0, *own_args, own_probs, own_mixed, own_dmixed, heads=(half, width // DH - half), base=part
    )
    peer_dq, peer_dk, peer_dv, drel, late = attn_bwd(
        1, *peer_args, peer_probs, peer_mixed, sent_dmixed, (drel, late)
    )
    own_grads = (own_dq, own_dk, own_dv)
    peer_grads = (peer_dq, peer_dk, peer_dv)
    if direct:
        wide = (first_stage[0], swap(first_stage[1]))
        narrow = (first_stage[2], exchange(first_stage[3], 2))
        wide = (add(wide[0][0], wide[1][0]), add(wide[0][1], wide[1][1]))
        narrow = (add(narrow[0][0], narrow[1][0]), add(narrow[0][1], narrow[1][1]))
        drel, wide, narrow = lax.optimization_barrier((drel, wide, narrow))
        wide = (wide[0], exchange(wide[1], 2))
        narrow = (narrow[0], swap(narrow[1]))
    keep, send = weigh(
        place, tokens, peer_tokens, own_low, peer_low, phase, own_grads, peer_grads, drel, late, early, blocks
    )
    if direct:
        keep, send, wide, narrow = lax.optimization_barrier((keep, send, wide, narrow))
        sent = exchange(send, 1)
        held = (add(keep[0], sent[0]), add(keep[1], sent[1]))
        last = [
            jnp.concatenate([add(wide[0][d], wide[1][d]), add(narrow[0][d], narrow[1][d])], axis=-1)
            for d in range(4)
        ]
        peer_grads, held, last = lax.optimization_barrier((peer_grads, held, last))
        held = (held[0], exchange(held[1], 2))
    peer_part = token_grad(peer_grads, inwards, None, bf16)
    sent_tokens = swap(peer_part)
    if direct:
        grads = last[0].astype(f32)
        for d in range(1, 4):
            grads = grads + exchange(last[d], 4 * d).astype(f32)
        held = [add(held[0][d], held[1][d]) for d in range(4)]
        own_grads, held, _ = lax.optimization_barrier((own_grads, held, peer_part))
        pieces = [held[0]] + [exchange(held[d], 4 * d) for d in range(1, 4)]
        sent_tokens, pieces = lax.optimization_barrier((sent_tokens, pieces))
    else:

        def ordered(kept, sent, turned):
            value = jnp.stack([kept, sent])
            value = value.transpose((3, 1, 0, 2, 4, 5) if turned else (3, 2, 0, 1, 4, 5))
            value = jnp.where(tensor_part == 0, value, value[:, :, :, ::-1])
            return value.transpose(3, 0, 1, 2, 4, 5).reshape(2, dp_count, model // dp_count, -1)

        grads = jnp.concatenate([ordered(keep_w, send_w, False), ordered(keep_n, send_n, True), ordered(keep_c, send_c, True)], axis=-1)
        grads = lax.psum_scatter(
            grads.transpose(1, 0, 2, 3).reshape(2 * dp_count, model // dp_count, columns),
            ("dp", "tensor"),
            scatter_dimension=0,
            tiled=True,
        )[0].astype(f32)
        big = jnp.stack([keep, send])[:, :, :, : PARTS * depth]
        big = big.reshape(2, 2, blocks // 4, PARTS, depth, width).transpose(3, 2, 1, 0, 4, 5)
        big = lax.psum_scatter(big.reshape(PARTS, model, width), "dp", scatter_dimension=1, tiled=True)
        extras = lax.psum(keep[0, 0, PARTS * depth :].astype(f32), "dp").astype(bf16)
        pieces = [jnp.concatenate([big.reshape(-1, width), extras], axis=0)]
    projections_grad, offsets_grad, sameness_grad, bias_grad, *vectors = finish(
        place, pieces, depth if direct else model // dp_count, model, hidden
    )
    combiner_grad = grads[:, 2 * hidden :].T
    tokens_grad = token_grad(own_grads, inwards, dfirst_in, f32) + sent_tokens.astype(f32)
    return (
        result,
        tokens_grad,
        projections_grad,
        combiner_grad,
        offsets_grad,
        sameness_grad,
        vectors[0],
        vectors[1],
        vectors[2],
        grads[:, :hidden],
        bias_grad,
        grads[:, hidden : 2 * hidden].T,
        vectors[3],
        vectors[4],
        vectors[5],
    )


def solution(mesh):
    placed = (
        P(("dp", "tensor"), None),
        P("dp", None),
        P(None, "dp", "tensor"),
        P("tensor", "dp"),
        P(None, "tensor"),
        P(None, "tensor"),
        P(),
        P(),
        P(),
        P("dp", "tensor"),
        P("tensor"),
        P("tensor", "dp"),
        P(),
        P(),
        P(),
        P(("dp", "tensor"), None),
    )
    return jax.shard_map(
        shards,
        mesh=mesh,
        in_specs=placed,
        out_specs=(
            P(("dp", "tensor"), None),
            P(("dp", "tensor"), None),
            P(None, "dp", "tensor"),
            P("tensor", "dp"),
            P(None, "tensor"),
            P(None, "tensor"),
            P(),
            P(),
            P(),
            P("dp", "tensor"),
            P("tensor"),
            P("tensor", "dp"),
            P(),
            P(),
            P(),
        ),
        check_vma=False,
    )
```

```python
from functools import partial
import math

import jax
import jax.numpy as jnp
from jax import lax
from jax.experimental import pallas as pl
from jax.experimental.pallas import tpu as pltpu
from jax.sharding import PartitionSpec as P

epsilon = 1e-05
bf16=jnp.bfloat16; f32=jnp.float32
DH=64
AUG=16
TN=(((0,),(0,)),((),()))
NT=(((1,),(1,)),((),()))
NN=(((1,),(0,)),((),()))

def split3(u):
    row=lax.broadcasted_iota(jnp.int32,u.shape,0)
    hi=u.astype(bf16).astype(f32)
    r1=u-hi
    mid=r1.astype(bf16).astype(f32)
    lo=r1-mid
    return jnp.where(row<3,hi,jnp.where(row<6,mid,jnp.where(row<9,lo,0.0))).astype(bf16)

def fwd_kernel(q_ref,k_ref,v_ref,r_ref,s_ref,segq_ref,segk_ref,p_ref,m_ref,ml_ref,c_sc,k_sc,*,tq):
    nq=q_ref.shape[1]; nk=k_ref.shape[1]
    q=q_ref[...].astype(f32)
    sm=s_ref[...]
    c_sc[:DH]=(q+sm[:,0:1]).astype(bf16)*jnp.asarray(0.125,bf16)
    pos=(q+sm[:,1:2]).astype(bf16)*jnp.asarray(0.125,bf16)
    typed=q+sm[:,2:3]
    t0=jnp.sum(typed*sm[:,3:4],axis=0,keepdims=True)*0.125
    t1=jnp.sum(typed*sm[:,4:5],axis=0,keepdims=True)*0.125
    kind=lax.rem(lax.broadcasted_iota(jnp.int32,(AUG,nq),0),3)
    c_sc[DH:]=split3(jnp.where(segq_ref[...]==kind,t1,t0))
    k_sc[:DH]=k_ref[...]
    rowk=lax.broadcasted_iota(jnp.int32,(AUG,nk),0)
    k_sc[DH:]=jnp.where((segk_ref[...]==lax.rem(rowk,3)) & (rowk<9),1.0,0.0).astype(bf16)

    tr=min(tq,128)
    def dense(b):
        i0=b*tq; w0=nk-2*i0-2*tq
        return lax.dot_general(pos[:,i0:i0+tq],r_ref[:,w0:w0+nk+2*tq],TN,preferred_element_type=f32)
    def cont(b):
        i0=b*tq
        return lax.dot_general(c_sc[:,i0:i0+tq],k_sc[...],TN,preferred_element_type=f32)
    def finish(b,c,d):
        i0=b*tq
        for t in range(tq//tr):
            lo=2*(tq-(t+1)*tr)
            g=pltpu.roll(d[t*tr:(t+1)*tr,lo:lo+nk+2*tr],nk,1,stride=2,stride_axis=0)
            s=c[t*tr:(t+1)*tr]+g[:,:nk]
            mx=jnp.max(s,axis=1,keepdims=True)
            e=jnp.exp(s-mx)
            l=jnp.sum(e,axis=1,keepdims=True)
            p_ref[i0+t*tr:i0+(t+1)*tr,:]=(e*(1.0/l)).astype(bf16)
    n=nq//tq
    prev=(cont(0),dense(0))
    for b in range(n):
        nxt=(cont(b+1),dense(b+1)) if b+1<n else None
        finish(b,*prev); prev=nxt
    mixed=lax.dot_general(v_ref[...],p_ref[...],NT,preferred_element_type=f32)
    m_ref[...]=mixed
    ml_ref[...]=mixed.astype(bf16)

def attn_fwd(qT,kT,vT,relT,small,segq,segk,row=0,tq=128):
    hd,nq=qT.shape; nk=kT.shape[1]; heads=hd//DH
    return pl.pallas_call(partial(fwd_kernel,tq=tq),grid=(heads,),
        in_specs=[pl.BlockSpec((DH,nq),lambda h:(h,0)),pl.BlockSpec((DH,nk),lambda h:(h,0)),pl.BlockSpec((DH,nk),lambda h:(h,0)),
          pl.BlockSpec((DH,2*nk),lambda h:(h,0)),pl.BlockSpec((DH,small.shape[1]),lambda h:(h,0)),
          pl.BlockSpec((None,1,nq),lambda h:(row,0,0)),pl.BlockSpec((None,1,nk),lambda h:(row,0,0))],
        out_specs=[pl.BlockSpec((None,nq,nk),lambda h:(h,0,0)),pl.BlockSpec((DH,nq),lambda h:(h,0)),pl.BlockSpec((DH,nq),lambda h:(h,0))],
        out_shape=[jax.ShapeDtypeStruct((heads,nq,nk),bf16),jax.ShapeDtypeStruct((hd,nq),f32),jax.ShapeDtypeStruct((hd,nq),bf16)],
        scratch_shapes=[pltpu.VMEM((DH+AUG,nq),bf16),pltpu.VMEM((DH+AUG,nk),bf16)],
        name="attend",**limits(15<<20))(qT,kT,vT,relT,small,segq,segk)

def bwd_kernel(q_ref,k_ref,v_ref,r_ref,s_ref,segq_ref,segk_ref,p_ref,m_ref,dm_ref,
               dq_ref,dk_ref,dv_ref,dr_ref,sg_ref,k_sc,v_sc,dm_sc,ds_sc,dg_sc,*,tq,first):
    nq=q_ref.shape[1]; nk=k_ref.shape[1]
    q=q_ref[...].astype(f32)
    sm=s_ref[...]
    content=(q+sm[:,0:1]).astype(bf16)*jnp.asarray(0.125,bf16)
    pos=(q+sm[:,1:2]).astype(bf16)*jnp.asarray(0.125,bf16)
    typed=q+sm[:,2:3]
    k_sc[:DH]=k_ref[...]
    rowk=lax.broadcasted_iota(jnp.int32,(AUG,nk),0)
    k_sc[DH:]=((segk_ref[...]==rowk)).astype(f32).astype(bf16)
    v_sc[:DH]=v_ref[...]
    v_sc[DH:]=jnp.where(rowk<3,1.0,0.0).astype(bf16)
    dm=dm_ref[...]
    dm_sc[:DH]=dm
    delta=-jnp.sum(dm.astype(f32)*m_ref[...],axis=0,keepdims=True)
    rowq=lax.broadcasted_iota(jnp.int32,(AUG,nq),0)
    hi=delta.astype(bf16).astype(f32); r1=delta-hi; mid=r1.astype(bf16).astype(f32); lo=r1-mid
    dm_sc[DH:]=jnp.where(rowq==0,hi,jnp.where(rowq==1,mid,jnp.where(rowq==2,lo,0.0))).astype(bf16)
    w=nk+2*tq
    flip=(lax.broadcasted_iota(jnp.int32,(tq,tq),0)+lax.broadcasted_iota(jnp.int32,(tq,tq),1)==tq-1).astype(f32).astype(bf16)
    def turn16(x):
        parts=[lax.dot_general(x[:,i:i+tq],flip,NN,preferred_element_type=f32) for i in range(0,nq,tq)]
        return jnp.concatenate(parts,axis=1).astype(bf16)
    def turn(x):
        hi=x.astype(bf16); r1=x-hi.astype(f32); mid=r1.astype(bf16); lo=(r1-mid.astype(f32)).astype(bf16)
        cat=jnp.concatenate([hi,mid,lo],axis=0)
        parts=[lax.dot_general(cat[:,i:i+tq],flip,NN,preferred_element_type=f32) for i in range(0,nq,tq)]
        y=jnp.concatenate(parts,axis=1)
        return y[:DH]+y[DH:2*DH]+y[2*DH:]

    @pl.when(pl.program_id(0)==0)
    def _():
        dg_sc[...]=jnp.zeros_like(dg_sc)
    def grad(b):
        i0=b*tq
        return lax.dot_general(dm_sc[:,i0:i0+tq],v_sc[...],TN,preferred_element_type=f32)
    def shift(b,dp):
        i0=b*tq
        w0=nk-2*i0-2*tq
        ds16=(p_ref[i0:i0+tq,:].astype(f32)*dp).astype(bf16)
        ds_sc[i0:i0+tq,:]=ds16
        back=lax.dot_general(flip,ds16,NN,preferred_element_type=f32)
        g=jnp.concatenate([back,jnp.zeros((tq,2*tq),f32)],axis=1)
        g=pltpu.roll(g,2,1,stride=2,stride_axis=0)
        dg_sc[i0:i0+tq,w0:w0+w]=g.astype(bf16)
    n=nq//tq
    for b in range(n): shift(b,grad(b))
    dv_ref[...]=lax.dot_general(dm,p_ref[...],NN,preferred_element_type=f32).astype(bf16)
    dk_ref[...]=lax.dot_general(content,ds_sc[...],NN,preferred_element_type=f32).astype(bf16)
    dc=lax.dot_general(k_sc[...],ds_sc[...],NT,preferred_element_type=f32)
    half=256
    tpos=turn16(pos)
    parts=[];drs=[]
    for c0 in range(0,nq,half):
        v0=nk-2*c0-2*half
        g=dg_sc[c0:c0+half,v0:v0+nk+2*half]
        parts.append(lax.dot_general(r_ref[:,v0:v0+nk+2*half],g,NT,preferred_element_type=f32))
        drs.append(lax.dot_general(tpos[:,c0:c0+half],g,NN,preferred_element_type=f32))
    dpos=turn(jnp.concatenate(parts,axis=1))*0.125
    z=jnp.zeros((DH,2*half),f32)
    dr=jnp.concatenate([z,drs[0]],axis=1)+jnp.concatenate([drs[1],z],axis=1)
    if first is None:
        dr_ref[...]=dr
    else:
        dr_ref[...]=first[0][...]+dr
    dcontent=dc[:DH]*0.125
    seg=dc[DH:]*0.125
    rows=lax.broadcasted_iota(jnp.int32,(AUG,nq),0)
    g1=jnp.sum(jnp.where(segq_ref[...]==rows,seg,0.0),axis=0,keepdims=True)
    g0=jnp.sum(seg,axis=0,keepdims=True)-g1
    dtyped=sm[:,3:4]*g0+sm[:,4:5]*g1
    dq_ref[...]=(dcontent+dpos+dtyped).astype(bf16)
    lane=lax.broadcasted_iota(jnp.int32,(DH,128),1)
    total=jnp.zeros((DH,128),f32)
    for n,val in enumerate((dcontent,dpos,dtyped,typed*g0,typed*g1)):
        total=jnp.where(lane==n,jnp.sum(val,axis=1,keepdims=True),total)
    if first is None:
        sg_ref[...]=total
    else:
        sg_ref[...]=first[1][...]+total

def bwd_kernel_first(*refs,tq,skip):
    bwd_kernel(*refs[:10],*refs[10+skip:],tq=tq,first=None)
def bwd_kernel_next(*refs,tq,skip):
    bwd_kernel(*refs[:10],*refs[12+skip:],tq=tq,first=refs[10:12])

def attn_bwd(which,qT,kT,vT,relT,small,segq,segk,probs,mixedT,dmixedT,carry=None,tq=256,heads=None,base=None):
    hd,nq=qT.shape; nk=kT.shape[1]
    start,count=heads or (0,hd//DH)
    row=lambda n: pl.BlockSpec((DH,n),lambda h:(h+start if start else h,0))
    ins=[row(nq),row(nk),row(nk),row(2*nk),row(small.shape[1]),pl.BlockSpec((None,1,nq),lambda h:(which,0,0)),pl.BlockSpec((None,1,nk),lambda h:(which,0,0)),
         pl.BlockSpec((None,nq,nk),lambda h:(h+start if start else h,0,0)),row(nq),row(nq)]
    args=[qT,kT,vT,relT,small,segq,segk,probs,mixedT,dmixedT]
    kern=bwd_kernel_first
    if carry is not None:
        ins+= [row(2*nk),row(128)]; args+=list(carry); kern=bwd_kernel_next
    aliases={}
    if base is not None:
        aliases={len(args)+n:n for n in range(5)}
        ins+=[pl.BlockSpec(memory_space=pl.ANY)]*5; args+=list(base)
    return pl.pallas_call(partial(kern,tq=tq,skip=len(aliases)),grid=(count,),in_specs=ins,
        out_specs=[row(nq),row(nk),row(nk),row(2*nk),row(128)],
        out_shape=[jax.ShapeDtypeStruct((hd,nq),bf16),jax.ShapeDtypeStruct((hd,nk),bf16),jax.ShapeDtypeStruct((hd,nk),bf16),
           jax.ShapeDtypeStruct((hd,2*nk),f32),jax.ShapeDtypeStruct((hd,128),f32)],
        input_output_aliases=aliases,
        scratch_shapes=[pltpu.VMEM((DH+AUG,nk),bf16),pltpu.VMEM((DH+AUG,nk),bf16),pltpu.VMEM((DH+AUG,nq),bf16),pltpu.VMEM((nq,nk),bf16),pltpu.VMEM((nq,2*nk),bf16)],
        name="attend_back",**limits((15*count//6)<<20))(*args)


PARTS = 4
LATE = 5


def pair_matrix(count, axis):
    shape = (count, 2 * count) if axis == 1 else (2 * count, count)
    longer = lax.broadcasted_iota(jnp.int32, shape, axis)
    shorter = lax.broadcasted_iota(jnp.int32, shape, 1 - axis)
    return jnp.where(jnp.right_shift(longer, 1) == shorter, 0.5, 0.0).astype(bf16)


def spot(place_ref, core, column, line):
    return (
        4 * jnp.bitwise_xor(place_ref[0], line)
        + 2 * jnp.bitwise_xor(place_ref[1], column)
        + jnp.bitwise_xor(place_ref[2], core)
    )


def project_kernel(
    place_ref, near0_ref, near1_ref, far0_ref, far1_ref, own_ref, peer_ref, phase_ref,
    own_q, own_k, own_v, peer_q, peer_k, peer_v, rel_ref, pooled_ref, own_low, peer_low, weights_ref,
    turned_sc,
):
    @pl.when(pl.program_id(0) == 0)
    def _():
        for i in range(PARTS):
            for n, ref in enumerate((near0_ref, near1_ref, far0_ref, far1_ref)):
                for d in range(ref.shape[0]):
                    weights_ref[i, spot(place_ref, n // 2, n % 2, d)] = ref[d, i]
            turned_sc[i] = weights_ref[i].reshape(-1, near0_ref.shape[3]).T

    pairs = pair_matrix(own_ref.shape[0] // 2, 1)

    def sequence(rows_ref, q_ref, k_ref, v_ref, low_ref, keep_ref):
        rows = rows_ref[...]
        pooled = jnp.dot(pairs, rows, preferred_element_type=f32)
        low = pooled.astype(bf16)
        low_ref[...] = low
        if keep_ref is not None:
            keep_ref[...] = pooled
        for i, (source, target) in enumerate(((low, q_ref), (rows, k_ref), (rows, v_ref))):
            target[...] = lax.dot_general(turned_sc[i], source, NT, preferred_element_type=f32).astype(bf16)

    sequence(own_ref, own_q, own_k, own_v, own_low, pooled_ref)
    sequence(peer_ref, peer_q, peer_k, peer_v, peer_low, None)
    rel_ref[...] = lax.dot_general(turned_sc[3], phase_ref[...], NT, preferred_element_type=f32).astype(bf16)


def whole(array):
    return pl.BlockSpec(array.shape, lambda *step: (0,) * array.ndim, pipeline_mode=pl.Buffered(1))


def out(shape, dtype):
    return jax.ShapeDtypeStruct(shape, dtype)


def limits(moved):
    return dict(
        compiler_params=pltpu.CompilerParams(vmem_limit_bytes=56 << 20),
        cost_estimate=pl.CostEstimate(flops=moved, bytes_accessed=moved, transcendentals=0),
    )


def project(place, stacks, tokens, peer_tokens, phase, steps=4):
    length, model = tokens.shape
    half = length // 2
    count, _, depth, width = stacks[0].shape
    ins = [*stacks, tokens, peer_tokens, phase]
    outs = [
        out((width, half), bf16), out((width, length), bf16), out((width, length), bf16),
        out((width, half), bf16), out((width, length), bf16), out((width, length), bf16),
        out((width, 2 * length), bf16), out((half, model), f32), out((half, model), bf16), out((half, model), bf16),
        out((PARTS, 4 * count, depth, width), bf16),
    ]
    def rows(array):
        return pl.BlockSpec((array.shape[0] // steps, array.shape[1]), lambda s: (s, 0))

    def columns(array):
        return pl.BlockSpec((array.shape[0], array.shape[1] // steps), lambda s: (0, s))

    return pl.pallas_call(
        project_kernel,
        grid=(steps,),
        in_specs=[pl.BlockSpec(memory_space=pltpu.SMEM)] + [whole(a) for a in stacks] + [rows(a) for a in ins[4:]],
        out_specs=[columns(a) for a in outs[:7]] + [rows(a) for a in outs[7:10]] + [whole(outs[10])],
        out_shape=outs,
        scratch_shapes=[pltpu.VMEM((PARTS, width, model), bf16)],
        name="project",
        **limits(10 << 20),
    )(place, *ins)


def weigh_kernel(
    place_ref, own_rows, peer_rows, own_low, peer_low, phase_ref, own_dq, own_dk, own_dv, peer_dq, peer_dk, peer_dv,
    drel_ref, own_dc, sent_dc, late_ref, early_ref, keep_ref, send_ref, total_sc, value_sc, small_sc,
):
    step = pl.program_id(0)

    @pl.when(step == 0)
    def _():
        total_sc[...] = jnp.zeros_like(total_sc)

    for i, pairs in enumerate((
        ((own_dq, own_low), (peer_dq, peer_low)),
        ((own_dk, own_rows), (peer_dk, peer_rows)),
        ((own_dv, own_rows), (peer_dv, peer_rows)),
        ((drel_ref, phase_ref),),
    )):
        for grad, rows in pairs:
            total_sc[i] += jnp.dot(grad[...].astype(bf16), rows[...], preferred_element_type=f32)

    @pl.when(step == pl.num_programs(0) - 1)
    def _():
        columns, lines, _, width = keep_ref.shape
        depth = value_sc.shape[1]
        for i in range(PARTS + 1):
            if i < PARTS:
                value_sc[...] = total_sc[i].astype(bf16).T.reshape(value_sc.shape)
            else:
                value_sc[...] = (own_dc[...].astype(f32) + sent_dc[...].astype(f32)).astype(bf16)
            for core, ref in enumerate((keep_ref, send_ref)):
                for column in range(columns):
                    for line in range(lines):
                        ref[column, line, i * depth:(i + 1) * depth] = value_sc[spot(place_ref, core, column, line)]
        first, last = LATE, LATE + early_ref.shape[0]
        small_sc[...] = jnp.zeros_like(small_sc)
        small_sc[:first] = late_ref[...].T[:first]
        small_sc[first:last] = early_ref[:, :width]
        small_sc[last : 2 * last - first] = early_ref[:, width:]
        small = small_sc[...].astype(bf16)
        for column in range(columns):
            for line in range(lines):
                for ref in (keep_ref, send_ref):
                    ref[column, line, (PARTS + 1) * depth:] = small


def weigh(place, own_rows, peer_rows, own_low, peer_low, phase, own_grads, peer_grads, drel, own_dc, sent_dc, late, early, blocks, steps=4):
    model = own_rows.shape[1]
    depth = model // blocks
    width = drel.shape[0]
    extra = LATE + 2 * early.shape[0]
    extra += -extra % 16

    def rows(array):
        return pl.BlockSpec((array.shape[0] // steps, model), lambda s: (s, 0))

    def columns(array):
        return pl.BlockSpec((width, array.shape[1] // steps), lambda s: (0, s))

    ins = [own_rows, peer_rows, own_low, peer_low, phase]
    grads = [*own_grads, *peer_grads, drel]
    pieces = out((2, blocks // 4, (PARTS + 1) * depth + extra, width), bf16)
    return pl.pallas_call(
        weigh_kernel,
        grid=(steps,),
        in_specs=[pl.BlockSpec(memory_space=pltpu.SMEM)] + [rows(a) for a in ins] + [columns(a) for a in grads] + [whole(a) for a in (own_dc, sent_dc, late, early)],
        out_specs=[whole(pieces)] * 2,
        out_shape=[pieces] * 2,
        scratch_shapes=[pltpu.VMEM((PARTS, width, model), f32), pltpu.VMEM((blocks, depth, width), bf16), pltpu.VMEM((extra, width), f32)],
        name="weigh",
        **limits(8 << 20),
    )(place, *ins, *grads, own_dc, sent_dc, late, early)


def token_kernel(dq_ref, dk_ref, dv_ref, w_ref, *refs):
    model = refs[-1].shape[1]
    width = dk_ref.shape[0]
    half = dq_ref.shape[1]
    doubled = jnp.dot(dq_ref[...], pair_matrix(half, 1), preferred_element_type=f32).astype(bf16)
    total = None
    for i, grad in enumerate((doubled, dk_ref[...], dv_ref[...])):
        term = lax.dot_general(grad.T, w_ref[i].reshape(model, width), NT, preferred_element_type=f32)
        total = term if total is None else total + term
    if len(refs) > 1:
        high = refs[0][...].astype(bf16)
        low = (refs[0][...] - high.astype(f32)).astype(bf16)
        pairs = pair_matrix(half, 0)
        total = total + jnp.dot(pairs, high, preferred_element_type=f32) + jnp.dot(pairs, low, preferred_element_type=f32)
    refs[-1][...] = total.astype(refs[-1].dtype)


def token_grad(grads, weights, extra, dtype):
    length = grads[1].shape[1]
    model = weights.shape[1] * weights.shape[2]
    ins = [*grads, weights] + ([extra] if extra is not None else [])
    specs = [whole(a) for a in ins]
    result = out((length, model), dtype)
    return pl.pallas_call(
        token_kernel,
        grid=(1,),
        in_specs=specs,
        out_specs=whole(result),
        out_shape=result,
        name="token_grad",
        **limits(1 << 18),
    )(*ins)


def finish_kernel(place_ref, *refs, sources):
    total = refs[0][...].astype(f32)
    for ref in refs[1:sources]:
        total = total + ref[...].astype(f32)
    grads_ref, combiner_ref, offsets_ref, sameness_ref, bias_ref, *vectors, total_sc = refs[sources:]
    parts, depth, width = grads_ref.shape
    for i in range(parts):
        grads_ref[i] = total[i * depth : (i + 1) * depth]
    combiner_ref[...] = total[parts * depth : (parts + 1) * depth]
    total_sc[...] = total[(parts + 1) * depth :]
    offsets_ref[...] = total_sc[:3]
    sameness_ref[...] = total_sc[3:LATE]
    count = len(vectors) + 4

    def row(n):
        return jnp.concatenate(
            [total_sc[LATE + n : LATE + n + 1], total_sc[LATE + count + n : LATE + count + n + 1]], axis=1
        )

    for n, ref in enumerate(vectors):
        ref[...] = row(n).reshape(ref.shape)
    n = len(vectors)
    first = place_ref[3] == 0
    bias = jnp.concatenate(
        [jnp.where(first, row(n), row(n + 2)), jnp.where(first, row(n + 1), row(n + 3))], axis=1
    )
    bias_ref[...] = bias.reshape(bias_ref.shape)


def finish(place, pieces, depth, model, hidden):
    extra = pieces[0].shape[0] - (PARTS + 1) * depth
    width = pieces[0].shape[1]
    outs = [
        out((PARTS, depth, width), f32), out((depth, width), f32), out((3, width), f32), out((2, width), f32), out((hidden,), f32),
    ] + [out((model,), f32)] * 6
    return pl.pallas_call(
        partial(finish_kernel, sources=len(pieces)),
        grid=(1,),
        in_specs=[pl.BlockSpec(memory_space=pltpu.SMEM)] + [whole(a) for a in pieces],
        out_specs=[whole(a) for a in outs],
        out_shape=outs,
        scratch_shapes=[pltpu.VMEM((extra, width), f32)],
        name="finish",
        **limits(1 << 20),
    )(place, *pieces)


SPLIT = 1


def layer_norm(values_in):
    row_mean = jnp.mean(values_in, axis=1, keepdims=True)
    centred = values_in - row_mean
    variance = jnp.mean(centred * centred, axis=1, keepdims=True)
    scale = lax.rsqrt(variance + epsilon)
    return centred * scale, scale


def layer_norm_back(grad, normed, scale, gain):
    inner = grad * gain
    return scale * (
        inner
        - jnp.mean(inner, axis=1, keepdims=True)
        - normed * jnp.mean(inner * normed, axis=1, keepdims=True)
    )


def row_sum(values_in):
    return jnp.sum(values_in, axis=0, keepdims=True)


def middle_kernel(
    place_ref, pooled_ref, mixed_ref, sent_ref, vec_ref, cot_ref, own_c_ref, peer_c_ref, weights_ref, own_bias_ref, peer_bias_ref,
    result_ref, dfirst_ref, own_dm_ref, peer_dm_ref, own_dc_ref, peer_dc_ref, sums_ref,
    keep_w_ref, send_w_ref, keep_n_ref, send_n_ref,
    held_sc, held_sem, slope_sc, act_sc, dhid_sc, first_sc, norm_sc, scale_sc, total_sc, low_sc, low_t_sc, dsec_sc, dsec_t_sc,
    *, chunks,
):
    step = pl.program_id(0)
    model = pooled_ref.shape[1]
    rows = pooled_ref.shape[0]
    part = own_bias_ref.shape[-1]
    each = own_bias_ref.shape[0]

    def fetch(chunk, kind):
        return pltpu.make_async_copy(
            weights_ref.at[:, chunk // each, :, pl.ds((kind * each + chunk % each) * part, part)],
            held_sc.at[chunk, kind],
            held_sem.at[chunk, kind],
        )
    vec = vec_ref[...]

    def store(value, keep_ref, send_ref):
        value = value.astype(bf16)
        for n, ref in enumerate((keep_ref, send_ref)):
            piece = value[n * (model // 2) : (n + 1) * (model // 2)]
            ref[...] = piece.reshape(ref.shape)

    def turn_rows(value, ref):
        value = value.T.reshape(ref.shape)
        count = ref.shape[0]
        for n in range(count):
            line, column, core = n // 4, n // 2 % 2, n % 2
            ref[
                (count // 2) * jnp.bitwise_xor(place_ref[2], core)
                + (count // 4) * jnp.bitwise_xor(place_ref[1], column)
                + jnp.bitwise_xor(place_ref[0], line)
            ] = value[n]

    postbias, scaling, centring = vec[0:1], vec[1:2], vec[2:3]
    narrowbias, rescale, recentre = vec[3:4], vec[4:5], vec[5:6]

    @pl.when(step == 0)
    def _():
        for chunk in range(chunks):
            for kind in range(2):
                fetch(chunk, kind).start()
        own_c = own_c_ref[...].reshape(model, -1)
        peer_c = peer_c_ref[...].reshape(model, -1)
        mixed = mixed_ref[...].astype(bf16).T
        sent = sent_ref[...].T
        branch = (
            lax.dot_general(mixed, own_c, NT, preferred_element_type=f32)
            + lax.dot_general(sent, peer_c, NT, preferred_element_type=f32)
            + postbias
        )
        normed, scale = layer_norm(pooled_ref[...] + branch)
        norm_sc[...] = normed
        scale_sc[...] = scale
        first = normed * scaling + centring
        first_sc[...] = first
        low = first.astype(bf16)
        low_sc[...] = low
        turn_rows(low, low_t_sc)
        total_sc[...] = jnp.zeros_like(total_sc)

    for chunk in range(chunks):

        @pl.when(step == chunk)
        def _():
            for kind in range(2):
                fetch(chunk, kind).wait()

    @pl.when(step < chunks)
    def _():
        wide = held_sc[step, 0].reshape(model, part)
        spot_bias = lax.rem(step, each)
        bias = jnp.where(step // each == place_ref[3], own_bias_ref[spot_bias], peer_bias_ref[spot_bias])
        hidden = jnp.dot(low_sc[...], wide, preferred_element_type=f32) + bias
        square = hidden * hidden
        root = math.sqrt(2.0 / math.pi)
        turn = jnp.tanh(hidden * (root + (root * 0.044715) * square))
        half = 0.5 * turn + 0.5
        act = (hidden * half).astype(bf16)
        slope_sc[step] = half + hidden * (half * (1.0 - turn)) * (root + (3.0 * root * 0.044715) * square)
        act_sc[step] = act
        narrow = held_sc[step, 1].reshape(model, part)
        total_sc[...] += lax.dot_general(act, narrow, NT, preferred_element_type=f32)

    @pl.when(step == chunks - 1)
    def _():
        normed, scale = layer_norm(first_sc[...] + (total_sc[...] + narrowbias))
        result_ref[...] = (normed * rescale + recentre).astype(bf16)
        cot = cot_ref[...].astype(f32)
        dfinal = layer_norm_back(cot, normed, scale, rescale)
        dsec = dfinal.astype(bf16)
        dsec_sc[...] = dsec
        turn_rows(dsec, dsec_t_sc)
        sums_ref[3:4] = row_sum(dsec.astype(f32))
        sums_ref[4:5] = row_sum(cot * normed)
        sums_ref[5:6] = row_sum(cot)
        total_sc[...] = dfinal

    back = step - chunks

    @pl.when((back >= 0) & (lax.rem(back, 2) == 0))
    def _():
        chunk = back // 2
        narrow = held_sc[chunk, 1].reshape(model, part)
        dact = jnp.dot(dsec_sc[...], narrow, preferred_element_type=f32)
        dhid = (dact * slope_sc[chunk]).astype(bf16)
        dhid_sc[...] = dhid
        bias_sum = row_sum(dhid.astype(f32))
        for n in range(part // model):
            sums_ref[pl.ds(6 + chunk * (part // model) + n, 1)] = bias_sum[:, n * model : (n + 1) * model]
        grad = jnp.dot(dsec_t_sc[...].reshape(model, rows), act_sc[chunk], preferred_element_type=f32)
        store(grad, keep_n_ref, send_n_ref)

    @pl.when((back >= 0) & (lax.rem(back, 2) == 1))
    def _():
        wide = held_sc[back // 2, 0].reshape(model, part)
        total_sc[...] += lax.dot_general(dhid_sc[...], wide, NT, preferred_element_type=f32)
        grad = jnp.dot(low_t_sc[...].reshape(model, rows), dhid_sc[...], preferred_element_type=f32)
        store(grad, keep_w_ref, send_w_ref)

    @pl.when(back == 2 * chunks - 1)
    def _():
        dfirst = total_sc[...]
        normed = norm_sc[...]
        dfirst_in = layer_norm_back(dfirst, normed, scale_sc[...], scaling)
        dfirst_ref[...] = dfirst_in
        dbranch = dfirst_in.astype(bf16)
        sums_ref[0:1] = row_sum(dbranch.astype(f32))
        sums_ref[1:2] = row_sum(dfirst * normed)
        sums_ref[2:3] = row_sum(dfirst)
        dbranch_t = dbranch.T
        for c_ref, m_ref, dm_ref, dc_ref in (
            (own_c_ref, mixed_ref, own_dm_ref, own_dc_ref),
            (peer_c_ref, sent_ref, peer_dm_ref, peer_dc_ref),
        ):
            c = c_ref[...].reshape(model, -1)
            dm_ref[...] = lax.dot_general(c, dbranch_t, TN, preferred_element_type=f32).astype(bf16)
            dc = lax.dot_general(dbranch_t, m_ref[...].astype(bf16), NT, preferred_element_type=f32)
            dc_ref[...] = dc.astype(bf16).reshape(dc_ref.shape)


def middle(place, pooled, mixed, sent, vec, cot, weights, own_bias, peer_bias):
    rows, model = pooled.shape
    blocks, halves, depth, columns = weights.shape
    width = mixed.shape[0]
    hidden = (columns - width) // 2
    part = hidden // SPLIT
    each = hidden // part
    chunks = halves * each

    def combiner_spec(flip):
        def index(step, place_ref):
            return (0, jnp.bitwise_xor(place_ref[3], flip), 0, 2 * hidden // width)

        return pl.BlockSpec((blocks, None, depth, width), index, pipeline_mode=pl.Buffered(1))

    def wide_index(step, place_ref):
        c = jnp.maximum(step - chunks - 1, 0) // 2
        return (jnp.bitwise_xor(c // each, place_ref[3]), 0, 0, 0, lax.rem(c, each))

    def narrow_index(step, place_ref):
        c = jnp.maximum(step - chunks, 0) // 2
        return (0, jnp.bitwise_xor(c // each, place_ref[3]), 0, 0, lax.rem(c, each))

    lines = blocks // 4
    outs = [
        out((rows, model), bf16), out((rows, model), f32), out(mixed.shape, bf16), out(mixed.shape, bf16),
        out((blocks, depth, width), bf16), out((blocks, depth, width), bf16), out((6 + halves * hidden // model, model), f32),
    ]
    wide_grads = out((halves, 2, lines, depth, hidden), bf16)
    narrow_grads = out((2, halves, lines, depth, hidden), bf16)
    whole_ins = [pooled, mixed, sent, vec, cot]
    grad_spec = [pl.BlockSpec((1, 2, lines, depth, part), wide_index)] * 2
    grad_spec += [pl.BlockSpec((2, 1, lines, depth, part), narrow_index)] * 2
    return pl.pallas_call(
        partial(middle_kernel, chunks=chunks),
        grid_spec=pltpu.PrefetchScalarGridSpec(
            num_scalar_prefetch=1,
            grid=(3 * chunks,),
            in_specs=[whole(a) for a in whole_ins]
            + [combiner_spec(0), combiner_spec(1), pl.BlockSpec(memory_space=pl.ANY)]
            + [pl.BlockSpec((each, 1, part), lambda s, p: (0, 0, 0))] * 2,
            out_specs=[whole(a) for a in outs]
            + grad_spec,
            scratch_shapes=[
                pltpu.VMEM((chunks, 2, blocks, depth, part), bf16),
                pltpu.SemaphoreType.DMA((chunks, 2)),
                pltpu.VMEM((chunks, rows, part), f32),
                pltpu.VMEM((chunks, rows, part), bf16),
                pltpu.VMEM((rows, part), bf16),
                pltpu.VMEM((rows, model), f32),
                pltpu.VMEM((rows, model), f32),
                pltpu.VMEM((rows, 1), f32),
                pltpu.VMEM((rows, model), f32),
                pltpu.VMEM((rows, model), bf16),
                pltpu.VMEM((blocks, depth, rows), bf16),
                pltpu.VMEM((rows, model), bf16),
                pltpu.VMEM((blocks, depth, rows), bf16),
            ],
        ),
        out_shape=outs + [wide_grads] * 2 + [narrow_grads] * 2,
        name="middle",
        **limits(24 << 20),
    )(place, *whole_ins, weights, weights, weights, own_bias.reshape(each, 1, part), peer_bias.reshape(each, 1, part))


def position_table(length, model_width):
    row_index = jnp.arange(2 * length, dtype=jnp.float32)
    offset = length - row_index
    half_width = model_width // 2
    frequency = jnp.exp(
        jnp.arange(half_width, dtype=jnp.float32) * (-math.log(10000.0) / half_width)
    )
    angles = offset[:, None] * frequency[None, :]
    return jnp.concatenate([jnp.sin(angles), jnp.cos(angles)], axis=1)


BLOCKS = 16


def swap(piece):
    return lax.ppermute(piece, "tensor", [(0, 1), (1, 0)])


def exchange(piece, mask):
    count = lax.axis_size("dp")
    return lax.ppermute(piece, "dp", [(i, i ^ mask) for i in range(count)])


def shards(
    tokens,
    segments,
    projections,
    combiner,
    offsets,
    sameness,
    postbias,
    scaling,
    centring,
    widener,
    widebias,
    narrower,
    narrowbias,
    rescale,
    recentre,
    cotangent,
):
    tensor_part = lax.axis_index("tensor")
    dp_part = lax.axis_index("dp")
    dp_count = lax.axis_size("dp")
    length, model = tokens.shape
    width = offsets.shape[1]
    hidden = widener.shape[1]
    blocks = BLOCKS
    depth = model // blocks
    direct = dp_count == blocks
    if direct:
        place = jnp.stack([dp_part // 4, (dp_part // 2) % 2, dp_part % 2, tensor_part]).astype(jnp.int32)
    else:
        place = jnp.stack([tensor_part * 0] * 3 + [tensor_part]).astype(jnp.int32)

    mine = jnp.concatenate([widener, narrower.T, combiner.T], axis=1)
    mine, projections = lax.optimization_barrier((mine, projections))
    phase = position_table(length, model).astype(bf16)
    if direct:
        near0 = jnp.stack([projections] + [exchange(projections, 4 * d) for d in range(1, 4)])
        near0, phase = lax.optimization_barrier((near0, phase))
        near1 = exchange(near0, 2)
        stacks = (near0, near1, exchange(near0, 1), exchange(near1, 1))
    else:
        every = lax.all_gather(projections, "dp", axis=1, tiled=True)
        every = every.reshape(PARTS, blocks // 4, 2, 2, depth, width).transpose(3, 2, 1, 0, 4, 5)
        stacks = (every[0, 0], every[0, 1], every[1, 0], every[1, 1])
    peer_tokens = swap(tokens)
    columns = mine.shape[1]
    weights = lax.all_gather(mine, ("dp", "tensor"), axis=0, tiled=False)
    if not direct:
        weights = weights.reshape(dp_count, 2, model // dp_count, columns).transpose(1, 0, 2, 3)
        weights = weights.reshape(2, blocks, depth, columns).transpose(1, 0, 2, 3)
    weights = weights.reshape(blocks, 2, depth, columns)
    small = jnp.concatenate([offsets, sameness], axis=0).T
    seg = jnp.where(tensor_part == 0, segments, jnp.concatenate([segments[1:], segments[:1]]))[:, None]
    vec = jnp.stack([postbias, scaling, centring, narrowbias, rescale, recentre, postbias, postbias])
    peer_tokens, peer_bias, small, seg, seg_q, vec = lax.optimization_barrier(
        (peer_tokens, swap(widebias), small, seg, seg[:, :, ::2], vec)
    )
    own_q, own_k, own_v, peer_q, peer_k, peer_v, relative, pooled, own_low, peer_low, inwards = project(
        place, stacks, tokens, peer_tokens, phase
    )
    own_args = (own_q, own_k, own_v, relative, small, seg_q, seg)
    peer_args = (peer_q, peer_k, peer_v, relative, small, seg_q, seg)
    peer_probs, peer_mixed, peer_mixed_low = attn_fwd(*peer_args, 1)
    sent_mixed = swap(peer_mixed_low)
    own_probs, own_mixed, own_mixed_low = attn_fwd(*own_args, 0)
    result, dfirst_in, own_dmixed, peer_dmixed, own_dc, peer_dc, early, keep_w, send_w, keep_n, send_n = middle(
        place, pooled, own_mixed_low, sent_mixed, vec, cotangent, weights, widebias, peer_bias
    )
    sent_dmixed = swap(peer_dmixed)
    sent_dc = swap(peer_dc)
    half = width // DH // 2
    part = attn_bwd(0, *own_args, own_probs, own_mixed, own_dmixed, heads=(0, half))
    early = early + swap(early)
    if direct:

        def add(kept, sent):
            return (kept.astype(f32) + sent.astype(f32)).astype(bf16)

        wide = (keep_w, exchange(send_w, 1))
        narrow = (keep_n, exchange(send_n, 1))
        first_stage = (
            add(wide[0][0], wide[1][0]),
            add(wide[0][1], wide[1][1]),
            add(narrow[0][0], narrow[1][0]),
            add(narrow[0][1], narrow[1][1]),
        )
        part, early, first_stage, sent_dmixed, sent_dc = lax.optimization_barrier(
            (part, early, first_stage, sent_dmixed, sent_dc)
        )

    own_dq, own_dk, own_dv, drel, late = attn_bwd(
        0, *own_args, own_probs, own_mixed, own_dmixed, heads=(half, width // DH - half), base=part
    )
    peer_dq, peer_dk, peer_dv, drel, late = attn_bwd(
        1, *peer_args, peer_probs, peer_mixed, sent_dmixed, (drel, late)
    )
    own_grads = (own_dq, own_dk, own_dv)
    peer_grads = (peer_dq, peer_dk, peer_dv)
    if direct:
        wide = (first_stage[0], swap(first_stage[1]))
        narrow = (first_stage[2], exchange(first_stage[3], 2))
        wide = (add(wide[0][0], wide[1][0]), add(wide[0][1], wide[1][1]))
        narrow = (add(narrow[0][0], narrow[1][0]), add(narrow[0][1], narrow[1][1]))
        drel, wide, narrow = lax.optimization_barrier((drel, wide, narrow))
        wide = (wide[0], exchange(wide[1], 2))
        narrow = (narrow[0], swap(narrow[1]))
    keep, send = weigh(
        place, tokens, peer_tokens, own_low, peer_low, phase, own_grads, peer_grads, drel, own_dc, sent_dc, late, early, blocks
    )
    if direct:
        keep, send, wide, narrow = lax.optimization_barrier((keep, send, wide, narrow))
        sent = exchange(send, 1)
        held = (add(keep[0], sent[0]), add(keep[1], sent[1]))
        last = [
            jnp.concatenate([add(wide[0][d], wide[1][d]), add(narrow[0][d], narrow[1][d])], axis=-1)
            for d in range(4)
        ]
        peer_grads, held, last = lax.optimization_barrier((peer_grads, held, last))
        held = (held[0], exchange(held[1], 2))
    peer_part = token_grad(peer_grads, inwards, None, bf16)
    sent_tokens = swap(peer_part)
    own_grads, _ = lax.optimization_barrier((own_grads, peer_part))
    own_part = token_grad(own_grads, inwards, dfirst_in, f32)
    if direct:
        grads = last[0].astype(f32)
        for d in range(1, 4):
            grads = grads + exchange(last[d], 4 * d).astype(f32)
        held = [add(held[0][d], held[1][d]) for d in range(4)]
        own_part, held = lax.optimization_barrier((own_part, held))
        pieces = [held[0]] + [exchange(held[d], 4 * d) for d in range(1, 4)]
        tokens_grad, pieces = lax.optimization_barrier((own_part + sent_tokens.astype(f32), pieces))
    else:

        def ordered(kept, sent, turned):
            value = jnp.stack([kept, sent])
            value = value.transpose((3, 1, 0, 2, 4, 5) if turned else (3, 2, 0, 1, 4, 5))
            value = jnp.where(tensor_part == 0, value, value[:, :, :, ::-1])
            return value.transpose(3, 0, 1, 2, 4, 5).reshape(2, dp_count, model // dp_count, -1)

        grads = jnp.concatenate([ordered(keep_w, send_w, False), ordered(keep_n, send_n, True)], axis=-1)
        grads = lax.psum_scatter(
            grads.transpose(1, 0, 2, 3).reshape(2 * dp_count, model // dp_count, 2 * hidden),
            ("dp", "tensor"),
            scatter_dimension=0,
            tiled=True,
        )[0].astype(f32)
        big = jnp.stack([keep, send])[:, :, :, : (PARTS + 1) * depth]
        big = big.reshape(2, 2, blocks // 4, PARTS + 1, depth, width).transpose(3, 2, 1, 0, 4, 5)
        big = lax.psum_scatter(big.reshape(PARTS + 1, model, width), "dp", scatter_dimension=1, tiled=True)
        extras = lax.psum(keep[0, 0, (PARTS + 1) * depth :].astype(f32), "dp").astype(bf16)
        pieces = [jnp.concatenate([big.reshape(-1, width), extras], axis=0)]
        tokens_grad = own_part + sent_tokens.astype(f32)
    projections_grad, combiner_grad, offsets_grad, sameness_grad, bias_grad, *vectors = finish(
        place, pieces, depth if direct else model // dp_count, model, hidden
    )
    return (
        result,
        tokens_grad,
        projections_grad,
        combiner_grad.T,
        offsets_grad,
        sameness_grad,
        vectors[0],
        vectors[1],
        vectors[2],
        grads[:, :hidden],
        bias_grad,
        grads[:, hidden:].T,
        vectors[3],
        vectors[4],
        vectors[5],
    )


def solution(mesh):
    placed = (
        P(("dp", "tensor"), None),
        P("dp", None),
        P(None, "dp", "tensor"),
        P("tensor", "dp"),
        P(None, "tensor"),
        P(None, "tensor"),
        P(),
        P(),
        P(),
        P("dp", "tensor"),
        P("tensor"),
        P("tensor", "dp"),
        P(),
        P(),
        P(),
        P(("dp", "tensor"), None),
    )
    return jax.shard_map(
        shards,
        mesh=mesh,
        in_specs=placed,
        out_specs=(
            P(("dp", "tensor"), None),
            P(("dp", "tensor"), None),
            P(None, "dp", "tensor"),
            P("tensor", "dp"),
            P(None, "tensor"),
            P(None, "tensor"),
            P(),
            P(),
            P(),
            P("dp", "tensor"),
            P("tensor"),
            P("tensor", "dp"),
            P(),
            P(),
            P(),
        ),
        check_vma=False,
    )
```

```python
from functools import partial
import math

import jax
import jax.numpy as jnp
from jax import lax
from jax.experimental import pallas as pl
from jax.experimental.pallas import tpu as pltpu
from jax.sharding import PartitionSpec as P

epsilon = 1e-05
bf16=jnp.bfloat16; f32=jnp.float32
DH=64
AUG=16
TN=(((0,),(0,)),((),()))
NT=(((1,),(1,)),((),()))
NN=(((1,),(0,)),((),()))

def split3(u):
    row=lax.broadcasted_iota(jnp.int32,u.shape,0)
    hi=u.astype(bf16).astype(f32)
    r1=u-hi
    mid=r1.astype(bf16).astype(f32)
    lo=r1-mid
    return jnp.where(row<3,hi,jnp.where(row<6,mid,jnp.where(row<9,lo,0.0))).astype(bf16)

def fwd_kernel(q_ref,k_ref,v_ref,r_ref,s_ref,segq_ref,segk_ref,p_ref,m_ref,ml_ref,c_sc,k_sc,*,tq):
    nq=q_ref.shape[1]; nk=k_ref.shape[1]
    q=q_ref[...].astype(f32)
    sm=s_ref[...]
    c_sc[:DH]=(q+sm[:,0:1]).astype(bf16)*jnp.asarray(0.125,bf16)
    pos=(q+sm[:,1:2]).astype(bf16)*jnp.asarray(0.125,bf16)
    typed=q+sm[:,2:3]
    t0=jnp.sum(typed*sm[:,3:4],axis=0,keepdims=True)*0.125
    t1=jnp.sum(typed*sm[:,4:5],axis=0,keepdims=True)*0.125
    kind=lax.rem(lax.broadcasted_iota(jnp.int32,(AUG,nq),0),3)
    c_sc[DH:]=split3(jnp.where(segq_ref[...]==kind,t1,t0))
    k_sc[:DH]=k_ref[...]
    rowk=lax.broadcasted_iota(jnp.int32,(AUG,nk),0)
    k_sc[DH:]=jnp.where((segk_ref[...]==lax.rem(rowk,3)) & (rowk<9),1.0,0.0).astype(bf16)

    tr=min(tq,128)
    def dense(b):
        i0=b*tq; w0=nk-2*i0-2*tq
        return lax.dot_general(pos[:,i0:i0+tq],r_ref[:,w0:w0+nk+2*tq],TN,preferred_element_type=f32)
    def cont(b):
        i0=b*tq
        return lax.dot_general(c_sc[:,i0:i0+tq],k_sc[...],TN,preferred_element_type=f32)
    def finish(b,c,d):
        i0=b*tq
        for t in range(tq//tr):
            lo=2*(tq-(t+1)*tr)
            g=pltpu.roll(d[t*tr:(t+1)*tr,lo:lo+nk+2*tr],nk,1,stride=2,stride_axis=0)
            s=c[t*tr:(t+1)*tr]+g[:,:nk]
            mx=jnp.max(s,axis=1,keepdims=True)
            e=jnp.exp(s-mx)
            l=jnp.sum(e,axis=1,keepdims=True)
            p_ref[i0+t*tr:i0+(t+1)*tr,:]=(e*(1.0/l)).astype(bf16)
    n=nq//tq
    prev=(cont(0),dense(0))
    for b in range(n):
        nxt=(cont(b+1),dense(b+1)) if b+1<n else None
        finish(b,*prev); prev=nxt
    mixed=lax.dot_general(v_ref[...],p_ref[...],NT,preferred_element_type=f32)
    m_ref[...]=mixed
    ml_ref[...]=mixed.astype(bf16)

def attn_fwd(qT,kT,vT,relT,small,segq,segk,row=0,tq=128):
    hd,nq=qT.shape; nk=kT.shape[1]; heads=hd//DH
    return pl.pallas_call(partial(fwd_kernel,tq=tq),grid=(heads,),
        in_specs=[pl.BlockSpec((DH,nq),lambda h:(h,0)),pl.BlockSpec((DH,nk),lambda h:(h,0)),pl.BlockSpec((DH,nk),lambda h:(h,0)),
          pl.BlockSpec((DH,2*nk),lambda h:(h,0)),pl.BlockSpec((DH,small.shape[1]),lambda h:(h,0)),
          pl.BlockSpec((None,1,nq),lambda h:(row,0,0)),pl.BlockSpec((None,1,nk),lambda h:(row,0,0))],
        out_specs=[pl.BlockSpec((None,nq,nk),lambda h:(h,0,0)),pl.BlockSpec((DH,nq),lambda h:(h,0)),pl.BlockSpec((DH,nq),lambda h:(h,0))],
        out_shape=[jax.ShapeDtypeStruct((heads,nq,nk),bf16),jax.ShapeDtypeStruct((hd,nq),f32),jax.ShapeDtypeStruct((hd,nq),bf16)],
        scratch_shapes=[pltpu.VMEM((DH+AUG,nq),bf16),pltpu.VMEM((DH+AUG,nk),bf16)],
        name="attend",**limits(15<<20))(qT,kT,vT,relT,small,segq,segk)

def bwd_kernel(q_ref,k_ref,v_ref,r_ref,s_ref,segq_ref,segk_ref,p_ref,m_ref,dm_ref,
               dq_ref,dk_ref,dv_ref,dr_ref,sg_ref,k_sc,v_sc,dm_sc,ds_sc,dg_sc,*,tq,first):
    nq=q_ref.shape[1]; nk=k_ref.shape[1]
    q=q_ref[...].astype(f32)
    sm=s_ref[...]
    content=(q+sm[:,0:1]).astype(bf16)*jnp.asarray(0.125,bf16)
    pos=(q+sm[:,1:2]).astype(bf16)*jnp.asarray(0.125,bf16)
    typed=q+sm[:,2:3]
    k_sc[:DH]=k_ref[...]
    rowk=lax.broadcasted_iota(jnp.int32,(AUG,nk),0)
    k_sc[DH:]=((segk_ref[...]==rowk)).astype(f32).astype(bf16)
    v_sc[:DH]=v_ref[...]
    v_sc[DH:]=jnp.where(rowk<3,1.0,0.0).astype(bf16)
    dm=dm_ref[...]
    dm_sc[:DH]=dm
    delta=-jnp.sum(dm.astype(f32)*m_ref[...],axis=0,keepdims=True)
    rowq=lax.broadcasted_iota(jnp.int32,(AUG,nq),0)
    hi=delta.astype(bf16).astype(f32); r1=delta-hi; mid=r1.astype(bf16).astype(f32); lo=r1-mid
    dm_sc[DH:]=jnp.where(rowq==0,hi,jnp.where(rowq==1,mid,jnp.where(rowq==2,lo,0.0))).astype(bf16)
    w=nk+2*tq
    flip=(lax.broadcasted_iota(jnp.int32,(tq,tq),0)+lax.broadcasted_iota(jnp.int32,(tq,tq),1)==tq-1).astype(f32).astype(bf16)
    def turn16(x):
        parts=[lax.dot_general(x[:,i:i+tq],flip,NN,preferred_element_type=f32) for i in range(0,nq,tq)]
        return jnp.concatenate(parts,axis=1).astype(bf16)
    def turn(x):
        hi=x.astype(bf16); r1=x-hi.astype(f32); mid=r1.astype(bf16); lo=(r1-mid.astype(f32)).astype(bf16)
        cat=jnp.concatenate([hi,mid,lo],axis=0)
        parts=[lax.dot_general(cat[:,i:i+tq],flip,NN,preferred_element_type=f32) for i in range(0,nq,tq)]
        y=jnp.concatenate(parts,axis=1)
        return y[:DH]+y[DH:2*DH]+y[2*DH:]

    @pl.when(pl.program_id(0)==0)
    def _():
        dg_sc[...]=jnp.zeros_like(dg_sc)
    def grad(b):
        i0=b*tq
        return lax.dot_general(dm_sc[:,i0:i0+tq],v_sc[...],TN,preferred_element_type=f32)
    def shift(b,dp):
        i0=b*tq
        w0=nk-2*i0-2*tq
        ds16=(p_ref[i0:i0+tq,:].astype(f32)*dp).astype(bf16)
        ds_sc[i0:i0+tq,:]=ds16
        back=lax.dot_general(flip,ds16,NN,preferred_element_type=f32)
        g=jnp.concatenate([back,jnp.zeros((tq,2*tq),f32)],axis=1)
        g=pltpu.roll(g,2,1,stride=2,stride_axis=0)
        dg_sc[i0:i0+tq,w0:w0+w]=g.astype(bf16)
    n=nq//tq
    for b in range(n): shift(b,grad(b))
    dv_ref[...]=lax.dot_general(dm,p_ref[...],NN,preferred_element_type=f32).astype(bf16)
    dk_ref[...]=lax.dot_general(content,ds_sc[...],NN,preferred_element_type=f32).astype(bf16)
    dc=lax.dot_general(k_sc[...],ds_sc[...],NT,preferred_element_type=f32)
    half=256
    tpos=turn16(pos)
    parts=[];drs=[]
    for c0 in range(0,nq,half):
        v0=nk-2*c0-2*half
        g=dg_sc[c0:c0+half,v0:v0+nk+2*half]
        parts.append(lax.dot_general(r_ref[:,v0:v0+nk+2*half],g,NT,preferred_element_type=f32))
        drs.append(lax.dot_general(tpos[:,c0:c0+half],g,NN,preferred_element_type=f32))
    dpos=turn(jnp.concatenate(parts,axis=1))*0.125
    z=jnp.zeros((DH,2*half),f32)
    dr=jnp.concatenate([z,drs[0]],axis=1)+jnp.concatenate([drs[1],z],axis=1)
    if first is None:
        dr_ref[...]=dr
    else:
        dr_ref[...]=first[0][...]+dr
    dcontent=dc[:DH]*0.125
    seg=dc[DH:]*0.125
    rows=lax.broadcasted_iota(jnp.int32,(AUG,nq),0)
    g1=jnp.sum(jnp.where(segq_ref[...]==rows,seg,0.0),axis=0,keepdims=True)
    g0=jnp.sum(seg,axis=0,keepdims=True)-g1
    dtyped=sm[:,3:4]*g0+sm[:,4:5]*g1
    dq_ref[...]=(dcontent+dpos+dtyped).astype(bf16)
    lane=lax.broadcasted_iota(jnp.int32,(DH,128),1)
    total=jnp.zeros((DH,128),f32)
    for n,val in enumerate((dcontent,dpos,dtyped,typed*g0,typed*g1)):
        total=jnp.where(lane==n,jnp.sum(val,axis=1,keepdims=True),total)
    if first is None:
        sg_ref[...]=total
    else:
        sg_ref[...]=first[1][...]+total

def bwd_kernel_first(*refs,tq,skip):
    bwd_kernel(*refs[:10],*refs[10+skip:],tq=tq,first=None)
def bwd_kernel_next(*refs,tq,skip):
    bwd_kernel(*refs[:10],*refs[12+skip:],tq=tq,first=refs[10:12])

def attn_bwd(which,qT,kT,vT,relT,small,segq,segk,probs,mixedT,dmixedT,carry=None,tq=256,heads=None,base=None):
    hd,nq=qT.shape; nk=kT.shape[1]
    start,count=heads or (0,hd//DH)
    row=lambda n: pl.BlockSpec((DH,n),lambda h:(h+start if start else h,0))
    ins=[row(nq),row(nk),row(nk),row(2*nk),row(small.shape[1]),pl.BlockSpec((None,1,nq),lambda h:(which,0,0)),pl.BlockSpec((None,1,nk),lambda h:(which,0,0)),
         pl.BlockSpec((None,nq,nk),lambda h:(h+start if start else h,0,0)),row(nq),row(nq)]
    args=[qT,kT,vT,relT,small,segq,segk,probs,mixedT,dmixedT]
    kern=bwd_kernel_first
    if carry is not None:
        ins+= [row(2*nk),row(128)]; args+=list(carry); kern=bwd_kernel_next
    aliases={}
    if base is not None:
        aliases={len(args)+n:n for n in range(5)}
        ins+=[pl.BlockSpec(memory_space=pl.ANY)]*5; args+=list(base)
    return pl.pallas_call(partial(kern,tq=tq,skip=len(aliases)),grid=(count,),in_specs=ins,
        out_specs=[row(nq),row(nk),row(nk),row(2*nk),row(128)],
        out_shape=[jax.ShapeDtypeStruct((hd,nq),bf16),jax.ShapeDtypeStruct((hd,nk),bf16),jax.ShapeDtypeStruct((hd,nk),bf16),
           jax.ShapeDtypeStruct((hd,2*nk),f32),jax.ShapeDtypeStruct((hd,128),f32)],
        input_output_aliases=aliases,
        scratch_shapes=[pltpu.VMEM((DH+AUG,nk),bf16),pltpu.VMEM((DH+AUG,nk),bf16),pltpu.VMEM((DH+AUG,nq),bf16),pltpu.VMEM((nq,nk),bf16),pltpu.VMEM((nq,2*nk),bf16)],
        name="attend_back",**limits((15*count//6)<<20))(*args)


PARTS = 4
LATE = 5


def pair_matrix(count, axis):
    shape = (count, 2 * count) if axis == 1 else (2 * count, count)
    longer = lax.broadcasted_iota(jnp.int32, shape, axis)
    shorter = lax.broadcasted_iota(jnp.int32, shape, 1 - axis)
    return jnp.where(jnp.right_shift(longer, 1) == shorter, 0.5, 0.0).astype(bf16)


def spot(place_ref, core, column, line):
    return (
        4 * jnp.bitwise_xor(place_ref[0], line)
        + 2 * jnp.bitwise_xor(place_ref[1], column)
        + jnp.bitwise_xor(place_ref[2], core)
    )


def project_kernel(
    place_ref, near0_ref, near1_ref, far0_ref, far1_ref, own_ref, peer_ref, phase_ref,
    own_q, own_k, own_v, peer_q, peer_k, peer_v, rel_ref, pooled_ref, own_low, peer_low, weights_ref, combiner_ref,
    turned_sc,
):
    @pl.when(pl.program_id(0) == 0)
    def _():
        for n, ref in enumerate((near0_ref, near1_ref, far0_ref, far1_ref)):
            for d in range(ref.shape[0]):
                block = spot(place_ref, n // 2, n % 2, d)
                for i in range(PARTS):
                    weights_ref[i, block] = ref[d, i]
                combiner_ref[block] = ref[d, PARTS]
        for i in range(PARTS):
            turned_sc[i] = weights_ref[i].reshape(-1, near0_ref.shape[3]).T

    pairs = pair_matrix(own_ref.shape[0] // 2, 1)

    def sequence(rows_ref, q_ref, k_ref, v_ref, low_ref, keep_ref):
        rows = rows_ref[...]
        pooled = jnp.dot(pairs, rows, preferred_element_type=f32)
        low = pooled.astype(bf16)
        low_ref[...] = low
        if keep_ref is not None:
            keep_ref[...] = pooled
        for i, (source, target) in enumerate(((low, q_ref), (rows, k_ref), (rows, v_ref))):
            target[...] = lax.dot_general(turned_sc[i], source, NT, preferred_element_type=f32).astype(bf16)

    sequence(own_ref, own_q, own_k, own_v, own_low, pooled_ref)
    sequence(peer_ref, peer_q, peer_k, peer_v, peer_low, None)
    rel_ref[...] = lax.dot_general(turned_sc[3], phase_ref[...], NT, preferred_element_type=f32).astype(bf16)


def whole(array):
    return pl.BlockSpec(array.shape, lambda *step: (0,) * array.ndim, pipeline_mode=pl.Buffered(1))


def out(shape, dtype):
    return jax.ShapeDtypeStruct(shape, dtype)


def limits(moved):
    return dict(
        compiler_params=pltpu.CompilerParams(vmem_limit_bytes=56 << 20),
        cost_estimate=pl.CostEstimate(flops=moved, bytes_accessed=moved, transcendentals=0),
    )


def project(place, stacks, tokens, peer_tokens, phase, steps=4):
    length, model = tokens.shape
    half = length // 2
    count, _, depth, width = stacks[0].shape
    ins = [*stacks, tokens, peer_tokens, phase]
    outs = [
        out((width, half), bf16), out((width, length), bf16), out((width, length), bf16),
        out((width, half), bf16), out((width, length), bf16), out((width, length), bf16),
        out((width, 2 * length), bf16), out((half, model), f32), out((half, model), bf16), out((half, model), bf16),
        out((PARTS, 4 * count, depth, width), bf16), out((4 * count, depth, width), bf16),
    ]
    def rows(array):
        return pl.BlockSpec((array.shape[0] // steps, array.shape[1]), lambda s: (s, 0))

    def columns(array):
        return pl.BlockSpec((array.shape[0], array.shape[1] // steps), lambda s: (0, s))

    return pl.pallas_call(
        project_kernel,
        grid=(steps,),
        in_specs=[pl.BlockSpec(memory_space=pltpu.SMEM)] + [whole(a) for a in stacks] + [rows(a) for a in ins[4:]],
        out_specs=[columns(a) for a in outs[:7]] + [rows(a) for a in outs[7:10]] + [whole(a) for a in outs[10:]],
        out_shape=outs,
        scratch_shapes=[pltpu.VMEM((PARTS, width, model), bf16)],
        name="project",
        **limits(10 << 20),
    )(place, *ins)


def weigh_kernel(
    place_ref, own_rows, peer_rows, own_low, peer_low, phase_ref, own_dq, own_dk, own_dv, peer_dq, peer_dk, peer_dv,
    drel_ref, own_dc, sent_dc, late_ref, early_ref, keep_ref, send_ref, total_sc, value_sc, small_sc,
):
    step = pl.program_id(0)

    @pl.when(step == 0)
    def _():
        total_sc[...] = jnp.zeros_like(total_sc)

    for i, pairs in enumerate((
        ((own_dq, own_low), (peer_dq, peer_low)),
        ((own_dk, own_rows), (peer_dk, peer_rows)),
        ((own_dv, own_rows), (peer_dv, peer_rows)),
        ((drel_ref, phase_ref),),
    )):
        for grad, rows in pairs:
            total_sc[i] += jnp.dot(grad[...].astype(bf16), rows[...], preferred_element_type=f32)

    @pl.when(step == pl.num_programs(0) - 1)
    def _():
        columns, lines, _, width = keep_ref.shape
        depth = value_sc.shape[1]
        for i in range(PARTS + 1):
            if i < PARTS:
                value_sc[...] = total_sc[i].astype(bf16).T.reshape(value_sc.shape)
            else:
                value_sc[...] = (own_dc[...].astype(f32) + sent_dc[...].astype(f32)).astype(bf16)
            for core, ref in enumerate((keep_ref, send_ref)):
                for column in range(columns):
                    for line in range(lines):
                        ref[column, line, i * depth:(i + 1) * depth] = value_sc[spot(place_ref, core, column, line)]
        first, last = LATE, LATE + early_ref.shape[0]
        small_sc[...] = jnp.zeros_like(small_sc)
        small_sc[:first] = late_ref[...].T[:first]
        small_sc[first:last] = early_ref[:, :width]
        small_sc[last : 2 * last - first] = early_ref[:, width:]
        small = small_sc[...].astype(bf16)
        for column in range(columns):
            for line in range(lines):
                for ref in (keep_ref, send_ref):
                    ref[column, line, (PARTS + 1) * depth:] = small


def weigh(place, own_rows, peer_rows, own_low, peer_low, phase, own_grads, peer_grads, drel, own_dc, sent_dc, late, early, blocks, steps=4):
    model = own_rows.shape[1]
    depth = model // blocks
    width = drel.shape[0]
    extra = LATE + 2 * early.shape[0]
    extra += -extra % 16

    def rows(array):
        return pl.BlockSpec((array.shape[0] // steps, model), lambda s: (s, 0))

    def columns(array):
        return pl.BlockSpec((width, array.shape[1] // steps), lambda s: (0, s))

    ins = [own_rows, peer_rows, own_low, peer_low, phase]
    grads = [*own_grads, *peer_grads, drel]
    pieces = out((2, blocks // 4, (PARTS + 1) * depth + extra, width), bf16)
    return pl.pallas_call(
        weigh_kernel,
        grid=(steps,),
        in_specs=[pl.BlockSpec(memory_space=pltpu.SMEM)] + [rows(a) for a in ins] + [columns(a) for a in grads] + [whole(a) for a in (own_dc, sent_dc, late, early)],
        out_specs=[whole(pieces)] * 2,
        out_shape=[pieces] * 2,
        scratch_shapes=[pltpu.VMEM((PARTS, width, model), f32), pltpu.VMEM((blocks, depth, width), bf16), pltpu.VMEM((extra, width), f32)],
        name="weigh",
        **limits(8 << 20),
    )(place, *ins, *grads, own_dc, sent_dc, late, early)


def token_kernel(dq_ref, dk_ref, dv_ref, w_ref, *refs):
    model = refs[-1].shape[1]
    width = dk_ref.shape[0]
    half = dq_ref.shape[1]
    doubled = jnp.dot(dq_ref[...], pair_matrix(half, 1), preferred_element_type=f32).astype(bf16)
    total = None
    for i, grad in enumerate((doubled, dk_ref[...], dv_ref[...])):
        term = lax.dot_general(grad.T, w_ref[i].reshape(model, width), NT, preferred_element_type=f32)
        total = term if total is None else total + term
    if len(refs) > 1:
        high = refs[0][...].astype(bf16)
        low = (refs[0][...] - high.astype(f32)).astype(bf16)
        pairs = pair_matrix(half, 0)
        total = total + jnp.dot(pairs, high, preferred_element_type=f32) + jnp.dot(pairs, low, preferred_element_type=f32)
    refs[-1][...] = total.astype(refs[-1].dtype)


def token_grad(grads, weights, extra, dtype):
    length = grads[1].shape[1]
    model = weights.shape[1] * weights.shape[2]
    ins = [*grads, weights] + ([extra] if extra is not None else [])
    specs = [whole(a) for a in ins]
    result = out((length, model), dtype)
    return pl.pallas_call(
        token_kernel,
        grid=(1,),
        in_specs=specs,
        out_specs=whole(result),
        out_shape=result,
        name="token_grad",
        **limits(1 << 18),
    )(*ins)


def finish_kernel(place_ref, *refs, sources):
    total = refs[0][...].astype(f32)
    for ref in refs[1:sources]:
        total = total + ref[...].astype(f32)
    grads_ref, combiner_ref, offsets_ref, sameness_ref, bias_ref, *vectors, total_sc = refs[sources:]
    parts, depth, width = grads_ref.shape
    for i in range(parts):
        grads_ref[i] = total[i * depth : (i + 1) * depth]
    combiner_ref[...] = total[parts * depth : (parts + 1) * depth]
    total_sc[...] = total[(parts + 1) * depth :]
    offsets_ref[...] = total_sc[:3]
    sameness_ref[...] = total_sc[3:LATE]
    count = len(vectors) + 4

    def row(n):
        return jnp.concatenate(
            [total_sc[LATE + n : LATE + n + 1], total_sc[LATE + count + n : LATE + count + n + 1]], axis=1
        )

    for n, ref in enumerate(vectors):
        ref[...] = row(n).reshape(ref.shape)
    n = len(vectors)
    first = place_ref[3] == 0
    bias = jnp.concatenate(
        [jnp.where(first, row(n), row(n + 2)), jnp.where(first, row(n + 1), row(n + 3))], axis=1
    )
    bias_ref[...] = bias.reshape(bias_ref.shape)


def finish(place, pieces, depth, model, hidden):
    extra = pieces[0].shape[0] - (PARTS + 1) * depth
    width = pieces[0].shape[1]
    outs = [
        out((PARTS, depth, width), f32), out((depth, width), f32), out((3, width), f32), out((2, width), f32), out((hidden,), f32),
    ] + [out((model,), f32)] * 6
    return pl.pallas_call(
        partial(finish_kernel, sources=len(pieces)),
        grid=(1,),
        in_specs=[pl.BlockSpec(memory_space=pltpu.SMEM)] + [whole(a) for a in pieces],
        out_specs=[whole(a) for a in outs],
        out_shape=outs,
        scratch_shapes=[pltpu.VMEM((extra, width), f32)],
        name="finish",
        **limits(1 << 20),
    )(place, *pieces)


SPLIT = 1


def layer_norm(values_in):
    row_mean = jnp.mean(values_in, axis=1, keepdims=True)
    centred = values_in - row_mean
    variance = jnp.mean(centred * centred, axis=1, keepdims=True)
    scale = lax.rsqrt(variance + epsilon)
    return centred * scale, scale


def layer_norm_back(grad, normed, scale, gain):
    inner = grad * gain
    return scale * (
        inner
        - jnp.mean(inner, axis=1, keepdims=True)
        - normed * jnp.mean(inner * normed, axis=1, keepdims=True)
    )


def row_sum(values_in):
    return jnp.sum(values_in, axis=0, keepdims=True)


def middle_kernel(
    place_ref, pooled_ref, mixed_ref, sent_ref, vec_ref, cot_ref, own_c_ref, peer_c_ref, weights_ref, own_bias_ref, peer_bias_ref,
    result_ref, dfirst_ref, own_dm_ref, peer_dm_ref, own_dc_ref, peer_dc_ref, sums_ref,
    keep_w_ref, send_w_ref, keep_n_ref, send_n_ref,
    held_sc, held_sem, slope_sc, act_sc, dhid_sc, first_sc, norm_sc, scale_sc, total_sc, low_sc, low_t_sc, dsec_sc, dsec_t_sc,
    *, chunks,
):
    step = pl.program_id(0)
    model = pooled_ref.shape[1]
    rows = pooled_ref.shape[0]
    part = own_bias_ref.shape[-1]
    each = own_bias_ref.shape[0]

    def fetch(chunk, kind):
        return pltpu.make_async_copy(
            weights_ref.at[:, chunk // each, :, pl.ds((kind * each + chunk % each) * part, part)],
            held_sc.at[chunk, kind],
            held_sem.at[chunk, kind],
        )
    vec = vec_ref[...]

    def store(value, keep_ref, send_ref):
        value = value.astype(bf16)
        for n, ref in enumerate((keep_ref, send_ref)):
            piece = value[n * (model // 2) : (n + 1) * (model // 2)]
            ref[...] = piece.reshape(ref.shape)

    def turn_rows(value, ref):
        value = value.T.reshape(ref.shape)
        count = ref.shape[0]
        for n in range(count):
            line, column, core = n // 4, n // 2 % 2, n % 2
            ref[
                (count // 2) * jnp.bitwise_xor(place_ref[2], core)
                + (count // 4) * jnp.bitwise_xor(place_ref[1], column)
                + jnp.bitwise_xor(place_ref[0], line)
            ] = value[n]

    postbias, scaling, centring = vec[0:1], vec[1:2], vec[2:3]
    narrowbias, rescale, recentre = vec[3:4], vec[4:5], vec[5:6]

    @pl.when(step == 0)
    def _():
        for chunk in range(chunks):
            for kind in range(2):
                fetch(chunk, kind).start()
        own_c = own_c_ref[...].reshape(model, -1)
        peer_c = peer_c_ref[...].reshape(model, -1)
        mixed = mixed_ref[...].astype(bf16).T
        sent = sent_ref[...].T
        branch = (
            lax.dot_general(mixed, own_c, NT, preferred_element_type=f32)
            + lax.dot_general(sent, peer_c, NT, preferred_element_type=f32)
            + postbias
        )
        normed, scale = layer_norm(pooled_ref[...] + branch)
        norm_sc[...] = normed
        scale_sc[...] = scale
        first = normed * scaling + centring
        first_sc[...] = first
        low = first.astype(bf16)
        low_sc[...] = low
        turn_rows(low, low_t_sc)
        total_sc[...] = jnp.zeros_like(total_sc)

    for chunk in range(chunks):

        @pl.when(step == chunk)
        def _():
            for kind in range(2):
                fetch(chunk, kind).wait()

    @pl.when(step < chunks)
    def _():
        wide = held_sc[step, 0].reshape(model, part)
        spot_bias = lax.rem(step, each)
        bias = jnp.where(step // each == place_ref[3], own_bias_ref[spot_bias], peer_bias_ref[spot_bias])
        hidden = jnp.dot(low_sc[...], wide, preferred_element_type=f32) + bias
        square = hidden * hidden
        root = math.sqrt(2.0 / math.pi)
        turn = jnp.tanh(hidden * (root + (root * 0.044715) * square))
        half = 0.5 * turn + 0.5
        act = (hidden * half).astype(bf16)
        slope_sc[step] = half + hidden * (half * (1.0 - turn)) * (root + (3.0 * root * 0.044715) * square)
        act_sc[step] = act
        narrow = held_sc[step, 1].reshape(model, part)
        total_sc[...] += lax.dot_general(act, narrow, NT, preferred_element_type=f32)

    @pl.when(step == chunks - 1)
    def _():
        normed, scale = layer_norm(first_sc[...] + (total_sc[...] + narrowbias))
        result_ref[...] = (normed * rescale + recentre).astype(bf16)
        cot = cot_ref[...].astype(f32)
        dfinal = layer_norm_back(cot, normed, scale, rescale)
        dsec = dfinal.astype(bf16)
        dsec_sc[...] = dsec
        turn_rows(dsec, dsec_t_sc)
        sums_ref[3:4] = row_sum(dsec.astype(f32))
        sums_ref[4:5] = row_sum(cot * normed)
        sums_ref[5:6] = row_sum(cot)
        total_sc[...] = dfinal

    back = step - chunks

    @pl.when((back >= 0) & (lax.rem(back, 2) == 0))
    def _():
        chunk = back // 2
        narrow = held_sc[chunk, 1].reshape(model, part)
        dact = jnp.dot(dsec_sc[...], narrow, preferred_element_type=f32)
        dhid = (dact * slope_sc[chunk]).astype(bf16)
        dhid_sc[...] = dhid
        bias_sum = row_sum(dhid.astype(f32))
        for n in range(part // model):
            sums_ref[pl.ds(6 + chunk * (part // model) + n, 1)] = bias_sum[:, n * model : (n + 1) * model]
        grad = jnp.dot(dsec_t_sc[...].reshape(model, rows), act_sc[chunk], preferred_element_type=f32)
        store(grad, keep_n_ref, send_n_ref)

    @pl.when((back >= 0) & (lax.rem(back, 2) == 1))
    def _():
        wide = held_sc[back // 2, 0].reshape(model, part)
        total_sc[...] += lax.dot_general(dhid_sc[...], wide, NT, preferred_element_type=f32)
        grad = jnp.dot(low_t_sc[...].reshape(model, rows), dhid_sc[...], preferred_element_type=f32)
        store(grad, keep_w_ref, send_w_ref)

    @pl.when(back == 2 * chunks - 1)
    def _():
        dfirst = total_sc[...]
        normed = norm_sc[...]
        dfirst_in = layer_norm_back(dfirst, normed, scale_sc[...], scaling)
        dfirst_ref[...] = dfirst_in
        dbranch = dfirst_in.astype(bf16)
        sums_ref[0:1] = row_sum(dbranch.astype(f32))
        sums_ref[1:2] = row_sum(dfirst * normed)
        sums_ref[2:3] = row_sum(dfirst)
        dbranch_t = dbranch.T
        for c_ref, m_ref, dm_ref, dc_ref in (
            (own_c_ref, mixed_ref, own_dm_ref, own_dc_ref),
            (peer_c_ref, sent_ref, peer_dm_ref, peer_dc_ref),
        ):
            c = c_ref[...].reshape(model, -1)
            dm_ref[...] = lax.dot_general(c, dbranch_t, TN, preferred_element_type=f32).astype(bf16)
            dc = lax.dot_general(dbranch_t, m_ref[...].astype(bf16), NT, preferred_element_type=f32)
            dc_ref[...] = dc.astype(bf16).reshape(dc_ref.shape)


def middle(place, pooled, mixed, sent, vec, cot, own_c, peer_c, weights, own_bias, peer_bias):
    rows, model = pooled.shape
    blocks, halves, depth, columns = weights.shape
    width = mixed.shape[0]
    hidden = columns // 2
    part = hidden // SPLIT
    each = hidden // part
    chunks = halves * each

    def wide_index(step, place_ref):
        c = jnp.maximum(step - chunks - 1, 0) // 2
        return (jnp.bitwise_xor(c // each, place_ref[3]), 0, 0, 0, lax.rem(c, each))

    def narrow_index(step, place_ref):
        c = jnp.maximum(step - chunks, 0) // 2
        return (0, jnp.bitwise_xor(c // each, place_ref[3]), 0, 0, lax.rem(c, each))

    lines = blocks // 4
    outs = [
        out((rows, model), bf16), out((rows, model), f32), out(mixed.shape, bf16), out(mixed.shape, bf16),
        out((blocks, depth, width), bf16), out((blocks, depth, width), bf16), out((6 + halves * hidden // model, model), f32),
    ]
    wide_grads = out((halves, 2, lines, depth, hidden), bf16)
    narrow_grads = out((2, halves, lines, depth, hidden), bf16)
    whole_ins = [pooled, mixed, sent, vec, cot, own_c, peer_c]
    grad_spec = [pl.BlockSpec((1, 2, lines, depth, part), wide_index)] * 2
    grad_spec += [pl.BlockSpec((2, 1, lines, depth, part), narrow_index)] * 2
    return pl.pallas_call(
        partial(middle_kernel, chunks=chunks),
        grid_spec=pltpu.PrefetchScalarGridSpec(
            num_scalar_prefetch=1,
            grid=(3 * chunks,),
            in_specs=[whole(a) for a in whole_ins]
            + [pl.BlockSpec(memory_space=pl.ANY)]
            + [pl.BlockSpec((each, 1, part), lambda s, p: (0, 0, 0))] * 2,
            out_specs=[whole(a) for a in outs]
            + grad_spec,
            scratch_shapes=[
                pltpu.VMEM((chunks, 2, blocks, depth, part), bf16),
                pltpu.SemaphoreType.DMA((chunks, 2)),
                pltpu.VMEM((chunks, rows, part), f32),
                pltpu.VMEM((chunks, rows, part), bf16),
                pltpu.VMEM((rows, part), bf16),
                pltpu.VMEM((rows, model), f32),
                pltpu.VMEM((rows, model), f32),
                pltpu.VMEM((rows, 1), f32),
                pltpu.VMEM((rows, model), f32),
                pltpu.VMEM((rows, model), bf16),
                pltpu.VMEM((blocks, depth, rows), bf16),
                pltpu.VMEM((rows, model), bf16),
                pltpu.VMEM((blocks, depth, rows), bf16),
            ],
        ),
        out_shape=outs + [wide_grads] * 2 + [narrow_grads] * 2,
        name="middle",
        **limits(24 << 20),
    )(place, *whole_ins, weights, own_bias.reshape(each, 1, part), peer_bias.reshape(each, 1, part))


def position_table(length, model_width):
    row_index = jnp.arange(2 * length, dtype=jnp.float32)
    offset = length - row_index
    half_width = model_width // 2
    frequency = jnp.exp(
        jnp.arange(half_width, dtype=jnp.float32) * (-math.log(10000.0) / half_width)
    )
    angles = offset[:, None] * frequency[None, :]
    return jnp.concatenate([jnp.sin(angles), jnp.cos(angles)], axis=1)


BLOCKS = 16


def swap(piece):
    return lax.ppermute(piece, "tensor", [(0, 1), (1, 0)])


def exchange(piece, mask):
    count = lax.axis_size("dp")
    return lax.ppermute(piece, "dp", [(i, i ^ mask) for i in range(count)])


def shards(
    tokens,
    segments,
    projections,
    combiner,
    offsets,
    sameness,
    postbias,
    scaling,
    centring,
    widener,
    widebias,
    narrower,
    narrowbias,
    rescale,
    recentre,
    cotangent,
):
    tensor_part = lax.axis_index("tensor")
    dp_part = lax.axis_index("dp")
    dp_count = lax.axis_size("dp")
    length, model = tokens.shape
    width = offsets.shape[1]
    hidden = widener.shape[1]
    blocks = BLOCKS
    depth = model // blocks
    direct = dp_count == blocks
    if direct:
        place = jnp.stack([dp_part // 4, (dp_part // 2) % 2, dp_part % 2, tensor_part]).astype(jnp.int32)
    else:
        place = jnp.stack([tensor_part * 0] * 3 + [tensor_part]).astype(jnp.int32)

    mine = jnp.concatenate([widener, narrower.T], axis=1)
    mine, own_piece = lax.optimization_barrier((mine, jnp.concatenate([projections, combiner.T[None]], axis=0)))
    phase = position_table(length, model).astype(bf16)
    if direct:
        near0 = jnp.stack([own_piece] + [exchange(own_piece, 4 * d) for d in range(1, 4)])
        near0, phase = lax.optimization_barrier((near0, phase))
        near1 = exchange(near0, 2)
        stacks = (near0, near1, exchange(near0, 1), exchange(near1, 1))
    else:
        every = lax.all_gather(own_piece, "dp", axis=1, tiled=True)
        every = every.reshape(PARTS + 1, blocks // 4, 2, 2, depth, width).transpose(3, 2, 1, 0, 4, 5)
        stacks = (every[0, 0], every[0, 1], every[1, 0], every[1, 1])
    peer_tokens = swap(tokens)
    columns = mine.shape[1]
    weights = lax.all_gather(mine, ("dp", "tensor"), axis=0, tiled=False)
    if not direct:
        weights = weights.reshape(dp_count, 2, model // dp_count, columns).transpose(1, 0, 2, 3)
        weights = weights.reshape(2, blocks, depth, columns).transpose(1, 0, 2, 3)
    weights = weights.reshape(blocks, 2, depth, columns)
    small = jnp.concatenate([offsets, sameness], axis=0).T
    seg = jnp.where(tensor_part == 0, segments, jnp.concatenate([segments[1:], segments[:1]]))[:, None]
    vec = jnp.stack([postbias, scaling, centring, narrowbias, rescale, recentre, postbias, postbias])
    peer_tokens, peer_bias, small, seg, seg_q, vec = lax.optimization_barrier(
        (peer_tokens, swap(widebias), small, seg, seg[:, :, ::2], vec)
    )
    own_q, own_k, own_v, peer_q, peer_k, peer_v, relative, pooled, own_low, peer_low, inwards, own_c = project(
        place, stacks, tokens, peer_tokens, phase
    )
    peer_c = swap(own_c)
    own_args = (own_q, own_k, own_v, relative, small, seg_q, seg)
    peer_args = (peer_q, peer_k, peer_v, relative, small, seg_q, seg)
    peer_probs, peer_mixed, peer_mixed_low = attn_fwd(*peer_args, 1)
    sent_mixed = swap(peer_mixed_low)
    own_probs, own_mixed, own_mixed_low = attn_fwd(*own_args, 0)
    result, dfirst_in, own_dmixed, peer_dmixed, own_dc, peer_dc, early, keep_w, send_w, keep_n, send_n = middle(
        place, pooled, own_mixed_low, sent_mixed, vec, cotangent, own_c, peer_c, weights, widebias, peer_bias
    )
    sent_dmixed = swap(peer_dmixed)
    half = width // DH // 2
    part = attn_bwd(0, *own_args, own_probs, own_mixed, own_dmixed, heads=(0, half))
    early = early + swap(early)
    if direct:

        def add(kept, sent):
            return (kept.astype(f32) + sent.astype(f32)).astype(bf16)

        wide = (keep_w, exchange(send_w, 1))
        narrow = (keep_n, exchange(send_n, 1))
        first_stage = (
            add(wide[0][0], wide[1][0]),
            add(wide[0][1], wide[1][1]),
            add(narrow[0][0], narrow[1][0]),
            add(narrow[0][1], narrow[1][1]),
        )
        part, early, first_stage, sent_dmixed = lax.optimization_barrier((part, early, first_stage, sent_dmixed))

    own_dq, own_dk, own_dv, drel, late = attn_bwd(
        0, *own_args, own_probs, own_mixed, own_dmixed, heads=(half, width // DH - half), base=part
    )
    drel, late, peer_dc = lax.optimization_barrier((drel, late, peer_dc))
    sent_dc = swap(peer_dc)
    peer_dq, peer_dk, peer_dv, drel, late = attn_bwd(
        1, *peer_args, peer_probs, peer_mixed, sent_dmixed, (drel, late)
    )
    own_grads = (own_dq, own_dk, own_dv)
    peer_grads = (peer_dq, peer_dk, peer_dv)
    if direct:
        wide = (first_stage[0], swap(first_stage[1]))
        narrow = (first_stage[2], exchange(first_stage[3], 2))
        wide = (add(wide[0][0], wide[1][0]), add(wide[0][1], wide[1][1]))
        narrow = (add(narrow[0][0], narrow[1][0]), add(narrow[0][1], narrow[1][1]))
        drel, wide, narrow = lax.optimization_barrier((drel, wide, narrow))
        wide = (wide[0], exchange(wide[1], 2))
        narrow = (narrow[0], swap(narrow[1]))
    keep, send = weigh(
        place, tokens, peer_tokens, own_low, peer_low, phase, own_grads, peer_grads, drel, own_dc, sent_dc, late, early, blocks
    )
    if direct:
        keep, send, wide, narrow = lax.optimization_barrier((keep, send, wide, narrow))
        sent = exchange(send, 1)
        held = (add(keep[0], sent[0]), add(keep[1], sent[1]))
        last = [
            jnp.concatenate([add(wide[0][d], wide[1][d]), add(narrow[0][d], narrow[1][d])], axis=-1)
            for d in range(4)
        ]
        peer_grads, held, last = lax.optimization_barrier((peer_grads, held, last))
        held = (held[0], exchange(held[1], 2))
    peer_part = token_grad(peer_grads, inwards, None, bf16)
    sent_tokens = swap(peer_part)
    own_grads, _ = lax.optimization_barrier((own_grads, peer_part))
    own_part = token_grad(own_grads, inwards, dfirst_in, f32)
    if direct:
        grads = last[0].astype(f32)
        for d in range(1, 4):
            grads = grads + exchange(last[d], 4 * d).astype(f32)
        held = [add(held[0][d], held[1][d]) for d in range(4)]
        own_part, held = lax.optimization_barrier((own_part, held))
        pieces = [held[0]] + [exchange(held[d], 4 * d) for d in range(1, 4)]
        tokens_grad, pieces = lax.optimization_barrier((own_part + sent_tokens.astype(f32), pieces))
    else:

        def ordered(kept, sent, turned):
            value = jnp.stack([kept, sent])
            value = value.transpose((3, 1, 0, 2, 4, 5) if turned else (3, 2, 0, 1, 4, 5))
            value = jnp.where(tensor_part == 0, value, value[:, :, :, ::-1])
            return value.transpose(3, 0, 1, 2, 4, 5).reshape(2, dp_count, model // dp_count, -1)

        grads = jnp.concatenate([ordered(keep_w, send_w, False), ordered(keep_n, send_n, True)], axis=-1)
        grads = lax.psum_scatter(
            grads.transpose(1, 0, 2, 3).reshape(2 * dp_count, model // dp_count, 2 * hidden),
            ("dp", "tensor"),
            scatter_dimension=0,
            tiled=True,
        )[0].astype(f32)
        big = jnp.stack([keep, send])[:, :, :, : (PARTS + 1) * depth]
        big = big.reshape(2, 2, blocks // 4, PARTS + 1, depth, width).transpose(3, 2, 1, 0, 4, 5)
        big = lax.psum_scatter(big.reshape(PARTS + 1, model, width), "dp", scatter_dimension=1, tiled=True)
        extras = lax.psum(keep[0, 0, (PARTS + 1) * depth :].astype(f32), "dp").astype(bf16)
        pieces = [jnp.concatenate([big.reshape(-1, width), extras], axis=0)]
        tokens_grad = own_part + sent_tokens.astype(f32)
    projections_grad, combiner_grad, offsets_grad, sameness_grad, bias_grad, *vectors = finish(
        place, pieces, depth if direct else model // dp_count, model, hidden
    )
    return (
        result,
        tokens_grad,
        projections_grad,
        combiner_grad.T,
        offsets_grad,
        sameness_grad,
        vectors[0],
        vectors[1],
        vectors[2],
        grads[:, :hidden],
        bias_grad,
        grads[:, hidden:].T,
        vectors[3],
        vectors[4],
        vectors[5],
    )


def solution(mesh):
    placed = (
        P(("dp", "tensor"), None),
        P("dp", None),
        P(None, "dp", "tensor"),
        P("tensor", "dp"),
        P(None, "tensor"),
        P(None, "tensor"),
        P(),
        P(),
        P(),
        P("dp", "tensor"),
        P("tensor"),
        P("tensor", "dp"),
        P(),
        P(),
        P(),
        P(("dp", "tensor"), None),
    )
    return jax.shard_map(
        shards,
        mesh=mesh,
        in_specs=placed,
        out_specs=(
            P(("dp", "tensor"), None),
            P(("dp", "tensor"), None),
            P(None, "dp", "tensor"),
            P("tensor", "dp"),
            P(None, "tensor"),
            P(None, "tensor"),
            P(),
            P(),
            P(),
            P("dp", "tensor"),
            P("tensor"),
            P("tensor", "dp"),
            P(),
            P(),
            P(),
        ),
        check_vma=False,
    )
```

```python
from functools import partial
import math

import jax
import jax.numpy as jnp
from jax import lax
from jax.experimental import pallas as pl
from jax.experimental.pallas import tpu as pltpu
from jax.sharding import PartitionSpec as P

epsilon = 1e-05
bf16=jnp.bfloat16; f32=jnp.float32
DH=64
AUG=16
TN=(((0,),(0,)),((),()))
NT=(((1,),(1,)),((),()))
NN=(((1,),(0,)),((),()))

def split3(u):
    row=lax.broadcasted_iota(jnp.int32,u.shape,0)
    hi=u.astype(bf16).astype(f32)
    r1=u-hi
    mid=r1.astype(bf16).astype(f32)
    lo=r1-mid
    return jnp.where(row<3,hi,jnp.where(row<6,mid,jnp.where(row<9,lo,0.0))).astype(bf16)

def fwd_kernel(q_ref,k_ref,v_ref,r_ref,s_ref,segq_ref,segk_ref,p_ref,m_ref,ml_ref,c_sc,k_sc,*,tq):
    nq=q_ref.shape[1]; nk=k_ref.shape[1]
    q=q_ref[...].astype(f32)
    sm=s_ref[...]
    c_sc[:DH]=(q+sm[:,0:1]).astype(bf16)*jnp.asarray(0.125,bf16)
    pos=(q+sm[:,1:2]).astype(bf16)*jnp.asarray(0.125,bf16)
    typed=q+sm[:,2:3]
    t0=jnp.sum(typed*sm[:,3:4],axis=0,keepdims=True)*0.125
    t1=jnp.sum(typed*sm[:,4:5],axis=0,keepdims=True)*0.125
    kind=lax.rem(lax.broadcasted_iota(jnp.int32,(AUG,nq),0),3)
    c_sc[DH:]=split3(jnp.where(segq_ref[...]==kind,t1,t0))
    k_sc[:DH]=k_ref[...]
    rowk=lax.broadcasted_iota(jnp.int32,(AUG,nk),0)
    k_sc[DH:]=jnp.where((segk_ref[...]==lax.rem(rowk,3)) & (rowk<9),1.0,0.0).astype(bf16)

    tr=min(tq,128)
    def dense(b):
        i0=b*tq; w0=nk-2*i0-2*tq
        return lax.dot_general(pos[:,i0:i0+tq],r_ref[:,w0:w0+nk+2*tq],TN,preferred_element_type=f32)
    def cont(b):
        i0=b*tq
        return lax.dot_general(c_sc[:,i0:i0+tq],k_sc[...],TN,preferred_element_type=f32)
    def finish(b,c,d):
        i0=b*tq
        for t in range(tq//tr):
            lo=2*(tq-(t+1)*tr)
            g=pltpu.roll(d[t*tr:(t+1)*tr,lo:lo+nk+2*tr],nk,1,stride=2,stride_axis=0)
            s=c[t*tr:(t+1)*tr]+g[:,:nk]
            mx=jnp.max(s,axis=1,keepdims=True)
            e=jnp.exp(s-mx)
            l=jnp.sum(e,axis=1,keepdims=True)
            p_ref[i0+t*tr:i0+(t+1)*tr,:]=(e*(1.0/l)).astype(bf16)
    n=nq//tq
    prev=(cont(0),dense(0))
    for b in range(n):
        nxt=(cont(b+1),dense(b+1)) if b+1<n else None
        finish(b,*prev); prev=nxt
    mixed=lax.dot_general(v_ref[...],p_ref[...],NT,preferred_element_type=f32)
    m_ref[...]=mixed
    ml_ref[...]=mixed.astype(bf16)

def attn_fwd(qT,kT,vT,relT,small,segq,segk,row=0,tq=128):
    hd,nq=qT.shape; nk=kT.shape[1]; heads=hd//DH
    return pl.pallas_call(partial(fwd_kernel,tq=tq),grid=(heads,),
        in_specs=[pl.BlockSpec((DH,nq),lambda h:(h,0)),pl.BlockSpec((DH,nk),lambda h:(h,0)),pl.BlockSpec((DH,nk),lambda h:(h,0)),
          pl.BlockSpec((DH,2*nk),lambda h:(h,0)),pl.BlockSpec((DH,small.shape[1]),lambda h:(h,0)),
          pl.BlockSpec((None,1,nq),lambda h:(row,0,0)),pl.BlockSpec((None,1,nk),lambda h:(row,0,0))],
        out_specs=[pl.BlockSpec((None,nq,nk),lambda h:(h,0,0)),pl.BlockSpec((DH,nq),lambda h:(h,0)),pl.BlockSpec((DH,nq),lambda h:(h,0))],
        out_shape=[jax.ShapeDtypeStruct((heads,nq,nk),bf16),jax.ShapeDtypeStruct((hd,nq),f32),jax.ShapeDtypeStruct((hd,nq),bf16)],
        scratch_shapes=[pltpu.VMEM((DH+AUG,nq),bf16),pltpu.VMEM((DH+AUG,nk),bf16)],
        name="attend",**limits(15<<20))(qT,kT,vT,relT,small,segq,segk)

def bwd_kernel(q_ref,k_ref,v_ref,r_ref,s_ref,segq_ref,segk_ref,p_ref,m_ref,dm_ref,
               dq_ref,dk_ref,dv_ref,dr_ref,sg_ref,k_sc,v_sc,dm_sc,ds_sc,dg_sc,*,tq,first):
    nq=q_ref.shape[1]; nk=k_ref.shape[1]
    q=q_ref[...].astype(f32)
    sm=s_ref[...]
    content=(q+sm[:,0:1]).astype(bf16)*jnp.asarray(0.125,bf16)
    pos=(q+sm[:,1:2]).astype(bf16)*jnp.asarray(0.125,bf16)
    typed=q+sm[:,2:3]
    k_sc[:DH]=k_ref[...]
    rowk=lax.broadcasted_iota(jnp.int32,(AUG,nk),0)
    k_sc[DH:]=((segk_ref[...]==rowk)).astype(f32).astype(bf16)
    v_sc[:DH]=v_ref[...]
    v_sc[DH:]=jnp.where(rowk<3,1.0,0.0).astype(bf16)
    dm=dm_ref[...]
    dm_sc[:DH]=dm
    delta=-jnp.sum(dm.astype(f32)*m_ref[...],axis=0,keepdims=True)
    rowq=lax.broadcasted_iota(jnp.int32,(AUG,nq),0)
    hi=delta.astype(bf16).astype(f32); r1=delta-hi; mid=r1.astype(bf16).astype(f32); lo=r1-mid
    dm_sc[DH:]=jnp.where(rowq==0,hi,jnp.where(rowq==1,mid,jnp.where(rowq==2,lo,0.0))).astype(bf16)
    w=nk+2*tq
    flip=(lax.broadcasted_iota(jnp.int32,(tq,tq),0)+lax.broadcasted_iota(jnp.int32,(tq,tq),1)==tq-1).astype(f32).astype(bf16)
    def turn16(x):
        parts=[lax.dot_general(x[:,i:i+tq],flip,NN,preferred_element_type=f32) for i in range(0,nq,tq)]
        return jnp.concatenate(parts,axis=1).astype(bf16)
    def turn(x):
        hi=x.astype(bf16); r1=x-hi.astype(f32); mid=r1.astype(bf16); lo=(r1-mid.astype(f32)).astype(bf16)
        cat=jnp.concatenate([hi,mid,lo],axis=0)
        parts=[lax.dot_general(cat[:,i:i+tq],flip,NN,preferred_element_type=f32) for i in range(0,nq,tq)]
        y=jnp.concatenate(parts,axis=1)
        return y[:DH]+y[DH:2*DH]+y[2*DH:]

    @pl.when(pl.program_id(0)==0)
    def _():
        dg_sc[...]=jnp.zeros_like(dg_sc)
    def grad(b):
        i0=b*tq
        return lax.dot_general(dm_sc[:,i0:i0+tq],v_sc[...],TN,preferred_element_type=f32)
    def shift(b,dp):
        i0=b*tq
        w0=nk-2*i0-2*tq
        ds16=(p_ref[i0:i0+tq,:].astype(f32)*dp).astype(bf16)
        ds_sc[i0:i0+tq,:]=ds16
        back=lax.dot_general(flip,ds16,NN,preferred_element_type=f32)
        g=jnp.concatenate([back,jnp.zeros((tq,2*tq),f32)],axis=1)
        g=pltpu.roll(g,2,1,stride=2,stride_axis=0)
        dg_sc[i0:i0+tq,w0:w0+w]=g.astype(bf16)
    n=nq//tq
    for b in range(n): shift(b,grad(b))
    dv_ref[...]=lax.dot_general(dm,p_ref[...],NN,preferred_element_type=f32).astype(bf16)
    dk_ref[...]=lax.dot_general(content,ds_sc[...],NN,preferred_element_type=f32).astype(bf16)
    dc=lax.dot_general(k_sc[...],ds_sc[...],NT,preferred_element_type=f32)
    half=256
    tpos=turn16(pos)
    parts=[];drs=[]
    for c0 in range(0,nq,half):
        v0=nk-2*c0-2*half
        g=dg_sc[c0:c0+half,v0:v0+nk+2*half]
        parts.append(lax.dot_general(r_ref[:,v0:v0+nk+2*half],g,NT,preferred_element_type=f32))
        drs.append(lax.dot_general(tpos[:,c0:c0+half],g,NN,preferred_element_type=f32))
    dpos=turn(jnp.concatenate(parts,axis=1))*0.125
    z=jnp.zeros((DH,2*half),f32)
    dr=jnp.concatenate([z,drs[0]],axis=1)+jnp.concatenate([drs[1],z],axis=1)
    if first is None:
        dr_ref[...]=dr
    else:
        dr_ref[...]=first[0][...]+dr
    dcontent=dc[:DH]*0.125
    seg=dc[DH:]*0.125
    rows=lax.broadcasted_iota(jnp.int32,(AUG,nq),0)
    g1=jnp.sum(jnp.where(segq_ref[...]==rows,seg,0.0),axis=0,keepdims=True)
    g0=jnp.sum(seg,axis=0,keepdims=True)-g1
    dtyped=sm[:,3:4]*g0+sm[:,4:5]*g1
    dq_ref[...]=(dcontent+dpos+dtyped).astype(bf16)
    lane=lax.broadcasted_iota(jnp.int32,(DH,128),1)
    total=jnp.zeros((DH,128),f32)
    for n,val in enumerate((dcontent,dpos,dtyped,typed*g0,typed*g1)):
        total=jnp.where(lane==n,jnp.sum(val,axis=1,keepdims=True),total)
    if first is None:
        sg_ref[...]=total
    else:
        sg_ref[...]=first[1][...]+total

def bwd_kernel_first(*refs,tq,skip):
    bwd_kernel(*refs[:10],*refs[10+skip:],tq=tq,first=None)
def bwd_kernel_next(*refs,tq,skip):
    bwd_kernel(*refs[:10],*refs[12+skip:],tq=tq,first=refs[10:12])

def attn_bwd(which,qT,kT,vT,relT,small,segq,segk,probs,mixedT,dmixedT,carry=None,tq=256,heads=None,base=None):
    hd,nq=qT.shape; nk=kT.shape[1]
    start,count=heads or (0,hd//DH)
    row=lambda n: pl.BlockSpec((DH,n),lambda h:(h+start if start else h,0))
    ins=[row(nq),row(nk),row(nk),row(2*nk),row(small.shape[1]),pl.BlockSpec((None,1,nq),lambda h:(which,0,0)),pl.BlockSpec((None,1,nk),lambda h:(which,0,0)),
         pl.BlockSpec((None,nq,nk),lambda h:(h+start if start else h,0,0)),row(nq),row(nq)]
    args=[qT,kT,vT,relT,small,segq,segk,probs,mixedT,dmixedT]
    kern=bwd_kernel_first
    if carry is not None:
        ins+= [row(2*nk),row(128)]; args+=list(carry); kern=bwd_kernel_next
    aliases={}
    if base is not None:
        aliases={len(args)+n:n for n in range(5)}
        ins+=[pl.BlockSpec(memory_space=pl.ANY)]*5; args+=list(base)
    return pl.pallas_call(partial(kern,tq=tq,skip=len(aliases)),grid=(count,),in_specs=ins,
        out_specs=[row(nq),row(nk),row(nk),row(2*nk),row(128)],
        out_shape=[jax.ShapeDtypeStruct((hd,nq),bf16),jax.ShapeDtypeStruct((hd,nk),bf16),jax.ShapeDtypeStruct((hd,nk),bf16),
           jax.ShapeDtypeStruct((hd,2*nk),f32),jax.ShapeDtypeStruct((hd,128),f32)],
        input_output_aliases=aliases,
        scratch_shapes=[pltpu.VMEM((DH+AUG,nk),bf16),pltpu.VMEM((DH+AUG,nk),bf16),pltpu.VMEM((DH+AUG,nq),bf16),pltpu.VMEM((nq,nk),bf16),pltpu.VMEM((nq,2*nk),bf16)],
        name="attend_back",**limits((15*count//6)<<20))(*args)


PARTS = 4
LATE = 5


def pair_matrix(count, axis):
    shape = (count, 2 * count) if axis == 1 else (2 * count, count)
    longer = lax.broadcasted_iota(jnp.int32, shape, axis)
    shorter = lax.broadcasted_iota(jnp.int32, shape, 1 - axis)
    return jnp.where(jnp.right_shift(longer, 1) == shorter, 0.5, 0.0).astype(bf16)


def spot(place_ref, core, column, line):
    return (
        4 * jnp.bitwise_xor(place_ref[0], line)
        + 2 * jnp.bitwise_xor(place_ref[1], column)
        + jnp.bitwise_xor(place_ref[2], core)
    )


def project_kernel(
    place_ref, near0_ref, near1_ref, far0_ref, far1_ref, own_ref, peer_ref, phase_ref,
    own_q, own_k, own_v, peer_q, peer_k, peer_v, rel_ref, pooled_ref, own_low, peer_low, weights_ref,
    turned_sc,
):
    @pl.when(pl.program_id(0) == 0)
    def _():
        for i in range(PARTS):
            for n, ref in enumerate((near0_ref, near1_ref, far0_ref, far1_ref)):
                for d in range(ref.shape[0]):
                    weights_ref[i, spot(place_ref, n // 2, n % 2, d)] = ref[d, i]
            turned_sc[i] = weights_ref[i].reshape(-1, near0_ref.shape[3]).T

    pairs = pair_matrix(own_ref.shape[0] // 2, 1)

    def sequence(rows_ref, q_ref, k_ref, v_ref, low_ref, keep_ref):
        rows = rows_ref[...]
        pooled = jnp.dot(pairs, rows, preferred_element_type=f32)
        low = pooled.astype(bf16)
        low_ref[...] = low
        if keep_ref is not None:
            keep_ref[...] = pooled
        for i, (source, target) in enumerate(((low, q_ref), (rows, k_ref), (rows, v_ref))):
            target[...] = lax.dot_general(turned_sc[i], source, NT, preferred_element_type=f32).astype(bf16)

    sequence(own_ref, own_q, own_k, own_v, own_low, pooled_ref)
    sequence(peer_ref, peer_q, peer_k, peer_v, peer_low, None)
    rel_ref[...] = lax.dot_general(turned_sc[3], phase_ref[...], NT, preferred_element_type=f32).astype(bf16)


def whole(array):
    return pl.BlockSpec(array.shape, lambda *step: (0,) * array.ndim, pipeline_mode=pl.Buffered(1))


def out(shape, dtype):
    return jax.ShapeDtypeStruct(shape, dtype)


def limits(moved):
    return dict(
        compiler_params=pltpu.CompilerParams(vmem_limit_bytes=56 << 20),
        cost_estimate=pl.CostEstimate(flops=moved, bytes_accessed=moved, transcendentals=0),
    )


def project(place, stacks, tokens, peer_tokens, phase, steps=4):
    length, model = tokens.shape
    half = length // 2
    count, _, depth, width = stacks[0].shape
    ins = [*stacks, tokens, peer_tokens, phase]
    outs = [
        out((width, half), bf16), out((width, length), bf16), out((width, length), bf16),
        out((width, half), bf16), out((width, length), bf16), out((width, length), bf16),
        out((width, 2 * length), bf16), out((half, model), f32), out((half, model), bf16), out((half, model), bf16),
        out((PARTS, 4 * count, depth, width), bf16),
    ]
    def rows(array):
        return pl.BlockSpec((array.shape[0] // steps, array.shape[1]), lambda s: (s, 0))

    def columns(array):
        return pl.BlockSpec((array.shape[0], array.shape[1] // steps), lambda s: (0, s))

    return pl.pallas_call(
        project_kernel,
        grid=(steps,),
        in_specs=[pl.BlockSpec(memory_space=pltpu.SMEM)] + [whole(a) for a in stacks] + [rows(a) for a in ins[4:]],
        out_specs=[columns(a) for a in outs[:7]] + [rows(a) for a in outs[7:10]] + [whole(outs[10])],
        out_shape=outs,
        scratch_shapes=[pltpu.VMEM((PARTS, width, model), bf16)],
        name="project",
        **limits(10 << 20),
    )(place, *ins)


def weigh_kernel(
    place_ref, own_rows, peer_rows, own_low, peer_low, phase_ref, own_dq, own_dk, own_dv, peer_dq, peer_dk, peer_dv,
    drel_ref, own_dc, sent_dc, late_ref, early_ref, keep_ref, send_ref, total_sc, value_sc, small_sc,
):
    step = pl.program_id(0)

    @pl.when(step == 0)
    def _():
        total_sc[...] = jnp.zeros_like(total_sc)

    for i, pairs in enumerate((
        ((own_dq, own_low), (peer_dq, peer_low)),
        ((own_dk, own_rows), (peer_dk, peer_rows)),
        ((own_dv, own_rows), (peer_dv, peer_rows)),
        ((drel_ref, phase_ref),),
    )):
        for grad, rows in pairs:
            total_sc[i] += jnp.dot(grad[...].astype(bf16), rows[...], preferred_element_type=f32)

    @pl.when(step == pl.num_programs(0) - 1)
    def _():
        columns, lines, _, width = keep_ref.shape
        depth = value_sc.shape[1]
        for i in range(PARTS + 1):
            if i < PARTS:
                value_sc[...] = total_sc[i].astype(bf16).T.reshape(value_sc.shape)
            else:
                value_sc[...] = (own_dc[...].astype(f32) + sent_dc[...].astype(f32)).astype(bf16)
            for core, ref in enumerate((keep_ref, send_ref)):
                for column in range(columns):
                    for line in range(lines):
                        ref[column, line, i * depth:(i + 1) * depth] = value_sc[spot(place_ref, core, column, line)]
        first, last = LATE, LATE + early_ref.shape[0]
        small_sc[...] = jnp.zeros_like(small_sc)
        small_sc[:first] = late_ref[...].T[:first]
        small_sc[first:last] = early_ref[:, :width]
        small_sc[last : 2 * last - first] = early_ref[:, width:]
        small = small_sc[...].astype(bf16)
        for column in range(columns):
            for line in range(lines):
                for ref in (keep_ref, send_ref):
                    ref[column, line, (PARTS + 1) * depth:] = small


def weigh(place, own_rows, peer_rows, own_low, peer_low, phase, own_grads, peer_grads, drel, own_dc, sent_dc, late, early, blocks, steps=4):
    model = own_rows.shape[1]
    depth = model // blocks
    width = drel.shape[0]
    extra = LATE + 2 * early.shape[0]
    extra += -extra % 16

    def rows(array):
        return pl.BlockSpec((array.shape[0] // steps, model), lambda s: (s, 0))

    def columns(array):
        return pl.BlockSpec((width, array.shape[1] // steps), lambda s: (0, s))

    ins = [own_rows, peer_rows, own_low, peer_low, phase]
    grads = [*own_grads, *peer_grads, drel]
    pieces = out((2, blocks // 4, (PARTS + 1) * depth + extra, width), bf16)
    return pl.pallas_call(
        weigh_kernel,
        grid=(steps,),
        in_specs=[pl.BlockSpec(memory_space=pltpu.SMEM)] + [rows(a) for a in ins] + [columns(a) for a in grads] + [whole(a) for a in (own_dc, sent_dc, late, early)],
        out_specs=[whole(pieces)] * 2,
        out_shape=[pieces] * 2,
        scratch_shapes=[pltpu.VMEM((PARTS, width, model), f32), pltpu.VMEM((blocks, depth, width), bf16), pltpu.VMEM((extra, width), f32)],
        name="weigh",
        **limits(8 << 20),
    )(place, *ins, *grads, own_dc, sent_dc, late, early)


def token_total(dq_ref, dk_ref, dv_ref, w_ref):
    model = w_ref.shape[1] * w_ref.shape[2]
    width = dk_ref.shape[0]
    doubled = jnp.dot(dq_ref[...], pair_matrix(dq_ref.shape[1], 1), preferred_element_type=f32).astype(bf16)
    total = None
    for i, grad in enumerate((doubled, dk_ref[...], dv_ref[...])):
        term = lax.dot_general(grad.T, w_ref[i].reshape(model, width), NT, preferred_element_type=f32)
        total = term if total is None else total + term
    return total


def peer_token_kernel(dq_ref, dk_ref, dv_ref, w_ref, first_ref, second_ref):
    total = token_total(dq_ref, dk_ref, dv_ref, w_ref).astype(bf16)
    half = first_ref.shape[0]
    first_ref[...] = total[:half]
    second_ref[...] = total[half:]


def own_token_kernel(dq_ref, dk_ref, dv_ref, w_ref, pooled_ref, sent_ref, out_ref):
    total = token_total(dq_ref, dk_ref, dv_ref, w_ref)
    high = pooled_ref[...].astype(bf16)
    low = (pooled_ref[...] - high.astype(f32)).astype(bf16)
    half = sent_ref.shape[0]
    pairs = pair_matrix(dq_ref.shape[1], 0)
    total = total + jnp.dot(pairs, high, preferred_element_type=f32) + jnp.dot(pairs, low, preferred_element_type=f32)
    out_ref[:half] = total[:half] + sent_ref[...].astype(f32)
    out_ref[half:] = total[half:]


def token_grad(grads, weights, *extra):
    length = grads[1].shape[1]
    model = weights.shape[1] * weights.shape[2]
    ins = [*grads, weights, *extra]
    outs = [out((length, model), f32)] if extra else [out((length // 2, model), bf16)] * 2
    result = pl.pallas_call(
        own_token_kernel if extra else peer_token_kernel,
        grid=(1,),
        in_specs=[whole(a) for a in ins],
        out_specs=[whole(a) for a in outs],
        out_shape=outs,
        name="token_grad",
        **limits(1 << 18),
    )(*ins)
    return result[0] if extra else result


def finish_kernel(place_ref, *refs, sources):
    total = refs[0][...].astype(f32)
    for ref in refs[1:sources]:
        total = total + ref[...].astype(f32)
    grads_ref, combiner_ref, offsets_ref, sameness_ref, bias_ref, *vectors, total_sc = refs[sources:]
    parts, depth, width = grads_ref.shape
    for i in range(parts):
        grads_ref[i] = total[i * depth : (i + 1) * depth]
    combiner_ref[...] = total[parts * depth : (parts + 1) * depth]
    total_sc[...] = total[(parts + 1) * depth :]
    offsets_ref[...] = total_sc[:3]
    sameness_ref[...] = total_sc[3:LATE]
    count = len(vectors) + 4

    def row(n):
        return jnp.concatenate(
            [total_sc[LATE + n : LATE + n + 1], total_sc[LATE + count + n : LATE + count + n + 1]], axis=1
        )

    for n, ref in enumerate(vectors):
        ref[...] = row(n).reshape(ref.shape)
    n = len(vectors)
    first = place_ref[3] == 0
    bias = jnp.concatenate(
        [jnp.where(first, row(n), row(n + 2)), jnp.where(first, row(n + 1), row(n + 3))], axis=1
    )
    bias_ref[...] = bias.reshape(bias_ref.shape)


def finish(place, pieces, depth, model, hidden):
    extra = pieces[0].shape[0] - (PARTS + 1) * depth
    width = pieces[0].shape[1]
    outs = [
        out((PARTS, depth, width), f32), out((depth, width), f32), out((3, width), f32), out((2, width), f32), out((hidden,), f32),
    ] + [out((model,), f32)] * 6
    return pl.pallas_call(
        partial(finish_kernel, sources=len(pieces)),
        grid=(1,),
        in_specs=[pl.BlockSpec(memory_space=pltpu.SMEM)] + [whole(a) for a in pieces],
        out_specs=[whole(a) for a in outs],
        out_shape=outs,
        scratch_shapes=[pltpu.VMEM((extra, width), f32)],
        name="finish",
        **limits(1 << 20),
    )(place, *pieces)


SPLIT = 1


def layer_norm(values_in):
    row_mean = jnp.mean(values_in, axis=1, keepdims=True)
    centred = values_in - row_mean
    variance = jnp.mean(centred * centred, axis=1, keepdims=True)
    scale = lax.rsqrt(variance + epsilon)
    return centred * scale, scale


def layer_norm_back(grad, normed, scale, gain):
    inner = grad * gain
    return scale * (
        inner
        - jnp.mean(inner, axis=1, keepdims=True)
        - normed * jnp.mean(inner * normed, axis=1, keepdims=True)
    )


def row_sum(values_in):
    return jnp.sum(values_in, axis=0, keepdims=True)


def middle_kernel(
    place_ref, pooled_ref, mixed_ref, sent_ref, vec_ref, cot_ref, own_c_ref, peer_c_ref, weights_ref, own_bias_ref, peer_bias_ref,
    result_ref, dfirst_ref, own_dm_ref, peer_dm_ref, own_dc_ref, peer_dc_ref, sums_ref,
    keep_w_ref, send_w_ref, keep_n_ref, send_n_ref,
    held_sc, held_sem, slope_sc, act_sc, dhid_sc, first_sc, norm_sc, scale_sc, total_sc, low_sc, low_t_sc, dsec_sc, dsec_t_sc,
    *, chunks,
):
    step = pl.program_id(0)
    model = pooled_ref.shape[1]
    rows = pooled_ref.shape[0]
    part = own_bias_ref.shape[-1]
    each = own_bias_ref.shape[0]

    def fetch(chunk, kind):
        return pltpu.make_async_copy(
            weights_ref.at[:, chunk // each, :, pl.ds((kind * each + chunk % each) * part, part)],
            held_sc.at[chunk, kind],
            held_sem.at[chunk, kind],
        )
    vec = vec_ref[...]

    def store(value, keep_ref, send_ref):
        value = value.astype(bf16)
        for n, ref in enumerate((keep_ref, send_ref)):
            piece = value[n * (model // 2) : (n + 1) * (model // 2)]
            ref[...] = piece.reshape(ref.shape)

    def turn_rows(value, ref):
        value = value.T.reshape(ref.shape)
        count = ref.shape[0]
        for n in range(count):
            line, column, core = n // 4, n // 2 % 2, n % 2
            ref[
                (count // 2) * jnp.bitwise_xor(place_ref[2], core)
                + (count // 4) * jnp.bitwise_xor(place_ref[1], column)
                + jnp.bitwise_xor(place_ref[0], line)
            ] = value[n]

    postbias, scaling, centring = vec[0:1], vec[1:2], vec[2:3]
    narrowbias, rescale, recentre = vec[3:4], vec[4:5], vec[5:6]

    @pl.when(step == 0)
    def _():
        for chunk in range(chunks):
            for kind in range(2):
                fetch(chunk, kind).start()
        own_c = own_c_ref[...].reshape(model, -1)
        peer_c = peer_c_ref[...].reshape(model, -1)
        mixed = mixed_ref[...].astype(bf16).T
        sent = sent_ref[...].T
        branch = (
            lax.dot_general(mixed, own_c, NT, preferred_element_type=f32)
            + lax.dot_general(sent, peer_c, NT, preferred_element_type=f32)
            + postbias
        )
        normed, scale = layer_norm(pooled_ref[...] + branch)
        norm_sc[...] = normed
        scale_sc[...] = scale
        first = normed * scaling + centring
        first_sc[...] = first
        low = first.astype(bf16)
        low_sc[...] = low
        turn_rows(low, low_t_sc)
        total_sc[...] = jnp.zeros_like(total_sc)

    for chunk in range(chunks):

        @pl.when(step == chunk)
        def _():
            for kind in range(2):
                fetch(chunk, kind).wait()

    @pl.when(step < chunks)
    def _():
        wide = held_sc[step, 0].reshape(model, part)
        spot_bias = lax.rem(step, each)
        bias = jnp.where(step // each == place_ref[3], own_bias_ref[spot_bias], peer_bias_ref[spot_bias])
        hidden = jnp.dot(low_sc[...], wide, preferred_element_type=f32) + bias
        square = hidden * hidden
        root = math.sqrt(2.0 / math.pi)
        turn = jnp.tanh(hidden * (root + (root * 0.044715) * square))
        half = 0.5 * turn + 0.5
        act = (hidden * half).astype(bf16)
        slope_sc[step] = half + hidden * (half * (1.0 - turn)) * (root + (3.0 * root * 0.044715) * square)
        act_sc[step] = act
        narrow = held_sc[step, 1].reshape(model, part)
        total_sc[...] += lax.dot_general(act, narrow, NT, preferred_element_type=f32)

    @pl.when(step == chunks - 1)
    def _():
        normed, scale = layer_norm(first_sc[...] + (total_sc[...] + narrowbias))
        result_ref[...] = (normed * rescale + recentre).astype(bf16)
        cot = cot_ref[...].astype(f32)
        dfinal = layer_norm_back(cot, normed, scale, rescale)
        dsec = dfinal.astype(bf16)
        dsec_sc[...] = dsec
        turn_rows(dsec, dsec_t_sc)
        sums_ref[3:4] = row_sum(dsec.astype(f32))
        sums_ref[4:5] = row_sum(cot * normed)
        sums_ref[5:6] = row_sum(cot)
        total_sc[...] = dfinal

    back = step - chunks

    @pl.when((back >= 0) & (lax.rem(back, 2) == 0))
    def _():
        chunk = back // 2
        narrow = held_sc[chunk, 1].reshape(model, part)
        dact = jnp.dot(dsec_sc[...], narrow, preferred_element_type=f32)
        dhid = (dact * slope_sc[chunk]).astype(bf16)
        dhid_sc[...] = dhid
        bias_sum = row_sum(dhid.astype(f32))
        for n in range(part // model):
            sums_ref[pl.ds(6 + chunk * (part // model) + n, 1)] = bias_sum[:, n * model : (n + 1) * model]
        grad = jnp.dot(dsec_t_sc[...].reshape(model, rows), act_sc[chunk], preferred_element_type=f32)
        store(grad, keep_n_ref, send_n_ref)

    @pl.when((back >= 0) & (lax.rem(back, 2) == 1))
    def _():
        wide = held_sc[back // 2, 0].reshape(model, part)
        total_sc[...] += lax.dot_general(dhid_sc[...], wide, NT, preferred_element_type=f32)
        grad = jnp.dot(low_t_sc[...].reshape(model, rows), dhid_sc[...], preferred_element_type=f32)
        store(grad, keep_w_ref, send_w_ref)

    @pl.when(back == 2 * chunks - 1)
    def _():
        dfirst = total_sc[...]
        normed = norm_sc[...]
        dfirst_in = layer_norm_back(dfirst, normed, scale_sc[...], scaling)
        dfirst_ref[...] = dfirst_in
        dbranch = dfirst_in.astype(bf16)
        sums_ref[0:1] = row_sum(dbranch.astype(f32))
        sums_ref[1:2] = row_sum(dfirst * normed)
        sums_ref[2:3] = row_sum(dfirst)
        dbranch_t = dbranch.T
        for c_ref, m_ref, dm_ref, dc_ref in (
            (own_c_ref, mixed_ref, own_dm_ref, own_dc_ref),
            (peer_c_ref, sent_ref, peer_dm_ref, peer_dc_ref),
        ):
            c = c_ref[...].reshape(model, -1)
            dm_ref[...] = lax.dot_general(c, dbranch_t, TN, preferred_element_type=f32).astype(bf16)
            dc = lax.dot_general(dbranch_t, m_ref[...].astype(bf16), NT, preferred_element_type=f32)
            dc_ref[...] = dc.astype(bf16).reshape(dc_ref.shape)


def middle(place, pooled, mixed, sent, vec, cot, weights, own_bias, peer_bias):
    rows, model = pooled.shape
    blocks, halves, depth, columns = weights.shape
    width = mixed.shape[0]
    hidden = (columns - width) // 2
    part = hidden // SPLIT
    each = hidden // part
    chunks = halves * each

    def combiner_spec(flip):
        def index(step, place_ref):
            return (0, jnp.bitwise_xor(place_ref[3], flip), 0, 2 * hidden // width)

        return pl.BlockSpec((blocks, None, depth, width), index, pipeline_mode=pl.Buffered(1))

    def wide_index(step, place_ref):
        c = jnp.maximum(step - chunks - 1, 0) // 2
        return (jnp.bitwise_xor(c // each, place_ref[3]), 0, 0, 0, lax.rem(c, each))

    def narrow_index(step, place_ref):
        c = jnp.maximum(step - chunks, 0) // 2
        return (0, jnp.bitwise_xor(c // each, place_ref[3]), 0, 0, lax.rem(c, each))

    lines = blocks // 4
    outs = [
        out((rows, model), bf16), out((rows, model), f32), out(mixed.shape, bf16), out(mixed.shape, bf16),
        out((blocks, depth, width), bf16), out((blocks, depth, width), bf16), out((6 + halves * hidden // model, model), f32),
    ]
    wide_grads = out((halves, 2, lines, depth, hidden), bf16)
    narrow_grads = out((2, halves, lines, depth, hidden), bf16)
    whole_ins = [pooled, mixed, sent, vec, cot]
    grad_spec = [pl.BlockSpec((1, 2, lines, depth, part), wide_index)] * 2
    grad_spec += [pl.BlockSpec((2, 1, lines, depth, part), narrow_index)] * 2
    return pl.pallas_call(
        partial(middle_kernel, chunks=chunks),
        grid_spec=pltpu.PrefetchScalarGridSpec(
            num_scalar_prefetch=1,
            grid=(3 * chunks,),
            in_specs=[whole(a) for a in whole_ins]
            + [combiner_spec(0), combiner_spec(1), pl.BlockSpec(memory_space=pl.ANY)]
            + [pl.BlockSpec((each, 1, part), lambda s, p: (0, 0, 0))] * 2,
            out_specs=[whole(a) for a in outs]
            + grad_spec,
            scratch_shapes=[
                pltpu.VMEM((chunks, 2, blocks, depth, part), bf16),
                pltpu.SemaphoreType.DMA((chunks, 2)),
                pltpu.VMEM((chunks, rows, part), f32),
                pltpu.VMEM((chunks, rows, part), bf16),
                pltpu.VMEM((rows, part), bf16),
                pltpu.VMEM((rows, model), f32),
                pltpu.VMEM((rows, model), f32),
                pltpu.VMEM((rows, 1), f32),
                pltpu.VMEM((rows, model), f32),
                pltpu.VMEM((rows, model), bf16),
                pltpu.VMEM((blocks, depth, rows), bf16),
                pltpu.VMEM((rows, model), bf16),
                pltpu.VMEM((blocks, depth, rows), bf16),
            ],
        ),
        out_shape=outs + [wide_grads] * 2 + [narrow_grads] * 2,
        name="middle",
        **limits(24 << 20),
    )(place, *whole_ins, weights, weights, weights, own_bias.reshape(each, 1, part), peer_bias.reshape(each, 1, part))


def position_table(length, model_width):
    row_index = jnp.arange(2 * length, dtype=jnp.float32)
    offset = length - row_index
    half_width = model_width // 2
    frequency = jnp.exp(
        jnp.arange(half_width, dtype=jnp.float32) * (-math.log(10000.0) / half_width)
    )
    angles = offset[:, None] * frequency[None, :]
    return jnp.concatenate([jnp.sin(angles), jnp.cos(angles)], axis=1)


BLOCKS = 16


def swap(piece):
    return lax.ppermute(piece, "tensor", [(0, 1), (1, 0)])


def late_tokens(piece):
    return jnp.concatenate([jnp.zeros(piece.shape, f32), piece.astype(f32)], axis=0)


def exchange(piece, mask):
    count = lax.axis_size("dp")
    return lax.ppermute(piece, "dp", [(i, i ^ mask) for i in range(count)])


def shards(
    tokens,
    segments,
    projections,
    combiner,
    offsets,
    sameness,
    postbias,
    scaling,
    centring,
    widener,
    widebias,
    narrower,
    narrowbias,
    rescale,
    recentre,
    cotangent,
):
    tensor_part = lax.axis_index("tensor")
    dp_part = lax.axis_index("dp")
    dp_count = lax.axis_size("dp")
    length, model = tokens.shape
    width = offsets.shape[1]
    hidden = widener.shape[1]
    blocks = BLOCKS
    depth = model // blocks
    direct = dp_count == blocks
    if direct:
        place = jnp.stack([dp_part // 4, (dp_part // 2) % 2, dp_part % 2, tensor_part]).astype(jnp.int32)
    else:
        place = jnp.stack([tensor_part * 0] * 3 + [tensor_part]).astype(jnp.int32)

    mine = jnp.concatenate([widener, narrower.T, combiner.T], axis=1)
    mine, projections = lax.optimization_barrier((mine, projections))
    phase = position_table(length, model).astype(bf16)
    if direct:
        near0 = jnp.stack([projections] + [exchange(projections, 4 * d) for d in range(1, 4)])
        near0, phase = lax.optimization_barrier((near0, phase))
        near1 = exchange(near0, 2)
        stacks = (near0, near1, exchange(near0, 1), exchange(near1, 1))
    else:
        every = lax.all_gather(projections, "dp", axis=1, tiled=True)
        every = every.reshape(PARTS, blocks // 4, 2, 2, depth, width).transpose(3, 2, 1, 0, 4, 5)
        stacks = (every[0, 0], every[0, 1], every[1, 0], every[1, 1])
    peer_tokens = swap(tokens)
    columns = mine.shape[1]
    weights = lax.all_gather(mine, ("dp", "tensor"), axis=0, tiled=False)
    if not direct:
        weights = weights.reshape(dp_count, 2, model // dp_count, columns).transpose(1, 0, 2, 3)
        weights = weights.reshape(2, blocks, depth, columns).transpose(1, 0, 2, 3)
    weights = weights.reshape(blocks, 2, depth, columns)
    small = jnp.concatenate([offsets, sameness], axis=0).T
    seg = jnp.where(tensor_part == 0, segments, jnp.concatenate([segments[1:], segments[:1]]))[:, None]
    vec = jnp.stack([postbias, scaling, centring, narrowbias, rescale, recentre, postbias, postbias])
    peer_tokens, peer_bias, small, seg, seg_q, vec = lax.optimization_barrier(
        (peer_tokens, swap(widebias), small, seg, seg[:, :, ::2], vec)
    )
    own_q, own_k, own_v, peer_q, peer_k, peer_v, relative, pooled, own_low, peer_low, inwards = project(
        place, stacks, tokens, peer_tokens, phase
    )
    own_args = (own_q, own_k, own_v, relative, small, seg_q, seg)
    peer_args = (peer_q, peer_k, peer_v, relative, small, seg_q, seg)
    peer_probs, peer_mixed, peer_mixed_low = attn_fwd(*peer_args, 1)
    sent_mixed = swap(peer_mixed_low)
    own_probs, own_mixed, own_mixed_low = attn_fwd(*own_args, 0)
    result, dfirst_in, own_dmixed, peer_dmixed, own_dc, peer_dc, early, keep_w, send_w, keep_n, send_n = middle(
        place, pooled, own_mixed_low, sent_mixed, vec, cotangent, weights, widebias, peer_bias
    )
    sent_dmixed = swap(peer_dmixed)
    half = width // DH // 2
    part = attn_bwd(0, *own_args, own_probs, own_mixed, own_dmixed, heads=(0, half))
    early = early + swap(early)
    if direct:

        def add(kept, sent):
            return (kept.astype(f32) + sent.astype(f32)).astype(bf16)

        wide = (keep_w, exchange(send_w, 1))
        narrow = (keep_n, exchange(send_n, 1))
        first_stage = (
            add(wide[0][0], wide[1][0]),
            add(wide[0][1], wide[1][1]),
            add(narrow[0][0], narrow[1][0]),
            add(narrow[0][1], narrow[1][1]),
        )
        part, early, first_stage, sent_dmixed = lax.optimization_barrier((part, early, first_stage, sent_dmixed))

    own_dq, own_dk, own_dv, drel, late = attn_bwd(
        0, *own_args, own_probs, own_mixed, own_dmixed, heads=(half, width // DH - half), base=part
    )
    drel, late, peer_dc = lax.optimization_barrier((drel, late, peer_dc))
    sent_dc = swap(peer_dc)
    peer_dq, peer_dk, peer_dv, drel, late = attn_bwd(
        1, *peer_args, peer_probs, peer_mixed, sent_dmixed, (drel, late)
    )
    own_grads = (own_dq, own_dk, own_dv)
    peer_grads = (peer_dq, peer_dk, peer_dv)
    if direct:
        wide = (first_stage[0], swap(first_stage[1]))
        narrow = (first_stage[2], exchange(first_stage[3], 2))
        wide = (add(wide[0][0], wide[1][0]), add(wide[0][1], wide[1][1]))
        narrow = (add(narrow[0][0], narrow[1][0]), add(narrow[0][1], narrow[1][1]))
        drel, peer_grads, wide, narrow = lax.optimization_barrier((drel, peer_grads, wide, narrow))
        wide = (wide[0], exchange(wide[1], 2))
        narrow = (narrow[0], swap(narrow[1]))
    peer_part = token_grad(peer_grads, inwards)
    sent_first = swap(peer_part[0])
    drel, _ = lax.optimization_barrier((drel, peer_part))
    keep, send = weigh(
        place, tokens, peer_tokens, own_low, peer_low, phase, own_grads, peer_grads, drel, own_dc, sent_dc, late, early, blocks
    )
    if direct:
        keep, send, wide, narrow = lax.optimization_barrier((keep, send, wide, narrow))
        sent = exchange(send, 1)
        held = (add(keep[0], sent[0]), add(keep[1], sent[1]))
        last = [
            jnp.concatenate([add(wide[0][d], wide[1][d]), add(narrow[0][d], narrow[1][d])], axis=-1)
            for d in range(4)
        ]
        own_grads, held, last = lax.optimization_barrier((own_grads, held, last))
        held = (held[0], exchange(held[1], 2))
    last_part, sent_first = lax.optimization_barrier((peer_part[1], sent_first))
    sent_last = swap(last_part)
    own_part = token_grad(own_grads, inwards, dfirst_in, sent_first)
    if direct:
        grads = last[0].astype(f32)
        for d in range(1, 4):
            grads = grads + exchange(last[d], 4 * d).astype(f32)
        held = [add(held[0][d], held[1][d]) for d in range(4)]
        own_part, held = lax.optimization_barrier((own_part, held))
        pieces = [held[0]] + [exchange(held[d], 4 * d) for d in range(1, 4)]
        tokens_grad, pieces = lax.optimization_barrier((own_part + late_tokens(sent_last), pieces))
    else:

        def ordered(kept, sent, turned):
            value = jnp.stack([kept, sent])
            value = value.transpose((3, 1, 0, 2, 4, 5) if turned else (3, 2, 0, 1, 4, 5))
            value = jnp.where(tensor_part == 0, value, value[:, :, :, ::-1])
            return value.transpose(3, 0, 1, 2, 4, 5).reshape(2, dp_count, model // dp_count, -1)

        grads = jnp.concatenate([ordered(keep_w, send_w, False), ordered(keep_n, send_n, True)], axis=-1)
        grads = lax.psum_scatter(
            grads.transpose(1, 0, 2, 3).reshape(2 * dp_count, model // dp_count, 2 * hidden),
            ("dp", "tensor"),
            scatter_dimension=0,
            tiled=True,
        )[0].astype(f32)
        big = jnp.stack([keep, send])[:, :, :, : (PARTS + 1) * depth]
        big = big.reshape(2, 2, blocks // 4, PARTS + 1, depth, width).transpose(3, 2, 1, 0, 4, 5)
        big = lax.psum_scatter(big.reshape(PARTS + 1, model, width), "dp", scatter_dimension=1, tiled=True)
        extras = lax.psum(keep[0, 0, (PARTS + 1) * depth :].astype(f32), "dp").astype(bf16)
        pieces = [jnp.concatenate([big.reshape(-1, width), extras], axis=0)]
        tokens_grad = own_part + late_tokens(sent_last)
    projections_grad, combiner_grad, offsets_grad, sameness_grad, bias_grad, *vectors = finish(
        place, pieces, depth if direct else model // dp_count, model, hidden
    )
    return (
        result,
        tokens_grad,
        projections_grad,
        combiner_grad.T,
        offsets_grad,
        sameness_grad,
        vectors[0],
        vectors[1],
        vectors[2],
        grads[:, :hidden],
        bias_grad,
        grads[:, hidden:].T,
        vectors[3],
        vectors[4],
        vectors[5],
    )


def solution(mesh):
    placed = (
        P(("dp", "tensor"), None),
        P("dp", None),
        P(None, "dp", "tensor"),
        P("tensor", "dp"),
        P(None, "tensor"),
        P(None, "tensor"),
        P(),
        P(),
        P(),
        P("dp", "tensor"),
        P("tensor"),
        P("tensor", "dp"),
        P(),
        P(),
        P(),
        P(("dp", "tensor"), None),
    )
    return jax.shard_map(
        shards,
        mesh=mesh,
        in_specs=placed,
        out_specs=(
            P(("dp", "tensor"), None),
            P(("dp", "tensor"), None),
            P(None, "dp", "tensor"),
            P("tensor", "dp"),
            P(None, "tensor"),
            P(None, "tensor"),
            P(),
            P(),
            P(),
            P("dp", "tensor"),
            P("tensor"),
            P("tensor", "dp"),
            P(),
            P(),
            P(),
        ),
        check_vma=False,
    )
```

```python
from functools import partial
import math

import jax
import jax.numpy as jnp
from jax import lax
from jax.experimental import pallas as pl
from jax.experimental.pallas import tpu as pltpu
from jax.sharding import PartitionSpec as P

epsilon = 1e-05
bf16=jnp.bfloat16; f32=jnp.float32
DH=64
AUG=16
TN=(((0,),(0,)),((),()))
NT=(((1,),(1,)),((),()))
NN=(((1,),(0,)),((),()))

def split3(u):
    row=lax.broadcasted_iota(jnp.int32,u.shape,0)
    hi=u.astype(bf16).astype(f32)
    r1=u-hi
    mid=r1.astype(bf16).astype(f32)
    lo=r1-mid
    return jnp.where(row<3,hi,jnp.where(row<6,mid,jnp.where(row<9,lo,0.0))).astype(bf16)

def fwd_kernel(q_ref,k_ref,v_ref,r_ref,s_ref,segq_ref,segk_ref,p_ref,m_ref,ml_ref,c_sc,k_sc,*,tq):
    nq=q_ref.shape[1]; nk=k_ref.shape[1]
    q=q_ref[...].astype(f32)
    sm=s_ref[...]
    c_sc[:DH]=(q+sm[:,0:1]).astype(bf16)*jnp.asarray(0.125,bf16)
    pos=(q+sm[:,1:2]).astype(bf16)*jnp.asarray(0.125,bf16)
    typed=q+sm[:,2:3]
    t0=jnp.sum(typed*sm[:,3:4],axis=0,keepdims=True)*0.125
    t1=jnp.sum(typed*sm[:,4:5],axis=0,keepdims=True)*0.125
    kind=lax.rem(lax.broadcasted_iota(jnp.int32,(AUG,nq),0),3)
    c_sc[DH:]=split3(jnp.where(segq_ref[...]==kind,t1,t0))
    k_sc[:DH]=k_ref[...]
    rowk=lax.broadcasted_iota(jnp.int32,(AUG,nk),0)
    k_sc[DH:]=jnp.where((segk_ref[...]==lax.rem(rowk,3)) & (rowk<9),1.0,0.0).astype(bf16)

    tr=min(tq,128)
    def dense(b):
        i0=b*tq; w0=nk-2*i0-2*tq
        return lax.dot_general(pos[:,i0:i0+tq],r_ref[:,w0:w0+nk+2*tq],TN,preferred_element_type=f32)
    def cont(b):
        i0=b*tq
        return lax.dot_general(c_sc[:,i0:i0+tq],k_sc[...],TN,preferred_element_type=f32)
    def finish(b,c,d):
        i0=b*tq
        for t in range(tq//tr):
            lo=2*(tq-(t+1)*tr)
            g=pltpu.roll(d[t*tr:(t+1)*tr,lo:lo+nk+2*tr],nk,1,stride=2,stride_axis=0)
            s=c[t*tr:(t+1)*tr]+g[:,:nk]
            mx=jnp.max(s,axis=1,keepdims=True)
            e=jnp.exp(s-mx)
            l=jnp.sum(e,axis=1,keepdims=True)
            p_ref[i0+t*tr:i0+(t+1)*tr,:]=(e*(1.0/l)).astype(bf16)
    n=nq//tq
    prev=(cont(0),dense(0))
    for b in range(n):
        nxt=(cont(b+1),dense(b+1)) if b+1<n else None
        finish(b,*prev); prev=nxt
    mixed=lax.dot_general(v_ref[...],p_ref[...],NT,preferred_element_type=f32)
    m_ref[...]=mixed
    ml_ref[...]=mixed.astype(bf16)

def attn_fwd(qT,kT,vT,relT,small,segq,segk,row=0,tq=128):
    hd,nq=qT.shape; nk=kT.shape[1]; heads=hd//DH
    return pl.pallas_call(partial(fwd_kernel,tq=tq),grid=(heads,),
        in_specs=[pl.BlockSpec((DH,nq),lambda h:(h,0)),pl.BlockSpec((DH,nk),lambda h:(h,0)),pl.BlockSpec((DH,nk),lambda h:(h,0)),
          pl.BlockSpec((DH,2*nk),lambda h:(h,0)),pl.BlockSpec((DH,small.shape[1]),lambda h:(h,0)),
          pl.BlockSpec((None,1,nq),lambda h:(row,0,0)),pl.BlockSpec((None,1,nk),lambda h:(row,0,0))],
        out_specs=[pl.BlockSpec((None,nq,nk),lambda h:(h,0,0)),pl.BlockSpec((DH,nq),lambda h:(h,0)),pl.BlockSpec((DH,nq),lambda h:(h,0))],
        out_shape=[jax.ShapeDtypeStruct((heads,nq,nk),bf16),jax.ShapeDtypeStruct((hd,nq),f32),jax.ShapeDtypeStruct((hd,nq),bf16)],
        scratch_shapes=[pltpu.VMEM((DH+AUG,nq),bf16),pltpu.VMEM((DH+AUG,nk),bf16)],
        name="attend",**limits(15<<20))(qT,kT,vT,relT,small,segq,segk)

def bwd_kernel(q_ref,k_ref,v_ref,r_ref,s_ref,segq_ref,segk_ref,p_ref,m_ref,dm_ref,
               dq_ref,dk_ref,dv_ref,dr_ref,sg_ref,k_sc,v_sc,dm_sc,ds_sc,dg_sc,*,tq,first):
    nq=q_ref.shape[1]; nk=k_ref.shape[1]
    q=q_ref[...].astype(f32)
    sm=s_ref[...]
    content=(q+sm[:,0:1]).astype(bf16)*jnp.asarray(0.125,bf16)
    pos=(q+sm[:,1:2]).astype(bf16)*jnp.asarray(0.125,bf16)
    typed=q+sm[:,2:3]
    k_sc[:DH]=k_ref[...]
    rowk=lax.broadcasted_iota(jnp.int32,(AUG,nk),0)
    k_sc[DH:]=((segk_ref[...]==rowk)).astype(f32).astype(bf16)
    v_sc[:DH]=v_ref[...]
    v_sc[DH:]=jnp.where(rowk<3,1.0,0.0).astype(bf16)
    dm=dm_ref[...]
    dm_sc[:DH]=dm
    delta=-jnp.sum(dm.astype(f32)*m_ref[...],axis=0,keepdims=True)
    rowq=lax.broadcasted_iota(jnp.int32,(AUG,nq),0)
    hi=delta.astype(bf16).astype(f32); r1=delta-hi; mid=r1.astype(bf16).astype(f32); lo=r1-mid
    dm_sc[DH:]=jnp.where(rowq==0,hi,jnp.where(rowq==1,mid,jnp.where(rowq==2,lo,0.0))).astype(bf16)
    w=nk+2*tq
    flip=(lax.broadcasted_iota(jnp.int32,(tq,tq),0)+lax.broadcasted_iota(jnp.int32,(tq,tq),1)==tq-1).astype(f32).astype(bf16)
    def turn16(x):
        parts=[lax.dot_general(x[:,i:i+tq],flip,NN,preferred_element_type=f32) for i in range(0,nq,tq)]
        return jnp.concatenate(parts,axis=1).astype(bf16)
    def turn(x):
        hi=x.astype(bf16); r1=x-hi.astype(f32); mid=r1.astype(bf16); lo=(r1-mid.astype(f32)).astype(bf16)
        cat=jnp.concatenate([hi,mid,lo],axis=0)
        parts=[lax.dot_general(cat[:,i:i+tq],flip,NN,preferred_element_type=f32) for i in range(0,nq,tq)]
        y=jnp.concatenate(parts,axis=1)
        return y[:DH]+y[DH:2*DH]+y[2*DH:]

    @pl.when(pl.program_id(0)==0)
    def _():
        dg_sc[...]=jnp.zeros_like(dg_sc)
    def grad(b):
        i0=b*tq
        return lax.dot_general(dm_sc[:,i0:i0+tq],v_sc[...],TN,preferred_element_type=f32)
    def shift(b,dp):
        i0=b*tq
        w0=nk-2*i0-2*tq
        ds16=(p_ref[i0:i0+tq,:].astype(f32)*dp).astype(bf16)
        ds_sc[i0:i0+tq,:]=ds16
        back=lax.dot_general(flip,ds16,NN,preferred_element_type=f32)
        g=jnp.concatenate([back,jnp.zeros((tq,2*tq),f32)],axis=1)
        g=pltpu.roll(g,2,1,stride=2,stride_axis=0)
        dg_sc[i0:i0+tq,w0:w0+w]=g.astype(bf16)
    n=nq//tq
    for b in range(n): shift(b,grad(b))
    dv_ref[...]=lax.dot_general(dm,p_ref[...],NN,preferred_element_type=f32).astype(bf16)
    dk_ref[...]=lax.dot_general(content,ds_sc[...],NN,preferred_element_type=f32).astype(bf16)
    dc=lax.dot_general(k_sc[...],ds_sc[...],NT,preferred_element_type=f32)
    half=256
    tpos=turn16(pos)
    parts=[];drs=[]
    for c0 in range(0,nq,half):
        v0=nk-2*c0-2*half
        g=dg_sc[c0:c0+half,v0:v0+nk+2*half]
        parts.append(lax.dot_general(r_ref[:,v0:v0+nk+2*half],g,NT,preferred_element_type=f32))
        drs.append(lax.dot_general(tpos[:,c0:c0+half],g,NN,preferred_element_type=f32))
    dpos=turn(jnp.concatenate(parts,axis=1))*0.125
    z=jnp.zeros((DH,2*half),f32)
    dr=jnp.concatenate([z,drs[0]],axis=1)+jnp.concatenate([drs[1],z],axis=1)
    if first is None:
        dr_ref[...]=dr
    else:
        dr_ref[...]=first[0][...]+dr
    dcontent=dc[:DH]*0.125
    seg=dc[DH:]*0.125
    rows=lax.broadcasted_iota(jnp.int32,(AUG,nq),0)
    g1=jnp.sum(jnp.where(segq_ref[...]==rows,seg,0.0),axis=0,keepdims=True)
    g0=jnp.sum(seg,axis=0,keepdims=True)-g1
    dtyped=sm[:,3:4]*g0+sm[:,4:5]*g1
    dq_ref[...]=(dcontent+dpos+dtyped).astype(bf16)
    lane=lax.broadcasted_iota(jnp.int32,(DH,128),1)
    total=jnp.zeros((DH,128),f32)
    for n,val in enumerate((dcontent,dpos,dtyped,typed*g0,typed*g1)):
        total=jnp.where(lane==n,jnp.sum(val,axis=1,keepdims=True),total)
    if first is None:
        sg_ref[...]=total
    else:
        sg_ref[...]=first[1][...]+total

def bwd_kernel_first(*refs,tq,skip):
    bwd_kernel(*refs[:10],*refs[10+skip:],tq=tq,first=None)
def bwd_kernel_next(*refs,tq,skip):
    bwd_kernel(*refs[:10],*refs[12+skip:],tq=tq,first=refs[10:12])

def attn_bwd(which,qT,kT,vT,relT,small,segq,segk,probs,mixedT,dmixedT,carry=None,tq=256,heads=None,base=None):
    hd,nq=qT.shape; nk=kT.shape[1]
    start,count=heads or (0,hd//DH)
    row=lambda n: pl.BlockSpec((DH,n),lambda h:(h+start if start else h,0))
    ins=[row(nq),row(nk),row(nk),row(2*nk),row(small.shape[1]),pl.BlockSpec((None,1,nq),lambda h:(which,0,0)),pl.BlockSpec((None,1,nk),lambda h:(which,0,0)),
         pl.BlockSpec((None,nq,nk),lambda h:(h+start if start else h,0,0)),row(nq),row(nq)]
    args=[qT,kT,vT,relT,small,segq,segk,probs,mixedT,dmixedT]
    kern=bwd_kernel_first
    if carry is not None:
        ins+= [row(2*nk),row(128)]; args+=list(carry); kern=bwd_kernel_next
    aliases={}
    if base is not None:
        aliases={len(args)+n:n for n in range(5)}
        ins+=[pl.BlockSpec(memory_space=pl.ANY)]*5; args+=list(base)
    return pl.pallas_call(partial(kern,tq=tq,skip=len(aliases)),grid=(count,),in_specs=ins,
        out_specs=[row(nq),row(nk),row(nk),row(2*nk),row(128)],
        out_shape=[jax.ShapeDtypeStruct((hd,nq),bf16),jax.ShapeDtypeStruct((hd,nk),bf16),jax.ShapeDtypeStruct((hd,nk),bf16),
           jax.ShapeDtypeStruct((hd,2*nk),f32),jax.ShapeDtypeStruct((hd,128),f32)],
        input_output_aliases=aliases,
        scratch_shapes=[pltpu.VMEM((DH+AUG,nk),bf16),pltpu.VMEM((DH+AUG,nk),bf16),pltpu.VMEM((DH+AUG,nq),bf16),pltpu.VMEM((nq,nk),bf16),pltpu.VMEM((nq,2*nk),bf16)],
        name="attend_back",**limits((15*count//6)<<20))(*args)


PARTS = 4
LATE = 5


def pair_matrix(count, axis):
    shape = (count, 2 * count) if axis == 1 else (2 * count, count)
    longer = lax.broadcasted_iota(jnp.int32, shape, axis)
    shorter = lax.broadcasted_iota(jnp.int32, shape, 1 - axis)
    return jnp.where(jnp.right_shift(longer, 1) == shorter, 0.5, 0.0).astype(bf16)


def spot(place_ref, core, column, line):
    return (
        4 * jnp.bitwise_xor(place_ref[0], line)
        + 2 * jnp.bitwise_xor(place_ref[1], column)
        + jnp.bitwise_xor(place_ref[2], core)
    )


def project_kernel(
    place_ref, near0_ref, near1_ref, far0_ref, far1_ref, own_ref, peer_ref, phase_ref,
    own_q, own_k, own_v, peer_q, peer_k, peer_v, rel_ref, pooled_ref, own_low, peer_low, weights_ref,
    turned_sc,
):
    @pl.when(pl.program_id(0) == 0)
    def _():
        for i in range(PARTS):
            for n, ref in enumerate((near0_ref, near1_ref, far0_ref, far1_ref)):
                for d in range(ref.shape[0]):
                    weights_ref[i, spot(place_ref, n // 2, n % 2, d)] = ref[d, i]
            turned_sc[i] = weights_ref[i].reshape(-1, near0_ref.shape[3]).T

    pairs = pair_matrix(own_ref.shape[0] // 2, 1)

    def sequence(rows_ref, q_ref, k_ref, v_ref, low_ref, keep_ref):
        rows = rows_ref[...]
        pooled = jnp.dot(pairs, rows, preferred_element_type=f32)
        low = pooled.astype(bf16)
        low_ref[...] = low
        if keep_ref is not None:
            keep_ref[...] = pooled
        for i, (source, target) in enumerate(((low, q_ref), (rows, k_ref), (rows, v_ref))):
            target[...] = lax.dot_general(turned_sc[i], source, NT, preferred_element_type=f32).astype(bf16)

    sequence(own_ref, own_q, own_k, own_v, own_low, pooled_ref)
    sequence(peer_ref, peer_q, peer_k, peer_v, peer_low, None)
    rel_ref[...] = lax.dot_general(turned_sc[3], phase_ref[...], NT, preferred_element_type=f32).astype(bf16)


def whole(array):
    return pl.BlockSpec(array.shape, lambda *step: (0,) * array.ndim, pipeline_mode=pl.Buffered(1))


def out(shape, dtype):
    return jax.ShapeDtypeStruct(shape, dtype)


def limits(moved):
    return dict(
        compiler_params=pltpu.CompilerParams(vmem_limit_bytes=56 << 20),
        cost_estimate=pl.CostEstimate(flops=moved, bytes_accessed=moved, transcendentals=0),
    )


def project(place, stacks, tokens, peer_tokens, phase, steps=4):
    length, model = tokens.shape
    half = length // 2
    count, _, depth, width = stacks[0].shape
    ins = [*stacks, tokens, peer_tokens, phase]
    outs = [
        out((width, half), bf16), out((width, length), bf16), out((width, length), bf16),
        out((width, half), bf16), out((width, length), bf16), out((width, length), bf16),
        out((width, 2 * length), bf16), out((half, model), f32), out((half, model), bf16), out((half, model), bf16),
        out((PARTS, 4 * count, depth, width), bf16),
    ]
    def rows(array):
        return pl.BlockSpec((array.shape[0] // steps, array.shape[1]), lambda s: (s, 0))

    def columns(array):
        return pl.BlockSpec((array.shape[0], array.shape[1] // steps), lambda s: (0, s))

    return pl.pallas_call(
        project_kernel,
        grid=(steps,),
        in_specs=[pl.BlockSpec(memory_space=pltpu.SMEM)] + [whole(a) for a in stacks] + [rows(a) for a in ins[4:]],
        out_specs=[columns(a) for a in outs[:7]] + [rows(a) for a in outs[7:10]] + [whole(outs[10])],
        out_shape=outs,
        scratch_shapes=[pltpu.VMEM((PARTS, width, model), bf16)],
        name="project",
        **limits(10 << 20),
    )(place, *ins)


def weigh_kernel(
    place_ref, own_rows, peer_rows, own_low, peer_low, phase_ref, own_dq, own_dk, own_dv, peer_dq, peer_dk, peer_dv,
    drel_ref, late_ref, early_ref, keep_ref, send_ref, total_sc, value_sc, small_sc,
):
    step = pl.program_id(0)

    @pl.when(step == 0)
    def _():
        total_sc[...] = jnp.zeros_like(total_sc)

    for i, pairs in enumerate((
        ((own_dq, own_low), (peer_dq, peer_low)),
        ((own_dk, own_rows), (peer_dk, peer_rows)),
        ((own_dv, own_rows), (peer_dv, peer_rows)),
        ((drel_ref, phase_ref),),
    )):
        for grad, rows in pairs:
            total_sc[i] += jnp.dot(grad[...].astype(bf16), rows[...], preferred_element_type=f32)

    @pl.when(step == pl.num_programs(0) - 1)
    def _():
        columns, lines, _, width = keep_ref.shape
        depth = value_sc.shape[1]
        for i in range(PARTS):
            value_sc[...] = total_sc[i].astype(bf16).T.reshape(value_sc.shape)
            for core, ref in enumerate((keep_ref, send_ref)):
                for column in range(columns):
                    for line in range(lines):
                        ref[column, line, i * depth:(i + 1) * depth] = value_sc[spot(place_ref, core, column, line)]
        first, last = LATE, LATE + early_ref.shape[0]
        small_sc[...] = jnp.zeros_like(small_sc)
        small_sc[:first] = late_ref[...].T[:first]
        small_sc[first:last] = early_ref[:, :width]
        small_sc[last : 2 * last - first] = early_ref[:, width:]
        small = small_sc[...].astype(bf16)
        for column in range(columns):
            for line in range(lines):
                for ref in (keep_ref, send_ref):
                    ref[column, line, PARTS * depth:] = small


def weigh(place, own_rows, peer_rows, own_low, peer_low, phase, own_grads, peer_grads, drel, late, early, blocks, steps=4):
    model = own_rows.shape[1]
    depth = model // blocks
    width = drel.shape[0]
    extra = LATE + 2 * early.shape[0]
    extra += -extra % 16

    def rows(array):
        return pl.BlockSpec((array.shape[0] // steps, model), lambda s: (s, 0))

    def columns(array):
        return pl.BlockSpec((width, array.shape[1] // steps), lambda s: (0, s))

    ins = [own_rows, peer_rows, own_low, peer_low, phase]
    grads = [*own_grads, *peer_grads, drel]
    pieces = out((2, blocks // 4, PARTS * depth + extra, width), bf16)
    return pl.pallas_call(
        weigh_kernel,
        grid=(steps,),
        in_specs=[pl.BlockSpec(memory_space=pltpu.SMEM)] + [rows(a) for a in ins] + [columns(a) for a in grads] + [whole(late), whole(early)],
        out_specs=[whole(pieces)] * 2,
        out_shape=[pieces] * 2,
        scratch_shapes=[pltpu.VMEM((PARTS, width, model), f32), pltpu.VMEM((blocks, depth, width), bf16), pltpu.VMEM((extra, width), f32)],
        name="weigh",
        **limits(8 << 20),
    )(place, *ins, *grads, late, early)


def token_kernel(dq_ref, dk_ref, dv_ref, w_ref, *refs):
    model = refs[-1].shape[1]
    width = dk_ref.shape[0]
    half = dq_ref.shape[1]
    doubled = jnp.dot(dq_ref[...], pair_matrix(half, 1), preferred_element_type=f32).astype(bf16)
    total = None
    for i, grad in enumerate((doubled, dk_ref[...], dv_ref[...])):
        term = lax.dot_general(grad.T, w_ref[i].reshape(model, width), NT, preferred_element_type=f32)
        total = term if total is None else total + term
    if len(refs) > 1:
        high = refs[0][...].astype(bf16)
        low = (refs[0][...] - high.astype(f32)).astype(bf16)
        pairs = pair_matrix(half, 0)
        total = total + jnp.dot(pairs, high, preferred_element_type=f32) + jnp.dot(pairs, low, preferred_element_type=f32)
    refs[-1][...] = total.astype(refs[-1].dtype)


def token_grad(grads, weights, extra, dtype):
    length = grads[1].shape[1]
    model = weights.shape[1] * weights.shape[2]
    ins = [*grads, weights] + ([extra] if extra is not None else [])
    specs = [whole(a) for a in ins]
    result = out((length, model), dtype)
    return pl.pallas_call(
        token_kernel,
        grid=(1,),
        in_specs=specs,
        out_specs=whole(result),
        out_shape=result,
        name="token_grad",
        **limits(5 << 20),
    )(*ins)


def finish_kernel(place_ref, *refs, sources):
    total = refs[0][...].astype(f32)
    for ref in refs[1:sources]:
        total = total + ref[...].astype(f32)
    grads_ref, offsets_ref, sameness_ref, bias_ref, *vectors, total_sc = refs[sources:]
    parts, depth, width = grads_ref.shape
    for i in range(parts):
        grads_ref[i] = total[i * depth : (i + 1) * depth]
    total_sc[...] = total[parts * depth :]
    offsets_ref[...] = total_sc[:3]
    sameness_ref[...] = total_sc[3:LATE]
    count = len(vectors) + 4

    def row(n):
        return jnp.concatenate(
            [total_sc[LATE + n : LATE + n + 1], total_sc[LATE + count + n : LATE + count + n + 1]], axis=1
        )

    for n, ref in enumerate(vectors):
        ref[...] = row(n).reshape(ref.shape)
    n = len(vectors)
    first = place_ref[3] == 0
    bias = jnp.concatenate(
        [jnp.where(first, row(n), row(n + 2)), jnp.where(first, row(n + 1), row(n + 3))], axis=1
    )
    bias_ref[...] = bias.reshape(bias_ref.shape)


def finish(place, pieces, depth, model, hidden):
    extra = pieces[0].shape[0] - PARTS * depth
    width = pieces[0].shape[1]
    outs = [
        out((PARTS, depth, width), f32), out((3, width), f32), out((2, width), f32), out((hidden,), f32),
    ] + [out((model,), f32)] * 6
    return pl.pallas_call(
        partial(finish_kernel, sources=len(pieces)),
        grid=(1,),
        in_specs=[pl.BlockSpec(memory_space=pltpu.SMEM)] + [whole(a) for a in pieces],
        out_specs=[whole(a) for a in outs],
        out_shape=outs,
        scratch_shapes=[pltpu.VMEM((extra, width), f32)],
        name="finish",
        **limits(1 << 20),
    )(place, *pieces)


SPLIT = 1


def layer_norm(values_in):
    row_mean = jnp.mean(values_in, axis=1, keepdims=True)
    centred = values_in - row_mean
    variance = jnp.mean(centred * centred, axis=1, keepdims=True)
    scale = lax.rsqrt(variance + epsilon)
    return centred * scale, scale


def layer_norm_back(grad, normed, scale, gain):
    inner = grad * gain
    return scale * (
        inner
        - jnp.mean(inner, axis=1, keepdims=True)
        - normed * jnp.mean(inner * normed, axis=1, keepdims=True)
    )


def row_sum(values_in):
    return jnp.sum(values_in, axis=0, keepdims=True)


def middle_kernel(
    place_ref, pooled_ref, mixed_ref, sent_ref, vec_ref, cot_ref, own_c_ref, peer_c_ref, weights_ref, own_bias_ref, peer_bias_ref,
    result_ref, dfirst_ref, own_dm_ref, peer_dm_ref, keep_c_ref, send_c_ref, sums_ref,
    keep_w_ref, send_w_ref, keep_n_ref, send_n_ref,
    held_sc, held_sem, slope_sc, act_sc, dhid_sc, first_sc, norm_sc, scale_sc, total_sc, low_sc, low_t_sc, dsec_sc, dsec_t_sc,
    *, chunks,
):
    step = pl.program_id(0)
    model = pooled_ref.shape[1]
    rows = pooled_ref.shape[0]
    part = own_bias_ref.shape[-1]
    each = own_bias_ref.shape[0]

    def fetch(chunk, kind):
        return pltpu.make_async_copy(
            weights_ref.at[:, chunk // each, :, pl.ds((kind * each + chunk % each) * part, part)],
            held_sc.at[chunk, kind],
            held_sem.at[chunk, kind],
        )
    vec = vec_ref[...]

    def store(value, keep_ref, send_ref, *half):
        value = value.astype(bf16)
        for n, ref in enumerate((keep_ref, send_ref)):
            piece = value[n * (model // 2) : (n + 1) * (model // 2)]
            if half:
                shape = ref.shape[:1] + ref.shape[2:]
                ref[:, half[0]] = piece.reshape(shape)
            else:
                ref[...] = piece.reshape(ref.shape)

    def turn_rows(value, ref):
        value = value.T.reshape(ref.shape)
        count = ref.shape[0]
        for n in range(count):
            line, column, core = n // 4, n // 2 % 2, n % 2
            ref[
                (count // 2) * jnp.bitwise_xor(place_ref[2], core)
                + (count // 4) * jnp.bitwise_xor(place_ref[1], column)
                + jnp.bitwise_xor(place_ref[0], line)
            ] = value[n]

    postbias, scaling, centring = vec[0:1], vec[1:2], vec[2:3]
    narrowbias, rescale, recentre = vec[3:4], vec[4:5], vec[5:6]

    @pl.when(step == 0)
    def _():
        for chunk in range(chunks):
            for kind in range(2):
                fetch(chunk, kind).start()
        own_c = own_c_ref[...].reshape(model, -1)
        peer_c = peer_c_ref[...].reshape(model, -1)
        mixed = mixed_ref[...].astype(bf16).T
        sent = sent_ref[...].T
        branch = (
            lax.dot_general(mixed, own_c, NT, preferred_element_type=f32)
            + lax.dot_general(sent, peer_c, NT, preferred_element_type=f32)
            + postbias
        )
        normed, scale = layer_norm(pooled_ref[...] + branch)
        norm_sc[...] = normed
        scale_sc[...] = scale
        first = normed * scaling + centring
        first_sc[...] = first
        low = first.astype(bf16)
        low_sc[...] = low
        turn_rows(low, low_t_sc)
        total_sc[...] = jnp.zeros_like(total_sc)

    for chunk in range(chunks):

        @pl.when(step == chunk)
        def _():
            for kind in range(2):
                fetch(chunk, kind).wait()

    @pl.when(step < chunks)
    def _():
        wide = held_sc[step, 0].reshape(model, part)
        spot_bias = lax.rem(step, each)
        bias = jnp.where(step // each == place_ref[3], own_bias_ref[spot_bias], peer_bias_ref[spot_bias])
        hidden = jnp.dot(low_sc[...], wide, preferred_element_type=f32) + bias
        square = hidden * hidden
        root = math.sqrt(2.0 / math.pi)
        turn = jnp.tanh(hidden * (root + (root * 0.044715) * square))
        half = 0.5 * turn + 0.5
        act = (hidden * half).astype(bf16)
        slope_sc[step] = half + hidden * (half * (1.0 - turn)) * (root + (3.0 * root * 0.044715) * square)
        act_sc[step] = act
        narrow = held_sc[step, 1].reshape(model, part)
        total_sc[...] += lax.dot_general(act, narrow, NT, preferred_element_type=f32)

    @pl.when(step == chunks - 1)
    def _():
        normed, scale = layer_norm(first_sc[...] + (total_sc[...] + narrowbias))
        result_ref[...] = (normed * rescale + recentre).astype(bf16)
        cot = cot_ref[...].astype(f32)
        dfinal = layer_norm_back(cot, normed, scale, rescale)
        dsec = dfinal.astype(bf16)
        dsec_sc[...] = dsec
        turn_rows(dsec, dsec_t_sc)
        sums_ref[3:4] = row_sum(dsec.astype(f32))
        sums_ref[4:5] = row_sum(cot * normed)
        sums_ref[5:6] = row_sum(cot)
        total_sc[...] = dfinal

    back = step - chunks

    @pl.when((back >= 0) & (lax.rem(back, 2) == 0))
    def _():
        chunk = back // 2
        narrow = held_sc[chunk, 1].reshape(model, part)
        dact = jnp.dot(dsec_sc[...], narrow, preferred_element_type=f32)
        dhid = (dact * slope_sc[chunk]).astype(bf16)
        dhid_sc[...] = dhid
        bias_sum = row_sum(dhid.astype(f32))
        for n in range(part // model):
            sums_ref[pl.ds(6 + chunk * (part // model) + n, 1)] = bias_sum[:, n * model : (n + 1) * model]
        grad = jnp.dot(dsec_t_sc[...].reshape(model, rows), act_sc[chunk], preferred_element_type=f32)
        store(grad, keep_n_ref, send_n_ref)

    @pl.when((back >= 0) & (lax.rem(back, 2) == 1))
    def _():
        wide = held_sc[back // 2, 0].reshape(model, part)
        total_sc[...] += lax.dot_general(dhid_sc[...], wide, NT, preferred_element_type=f32)
        grad = jnp.dot(low_t_sc[...].reshape(model, rows), dhid_sc[...], preferred_element_type=f32)
        store(grad, keep_w_ref, send_w_ref)

    @pl.when(back == 2 * chunks - 1)
    def _():
        dfirst = total_sc[...]
        normed = norm_sc[...]
        dfirst_in = layer_norm_back(dfirst, normed, scale_sc[...], scaling)
        dfirst_ref[...] = dfirst_in
        dbranch = dfirst_in.astype(bf16)
        sums_ref[0:1] = row_sum(dbranch.astype(f32))
        sums_ref[1:2] = row_sum(dfirst * normed)
        sums_ref[2:3] = row_sum(dfirst)
        dbranch_t = dbranch.T
        turn_rows(dbranch, low_t_sc)
        turned = low_t_sc[...].reshape(model, rows)
        for half, c_ref, m_ref, dm_ref in (
            (0, own_c_ref, mixed_ref, own_dm_ref),
            (1, peer_c_ref, sent_ref, peer_dm_ref),
        ):
            c = c_ref[...].reshape(model, -1)
            dm_ref[...] = lax.dot_general(c, dbranch_t, TN, preferred_element_type=f32).astype(bf16)
            dc = lax.dot_general(turned, m_ref[...].astype(bf16), NT, preferred_element_type=f32)
            store(dc, keep_c_ref, send_c_ref, half)


def middle(place, pooled, mixed, sent, vec, cot, weights, own_bias, peer_bias):
    rows, model = pooled.shape
    blocks, halves, depth, columns = weights.shape
    width = mixed.shape[0]
    hidden = (columns - width) // 2
    part = hidden // SPLIT
    each = hidden // part
    chunks = halves * each

    def combiner_spec(flip):
        def index(step, place_ref):
            return (0, jnp.bitwise_xor(place_ref[3], flip), 0, 2 * hidden // width)

        return pl.BlockSpec((blocks, None, depth, width), index, pipeline_mode=pl.Buffered(1))

    def wide_index(step, place_ref):
        c = jnp.maximum(step - chunks - 1, 0) // 2
        return (jnp.bitwise_xor(c // each, place_ref[3]), 0, 0, 0, lax.rem(c, each))

    def narrow_index(step, place_ref):
        c = jnp.maximum(step - chunks, 0) // 2
        return (0, jnp.bitwise_xor(c // each, place_ref[3]), 0, 0, lax.rem(c, each))

    lines = blocks // 4
    outs = [
        out((rows, model), bf16), out((rows, model), f32), out(mixed.shape, bf16), out(mixed.shape, bf16),
        out((2, halves, lines, depth, width), bf16), out((2, halves, lines, depth, width), bf16), out((6 + halves * hidden // model, model), f32),
    ]
    wide_grads = out((halves, 2, lines, depth, hidden), bf16)
    narrow_grads = out((2, halves, lines, depth, hidden), bf16)
    whole_ins = [pooled, mixed, sent, vec, cot]
    grad_spec = [pl.BlockSpec((1, 2, lines, depth, part), wide_index)] * 2
    grad_spec += [pl.BlockSpec((2, 1, lines, depth, part), narrow_index)] * 2
    return pl.pallas_call(
        partial(middle_kernel, chunks=chunks),
        grid_spec=pltpu.PrefetchScalarGridSpec(
            num_scalar_prefetch=1,
            grid=(3 * chunks,),
            in_specs=[whole(a) for a in whole_ins]
            + [combiner_spec(0), combiner_spec(1), pl.BlockSpec(memory_space=pl.ANY)]
            + [pl.BlockSpec((each, 1, part), lambda s, p: (0, 0, 0))] * 2,
            out_specs=[whole(a) for a in outs]
            + grad_spec,
            scratch_shapes=[
                pltpu.VMEM((chunks, 2, blocks, depth, part), bf16),
                pltpu.SemaphoreType.DMA((chunks, 2)),
                pltpu.VMEM((chunks, rows, part), f32),
                pltpu.VMEM((chunks, rows, part), bf16),
                pltpu.VMEM((rows, part), bf16),
                pltpu.VMEM((rows, model), f32),
                pltpu.VMEM((rows, model), f32),
                pltpu.VMEM((rows, 1), f32),
                pltpu.VMEM((rows, model), f32),
                pltpu.VMEM((rows, model), bf16),
                pltpu.VMEM((blocks, depth, rows), bf16),
                pltpu.VMEM((rows, model), bf16),
                pltpu.VMEM((blocks, depth, rows), bf16),
            ],
        ),
        out_shape=outs + [wide_grads] * 2 + [narrow_grads] * 2,
        name="middle",
        **limits(24 << 20),
    )(place, *whole_ins, weights, weights, weights, own_bias.reshape(each, 1, part), peer_bias.reshape(each, 1, part))


def position_table(length, model_width):
    row_index = jnp.arange(2 * length, dtype=jnp.float32)
    offset = length - row_index
    half_width = model_width // 2
    frequency = jnp.exp(
        jnp.arange(half_width, dtype=jnp.float32) * (-math.log(10000.0) / half_width)
    )
    angles = offset[:, None] * frequency[None, :]
    return jnp.concatenate([jnp.sin(angles), jnp.cos(angles)], axis=1)


BLOCKS = 16


def swap(piece):
    return lax.ppermute(piece, "tensor", [(0, 1), (1, 0)])


def exchange(piece, mask):
    count = lax.axis_size("dp")
    return lax.ppermute(piece, "dp", [(i, i ^ mask) for i in range(count)])


def shards(
    tokens,
    segments,
    projections,
    combiner,
    offsets,
    sameness,
    postbias,
    scaling,
    centring,
    widener,
    widebias,
    narrower,
    narrowbias,
    rescale,
    recentre,
    cotangent,
):
    tensor_part = lax.axis_index("tensor")
    dp_part = lax.axis_index("dp")
    dp_count = lax.axis_size("dp")
    length, model = tokens.shape
    width = offsets.shape[1]
    hidden = widener.shape[1]
    blocks = BLOCKS
    depth = model // blocks
    direct = dp_count == blocks
    if direct:
        place = jnp.stack([dp_part // 4, (dp_part // 2) % 2, dp_part % 2, tensor_part]).astype(jnp.int32)
    else:
        place = jnp.stack([tensor_part * 0] * 3 + [tensor_part]).astype(jnp.int32)

    if direct:
        near0 = jnp.stack([projections] + [exchange(projections, 4 * d) for d in range(1, 4)])
        near1 = exchange(near0, 2)
        stacks = (near0, near1, exchange(near0, 1), exchange(near1, 1))
    else:
        every = lax.all_gather(projections, "dp", axis=1, tiled=True)
        every = every.reshape(PARTS, blocks // 4, 2, 2, depth, width).transpose(3, 2, 1, 0, 4, 5)
        stacks = (every[0, 0], every[0, 1], every[1, 0], every[1, 1])
    peer_tokens = swap(tokens)
    mine = jnp.concatenate([widener, narrower.T, combiner.T], axis=1)
    columns = mine.shape[1]
    weights = lax.all_gather(mine, ("dp", "tensor"), axis=0, tiled=False)
    if not direct:
        weights = weights.reshape(dp_count, 2, model // dp_count, columns).transpose(1, 0, 2, 3)
        weights = weights.reshape(2, blocks, depth, columns).transpose(1, 0, 2, 3)
    weights = weights.reshape(blocks, 2, depth, columns)
    small = jnp.concatenate([offsets, sameness], axis=0).T
    seg = jnp.where(tensor_part == 0, segments, jnp.concatenate([segments[1:], segments[:1]]))[:, None]
    vec = jnp.stack([postbias, scaling, centring, narrowbias, rescale, recentre, postbias, postbias])
    peer_tokens, peer_bias, small, seg, seg_q, vec = lax.optimization_barrier(
        (peer_tokens, swap(widebias), small, seg, seg[:, :, ::2], vec)
    )
    phase = position_table(length, model).astype(bf16)
    own_q, own_k, own_v, peer_q, peer_k, peer_v, relative, pooled, own_low, peer_low, inwards = project(
        place, stacks, tokens, peer_tokens, phase
    )
    own_args = (own_q, own_k, own_v, relative, small, seg_q, seg)
    peer_args = (peer_q, peer_k, peer_v, relative, small, seg_q, seg)
    peer_probs, peer_mixed, peer_mixed_low = attn_fwd(*peer_args, 1)
    sent_mixed = swap(peer_mixed_low)
    own_probs, own_mixed, own_mixed_low = attn_fwd(*own_args, 0)
    result, dfirst_in, own_dmixed, peer_dmixed, keep_c, send_c, early, keep_w, send_w, keep_n, send_n = middle(
        place, pooled, own_mixed_low, sent_mixed, vec, cotangent, weights, widebias, peer_bias
    )
    sent_dmixed = swap(peer_dmixed)
    half = width // DH // 2
    part = attn_bwd(0, *own_args, own_probs, own_mixed, own_dmixed, heads=(0, half))
    early = early + swap(early)
    if direct:

        def add(kept, sent):
            return (kept.astype(f32) + sent.astype(f32)).astype(bf16)

        wide = (keep_w, exchange(send_w, 1))
        narrow = (keep_n, exchange(send_n, 1))
        comb = (keep_c, exchange(send_c, 1))

        def joined(pick):
            return jnp.concatenate([add(*map(pick, narrow)), add(*map(pick, comb))], axis=-1)

        first_stage = (
            add(wide[0][0], wide[1][0]),
            add(wide[0][1], wide[1][1]),
            joined(lambda a: a[0]),
            joined(lambda a: a[1]),
        )
        part, early, first_stage, sent_dmixed = lax.optimization_barrier((part, early, first_stage, sent_dmixed))

    own_dq, own_dk, own_dv, drel, late = attn_bwd(
        0, *own_args, own_probs, own_mixed, own_dmixed, heads=(half, width // DH - half), base=part
    )
    peer_dq, peer_dk, peer_dv, drel, late = attn_bwd(
        1, *peer_args, peer_probs, peer_mixed, sent_dmixed, (drel, late)
    )
    own_grads = (own_dq, own_dk, own_dv)
    peer_grads = (peer_dq, peer_dk, peer_dv)
    if direct:
        wide = (first_stage[0], swap(first_stage[1]))
        narrow = (first_stage[2], exchange(first_stage[3], 2))
        wide = (add(wide[0][0], wide[1][0]), add(wide[0][1], wide[1][1]))
        narrow = (add(narrow[0][0], narrow[1][0]), add(narrow[0][1], narrow[1][1]))
        drel, wide, narrow = lax.optimization_barrier((drel, wide, narrow))
        wide = (wide[0], exchange(wide[1], 2))
        narrow = (narrow[0], swap(narrow[1]))
    keep, send = weigh(
        place, tokens, peer_tokens, own_low, peer_low, phase, own_grads, peer_grads, drel, late, early, blocks
    )
    if direct:
        keep, send, wide, narrow = lax.optimization_barrier((keep, send, wide, narrow))
        sent = exchange(send, 1)
        held = (add(keep[0], sent[0]), add(keep[1], sent[1]))
        last = [
            jnp.concatenate([add(wide[0][d], wide[1][d]), add(narrow[0][d], narrow[1][d])], axis=-1)
            for d in range(4)
        ]
        peer_grads, held, last = lax.optimization_barrier((peer_grads, held, last))
        held = (held[0], exchange(held[1], 2))
    peer_part = token_grad(peer_grads, inwards, None, bf16)
    sent_tokens = swap(peer_part)
    if direct:
        grads = last[0].astype(f32)
        for d in range(1, 4):
            grads = grads + exchange(last[d], 4 * d).astype(f32)
        held = [add(held[0][d], held[1][d]) for d in range(4)]
        own_grads, held, _ = lax.optimization_barrier((own_grads, held, peer_part))
        pieces = [held[0]] + [exchange(held[d], 4 * d) for d in range(1, 4)]
        own_part, grads = lax.optimization_barrier((token_grad(own_grads, inwards, dfirst_in, f32), grads))
        tokens_grad, pieces = lax.optimization_barrier((own_part + sent_tokens.astype(f32), pieces))
    else:

        def ordered(kept, sent, turned):
            value = jnp.stack([kept, sent])
            value = value.transpose((3, 1, 0, 2, 4, 5) if turned else (3, 2, 0, 1, 4, 5))
            value = jnp.where(tensor_part == 0, value, value[:, :, :, ::-1])
            return value.transpose(3, 0, 1, 2, 4, 5).reshape(2, dp_count, model // dp_count, -1)

        grads = jnp.concatenate([ordered(keep_w, send_w, False), ordered(keep_n, send_n, True), ordered(keep_c, send_c, True)], axis=-1)
        grads = lax.psum_scatter(
            grads.transpose(1, 0, 2, 3).reshape(2 * dp_count, model // dp_count, columns),
            ("dp", "tensor"),
            scatter_dimension=0,
            tiled=True,
        )[0].astype(f32)
        big = jnp.stack([keep, send])[:, :, :, : PARTS * depth]
        big = big.reshape(2, 2, blocks // 4, PARTS, depth, width).transpose(3, 2, 1, 0, 4, 5)
        big = lax.psum_scatter(big.reshape(PARTS, model, width), "dp", scatter_dimension=1, tiled=True)
        extras = lax.psum(keep[0, 0, PARTS * depth :].astype(f32), "dp").astype(bf16)
        pieces = [jnp.concatenate([big.reshape(-1, width), extras], axis=0)]
        tokens_grad = token_grad(own_grads, inwards, dfirst_in, f32) + sent_tokens.astype(f32)
    projections_grad, offsets_grad, sameness_grad, bias_grad, *vectors = finish(
        place, pieces, depth if direct else model // dp_count, model, hidden
    )
    combiner_grad = grads[:, 2 * hidden :].T
    return (
        result,
        tokens_grad,
        projections_grad,
        combiner_grad,
        offsets_grad,
        sameness_grad,
        vectors[0],
        vectors[1],
        vectors[2],
        grads[:, :hidden],
        bias_grad,
        grads[:, hidden : 2 * hidden].T,
        vectors[3],
        vectors[4],
        vectors[5],
    )


def solution(mesh):
    placed = (
        P(("dp", "tensor"), None),
        P("dp", None),
        P(None, "dp", "tensor"),
        P("tensor", "dp"),
        P(None, "tensor"),
        P(None, "tensor"),
        P(),
        P(),
        P(),
        P("dp", "tensor"),
        P("tensor"),
        P("tensor", "dp"),
        P(),
        P(),
        P(),
        P(("dp", "tensor"), None),
    )
    return jax.shard_map(
        shards,
        mesh=mesh,
        in_specs=placed,
        out_specs=(
            P(("dp", "tensor"), None),
            P(("dp", "tensor"), None),
            P(None, "dp", "tensor"),
            P("tensor", "dp"),
            P(None, "tensor"),
            P(None, "tensor"),
            P(),
            P(),
            P(),
            P("dp", "tensor"),
            P("tensor"),
            P("tensor", "dp"),
            P(),
            P(),
            P(),
        ),
        check_vma=False,
    )
```

```python
from functools import partial
import math

import jax
import jax.numpy as jnp
from jax import lax
from jax.experimental import pallas as pl
from jax.experimental.pallas import tpu as pltpu
from jax.sharding import PartitionSpec as P

epsilon = 1e-05
bf16=jnp.bfloat16; f32=jnp.float32
DH=64
AUG=16
TN=(((0,),(0,)),((),()))
NT=(((1,),(1,)),((),()))
NN=(((1,),(0,)),((),()))

def split3(u):
    row=lax.broadcasted_iota(jnp.int32,u.shape,0)
    hi=u.astype(bf16).astype(f32)
    r1=u-hi
    mid=r1.astype(bf16).astype(f32)
    lo=r1-mid
    return jnp.where(row<3,hi,jnp.where(row<6,mid,jnp.where(row<9,lo,0.0))).astype(bf16)

def fwd_kernel(q_ref,k_ref,v_ref,r_ref,s_ref,segq_ref,segk_ref,p_ref,m_ref,ml_ref,c_sc,k_sc,*,tq):
    nq=q_ref.shape[1]; nk=k_ref.shape[1]
    q=q_ref[...].astype(f32)
    sm=s_ref[...]
    c_sc[:DH]=(q+sm[:,0:1]).astype(bf16)*jnp.asarray(0.125,bf16)
    pos=(q+sm[:,1:2]).astype(bf16)*jnp.asarray(0.125,bf16)
    typed=q+sm[:,2:3]
    t0=jnp.sum(typed*sm[:,3:4],axis=0,keepdims=True)*0.125
    t1=jnp.sum(typed*sm[:,4:5],axis=0,keepdims=True)*0.125
    kind=lax.rem(lax.broadcasted_iota(jnp.int32,(AUG,nq),0),3)
    c_sc[DH:]=split3(jnp.where(segq_ref[...]==kind,t1,t0))
    k_sc[:DH]=k_ref[...]
    rowk=lax.broadcasted_iota(jnp.int32,(AUG,nk),0)
    k_sc[DH:]=jnp.where((segk_ref[...]==lax.rem(rowk,3)) & (rowk<9),1.0,0.0).astype(bf16)

    tr=min(tq,128)
    def dense(b):
        i0=b*tq; w0=nk-2*i0-2*tq
        return lax.dot_general(pos[:,i0:i0+tq],r_ref[:,w0:w0+nk+2*tq],TN,preferred_element_type=f32)
    def cont(b):
        i0=b*tq
        return lax.dot_general(c_sc[:,i0:i0+tq],k_sc[...],TN,preferred_element_type=f32)
    def finish(b,c,d):
        i0=b*tq
        for t in range(tq//tr):
            lo=2*(tq-(t+1)*tr)
            g=pltpu.roll(d[t*tr:(t+1)*tr,lo:lo+nk+2*tr],nk,1,stride=2,stride_axis=0)
            s=c[t*tr:(t+1)*tr]+g[:,:nk]
            mx=jnp.max(s,axis=1,keepdims=True)
            e=jnp.exp(s-mx)
            l=jnp.sum(e,axis=1,keepdims=True)
            p_ref[i0+t*tr:i0+(t+1)*tr,:]=(e*(1.0/l)).astype(bf16)
    n=nq//tq
    prev=(cont(0),dense(0))
    for b in range(n):
        nxt=(cont(b+1),dense(b+1)) if b+1<n else None
        finish(b,*prev); prev=nxt
    mixed=lax.dot_general(v_ref[...],p_ref[...],NT,preferred_element_type=f32)
    m_ref[...]=mixed
    ml_ref[...]=mixed.astype(bf16)

def attn_fwd(qT,kT,vT,relT,small,segq,segk,row=0,tq=128):
    hd,nq=qT.shape; nk=kT.shape[1]; heads=hd//DH
    return pl.pallas_call(partial(fwd_kernel,tq=tq),grid=(heads,),
        in_specs=[pl.BlockSpec((DH,nq),lambda h:(h,0)),pl.BlockSpec((DH,nk),lambda h:(h,0)),pl.BlockSpec((DH,nk),lambda h:(h,0)),
          pl.BlockSpec((DH,2*nk),lambda h:(h,0)),pl.BlockSpec((DH,small.shape[1]),lambda h:(h,0)),
          pl.BlockSpec((None,1,nq),lambda h:(row,0,0)),pl.BlockSpec((None,1,nk),lambda h:(row,0,0))],
        out_specs=[pl.BlockSpec((None,nq,nk),lambda h:(h,0,0)),pl.BlockSpec((DH,nq),lambda h:(h,0)),pl.BlockSpec((DH,nq),lambda h:(h,0))],
        out_shape=[jax.ShapeDtypeStruct((heads,nq,nk),bf16),jax.ShapeDtypeStruct((hd,nq),f32),jax.ShapeDtypeStruct((hd,nq),bf16)],
        scratch_shapes=[pltpu.VMEM((DH+AUG,nq),bf16),pltpu.VMEM((DH+AUG,nk),bf16)],
        name="attend",**limits(15<<20))(qT,kT,vT,relT,small,segq,segk)

def bwd_kernel(q_ref,k_ref,v_ref,r_ref,s_ref,segq_ref,segk_ref,p_ref,m_ref,dm_ref,
               dq_ref,dk_ref,dv_ref,dr_ref,sg_ref,k_sc,v_sc,dm_sc,ds_sc,dg_sc,*,tq,first):
    nq=q_ref.shape[1]; nk=k_ref.shape[1]
    q=q_ref[...].astype(f32)
    sm=s_ref[...]
    content=(q+sm[:,0:1]).astype(bf16)*jnp.asarray(0.125,bf16)
    pos=(q+sm[:,1:2]).astype(bf16)*jnp.asarray(0.125,bf16)
    typed=q+sm[:,2:3]
    k_sc[:DH]=k_ref[...]
    rowk=lax.broadcasted_iota(jnp.int32,(AUG,nk),0)
    k_sc[DH:]=((segk_ref[...]==rowk)).astype(f32).astype(bf16)
    v_sc[:DH]=v_ref[...]
    v_sc[DH:]=jnp.where(rowk<3,1.0,0.0).astype(bf16)
    dm=dm_ref[...]
    dm_sc[:DH]=dm
    delta=-jnp.sum(dm.astype(f32)*m_ref[...],axis=0,keepdims=True)
    rowq=lax.broadcasted_iota(jnp.int32,(AUG,nq),0)
    hi=delta.astype(bf16).astype(f32); r1=delta-hi; mid=r1.astype(bf16).astype(f32); lo=r1-mid
    dm_sc[DH:]=jnp.where(rowq==0,hi,jnp.where(rowq==1,mid,jnp.where(rowq==2,lo,0.0))).astype(bf16)
    w=nk+2*tq
    flip=(lax.broadcasted_iota(jnp.int32,(tq,tq),0)+lax.broadcasted_iota(jnp.int32,(tq,tq),1)==tq-1).astype(f32).astype(bf16)
    def turn16(x):
        parts=[lax.dot_general(x[:,i:i+tq],flip,NN,preferred_element_type=f32) for i in range(0,nq,tq)]
        return jnp.concatenate(parts,axis=1).astype(bf16)
    def turn(x):
        hi=x.astype(bf16); r1=x-hi.astype(f32); mid=r1.astype(bf16); lo=(r1-mid.astype(f32)).astype(bf16)
        cat=jnp.concatenate([hi,mid,lo],axis=0)
        parts=[lax.dot_general(cat[:,i:i+tq],flip,NN,preferred_element_type=f32) for i in range(0,nq,tq)]
        y=jnp.concatenate(parts,axis=1)
        return y[:DH]+y[DH:2*DH]+y[2*DH:]

    @pl.when(pl.program_id(0)==0)
    def _():
        dg_sc[...]=jnp.zeros_like(dg_sc)
    def grad(b):
        i0=b*tq
        return lax.dot_general(dm_sc[:,i0:i0+tq],v_sc[...],TN,preferred_element_type=f32)
    def shift(b,dp):
        i0=b*tq
        w0=nk-2*i0-2*tq
        ds16=(p_ref[i0:i0+tq,:].astype(f32)*dp).astype(bf16)
        ds_sc[i0:i0+tq,:]=ds16
        back=lax.dot_general(flip,ds16,NN,preferred_element_type=f32)
        g=jnp.concatenate([back,jnp.zeros((tq,2*tq),f32)],axis=1)
        g=pltpu.roll(g,2,1,stride=2,stride_axis=0)
        dg_sc[i0:i0+tq,w0:w0+w]=g.astype(bf16)
    n=nq//tq
    for b in range(n): shift(b,grad(b))
    dv_ref[...]=lax.dot_general(dm,p_ref[...],NN,preferred_element_type=f32).astype(bf16)
    dk_ref[...]=lax.dot_general(content,ds_sc[...],NN,preferred_element_type=f32).astype(bf16)
    dc=lax.dot_general(k_sc[...],ds_sc[...],NT,preferred_element_type=f32)
    half=256
    tpos=turn16(pos)
    parts=[];drs=[]
    for c0 in range(0,nq,half):
        v0=nk-2*c0-2*half
        g=dg_sc[c0:c0+half,v0:v0+nk+2*half]
        parts.append(lax.dot_general(r_ref[:,v0:v0+nk+2*half],g,NT,preferred_element_type=f32))
        drs.append(lax.dot_general(tpos[:,c0:c0+half],g,NN,preferred_element_type=f32))
    dpos=turn(jnp.concatenate(parts,axis=1))*0.125
    z=jnp.zeros((DH,2*half),f32)
    dr=jnp.concatenate([z,drs[0]],axis=1)+jnp.concatenate([drs[1],z],axis=1)
    if first is None:
        dr_ref[...]=dr
    else:
        dr_ref[...]=first[0][...]+dr
    dcontent=dc[:DH]*0.125
    seg=dc[DH:]*0.125
    rows=lax.broadcasted_iota(jnp.int32,(AUG,nq),0)
    g1=jnp.sum(jnp.where(segq_ref[...]==rows,seg,0.0),axis=0,keepdims=True)
    g0=jnp.sum(seg,axis=0,keepdims=True)-g1
    dtyped=sm[:,3:4]*g0+sm[:,4:5]*g1
    dq_ref[...]=(dcontent+dpos+dtyped).astype(bf16)
    lane=lax.broadcasted_iota(jnp.int32,(DH,128),1)
    total=jnp.zeros((DH,128),f32)
    for n,val in enumerate((dcontent,dpos,dtyped,typed*g0,typed*g1)):
        total=jnp.where(lane==n,jnp.sum(val,axis=1,keepdims=True),total)
    if first is None:
        sg_ref[...]=total
    else:
        sg_ref[...]=first[1][...]+total

def bwd_kernel_first(*refs,tq,skip):
    bwd_kernel(*refs[:10],*refs[10+skip:],tq=tq,first=None)
def bwd_kernel_next(*refs,tq,skip):
    bwd_kernel(*refs[:10],*refs[12+skip:],tq=tq,first=refs[10:12])

def attn_bwd(which,qT,kT,vT,relT,small,segq,segk,probs,mixedT,dmixedT,carry=None,tq=256,heads=None,base=None):
    hd,nq=qT.shape; nk=kT.shape[1]
    start,count=heads or (0,hd//DH)
    row=lambda n: pl.BlockSpec((DH,n),lambda h:(h+start if start else h,0))
    ins=[row(nq),row(nk),row(nk),row(2*nk),row(small.shape[1]),pl.BlockSpec((None,1,nq),lambda h:(which,0,0)),pl.BlockSpec((None,1,nk),lambda h:(which,0,0)),
         pl.BlockSpec((None,nq,nk),lambda h:(h+start if start else h,0,0)),row(nq),row(nq)]
    args=[qT,kT,vT,relT,small,segq,segk,probs,mixedT,dmixedT]
    kern=bwd_kernel_first
    if carry is not None:
        ins+= [row(2*nk),row(128)]; args+=list(carry); kern=bwd_kernel_next
    aliases={}
    if base is not None:
        aliases={len(args)+n:n for n in range(5)}
        ins+=[pl.BlockSpec(memory_space=pl.ANY)]*5; args+=list(base)
    return pl.pallas_call(partial(kern,tq=tq,skip=len(aliases)),grid=(count,),in_specs=ins,
        out_specs=[row(nq),row(nk),row(nk),row(2*nk),row(128)],
        out_shape=[jax.ShapeDtypeStruct((hd,nq),bf16),jax.ShapeDtypeStruct((hd,nk),bf16),jax.ShapeDtypeStruct((hd,nk),bf16),
           jax.ShapeDtypeStruct((hd,2*nk),f32),jax.ShapeDtypeStruct((hd,128),f32)],
        input_output_aliases=aliases,
        scratch_shapes=[pltpu.VMEM((DH+AUG,nk),bf16),pltpu.VMEM((DH+AUG,nk),bf16),pltpu.VMEM((DH+AUG,nq),bf16),pltpu.VMEM((nq,nk),bf16),pltpu.VMEM((nq,2*nk),bf16)],
        name="attend_back",**limits((15*count//6)<<20))(*args)


PARTS = 4
LATE = 5


def pair_matrix(count, axis):
    shape = (count, 2 * count) if axis == 1 else (2 * count, count)
    longer = lax.broadcasted_iota(jnp.int32, shape, axis)
    shorter = lax.broadcasted_iota(jnp.int32, shape, 1 - axis)
    return jnp.where(jnp.right_shift(longer, 1) == shorter, 0.5, 0.0).astype(bf16)


def spot(place_ref, core, column, line):
    return (
        4 * jnp.bitwise_xor(place_ref[0], line)
        + 2 * jnp.bitwise_xor(place_ref[1], column)
        + jnp.bitwise_xor(place_ref[2], core)
    )


def project_kernel(
    place_ref, near0_ref, near1_ref, far0_ref, far1_ref, own_ref, peer_ref, phase_ref,
    own_q, own_k, own_v, peer_q, peer_k, peer_v, rel_ref, pooled_ref, own_low, peer_low, weights_ref,
    turned_sc,
):
    @pl.when(pl.program_id(0) == 0)
    def _():
        for i in range(PARTS):
            for n, ref in enumerate((near0_ref, near1_ref, far0_ref, far1_ref)):
                for d in range(ref.shape[0]):
                    weights_ref[i, spot(place_ref, n // 2, n % 2, d)] = ref[d, i]
            turned_sc[i] = weights_ref[i].reshape(-1, near0_ref.shape[3]).T

    pairs = pair_matrix(own_ref.shape[0] // 2, 1)

    def sequence(rows_ref, q_ref, k_ref, v_ref, low_ref, keep_ref):
        rows = rows_ref[...]
        pooled = jnp.dot(pairs, rows, preferred_element_type=f32)
        low = pooled.astype(bf16)
        low_ref[...] = low
        if keep_ref is not None:
            keep_ref[...] = pooled
        for i, (source, target) in enumerate(((low, q_ref), (rows, k_ref), (rows, v_ref))):
            target[...] = lax.dot_general(turned_sc[i], source, NT, preferred_element_type=f32).astype(bf16)

    sequence(own_ref, own_q, own_k, own_v, own_low, pooled_ref)
    sequence(peer_ref, peer_q, peer_k, peer_v, peer_low, None)
    rel_ref[...] = lax.dot_general(turned_sc[3], phase_ref[...], NT, preferred_element_type=f32).astype(bf16)


def whole(array):
    return pl.BlockSpec(array.shape, lambda *step: (0,) * array.ndim, pipeline_mode=pl.Buffered(1))


def out(shape, dtype):
    return jax.ShapeDtypeStruct(shape, dtype)


def limits(moved):
    return dict(
        compiler_params=pltpu.CompilerParams(vmem_limit_bytes=56 << 20),
        cost_estimate=pl.CostEstimate(flops=moved, bytes_accessed=moved, transcendentals=0),
    )


def project(place, stacks, tokens, peer_tokens, phase, steps=4):
    length, model = tokens.shape
    half = length // 2
    count, _, depth, width = stacks[0].shape
    ins = [*stacks, tokens, peer_tokens, phase]
    outs = [
        out((width, half), bf16), out((width, length), bf16), out((width, length), bf16),
        out((width, half), bf16), out((width, length), bf16), out((width, length), bf16),
        out((width, 2 * length), bf16), out((half, model), f32), out((half, model), bf16), out((half, model), bf16),
        out((PARTS, 4 * count, depth, width), bf16),
    ]
    def rows(array):
        return pl.BlockSpec((array.shape[0] // steps, array.shape[1]), lambda s: (s, 0))

    def columns(array):
        return pl.BlockSpec((array.shape[0], array.shape[1] // steps), lambda s: (0, s))

    return pl.pallas_call(
        project_kernel,
        grid=(steps,),
        in_specs=[pl.BlockSpec(memory_space=pltpu.SMEM)] + [whole(a) for a in stacks] + [rows(a) for a in ins[4:]],
        out_specs=[columns(a) for a in outs[:7]] + [rows(a) for a in outs[7:10]] + [whole(outs[10])],
        out_shape=outs,
        scratch_shapes=[pltpu.VMEM((PARTS, width, model), bf16)],
        name="project",
        **limits(10 << 20),
    )(place, *ins)


def weigh_kernel(
    place_ref, own_rows, peer_rows, own_low, peer_low, phase_ref, own_dq, own_dk, own_dv, peer_dq, peer_dk, peer_dv,
    drel_ref, late_ref, early_ref, keep_ref, send_ref, total_sc, value_sc, small_sc,
):
    step = pl.program_id(0)

    @pl.when(step == 0)
    def _():
        total_sc[...] = jnp.zeros_like(total_sc)

    for i, pairs in enumerate((
        ((own_dq, own_low), (peer_dq, peer_low)),
        ((own_dk, own_rows), (peer_dk, peer_rows)),
        ((own_dv, own_rows), (peer_dv, peer_rows)),
        ((drel_ref, phase_ref),),
    )):
        for grad, rows in pairs:
            total_sc[i] += jnp.dot(grad[...].astype(bf16), rows[...], preferred_element_type=f32)

    @pl.when(step == pl.num_programs(0) - 1)
    def _():
        columns, lines, _, width = keep_ref.shape
        depth = value_sc.shape[1]
        for i in range(PARTS):
            value_sc[...] = total_sc[i].astype(bf16).T.reshape(value_sc.shape)
            for core, ref in enumerate((keep_ref, send_ref)):
                for column in range(columns):
                    for line in range(lines):
                        ref[column, line, i * depth:(i + 1) * depth] = value_sc[spot(place_ref, core, column, line)]
        first, last = LATE, LATE + early_ref.shape[0]
        small_sc[...] = jnp.zeros_like(small_sc)
        small_sc[:first] = late_ref[...].T[:first]
        small_sc[first:last] = early_ref[:, :width]
        small_sc[last : 2 * last - first] = early_ref[:, width:]
        small = small_sc[...].astype(bf16)
        for column in range(columns):
            for line in range(lines):
                for ref in (keep_ref, send_ref):
                    ref[column, line, PARTS * depth:] = small


def weigh(place, own_rows, peer_rows, own_low, peer_low, phase, own_grads, peer_grads, drel, late, early, blocks, steps=4):
    model = own_rows.shape[1]
    depth = model // blocks
    width = drel.shape[0]
    extra = LATE + 2 * early.shape[0]
    extra += -extra % 16

    def rows(array):
        return pl.BlockSpec((array.shape[0] // steps, model), lambda s: (s, 0))

    def columns(array):
        return pl.BlockSpec((width, array.shape[1] // steps), lambda s: (0, s))

    ins = [own_rows, peer_rows, own_low, peer_low, phase]
    grads = [*own_grads, *peer_grads, drel]
    pieces = out((2, blocks // 4, PARTS * depth + extra, width), bf16)
    return pl.pallas_call(
        weigh_kernel,
        grid=(steps,),
        in_specs=[pl.BlockSpec(memory_space=pltpu.SMEM)] + [rows(a) for a in ins] + [columns(a) for a in grads] + [whole(late), whole(early)],
        out_specs=[whole(pieces)] * 2,
        out_shape=[pieces] * 2,
        scratch_shapes=[pltpu.VMEM((PARTS, width, model), f32), pltpu.VMEM((blocks, depth, width), bf16), pltpu.VMEM((extra, width), f32)],
        name="weigh",
        **limits(8 << 20),
    )(place, *ins, *grads, late, early)


def token_kernel(dq_ref, dk_ref, dv_ref, w_ref, *refs):
    model = refs[-1].shape[1]
    width = dk_ref.shape[0]
    half = dq_ref.shape[1]
    doubled = jnp.dot(dq_ref[...], pair_matrix(half, 1), preferred_element_type=f32).astype(bf16)
    total = None
    for i, grad in enumerate((doubled, dk_ref[...], dv_ref[...])):
        term = lax.dot_general(grad.T, w_ref[i].reshape(model, width), NT, preferred_element_type=f32)
        total = term if total is None else total + term
    if len(refs) > 1:
        high = refs[0][...].astype(bf16)
        low = (refs[0][...] - high.astype(f32)).astype(bf16)
        pairs = pair_matrix(half, 0)
        total = total + jnp.dot(pairs, high, preferred_element_type=f32) + jnp.dot(pairs, low, preferred_element_type=f32)
    refs[-1][...] = total.astype(refs[-1].dtype)


def token_grad(grads, weights, extra, dtype):
    length = grads[1].shape[1]
    model = weights.shape[1] * weights.shape[2]
    ins = [*grads, weights] + ([extra] if extra is not None else [])
    specs = [whole(a) for a in ins]
    result = out((length, model), dtype)
    return pl.pallas_call(
        token_kernel,
        grid=(1,),
        in_specs=specs,
        out_specs=whole(result),
        out_shape=result,
        name="token_grad",
        **limits(5 << 20),
    )(*ins)


def finish_kernel(place_ref, *refs, sources):
    total = refs[0][...].astype(f32)
    for ref in refs[1:sources]:
        total = total + ref[...].astype(f32)
    grads_ref, offsets_ref, sameness_ref, bias_ref, *vectors, total_sc = refs[sources:]
    parts, depth, width = grads_ref.shape
    for i in range(parts):
        grads_ref[i] = total[i * depth : (i + 1) * depth]
    total_sc[...] = total[parts * depth :]
    offsets_ref[...] = total_sc[:3]
    sameness_ref[...] = total_sc[3:LATE]
    count = len(vectors) + 4

    def row(n):
        return jnp.concatenate(
            [total_sc[LATE + n : LATE + n + 1], total_sc[LATE + count + n : LATE + count + n + 1]], axis=1
        )

    for n, ref in enumerate(vectors):
        ref[...] = row(n).reshape(ref.shape)
    n = len(vectors)
    first = place_ref[3] == 0
    bias = jnp.concatenate(
        [jnp.where(first, row(n), row(n + 2)), jnp.where(first, row(n + 1), row(n + 3))], axis=1
    )
    bias_ref[...] = bias.reshape(bias_ref.shape)


def finish(place, pieces, depth, model, hidden):
    extra = pieces[0].shape[0] - PARTS * depth
    width = pieces[0].shape[1]
    outs = [
        out((PARTS, depth, width), f32), out((3, width), f32), out((2, width), f32), out((hidden,), f32),
    ] + [out((model,), f32)] * 6
    return pl.pallas_call(
        partial(finish_kernel, sources=len(pieces)),
        grid=(1,),
        in_specs=[pl.BlockSpec(memory_space=pltpu.SMEM)] + [whole(a) for a in pieces],
        out_specs=[whole(a) for a in outs],
        out_shape=outs,
        scratch_shapes=[pltpu.VMEM((extra, width), f32)],
        name="finish",
        **limits(1 << 20),
    )(place, *pieces)


SPLIT = 1


def layer_norm(values_in):
    row_mean = jnp.mean(values_in, axis=1, keepdims=True)
    centred = values_in - row_mean
    variance = jnp.mean(centred * centred, axis=1, keepdims=True)
    scale = lax.rsqrt(variance + epsilon)
    return centred * scale, scale


def layer_norm_back(grad, normed, scale, gain):
    inner = grad * gain
    return scale * (
        inner
        - jnp.mean(inner, axis=1, keepdims=True)
        - normed * jnp.mean(inner * normed, axis=1, keepdims=True)
    )


def row_sum(values_in):
    return jnp.sum(values_in, axis=0, keepdims=True)


def middle_kernel(
    place_ref, pooled_ref, mixed_ref, sent_ref, vec_ref, cot_ref, own_c_ref, peer_c_ref, weights_ref, own_bias_ref, peer_bias_ref,
    result_ref, dfirst_ref, own_dm_ref, peer_dm_ref, keep_c_ref, send_c_ref, sums_ref,
    keep_w_ref, send_w_ref, keep_n_ref, send_n_ref,
    held_sc, held_sem, slope_sc, act_sc, dhid_sc, first_sc, norm_sc, scale_sc, total_sc, low_sc, low_t_sc, dsec_sc, dsec_t_sc,
    *, chunks,
):
    step = pl.program_id(0)
    model = pooled_ref.shape[1]
    rows = pooled_ref.shape[0]
    part = own_bias_ref.shape[-1]
    each = own_bias_ref.shape[0]

    def fetch(chunk, kind):
        return pltpu.make_async_copy(
            weights_ref.at[:, chunk // each, :, pl.ds((kind * each + chunk % each) * part, part)],
            held_sc.at[chunk, kind],
            held_sem.at[chunk, kind],
        )
    vec = vec_ref[...]

    def store(value, keep_ref, send_ref, *half):
        value = value.astype(bf16)
        for n, ref in enumerate((keep_ref, send_ref)):
            piece = value[n * (model // 2) : (n + 1) * (model // 2)]
            if half:
                shape = ref.shape[:1] + ref.shape[2:]
                ref[:, half[0]] = piece.reshape(shape)
            else:
                ref[...] = piece.reshape(ref.shape)

    def turn_rows(value, ref):
        value = value.T.reshape(ref.shape)
        count = ref.shape[0]
        for n in range(count):
            line, column, core = n // 4, n // 2 % 2, n % 2
            ref[
                (count // 2) * jnp.bitwise_xor(place_ref[2], core)
                + (count // 4) * jnp.bitwise_xor(place_ref[1], column)
                + jnp.bitwise_xor(place_ref[0], line)
            ] = value[n]

    postbias, scaling, centring = vec[0:1], vec[1:2], vec[2:3]
    narrowbias, rescale, recentre = vec[3:4], vec[4:5], vec[5:6]

    @pl.when(step == 0)
    def _():
        for chunk in range(chunks):
            for kind in range(2):
                fetch(chunk, kind).start()
        own_c = own_c_ref[...].reshape(model, -1)
        peer_c = peer_c_ref[...].reshape(model, -1)
        mixed = mixed_ref[...].astype(bf16).T
        sent = sent_ref[...].T
        branch = (
            lax.dot_general(mixed, own_c, NT, preferred_element_type=f32)
            + lax.dot_general(sent, peer_c, NT, preferred_element_type=f32)
            + postbias
        )
        normed, scale = layer_norm(pooled_ref[...] + branch)
        norm_sc[...] = normed
        scale_sc[...] = scale
        first = normed * scaling + centring
        first_sc[...] = first
        low = first.astype(bf16)
        low_sc[...] = low
        turn_rows(low, low_t_sc)
        total_sc[...] = jnp.zeros_like(total_sc)

    for chunk in range(chunks):

        @pl.when(step == chunk)
        def _():
            for kind in range(2):
                fetch(chunk, kind).wait()

    @pl.when(step < chunks)
    def _():
        wide = held_sc[step, 0].reshape(model, part)
        spot_bias = lax.rem(step, each)
        bias = jnp.where(step // each == place_ref[3], own_bias_ref[spot_bias], peer_bias_ref[spot_bias])
        hidden = jnp.dot(low_sc[...], wide, preferred_element_type=f32) + bias
        square = hidden * hidden
        root = math.sqrt(2.0 / math.pi)
        turn = jnp.tanh(hidden * (root + (root * 0.044715) * square))
        half = 0.5 * turn + 0.5
        act = (hidden * half).astype(bf16)
        slope_sc[step] = half + hidden * (half * (1.0 - turn)) * (root + (3.0 * root * 0.044715) * square)
        act_sc[step] = act
        narrow = held_sc[step, 1].reshape(model, part)
        total_sc[...] += lax.dot_general(act, narrow, NT, preferred_element_type=f32)

    @pl.when(step == chunks - 1)
    def _():
        normed, scale = layer_norm(first_sc[...] + (total_sc[...] + narrowbias))
        result_ref[...] = (normed * rescale + recentre).astype(bf16)
        cot = cot_ref[...].astype(f32)
        dfinal = layer_norm_back(cot, normed, scale, rescale)
        dsec = dfinal.astype(bf16)
        dsec_sc[...] = dsec
        turn_rows(dsec, dsec_t_sc)
        sums_ref[3:4] = row_sum(dsec.astype(f32))
        sums_ref[4:5] = row_sum(cot * normed)
        sums_ref[5:6] = row_sum(cot)
        total_sc[...] = dfinal

    back = step - chunks

    @pl.when((back >= 0) & (lax.rem(back, 2) == 0))
    def _():
        chunk = back // 2
        narrow = held_sc[chunk, 1].reshape(model, part)
        dact = jnp.dot(dsec_sc[...], narrow, preferred_element_type=f32)
        dhid = (dact * slope_sc[chunk]).astype(bf16)
        dhid_sc[...] = dhid
        bias_sum = row_sum(dhid.astype(f32))
        for n in range(part // model):
            sums_ref[pl.ds(6 + chunk * (part // model) + n, 1)] = bias_sum[:, n * model : (n + 1) * model]
        grad = jnp.dot(dsec_t_sc[...].reshape(model, rows), act_sc[chunk], preferred_element_type=f32)
        store(grad, keep_n_ref, send_n_ref)

    @pl.when((back >= 0) & (lax.rem(back, 2) == 1))
    def _():
        wide = held_sc[back // 2, 0].reshape(model, part)
        total_sc[...] += lax.dot_general(dhid_sc[...], wide, NT, preferred_element_type=f32)
        grad = jnp.dot(low_t_sc[...].reshape(model, rows), dhid_sc[...], preferred_element_type=f32)
        store(grad, keep_w_ref, send_w_ref)

    @pl.when(back == 2 * chunks - 1)
    def _():
        dfirst = total_sc[...]
        normed = norm_sc[...]
        dfirst_in = layer_norm_back(dfirst, normed, scale_sc[...], scaling)
        dfirst_ref[...] = dfirst_in
        dbranch = dfirst_in.astype(bf16)
        sums_ref[0:1] = row_sum(dbranch.astype(f32))
        sums_ref[1:2] = row_sum(dfirst * normed)
        sums_ref[2:3] = row_sum(dfirst)
        dbranch_t = dbranch.T
        turn_rows(dbranch, low_t_sc)
        turned = low_t_sc[...].reshape(model, rows)
        for half, c_ref, m_ref, dm_ref in (
            (0, own_c_ref, mixed_ref, own_dm_ref),
            (1, peer_c_ref, sent_ref, peer_dm_ref),
        ):
            c = c_ref[...].reshape(model, -1)
            dm_ref[...] = lax.dot_general(c, dbranch_t, TN, preferred_element_type=f32).astype(bf16)
            dc = lax.dot_general(turned, m_ref[...].astype(bf16), NT, preferred_element_type=f32)
            store(dc, keep_c_ref, send_c_ref, half)


def middle(place, pooled, mixed, sent, vec, cot, weights, own_bias, peer_bias):
    rows, model = pooled.shape
    blocks, halves, depth, columns = weights.shape
    width = mixed.shape[0]
    hidden = (columns - width) // 2
    part = hidden // SPLIT
    each = hidden // part
    chunks = halves * each

    def combiner_spec(flip):
        def index(step, place_ref):
            return (0, jnp.bitwise_xor(place_ref[3], flip), 0, 2 * hidden // width)

        return pl.BlockSpec((blocks, None, depth, width), index, pipeline_mode=pl.Buffered(1))

    def wide_index(step, place_ref):
        c = jnp.maximum(step - chunks - 1, 0) // 2
        return (jnp.bitwise_xor(c // each, place_ref[3]), 0, 0, 0, lax.rem(c, each))

    def narrow_index(step, place_ref):
        c = jnp.maximum(step - chunks, 0) // 2
        return (0, jnp.bitwise_xor(c // each, place_ref[3]), 0, 0, lax.rem(c, each))

    lines = blocks // 4
    outs = [
        out((rows, model), bf16), out((rows, model), f32), out(mixed.shape, bf16), out(mixed.shape, bf16),
        out((2, halves, lines, depth, width), bf16), out((2, halves, lines, depth, width), bf16), out((6 + halves * hidden // model, model), f32),
    ]
    wide_grads = out((halves, 2, lines, depth, hidden), bf16)
    narrow_grads = out((2, halves, lines, depth, hidden), bf16)
    whole_ins = [pooled, mixed, sent, vec, cot]
    grad_spec = [pl.BlockSpec((1, 2, lines, depth, part), wide_index)] * 2
    grad_spec += [pl.BlockSpec((2, 1, lines, depth, part), narrow_index)] * 2
    return pl.pallas_call(
        partial(middle_kernel, chunks=chunks),
        grid_spec=pltpu.PrefetchScalarGridSpec(
            num_scalar_prefetch=1,
            grid=(3 * chunks,),
            in_specs=[whole(a) for a in whole_ins]
            + [combiner_spec(0), combiner_spec(1), pl.BlockSpec(memory_space=pl.ANY)]
            + [pl.BlockSpec((each, 1, part), lambda s, p: (0, 0, 0))] * 2,
            out_specs=[whole(a) for a in outs]
            + grad_spec,
            scratch_shapes=[
                pltpu.VMEM((chunks, 2, blocks, depth, part), bf16),
                pltpu.SemaphoreType.DMA((chunks, 2)),
                pltpu.VMEM((chunks, rows, part), f32),
                pltpu.VMEM((chunks, rows, part), bf16),
                pltpu.VMEM((rows, part), bf16),
                pltpu.VMEM((rows, model), f32),
                pltpu.VMEM((rows, model), f32),
                pltpu.VMEM((rows, 1), f32),
                pltpu.VMEM((rows, model), f32),
                pltpu.VMEM((rows, model), bf16),
                pltpu.VMEM((blocks, depth, rows), bf16),
                pltpu.VMEM((rows, model), bf16),
                pltpu.VMEM((blocks, depth, rows), bf16),
            ],
        ),
        out_shape=outs + [wide_grads] * 2 + [narrow_grads] * 2,
        name="middle",
        **limits(24 << 20),
    )(place, *whole_ins, weights, weights, weights, own_bias.reshape(each, 1, part), peer_bias.reshape(each, 1, part))


def position_table(length, model_width):
    row_index = jnp.arange(2 * length, dtype=jnp.float32)
    offset = length - row_index
    half_width = model_width // 2
    frequency = jnp.exp(
        jnp.arange(half_width, dtype=jnp.float32) * (-math.log(10000.0) / half_width)
    )
    angles = offset[:, None] * frequency[None, :]
    return jnp.concatenate([jnp.sin(angles), jnp.cos(angles)], axis=1)


BLOCKS = 16


def swap(piece):
    return lax.ppermute(piece, "tensor", [(0, 1), (1, 0)])


def exchange(piece, mask):
    count = lax.axis_size("dp")
    return lax.ppermute(piece, "dp", [(i, i ^ mask) for i in range(count)])


def shards(
    tokens,
    segments,
    projections,
    combiner,
    offsets,
    sameness,
    postbias,
    scaling,
    centring,
    widener,
    widebias,
    narrower,
    narrowbias,
    rescale,
    recentre,
    cotangent,
):
    tensor_part = lax.axis_index("tensor")
    dp_part = lax.axis_index("dp")
    dp_count = lax.axis_size("dp")
    length, model = tokens.shape
    width = offsets.shape[1]
    hidden = widener.shape[1]
    blocks = BLOCKS
    depth = model // blocks
    direct = dp_count == blocks
    if direct:
        place = jnp.stack([dp_part // 4, (dp_part // 2) % 2, dp_part % 2, tensor_part]).astype(jnp.int32)
    else:
        place = jnp.stack([tensor_part * 0] * 3 + [tensor_part]).astype(jnp.int32)

    if direct:
        near0 = jnp.stack([projections] + [exchange(projections, 4 * d) for d in range(1, 4)])
        near1 = exchange(near0, 2)
        stacks = (near0, near1, exchange(near0, 1), exchange(near1, 1))
    else:
        every = lax.all_gather(projections, "dp", axis=1, tiled=True)
        every = every.reshape(PARTS, blocks // 4, 2, 2, depth, width).transpose(3, 2, 1, 0, 4, 5)
        stacks = (every[0, 0], every[0, 1], every[1, 0], every[1, 1])
    peer_tokens = swap(tokens)
    mine = jnp.concatenate([widener, narrower.T, combiner.T], axis=1)
    columns = mine.shape[1]
    weights = lax.all_gather(mine, ("dp", "tensor"), axis=0, tiled=False)
    if not direct:
        weights = weights.reshape(dp_count, 2, model // dp_count, columns).transpose(1, 0, 2, 3)
        weights = weights.reshape(2, blocks, depth, columns).transpose(1, 0, 2, 3)
    weights = weights.reshape(blocks, 2, depth, columns)
    small = jnp.concatenate([offsets, sameness], axis=0).T
    seg = jnp.where(tensor_part == 0, segments, jnp.concatenate([segments[1:], segments[:1]]))[:, None]
    vec = jnp.stack([postbias, scaling, centring, narrowbias, rescale, recentre, postbias, postbias])
    peer_tokens, peer_bias, small, seg, seg_q, vec = lax.optimization_barrier(
        (peer_tokens, swap(widebias), small, seg, seg[:, :, ::2], vec)
    )
    phase = position_table(length, model).astype(bf16)
    own_q, own_k, own_v, peer_q, peer_k, peer_v, relative, pooled, own_low, peer_low, inwards = project(
        place, stacks, tokens, peer_tokens, phase
    )
    own_args = (own_q, own_k, own_v, relative, small, seg_q, seg)
    peer_args = (peer_q, peer_k, peer_v, relative, small, seg_q, seg)
    peer_probs, peer_mixed, peer_mixed_low = attn_fwd(*peer_args, 1)
    sent_mixed = swap(peer_mixed_low)
    own_probs, own_mixed, own_mixed_low = attn_fwd(*own_args, 0)
    result, dfirst_in, own_dmixed, peer_dmixed, keep_c, send_c, early, keep_w, send_w, keep_n, send_n = middle(
        place, pooled, own_mixed_low, sent_mixed, vec, cotangent, weights, widebias, peer_bias
    )
    sent_dmixed = swap(peer_dmixed)
    half = width // DH // 2
    part = attn_bwd(0, *own_args, own_probs, own_mixed, own_dmixed, heads=(0, half))
    early = early + swap(early)
    if direct:

        def add(kept, sent):
            return (kept.astype(f32) + sent.astype(f32)).astype(bf16)

        wide = (keep_w, exchange(send_w, 1))
        narrow = (keep_n, exchange(send_n, 1))
        comb = (keep_c, exchange(send_c, 1))

        def joined(pick):
            return jnp.concatenate([add(*map(pick, narrow)), add(*map(pick, comb))], axis=-1)

        first_stage = (
            add(wide[0][0], wide[1][0]),
            add(wide[0][1], wide[1][1]),
            joined(lambda a: a[0]),
            joined(lambda a: a[1]),
        )
        part, early, first_stage, sent_dmixed = lax.optimization_barrier((part, early, first_stage, sent_dmixed))

    own_dq, own_dk, own_dv, drel, late = attn_bwd(
        0, *own_args, own_probs, own_mixed, own_dmixed, heads=(half, width // DH - half), base=part
    )
    peer_dq, peer_dk, peer_dv, drel, late = attn_bwd(
        1, *peer_args, peer_probs, peer_mixed, sent_dmixed, (drel, late)
    )
    own_grads = (own_dq, own_dk, own_dv)
    peer_grads = (peer_dq, peer_dk, peer_dv)
    if direct:
        wide = (first_stage[0], swap(first_stage[1]))
        narrow = (first_stage[2], exchange(first_stage[3], 2))
        wide = (add(wide[0][0], wide[1][0]), add(wide[0][1], wide[1][1]))
        narrow = (add(narrow[0][0], narrow[1][0]), add(narrow[0][1], narrow[1][1]))
        drel, wide, narrow = lax.optimization_barrier((drel, wide, narrow))
        wide = (wide[0], exchange(wide[1], 2))
        narrow = (narrow[0], swap(narrow[1]))
    keep, send = weigh(
        place, tokens, peer_tokens, own_low, peer_low, phase, own_grads, peer_grads, drel, late, early, blocks
    )
    if direct:
        keep, send, wide, narrow = lax.optimization_barrier((keep, send, wide, narrow))
        sent = exchange(send, 1)
        held = (add(keep[0], sent[0]), add(keep[1], sent[1]))
        last = [
            jnp.concatenate([add(wide[0][d], wide[1][d]), add(narrow[0][d], narrow[1][d])], axis=-1)
            for d in range(4)
        ]
        peer_grads, held, last = lax.optimization_barrier((peer_grads, held, last))
        held = (held[0], exchange(held[1], 2))
    peer_part = token_grad(peer_grads, inwards, None, bf16)
    sent_tokens = swap(peer_part)
    if direct:
        grads = last[0].astype(f32)
        for d in range(1, 4):
            grads = grads + exchange(last[d], 4 * d).astype(f32)
        held = [add(held[0][d], held[1][d]) for d in range(4)]
        own_grads, held, _ = lax.optimization_barrier((own_grads, held, peer_part))
        pieces = [held[0]] + [exchange(held[d], 4 * d) for d in range(1, 4)]
        own_part = token_grad(own_grads, inwards, dfirst_in, f32)
        tokens_grad, pieces = lax.optimization_barrier((own_part + sent_tokens.astype(f32), pieces))
    else:

        def ordered(kept, sent, turned):
            value = jnp.stack([kept, sent])
            value = value.transpose((3, 1, 0, 2, 4, 5) if turned else (3, 2, 0, 1, 4, 5))
            value = jnp.where(tensor_part == 0, value, value[:, :, :, ::-1])
            return value.transpose(3, 0, 1, 2, 4, 5).reshape(2, dp_count, model // dp_count, -1)

        grads = jnp.concatenate([ordered(keep_w, send_w, False), ordered(keep_n, send_n, True), ordered(keep_c, send_c, True)], axis=-1)
        grads = lax.psum_scatter(
            grads.transpose(1, 0, 2, 3).reshape(2 * dp_count, model // dp_count, columns),
            ("dp", "tensor"),
            scatter_dimension=0,
            tiled=True,
        )[0].astype(f32)
        big = jnp.stack([keep, send])[:, :, :, : PARTS * depth]
        big = big.reshape(2, 2, blocks // 4, PARTS, depth, width).transpose(3, 2, 1, 0, 4, 5)
        big = lax.psum_scatter(big.reshape(PARTS, model, width), "dp", scatter_dimension=1, tiled=True)
        extras = lax.psum(keep[0, 0, PARTS * depth :].astype(f32), "dp").astype(bf16)
        pieces = [jnp.concatenate([big.reshape(-1, width), extras], axis=0)]
        tokens_grad = token_grad(own_grads, inwards, dfirst_in, f32) + sent_tokens.astype(f32)
    projections_grad, offsets_grad, sameness_grad, bias_grad, *vectors = finish(
        place, pieces, depth if direct else model // dp_count, model, hidden
    )
    combiner_grad = grads[:, 2 * hidden :].T
    return (
        result,
        tokens_grad,
        projections_grad,
        combiner_grad,
        offsets_grad,
        sameness_grad,
        vectors[0],
        vectors[1],
        vectors[2],
        grads[:, :hidden],
        bias_grad,
        grads[:, hidden : 2 * hidden].T,
        vectors[3],
        vectors[4],
        vectors[5],
    )


def solution(mesh):
    placed = (
        P(("dp", "tensor"), None),
        P("dp", None),
        P(None, "dp", "tensor"),
        P("tensor", "dp"),
        P(None, "tensor"),
        P(None, "tensor"),
        P(),
        P(),
        P(),
        P("dp", "tensor"),
        P("tensor"),
        P("tensor", "dp"),
        P(),
        P(),
        P(),
        P(("dp", "tensor"), None),
    )
    return jax.shard_map(
        shards,
        mesh=mesh,
        in_specs=placed,
        out_specs=(
            P(("dp", "tensor"), None),
            P(("dp", "tensor"), None),
            P(None, "dp", "tensor"),
            P("tensor", "dp"),
            P(None, "tensor"),
            P(None, "tensor"),
            P(),
            P(),
            P(),
            P("dp", "tensor"),
            P("tensor"),
            P("tensor", "dp"),
            P(),
            P(),
            P(),
        ),
        check_vma=False,
    )
```

```python
from functools import partial
import math

import jax
import jax.numpy as jnp
from jax import lax
from jax.experimental import pallas as pl
from jax.experimental.pallas import tpu as pltpu
from jax.sharding import PartitionSpec as P

epsilon = 1e-05
bf16=jnp.bfloat16; f32=jnp.float32
DH=64
AUG=16
TN=(((0,),(0,)),((),()))
NT=(((1,),(1,)),((),()))
NN=(((1,),(0,)),((),()))

def split3(u):
    row=lax.broadcasted_iota(jnp.int32,u.shape,0)
    hi=u.astype(bf16).astype(f32)
    r1=u-hi
    mid=r1.astype(bf16).astype(f32)
    lo=r1-mid
    return jnp.where(row<3,hi,jnp.where(row<6,mid,jnp.where(row<9,lo,0.0))).astype(bf16)

def fwd_kernel(q_ref,k_ref,v_ref,r_ref,s_ref,segq_ref,segk_ref,p_ref,m_ref,ml_ref,c_sc,k_sc,*,tq):
    nq=q_ref.shape[1]; nk=k_ref.shape[1]
    q=q_ref[...].astype(f32)
    sm=s_ref[...]
    c_sc[:DH]=(q+sm[:,0:1]).astype(bf16)*jnp.asarray(0.125,bf16)
    pos=(q+sm[:,1:2]).astype(bf16)*jnp.asarray(0.125,bf16)
    typed=q+sm[:,2:3]
    t0=jnp.sum(typed*sm[:,3:4],axis=0,keepdims=True)*0.125
    t1=jnp.sum(typed*sm[:,4:5],axis=0,keepdims=True)*0.125
    kind=lax.rem(lax.broadcasted_iota(jnp.int32,(AUG,nq),0),3)
    c_sc[DH:]=split3(jnp.where(segq_ref[...]==kind,t1,t0))
    k_sc[:DH]=k_ref[...]
    rowk=lax.broadcasted_iota(jnp.int32,(AUG,nk),0)
    k_sc[DH:]=jnp.where((segk_ref[...]==lax.rem(rowk,3)) & (rowk<9),1.0,0.0).astype(bf16)

    tr=min(tq,128)
    def dense(b):
        i0=b*tq; w0=nk-2*i0-2*tq
        return lax.dot_general(pos[:,i0:i0+tq],r_ref[:,w0:w0+nk+2*tq],TN,preferred_element_type=f32)
    def cont(b):
        i0=b*tq
        return lax.dot_general(c_sc[:,i0:i0+tq],k_sc[...],TN,preferred_element_type=f32)
    def finish(b,c,d):
        i0=b*tq
        for t in range(tq//tr):
            lo=2*(tq-(t+1)*tr)
            g=pltpu.roll(d[t*tr:(t+1)*tr,lo:lo+nk+2*tr],nk,1,stride=2,stride_axis=0)
            s=c[t*tr:(t+1)*tr]+g[:,:nk]
            mx=jnp.max(s,axis=1,keepdims=True)
            e=jnp.exp(s-mx)
            l=jnp.sum(e,axis=1,keepdims=True)
            p_ref[i0+t*tr:i0+(t+1)*tr,:]=(e*(1.0/l)).astype(bf16)
    n=nq//tq
    prev=(cont(0),dense(0))
    for b in range(n):
        nxt=(cont(b+1),dense(b+1)) if b+1<n else None
        finish(b,*prev); prev=nxt
    mixed=lax.dot_general(v_ref[...],p_ref[...],NT,preferred_element_type=f32)
    m_ref[...]=mixed
    ml_ref[...]=mixed.astype(bf16)

def attn_fwd(qT,kT,vT,relT,small,segq,segk,row=0,tq=128):
    hd,nq=qT.shape; nk=kT.shape[1]; heads=hd//DH
    return pl.pallas_call(partial(fwd_kernel,tq=tq),grid=(heads,),
        in_specs=[pl.BlockSpec((DH,nq),lambda h:(h,0)),pl.BlockSpec((DH,nk),lambda h:(h,0)),pl.BlockSpec((DH,nk),lambda h:(h,0)),
          pl.BlockSpec((DH,2*nk),lambda h:(h,0)),pl.BlockSpec((DH,small.shape[1]),lambda h:(h,0)),
          pl.BlockSpec((None,1,nq),lambda h:(row,0,0)),pl.BlockSpec((None,1,nk),lambda h:(row,0,0))],
        out_specs=[pl.BlockSpec((None,nq,nk),lambda h:(h,0,0)),pl.BlockSpec((DH,nq),lambda h:(h,0)),pl.BlockSpec((DH,nq),lambda h:(h,0))],
        out_shape=[jax.ShapeDtypeStruct((heads,nq,nk),bf16),jax.ShapeDtypeStruct((hd,nq),f32),jax.ShapeDtypeStruct((hd,nq),bf16)],
        scratch_shapes=[pltpu.VMEM((DH+AUG,nq),bf16),pltpu.VMEM((DH+AUG,nk),bf16)],
        name="attend",**limits(15<<20))(qT,kT,vT,relT,small,segq,segk)

def bwd_kernel(q_ref,k_ref,v_ref,r_ref,s_ref,segq_ref,segk_ref,p_ref,m_ref,dm_ref,
               dq_ref,dk_ref,dv_ref,dr_ref,sg_ref,k_sc,v_sc,dm_sc,ds_sc,dg_sc,*,tq,first):
    nq=q_ref.shape[1]; nk=k_ref.shape[1]
    q=q_ref[...].astype(f32)
    sm=s_ref[...]
    content=(q+sm[:,0:1]).astype(bf16)*jnp.asarray(0.125,bf16)
    pos=(q+sm[:,1:2]).astype(bf16)*jnp.asarray(0.125,bf16)
    typed=q+sm[:,2:3]
    k_sc[:DH]=k_ref[...]
    rowk=lax.broadcasted_iota(jnp.int32,(AUG,nk),0)
    k_sc[DH:]=((segk_ref[...]==rowk)).astype(f32).astype(bf16)
    v_sc[:DH]=v_ref[...]
    v_sc[DH:]=jnp.where(rowk<3,1.0,0.0).astype(bf16)
    dm=dm_ref[...]
    dm_sc[:DH]=dm
    delta=-jnp.sum(dm.astype(f32)*m_ref[...],axis=0,keepdims=True)
    rowq=lax.broadcasted_iota(jnp.int32,(AUG,nq),0)
    hi=delta.astype(bf16).astype(f32); r1=delta-hi; mid=r1.astype(bf16).astype(f32); lo=r1-mid
    dm_sc[DH:]=jnp.where(rowq==0,hi,jnp.where(rowq==1,mid,jnp.where(rowq==2,lo,0.0))).astype(bf16)
    w=nk+2*tq
    flip=(lax.broadcasted_iota(jnp.int32,(tq,tq),0)+lax.broadcasted_iota(jnp.int32,(tq,tq),1)==tq-1).astype(f32).astype(bf16)
    def turn16(x):
        parts=[lax.dot_general(x[:,i:i+tq],flip,NN,preferred_element_type=f32) for i in range(0,nq,tq)]
        return jnp.concatenate(parts,axis=1).astype(bf16)
    def turn(x):
        hi=x.astype(bf16); r1=x-hi.astype(f32); mid=r1.astype(bf16); lo=(r1-mid.astype(f32)).astype(bf16)
        cat=jnp.concatenate([hi,mid,lo],axis=0)
        parts=[lax.dot_general(cat[:,i:i+tq],flip,NN,preferred_element_type=f32) for i in range(0,nq,tq)]
        y=jnp.concatenate(parts,axis=1)
        return y[:DH]+y[DH:2*DH]+y[2*DH:]

    @pl.when(pl.program_id(0)==0)
    def _():
        dg_sc[...]=jnp.zeros_like(dg_sc)
    def grad(b):
        i0=b*tq
        return lax.dot_general(dm_sc[:,i0:i0+tq],v_sc[...],TN,preferred_element_type=f32)
    def shift(b,dp):
        i0=b*tq
        w0=nk-2*i0-2*tq
        ds16=(p_ref[i0:i0+tq,:].astype(f32)*dp).astype(bf16)
        ds_sc[i0:i0+tq,:]=ds16
        back=lax.dot_general(flip,ds16,NN,preferred_element_type=f32)
        g=jnp.concatenate([back,jnp.zeros((tq,2*tq),f32)],axis=1)
        g=pltpu.roll(g,2,1,stride=2,stride_axis=0)
        dg_sc[i0:i0+tq,w0:w0+w]=g.astype(bf16)
    n=nq//tq
    for b in range(n): shift(b,grad(b))
    dv_ref[...]=lax.dot_general(dm,p_ref[...],NN,preferred_element_type=f32).astype(bf16)
    dk_ref[...]=lax.dot_general(content,ds_sc[...],NN,preferred_element_type=f32).astype(bf16)
    dc=lax.dot_general(k_sc[...],ds_sc[...],NT,preferred_element_type=f32)
    half=256
    tpos=turn16(pos)
    parts=[];drs=[]
    for c0 in range(0,nq,half):
        v0=nk-2*c0-2*half
        g=dg_sc[c0:c0+half,v0:v0+nk+2*half]
        parts.append(lax.dot_general(r_ref[:,v0:v0+nk+2*half],g,NT,preferred_element_type=f32))
        drs.append(lax.dot_general(tpos[:,c0:c0+half],g,NN,preferred_element_type=f32))
    dpos=turn(jnp.concatenate(parts,axis=1))*0.125
    z=jnp.zeros((DH,2*half),f32)
    dr=jnp.concatenate([z,drs[0]],axis=1)+jnp.concatenate([drs[1],z],axis=1)
    if first is None:
        dr_ref[...]=dr
    else:
        dr_ref[...]=first[0][...]+dr
    dcontent=dc[:DH]*0.125
    seg=dc[DH:]*0.125
    rows=lax.broadcasted_iota(jnp.int32,(AUG,nq),0)
    g1=jnp.sum(jnp.where(segq_ref[...]==rows,seg,0.0),axis=0,keepdims=True)
    g0=jnp.sum(seg,axis=0,keepdims=True)-g1
    dtyped=sm[:,3:4]*g0+sm[:,4:5]*g1
    dq_ref[...]=(dcontent+dpos+dtyped).astype(bf16)
    lane=lax.broadcasted_iota(jnp.int32,(DH,128),1)
    total=jnp.zeros((DH,128),f32)
    for n,val in enumerate((dcontent,dpos,dtyped,typed*g0,typed*g1)):
        total=jnp.where(lane==n,jnp.sum(val,axis=1,keepdims=True),total)
    if first is None:
        sg_ref[...]=total
    else:
        sg_ref[...]=first[1][...]+total

def bwd_kernel_first(*refs,tq,skip):
    bwd_kernel(*refs[:10],*refs[10+skip:],tq=tq,first=None)
def bwd_kernel_next(*refs,tq,skip):
    bwd_kernel(*refs[:10],*refs[12+skip:],tq=tq,first=refs[10:12])

def attn_bwd(which,qT,kT,vT,relT,small,segq,segk,probs,mixedT,dmixedT,carry=None,tq=256,heads=None,base=None):
    hd,nq=qT.shape; nk=kT.shape[1]
    start,count=heads or (0,hd//DH)
    row=lambda n: pl.BlockSpec((DH,n),lambda h:(h+start if start else h,0))
    ins=[row(nq),row(nk),row(nk),row(2*nk),row(small.shape[1]),pl.BlockSpec((None,1,nq),lambda h:(which,0,0)),pl.BlockSpec((None,1,nk),lambda h:(which,0,0)),
         pl.BlockSpec((None,nq,nk),lambda h:(h+start if start else h,0,0)),row(nq),row(nq)]
    args=[qT,kT,vT,relT,small,segq,segk,probs,mixedT,dmixedT]
    kern=bwd_kernel_first
    if carry is not None:
        ins+= [row(2*nk),row(128)]; args+=list(carry); kern=bwd_kernel_next
    aliases={}
    if base is not None:
        aliases={len(args)+n:n for n in range(5)}
        ins+=[pl.BlockSpec(memory_space=pl.ANY)]*5; args+=list(base)
    return pl.pallas_call(partial(kern,tq=tq,skip=len(aliases)),grid=(count,),in_specs=ins,
        out_specs=[row(nq),row(nk),row(nk),row(2*nk),row(128)],
        out_shape=[jax.ShapeDtypeStruct((hd,nq),bf16),jax.ShapeDtypeStruct((hd,nk),bf16),jax.ShapeDtypeStruct((hd,nk),bf16),
           jax.ShapeDtypeStruct((hd,2*nk),f32),jax.ShapeDtypeStruct((hd,128),f32)],
        input_output_aliases=aliases,
        scratch_shapes=[pltpu.VMEM((DH+AUG,nk),bf16),pltpu.VMEM((DH+AUG,nk),bf16),pltpu.VMEM((DH+AUG,nq),bf16),pltpu.VMEM((nq,nk),bf16),pltpu.VMEM((nq,2*nk),bf16)],
        name="attend_back",**limits((15*count//6)<<20))(*args)


PARTS = 4
LATE = 5


def pair_matrix(count, axis):
    shape = (count, 2 * count) if axis == 1 else (2 * count, count)
    longer = lax.broadcasted_iota(jnp.int32, shape, axis)
    shorter = lax.broadcasted_iota(jnp.int32, shape, 1 - axis)
    return jnp.where(jnp.right_shift(longer, 1) == shorter, 0.5, 0.0).astype(bf16)


def spot(place_ref, core, column, line):
    return (
        4 * jnp.bitwise_xor(place_ref[0], line)
        + 2 * jnp.bitwise_xor(place_ref[1], column)
        + jnp.bitwise_xor(place_ref[2], core)
    )


def project_kernel(
    place_ref, near0_ref, near1_ref, far0_ref, far1_ref, own_ref, peer_ref, phase_ref,
    own_q, own_k, own_v, peer_q, peer_k, peer_v, rel_ref, pooled_ref, own_low, peer_low, weights_ref,
    turned_sc,
):
    @pl.when(pl.program_id(0) == 0)
    def _():
        for i in range(PARTS):
            for n, ref in enumerate((near0_ref, near1_ref, far0_ref, far1_ref)):
                for d in range(ref.shape[0]):
                    weights_ref[i, spot(place_ref, n // 2, n % 2, d)] = ref[d, i]
            turned_sc[i] = weights_ref[i].reshape(-1, near0_ref.shape[3]).T

    pairs = pair_matrix(own_ref.shape[0] // 2, 1)

    def sequence(rows_ref, q_ref, k_ref, v_ref, low_ref, keep_ref):
        rows = rows_ref[...]
        pooled = jnp.dot(pairs, rows, preferred_element_type=f32)
        low = pooled.astype(bf16)
        low_ref[...] = low
        if keep_ref is not None:
            keep_ref[...] = pooled
        for i, (source, target) in enumerate(((low, q_ref), (rows, k_ref), (rows, v_ref))):
            target[...] = lax.dot_general(turned_sc[i], source, NT, preferred_element_type=f32).astype(bf16)

    sequence(own_ref, own_q, own_k, own_v, own_low, pooled_ref)
    sequence(peer_ref, peer_q, peer_k, peer_v, peer_low, None)
    rel_ref[...] = lax.dot_general(turned_sc[3], phase_ref[...], NT, preferred_element_type=f32).astype(bf16)


def whole(array):
    return pl.BlockSpec(array.shape, lambda *step: (0,) * array.ndim, pipeline_mode=pl.Buffered(1))


def out(shape, dtype):
    return jax.ShapeDtypeStruct(shape, dtype)


def limits(moved):
    return dict(
        compiler_params=pltpu.CompilerParams(vmem_limit_bytes=56 << 20),
        cost_estimate=pl.CostEstimate(flops=moved, bytes_accessed=moved, transcendentals=0),
    )


def project(place, stacks, tokens, peer_tokens, phase, steps=4):
    length, model = tokens.shape
    half = length // 2
    count, _, depth, width = stacks[0].shape
    ins = [*stacks, tokens, peer_tokens, phase]
    outs = [
        out((width, half), bf16), out((width, length), bf16), out((width, length), bf16),
        out((width, half), bf16), out((width, length), bf16), out((width, length), bf16),
        out((width, 2 * length), bf16), out((half, model), f32), out((half, model), bf16), out((half, model), bf16),
        out((PARTS, 4 * count, depth, width), bf16),
    ]
    def rows(array):
        return pl.BlockSpec((array.shape[0] // steps, array.shape[1]), lambda s: (s, 0))

    def columns(array):
        return pl.BlockSpec((array.shape[0], array.shape[1] // steps), lambda s: (0, s))

    return pl.pallas_call(
        project_kernel,
        grid=(steps,),
        in_specs=[pl.BlockSpec(memory_space=pltpu.SMEM)] + [whole(a) for a in stacks] + [rows(a) for a in ins[4:]],
        out_specs=[columns(a) for a in outs[:7]] + [rows(a) for a in outs[7:10]] + [whole(outs[10])],
        out_shape=outs,
        scratch_shapes=[pltpu.VMEM((PARTS, width, model), bf16)],
        name="project",
        **limits(10 << 20),
    )(place, *ins)


def weigh_kernel(
    place_ref, own_rows, peer_rows, own_low, peer_low, phase_ref, own_dq, own_dk, own_dv, peer_dq, peer_dk, peer_dv,
    drel_ref, late_ref, early_ref, keep_ref, send_ref, total_sc, value_sc, small_sc,
):
    step = pl.program_id(0)

    @pl.when(step == 0)
    def _():
        total_sc[...] = jnp.zeros_like(total_sc)

    for i, pairs in enumerate((
        ((own_dq, own_low), (peer_dq, peer_low)),
        ((own_dk, own_rows), (peer_dk, peer_rows)),
        ((own_dv, own_rows), (peer_dv, peer_rows)),
        ((drel_ref, phase_ref),),
    )):
        for grad, rows in pairs:
            total_sc[i] += jnp.dot(grad[...].astype(bf16), rows[...], preferred_element_type=f32)

    @pl.when(step == pl.num_programs(0) - 1)
    def _():
        columns, lines, _, width = keep_ref.shape
        depth = value_sc.shape[1]
        for i in range(PARTS):
            value_sc[...] = total_sc[i].astype(bf16).T.reshape(value_sc.shape)
            for core, ref in enumerate((keep_ref, send_ref)):
                for column in range(columns):
                    for line in range(lines):
                        ref[column, line, i * depth:(i + 1) * depth] = value_sc[spot(place_ref, core, column, line)]
        first, last = LATE, LATE + early_ref.shape[0]
        small_sc[...] = jnp.zeros_like(small_sc)
        small_sc[:first] = late_ref[...].T[:first]
        small_sc[first:last] = early_ref[:, :width]
        small_sc[last : 2 * last - first] = early_ref[:, width:]
        small = small_sc[...].astype(bf16)
        for column in range(columns):
            for line in range(lines):
                for ref in (keep_ref, send_ref):
                    ref[column, line, PARTS * depth:] = small


def weigh(place, own_rows, peer_rows, own_low, peer_low, phase, own_grads, peer_grads, drel, late, early, blocks, steps=4):
    model = own_rows.shape[1]
    depth = model // blocks
    width = drel.shape[0]
    extra = LATE + 2 * early.shape[0]
    extra += -extra % 16

    def rows(array):
        return pl.BlockSpec((array.shape[0] // steps, model), lambda s: (s, 0))

    def columns(array):
        return pl.BlockSpec((width, array.shape[1] // steps), lambda s: (0, s))

    ins = [own_rows, peer_rows, own_low, peer_low, phase]
    grads = [*own_grads, *peer_grads, drel]
    pieces = out((2, blocks // 4, PARTS * depth + extra, width), bf16)
    return pl.pallas_call(
        weigh_kernel,
        grid=(steps,),
        in_specs=[pl.BlockSpec(memory_space=pltpu.SMEM)] + [rows(a) for a in ins] + [columns(a) for a in grads] + [whole(late), whole(early)],
        out_specs=[whole(pieces)] * 2,
        out_shape=[pieces] * 2,
        scratch_shapes=[pltpu.VMEM((PARTS, width, model), f32), pltpu.VMEM((blocks, depth, width), bf16), pltpu.VMEM((extra, width), f32)],
        name="weigh",
        **limits(8 << 20),
    )(place, *ins, *grads, late, early)


def token_kernel(dq_ref, dk_ref, dv_ref, w_ref, *refs):
    model = refs[-1].shape[1]
    width = dk_ref.shape[0]
    half = dq_ref.shape[1]
    doubled = jnp.dot(dq_ref[...], pair_matrix(half, 1), preferred_element_type=f32).astype(bf16)
    total = None
    for i, grad in enumerate((doubled, dk_ref[...], dv_ref[...])):
        term = lax.dot_general(grad.T, w_ref[i].reshape(model, width), NT, preferred_element_type=f32)
        total = term if total is None else total + term
    if len(refs) > 1:
        high = refs[0][...].astype(bf16)
        low = (refs[0][...] - high.astype(f32)).astype(bf16)
        pairs = pair_matrix(half, 0)
        total = total + jnp.dot(pairs, high, preferred_element_type=f32) + jnp.dot(pairs, low, preferred_element_type=f32)
    refs[-1][...] = total.astype(refs[-1].dtype)


def token_grad(grads, weights, extra, dtype):
    length = grads[1].shape[1]
    model = weights.shape[1] * weights.shape[2]
    ins = [*grads, weights] + ([extra] if extra is not None else [])
    specs = [whole(a) for a in ins]
    result = out((length, model), dtype)
    return pl.pallas_call(
        token_kernel,
        grid=(1,),
        in_specs=specs,
        out_specs=whole(result),
        out_shape=result,
        name="token_grad",
        **limits(5 << 20),
    )(*ins)


def finish_kernel(place_ref, *refs, sources):
    total = refs[0][...].astype(f32)
    for ref in refs[1:sources]:
        total = total + ref[...].astype(f32)
    grads_ref, offsets_ref, sameness_ref, bias_ref, *vectors, total_sc = refs[sources:]
    parts, depth, width = grads_ref.shape
    for i in range(parts):
        grads_ref[i] = total[i * depth : (i + 1) * depth]
    total_sc[...] = total[parts * depth :]
    offsets_ref[...] = total_sc[:3]
    sameness_ref[...] = total_sc[3:LATE]
    count = len(vectors) + 4

    def row(n):
        return jnp.concatenate(
            [total_sc[LATE + n : LATE + n + 1], total_sc[LATE + count + n : LATE + count + n + 1]], axis=1
        )

    for n, ref in enumerate(vectors):
        ref[...] = row(n).reshape(ref.shape)
    n = len(vectors)
    first = place_ref[3] == 0
    bias = jnp.concatenate(
        [jnp.where(first, row(n), row(n + 2)), jnp.where(first, row(n + 1), row(n + 3))], axis=1
    )
    bias_ref[...] = bias.reshape(bias_ref.shape)


def finish(place, pieces, depth, model, hidden):
    extra = pieces[0].shape[0] - PARTS * depth
    width = pieces[0].shape[1]
    outs = [
        out((PARTS, depth, width), f32), out((3, width), f32), out((2, width), f32), out((hidden,), f32),
    ] + [out((model,), f32)] * 6
    return pl.pallas_call(
        partial(finish_kernel, sources=len(pieces)),
        grid=(1,),
        in_specs=[pl.BlockSpec(memory_space=pltpu.SMEM)] + [whole(a) for a in pieces],
        out_specs=[whole(a) for a in outs],
        out_shape=outs,
        scratch_shapes=[pltpu.VMEM((extra, width), f32)],
        name="finish",
        **limits(1 << 20),
    )(place, *pieces)


SPLIT = 1


def layer_norm(values_in):
    row_mean = jnp.mean(values_in, axis=1, keepdims=True)
    centred = values_in - row_mean
    variance = jnp.mean(centred * centred, axis=1, keepdims=True)
    scale = lax.rsqrt(variance + epsilon)
    return centred * scale, scale


def layer_norm_back(grad, normed, scale, gain):
    inner = grad * gain
    return scale * (
        inner
        - jnp.mean(inner, axis=1, keepdims=True)
        - normed * jnp.mean(inner * normed, axis=1, keepdims=True)
    )


def row_sum(values_in):
    return jnp.sum(values_in, axis=0, keepdims=True)


def middle_kernel(
    place_ref, pooled_ref, mixed_ref, sent_ref, vec_ref, cot_ref, own_c_ref, peer_c_ref, weights_ref, own_bias_ref, peer_bias_ref,
    result_ref, dfirst_ref, own_dm_ref, peer_dm_ref, keep_c_ref, send_c_ref, sums_ref,
    keep_w_ref, send_w_ref, keep_n_ref, send_n_ref,
    held_sc, held_sem, slope_sc, act_sc, dhid_sc, first_sc, norm_sc, scale_sc, total_sc, low_sc, low_t_sc, dsec_sc, dsec_t_sc,
    *, chunks,
):
    step = pl.program_id(0)
    model = pooled_ref.shape[1]
    rows = pooled_ref.shape[0]
    part = own_bias_ref.shape[-1]
    each = own_bias_ref.shape[0]

    def fetch(chunk, kind):
        return pltpu.make_async_copy(
            weights_ref.at[:, chunk // each, :, pl.ds((kind * each + chunk % each) * part, part)],
            held_sc.at[chunk, kind],
            held_sem.at[chunk, kind],
        )
    vec = vec_ref[...]

    def store(value, keep_ref, send_ref, *half):
        value = value.astype(bf16)
        for n, ref in enumerate((keep_ref, send_ref)):
            piece = value[n * (model // 2) : (n + 1) * (model // 2)]
            if half:
                shape = ref.shape[:1] + ref.shape[2:]
                ref[:, half[0]] = piece.reshape(shape)
            else:
                ref[...] = piece.reshape(ref.shape)

    def turn_rows(value, ref):
        value = value.T.reshape(ref.shape)
        count = ref.shape[0]
        for n in range(count):
            line, column, core = n // 4, n // 2 % 2, n % 2
            ref[
                (count // 2) * jnp.bitwise_xor(place_ref[2], core)
                + (count // 4) * jnp.bitwise_xor(place_ref[1], column)
                + jnp.bitwise_xor(place_ref[0], line)
            ] = value[n]

    postbias, scaling, centring = vec[0:1], vec[1:2], vec[2:3]
    narrowbias, rescale, recentre = vec[3:4], vec[4:5], vec[5:6]

    @pl.when(step == 0)
    def _():
        for chunk in range(chunks):
            for kind in range(2):
                fetch(chunk, kind).start()
        own_c = own_c_ref[...].reshape(model, -1)
        peer_c = peer_c_ref[...].reshape(model, -1)
        mixed = mixed_ref[...].astype(bf16).T
        sent = sent_ref[...].T
        branch = (
            lax.dot_general(mixed, own_c, NT, preferred_element_type=f32)
            + lax.dot_general(sent, peer_c, NT, preferred_element_type=f32)
            + postbias
        )
        normed, scale = layer_norm(pooled_ref[...] + branch)
        norm_sc[...] = normed
        scale_sc[...] = scale
        first = normed * scaling + centring
        first_sc[...] = first
        low = first.astype(bf16)
        low_sc[...] = low
        turn_rows(low, low_t_sc)
        total_sc[...] = jnp.zeros_like(total_sc)

    for chunk in range(chunks):

        @pl.when(step == chunk)
        def _():
            for kind in range(2):
                fetch(chunk, kind).wait()

    @pl.when(step < chunks)
    def _():
        wide = held_sc[step, 0].reshape(model, part)
        spot_bias = lax.rem(step, each)
        bias = jnp.where(step // each == place_ref[3], own_bias_ref[spot_bias], peer_bias_ref[spot_bias])
        hidden = jnp.dot(low_sc[...], wide, preferred_element_type=f32) + bias
        square = hidden * hidden
        root = math.sqrt(2.0 / math.pi)
        turn = jnp.tanh(hidden * (root + (root * 0.044715) * square))
        half = 0.5 * turn + 0.5
        act = (hidden * half).astype(bf16)
        slope_sc[step] = half + hidden * (half * (1.0 - turn)) * (root + (3.0 * root * 0.044715) * square)
        act_sc[step] = act
        narrow = held_sc[step, 1].reshape(model, part)
        total_sc[...] += lax.dot_general(act, narrow, NT, preferred_element_type=f32)

    @pl.when(step == chunks - 1)
    def _():
        normed, scale = layer_norm(first_sc[...] + (total_sc[...] + narrowbias))
        result_ref[...] = (normed * rescale + recentre).astype(bf16)
        cot = cot_ref[...].astype(f32)
        dfinal = layer_norm_back(cot, normed, scale, rescale)
        dsec = dfinal.astype(bf16)
        dsec_sc[...] = dsec
        turn_rows(dsec, dsec_t_sc)
        sums_ref[3:4] = row_sum(dsec.astype(f32))
        sums_ref[4:5] = row_sum(cot * normed)
        sums_ref[5:6] = row_sum(cot)
        total_sc[...] = dfinal

    back = step - chunks

    @pl.when((back >= 0) & (lax.rem(back, 2) == 0))
    def _():
        chunk = back // 2
        narrow = held_sc[chunk, 1].reshape(model, part)
        dact = jnp.dot(dsec_sc[...], narrow, preferred_element_type=f32)
        dhid = (dact * slope_sc[chunk]).astype(bf16)
        dhid_sc[...] = dhid
        bias_sum = row_sum(dhid.astype(f32))
        for n in range(part // model):
            sums_ref[pl.ds(6 + chunk * (part // model) + n, 1)] = bias_sum[:, n * model : (n + 1) * model]
        grad = jnp.dot(dsec_t_sc[...].reshape(model, rows), act_sc[chunk], preferred_element_type=f32)
        store(grad, keep_n_ref, send_n_ref)

    @pl.when((back >= 0) & (lax.rem(back, 2) == 1))
    def _():
        wide = held_sc[back // 2, 0].reshape(model, part)
        total_sc[...] += lax.dot_general(dhid_sc[...], wide, NT, preferred_element_type=f32)
        grad = jnp.dot(low_t_sc[...].reshape(model, rows), dhid_sc[...], preferred_element_type=f32)
        store(grad, keep_w_ref, send_w_ref)

    @pl.when(back == 2 * chunks - 1)
    def _():
        dfirst = total_sc[...]
        normed = norm_sc[...]
        dfirst_in = layer_norm_back(dfirst, normed, scale_sc[...], scaling)
        dfirst_ref[...] = dfirst_in
        dbranch = dfirst_in.astype(bf16)
        sums_ref[0:1] = row_sum(dbranch.astype(f32))
        sums_ref[1:2] = row_sum(dfirst * normed)
        sums_ref[2:3] = row_sum(dfirst)
        dbranch_t = dbranch.T
        turn_rows(dbranch, low_t_sc)
        turned = low_t_sc[...].reshape(model, rows)
        for half, c_ref, m_ref, dm_ref in (
            (0, own_c_ref, mixed_ref, own_dm_ref),
            (1, peer_c_ref, sent_ref, peer_dm_ref),
        ):
            c = c_ref[...].reshape(model, -1)
            dm_ref[...] = lax.dot_general(c, dbranch_t, TN, preferred_element_type=f32).astype(bf16)
            dc = lax.dot_general(turned, m_ref[...].astype(bf16), NT, preferred_element_type=f32)
            store(dc, keep_c_ref, send_c_ref, half)


def middle(place, pooled, mixed, sent, vec, cot, weights, own_bias, peer_bias):
    rows, model = pooled.shape
    blocks, halves, depth, columns = weights.shape
    width = mixed.shape[0]
    hidden = (columns - width) // 2
    part = hidden // SPLIT
    each = hidden // part
    chunks = halves * each

    def combiner_spec(flip):
        def index(step, place_ref):
            return (0, jnp.bitwise_xor(place_ref[3], flip), 0, 2 * hidden // width)

        return pl.BlockSpec((blocks, None, depth, width), index, pipeline_mode=pl.Buffered(1))

    def wide_index(step, place_ref):
        c = jnp.maximum(step - chunks - 1, 0) // 2
        return (jnp.bitwise_xor(c // each, place_ref[3]), 0, 0, 0, lax.rem(c, each))

    def narrow_index(step, place_ref):
        c = jnp.maximum(step - chunks, 0) // 2
        return (0, jnp.bitwise_xor(c // each, place_ref[3]), 0, 0, lax.rem(c, each))

    lines = blocks // 4
    outs = [
        out((rows, model), bf16), out((rows, model), f32), out(mixed.shape, bf16), out(mixed.shape, bf16),
        out((2, halves, lines, depth, width), bf16), out((2, halves, lines, depth, width), bf16), out((6 + halves * hidden // model, model), f32),
    ]
    wide_grads = out((halves, 2, lines, depth, hidden), bf16)
    narrow_grads = out((2, halves, lines, depth, hidden), bf16)
    whole_ins = [pooled, mixed, sent, vec, cot]
    grad_spec = [pl.BlockSpec((1, 2, lines, depth, part), wide_index)] * 2
    grad_spec += [pl.BlockSpec((2, 1, lines, depth, part), narrow_index)] * 2
    return pl.pallas_call(
        partial(middle_kernel, chunks=chunks),
        grid_spec=pltpu.PrefetchScalarGridSpec(
            num_scalar_prefetch=1,
            grid=(3 * chunks,),
            in_specs=[whole(a) for a in whole_ins]
            + [combiner_spec(0), combiner_spec(1), pl.BlockSpec(memory_space=pl.ANY)]
            + [pl.BlockSpec((each, 1, part), lambda s, p: (0, 0, 0))] * 2,
            out_specs=[whole(a) for a in outs]
            + grad_spec,
            scratch_shapes=[
                pltpu.VMEM((chunks, 2, blocks, depth, part), bf16),
                pltpu.SemaphoreType.DMA((chunks, 2)),
                pltpu.VMEM((chunks, rows, part), f32),
                pltpu.VMEM((chunks, rows, part), bf16),
                pltpu.VMEM((rows, part), bf16),
                pltpu.VMEM((rows, model), f32),
                pltpu.VMEM((rows, model), f32),
                pltpu.VMEM((rows, 1), f32),
                pltpu.VMEM((rows, model), f32),
                pltpu.VMEM((rows, model), bf16),
                pltpu.VMEM((blocks, depth, rows), bf16),
                pltpu.VMEM((rows, model), bf16),
                pltpu.VMEM((blocks, depth, rows), bf16),
            ],
        ),
        out_shape=outs + [wide_grads] * 2 + [narrow_grads] * 2,
        name="middle",
        **limits(24 << 20),
    )(place, *whole_ins, weights, weights, weights, own_bias.reshape(each, 1, part), peer_bias.reshape(each, 1, part))


def position_table(length, model_width):
    row_index = jnp.arange(2 * length, dtype=jnp.float32)
    offset = length - row_index
    half_width = model_width // 2
    frequency = jnp.exp(
        jnp.arange(half_width, dtype=jnp.float32) * (-math.log(10000.0) / half_width)
    )
    angles = offset[:, None] * frequency[None, :]
    return jnp.concatenate([jnp.sin(angles), jnp.cos(angles)], axis=1)


BLOCKS = 16


def swap(piece):
    return lax.ppermute(piece, "tensor", [(0, 1), (1, 0)])


def exchange(piece, mask):
    count = lax.axis_size("dp")
    return lax.ppermute(piece, "dp", [(i, i ^ mask) for i in range(count)])


def shards(
    tokens,
    segments,
    projections,
    combiner,
    offsets,
    sameness,
    postbias,
    scaling,
    centring,
    widener,
    widebias,
    narrower,
    narrowbias,
    rescale,
    recentre,
    cotangent,
):
    tensor_part = lax.axis_index("tensor")
    dp_part = lax.axis_index("dp")
    dp_count = lax.axis_size("dp")
    length, model = tokens.shape
    width = offsets.shape[1]
    hidden = widener.shape[1]
    blocks = BLOCKS
    depth = model // blocks
    direct = dp_count == blocks
    if direct:
        place = jnp.stack([dp_part // 4, (dp_part // 2) % 2, dp_part % 2, tensor_part]).astype(jnp.int32)
    else:
        place = jnp.stack([tensor_part * 0] * 3 + [tensor_part]).astype(jnp.int32)

    if direct:
        near0 = jnp.stack([projections] + [exchange(projections, 4 * d) for d in range(1, 4)])
        near1 = exchange(near0, 2)
        stacks = (near0, near1, exchange(near0, 1), exchange(near1, 1))
    else:
        every = lax.all_gather(projections, "dp", axis=1, tiled=True)
        every = every.reshape(PARTS, blocks // 4, 2, 2, depth, width).transpose(3, 2, 1, 0, 4, 5)
        stacks = (every[0, 0], every[0, 1], every[1, 0], every[1, 1])
    peer_tokens = swap(tokens)
    mine = jnp.concatenate([widener, narrower.T, combiner.T], axis=1)
    columns = mine.shape[1]
    weights = lax.all_gather(mine, ("dp", "tensor"), axis=0, tiled=False)
    if not direct:
        weights = weights.reshape(dp_count, 2, model // dp_count, columns).transpose(1, 0, 2, 3)
        weights = weights.reshape(2, blocks, depth, columns).transpose(1, 0, 2, 3)
    weights = weights.reshape(blocks, 2, depth, columns)
    small = jnp.concatenate([offsets, sameness], axis=0).T
    seg = jnp.where(tensor_part == 0, segments, jnp.concatenate([segments[1:], segments[:1]]))[:, None]
    vec = jnp.stack([postbias, scaling, centring, narrowbias, rescale, recentre, postbias, postbias])
    peer_tokens, peer_bias, small, seg, seg_q, vec = lax.optimization_barrier(
        (peer_tokens, swap(widebias), small, seg, seg[:, :, ::2], vec)
    )
    phase = position_table(length, model).astype(bf16)
    own_q, own_k, own_v, peer_q, peer_k, peer_v, relative, pooled, own_low, peer_low, inwards = project(
        place, stacks, tokens, peer_tokens, phase
    )
    own_args = (own_q, own_k, own_v, relative, small, seg_q, seg)
    peer_args = (peer_q, peer_k, peer_v, relative, small, seg_q, seg)
    peer_probs, peer_mixed, peer_mixed_low = attn_fwd(*peer_args, 1)
    sent_mixed = swap(peer_mixed_low)
    own_probs, own_mixed, own_mixed_low = attn_fwd(*own_args, 0)
    result, dfirst_in, own_dmixed, peer_dmixed, keep_c, send_c, early, keep_w, send_w, keep_n, send_n = middle(
        place, pooled, own_mixed_low, sent_mixed, vec, cotangent, weights, widebias, peer_bias
    )
    sent_dmixed = swap(peer_dmixed)
    half = width // DH // 2
    part = attn_bwd(0, *own_args, own_probs, own_mixed, own_dmixed, heads=(0, half))
    early = early + swap(early)
    if direct:

        def add(kept, sent):
            return (kept.astype(f32) + sent.astype(f32)).astype(bf16)

        wide = (keep_w, exchange(send_w, 1))
        narrow = (keep_n, exchange(send_n, 1))
        comb = (keep_c, exchange(send_c, 1))

        def joined(pick):
            return jnp.concatenate([add(*map(pick, narrow)), add(*map(pick, comb))], axis=-1)

        first_stage = (
            add(wide[0][0], wide[1][0]),
            add(wide[0][1], wide[1][1]),
            joined(lambda a: a[0]),
            joined(lambda a: a[1]),
        )
        part, early, first_stage, sent_dmixed = lax.optimization_barrier((part, early, first_stage, sent_dmixed))

    own_dq, own_dk, own_dv, drel, late = attn_bwd(
        0, *own_args, own_probs, own_mixed, own_dmixed, heads=(half, width // DH - half), base=part
    )
    peer_dq, peer_dk, peer_dv, drel, late = attn_bwd(
        1, *peer_args, peer_probs, peer_mixed, sent_dmixed, (drel, late)
    )
    own_grads = (own_dq, own_dk, own_dv)
    peer_grads = (peer_dq, peer_dk, peer_dv)
    if direct:
        wide = (first_stage[0], swap(first_stage[1]))
        narrow = (first_stage[2], exchange(first_stage[3], 2))
        wide = (add(wide[0][0], wide[1][0]), add(wide[0][1], wide[1][1]))
        narrow = (add(narrow[0][0], narrow[1][0]), add(narrow[0][1], narrow[1][1]))
        drel, wide, narrow = lax.optimization_barrier((drel, wide, narrow))
        wide = (wide[0], exchange(wide[1], 2))
        narrow = (narrow[0], swap(narrow[1]))
    keep, send = weigh(
        place, tokens, peer_tokens, own_low, peer_low, phase, own_grads, peer_grads, drel, late, early, blocks
    )
    if direct:
        keep, send, wide, narrow = lax.optimization_barrier((keep, send, wide, narrow))
        sent = exchange(send, 1)
        held = (add(keep[0], sent[0]), add(keep[1], sent[1]))
        last = [
            jnp.concatenate([add(wide[0][d], wide[1][d]), add(narrow[0][d], narrow[1][d])], axis=-1)
            for d in range(4)
        ]
        peer_grads, last = lax.optimization_barrier((peer_grads, last))
        peer_grads, held = lax.optimization_barrier((peer_grads, held))
        held = (held[0], exchange(held[1], 2))
    peer_part = token_grad(peer_grads, inwards, None, bf16)
    sent_tokens = swap(peer_part)
    if direct:
        last = [last[0]] + [exchange(last[d], 4 * d) for d in range(1, 4)]
        held = [add(held[0][d], held[1][d]) for d in range(4)]
        held, last = lax.optimization_barrier((held, last))
        grads = last[0].astype(f32)
        for d in range(1, 4):
            grads = grads + last[d].astype(f32)
        own_grads, held, _ = lax.optimization_barrier((own_grads, held, peer_part))
        pieces = [held[0]] + [exchange(held[d], 4 * d) for d in range(1, 4)]
        own_part = token_grad(own_grads, inwards, dfirst_in, f32)
        tokens_grad, pieces = lax.optimization_barrier((own_part + sent_tokens.astype(f32), pieces))
    else:

        def ordered(kept, sent, turned):
            value = jnp.stack([kept, sent])
            value = value.transpose((3, 1, 0, 2, 4, 5) if turned else (3, 2, 0, 1, 4, 5))
            value = jnp.where(tensor_part == 0, value, value[:, :, :, ::-1])
            return value.transpose(3, 0, 1, 2, 4, 5).reshape(2, dp_count, model // dp_count, -1)

        grads = jnp.concatenate([ordered(keep_w, send_w, False), ordered(keep_n, send_n, True), ordered(keep_c, send_c, True)], axis=-1)
        grads = lax.psum_scatter(
            grads.transpose(1, 0, 2, 3).reshape(2 * dp_count, model // dp_count, columns),
            ("dp", "tensor"),
            scatter_dimension=0,
            tiled=True,
        )[0].astype(f32)
        big = jnp.stack([keep, send])[:, :, :, : PARTS * depth]
        big = big.reshape(2, 2, blocks // 4, PARTS, depth, width).transpose(3, 2, 1, 0, 4, 5)
        big = lax.psum_scatter(big.reshape(PARTS, model, width), "dp", scatter_dimension=1, tiled=True)
        extras = lax.psum(keep[0, 0, PARTS * depth :].astype(f32), "dp").astype(bf16)
        pieces = [jnp.concatenate([big.reshape(-1, width), extras], axis=0)]
        tokens_grad = token_grad(own_grads, inwards, dfirst_in, f32) + sent_tokens.astype(f32)
    projections_grad, offsets_grad, sameness_grad, bias_grad, *vectors = finish(
        place, pieces, depth if direct else model // dp_count, model, hidden
    )
    combiner_grad = grads[:, 2 * hidden :].T
    return (
        result,
        tokens_grad,
        projections_grad,
        combiner_grad,
        offsets_grad,
        sameness_grad,
        vectors[0],
        vectors[1],
        vectors[2],
        grads[:, :hidden],
        bias_grad,
        grads[:, hidden : 2 * hidden].T,
        vectors[3],
        vectors[4],
        vectors[5],
    )


def solution(mesh):
    placed = (
        P(("dp", "tensor"), None),
        P("dp", None),
        P(None, "dp", "tensor"),
        P("tensor", "dp"),
        P(None, "tensor"),
        P(None, "tensor"),
        P(),
        P(),
        P(),
        P("dp", "tensor"),
        P("tensor"),
        P("tensor", "dp"),
        P(),
        P(),
        P(),
        P(("dp", "tensor"), None),
    )
    return jax.shard_map(
        shards,
        mesh=mesh,
        in_specs=placed,
        out_specs=(
            P(("dp", "tensor"), None),
            P(("dp", "tensor"), None),
            P(None, "dp", "tensor"),
            P("tensor", "dp"),
            P(None, "tensor"),
            P(None, "tensor"),
            P(),
            P(),
            P(),
            P("dp", "tensor"),
            P("tensor"),
            P("tensor", "dp"),
            P(),
            P(),
            P(),
        ),
        check_vma=False,
    )
```
